32 devices in a mesh: dp: 4 (over x, core), row: 4 (over z), col: 2 (over y).
Axes of the slice: x: 2, y: 2, z: 4, core: 2. Of those that a mesh axis runs over, the one named last changes fastest.
Arguments:
- block_input: bfloat16 [7168, 2048], P(('dp', 'col'), 'row'), may hold values from -6 to 6
- segment_ids: int32 [7168], P(('dp', 'row')), may hold values from 0 to 111, never falling along the last dimension, each value on 1 to 448 neighbouring positions
- attn_gain: float32 [2048], P('row'), may hold values from 0.25 to 1.75
- mix_weight: bfloat16 [2048, 12288], P('row', 'col'), may hold values from -0.125 to 0.125
- decay_weight: bfloat16 [2048, 32], P('row', 'col'), may hold values from -0.125 to 0.125
- conv_weight: float32 [4, 8192], P(None, 'col'), may hold values from -2.5 to 2.5
- decay_log: float32 [16], P('col'), may hold values from -6.5 to -2.5
- decay_bias: float32 [16], P('col'), may hold values from -1.5 to 1
- out_gain: float32 [256], replicated, may hold values from 0.25 to 1.75
- out_weight: bfloat16 [4096, 2048], P('col', 'row'), may hold values from -0.1875 to 0.1875
- ffn_gain: float32 [2048], P('row'), may hold values from 0.25 to 1.75
- gate_weight: bfloat16 [2048, 5632], P('row', 'col'), may hold values from -0.125 to 0.125
- up_weight: bfloat16 [2048, 5632], P('row', 'col'), may hold values from -0.125 to 0.125
- down_weight: bfloat16 [5632, 2048], P('col', 'row'), may hold values from -0.15625 to 0.15625
- cotangent: bfloat16 [7168, 2048], P(('dp', 'col'), 'row'), may hold values from -6 to 6
Outputs:
- block_output: bfloat16 [7168, 2048], P(('dp', 'col'), 'row')
- input_grad: bfloat16 [7168, 2048], P(('dp', 'col'), 'row')
- attn_gain_grad: float32 [2048], P('row')
- mix_weight_grad: float32 [2048, 12288], P('row', 'col')
- decay_weight_grad: float32 [2048, 32], P('row', 'col')
- conv_weight_grad: float32 [4, 8192], P(None, 'col')
- decay_log_grad: float32 [16], P('col')
- decay_bias_grad: float32 [16], P('col')
- out_gain_grad: float32 [256], replicated
- out_weight_grad: float32 [4096, 2048], P('col', 'row')
- ffn_gain_grad: float32 [2048], P('row')
- gate_weight_grad: float32 [2048, 5632], P('row', 'col')
- up_weight_grad: float32 [2048, 5632], P('row', 'col')
- down_weight_grad: float32 [5632, 2048], P('col', 'row')
The draws below stay inside these ranges and needn't reach their ends.
Inputs may be any that keep to these rules, and one draw needn't show every extreme that they name: `segment_ids`: segment numbers never fall along the tokens; each document has 1 to 448 tokens and one has exactly 448.
All inputs are finite; a program needn't handle non-finite values.
Results may differ from the reference program's by a relative error of at most 0.025.
Values may be sent and summed in bfloat16 or wider, within the bound.
A program may use at most 320 MiB of HBM per device.

```python
import math
from functools import partial
import jax
import jax.numpy as jnp
import numpy as np
from jax import lax

D = 2048
H = 16
DK = 128
DV = 256
FF = 5632
CONV = 4
BLOCK = 64
SEQ = 448
TOKENS = 7168


def shard_levels(rng, extent, cuts, least, largest):
    level, own = 1.0, jax.random.fold_in(rng, 6)
    for dim, shards_of in cuts:
        steps = jnp.exp(jax.random.uniform(jax.random.fold_in(own, dim), (shards_of,), jnp.float32, least / len(cuts), largest / len(cuts)))
        level = level * jnp.repeat(steps, extent[dim] // shards_of).reshape([-1 if axis == dim else 1 for axis in range(len(extent))])
    return level


def profile(number_of, total, most, slope):
    loads = [(1 << 20) // math.isqrt(grade ** slope) + 1 for grade in range(2, number_of + 1)]
    surplus, counts = total - most - (number_of - 1), [1] * (number_of - 1)
    while surplus > 0:
        movable = [i for i in range(number_of - 1) if counts[i] < most]
        whole, budget = sum([loads[i] for i in movable]), surplus
        for i in movable:
            extra = min(most - counts[i], max(1, budget * loads[i] // whole), surplus)
            counts[i] = counts[i] + extra
            surplus = surplus - extra
    return np.array([most] + counts)


def ragged(stream_key, amount, total, bound, lean):
    if amount == 2:
        one = jax.random.randint(stream_key, (), max(1, total - bound), min(bound, total - 1) + 1)
        return jnp.stack([one, total - one])
    tallies = jnp.asarray(profile(amount, total, bound, lean), jnp.int32)
    twos = (amount - 1) // 2
    donor, sink = tallies[1:1 + 2 * twos:2], tallies[2:2 + 2 * twos:2]
    room = jnp.minimum(donor - 1, bound - sink)
    passed = jax.random.randint(jax.random.fold_in(stream_key, 1), (twos,), 0, 1 << 20) % (room + 1)
    tallies = tallies.at[1:1 + 2 * twos:2].set(donor - passed).at[2:2 + 2 * twos:2].set(sink + passed)
    return tallies[jax.random.permutation(jax.random.fold_in(stream_key, 2), amount)]


def centred(key, dims, scale, reach, pieces=(), kind=jnp.bfloat16):
    factor_of = shard_levels(key, dims, pieces, -0.22, 0.18) if pieces else 1.0
    drawn = jax.random.normal(key, dims, jnp.float32) * scale * factor_of
    return jnp.minimum(jnp.maximum(drawn, -reach), reach).astype(kind)


def setup_inputs(seed: int = 0) -> dict:
    arg_keys = jax.random.split(jax.random.key(seed), 16)
    return {
        "block_input": centred(arg_keys[0], (TOKENS, D), 1.0, 6.0, ((0, 8), (1, 4))),
        "segment_ids": jnp.searchsorted(jnp.cumsum(ragged(arg_keys[1], TOKENS // 64, TOKENS, SEQ, 2)), jnp.arange(TOKENS), side="right").astype(jnp.int32),
        "attn_gain": jnp.clip(1.0 + 0.15 * jax.random.normal(arg_keys[2], (D,), jnp.float32), 0.25, 1.75),
        "mix_weight": centred(arg_keys[3], (D, H * (2 * DK + 2 * DV)), D ** -0.5, 0.125, ((0, 4), (1, 2))),
        "decay_weight": centred(arg_keys[4], (D, 2 * H), D ** -0.5, 0.125, ((0, 4), (1, 2))),
        "conv_weight": centred(arg_keys[5], (CONV, H * (2 * DK + DV)), 0.5, 2.5, ((1, 2),), jnp.float32),
        "decay_log": jnp.clip(-6.5 + 4.0 * jax.random.uniform(arg_keys[6], (H,), jnp.float32) ** shard_levels(arg_keys[6], (H,), ((0, 2),), -0.2, 0.2), -6.5, -2.5),
        "decay_bias": jnp.clip(-1.5 + 2.5 * jax.random.uniform(arg_keys[7], (H,), jnp.float32) ** shard_levels(arg_keys[7], (H,), ((0, 2),), -0.2, 0.2), -1.5, 1.0),
        "out_gain": jnp.clip(1.0 + 0.15 * jax.random.normal(arg_keys[8], (DV,), jnp.float32), 0.25, 1.75),
        "out_weight": centred(arg_keys[9], (H * DV, D), (H * DV // 4) ** -0.5, 0.1875, ((0, 2), (1, 4))),
        "ffn_gain": jnp.clip(1.0 + 0.15 * jax.random.normal(arg_keys[10], (D,), jnp.float32), 0.25, 1.75),
        "gate_weight": centred(arg_keys[11], (D, FF), D ** -0.5, 0.125, ((0, 4), (1, 2))),
        "up_weight": centred(arg_keys[12], (D, FF), D ** -0.5, 0.125, ((0, 4), (1, 2))),
        "down_weight": centred(arg_keys[13], (FF, D), (FF // 4) ** -0.5, 0.15625, ((0, 2), (1, 4))),
        "cotangent": centred(arg_keys[14], (TOKENS, D), 1.0, 6.0, ((0, 8), (1, 4))),
    }


@jax.custom_vjp
def low(v):
    return lax.optimization_barrier(v.astype(jnp.bfloat16)).astype(jnp.float32)

@jax.custom_vjp
def low_back(v):
    return v

def low_keep(v):
    return (low(v), None)

def low_pass(kept, grad):
    return (grad,)

def back_keep(v):
    return (v, None)

def back_low(kept, grad):
    return (low(grad),)
low.defvjp(low_keep, low_pass)
low_back.defvjp(back_keep, back_low)

def block_step(state, inputs):
    query, key, value, beta, decay, starts = inputs
    highest = lax.Precision.HIGHEST
    total = jnp.cumsum(decay, axis=-1)
    marks = jnp.cumsum(starts, axis=-1)
    position = jnp.arange(BLOCK)
    lower = position[:, None] >= position[None, :]
    strict = (position[:, None] > position[None, :]).astype(key.dtype)
    same = (marks[..., :, None] == marks[..., None, :]) & lower
    spread = total[..., :, None] - total[..., None, :]
    weight = jnp.where(same, jnp.exp(jnp.where(same, spread, 0.0)), 0.0)
    carried = jnp.where(marks == 0.0, jnp.exp(total), 0.0)
    inner = jnp.einsum('chtk,chsk->chts', key, key, precision=highest)
    system = jnp.eye(BLOCK, dtype=key.dtype) + beta[..., None] * weight * strict * inner
    known = jnp.einsum('chtk,chkv->chtv', key, state, precision=highest)
    target = beta[..., None] * (value - carried[..., None] * known)
    fresh = jax.scipy.linalg.solve_triangular(system, target, lower=True, unit_diagonal=True)
    scores = jnp.einsum('chtk,chsk->chts', query, key, precision=highest) * weight
    result = carried[..., None] * jnp.einsum('chtk,chkv->chtv', query, state, precision=highest)
    result = result + jnp.einsum('chts,chsv->chtv', scores, fresh, precision=highest)
    last_row = weight[..., -1, :]
    new_state = carried[..., -1][..., None, None] * state
    new_state = new_state + jnp.einsum('chsk,chsv->chkv', key * last_row[..., None], fresh, precision=highest)
    return (new_state, result)

def mix_core(proj, decay_in, conv_w, decay_log, decay_bias, out_gain, segments):
    count, length, width = proj.shape
    heads = decay_log.shape[0]
    value_dim = out_gain.shape[0]
    per_head = width // heads
    key_dim = (per_head - 2 * value_dim) // 2
    inner_width = 2 * key_dim + value_dim
    split = proj.reshape(count, length, heads, per_head)
    conv_in = split[..., :inner_width].reshape(count, length, heads * inner_width)
    gate_out = split[..., inner_width:]
    taps = conv_w.shape[0]
    summed = jnp.zeros_like(conv_in)
    for lag in range(taps):
        moved = jnp.pad(conv_in, ((0, 0), (lag, 0), (0, 0)))[:, :length]
        moved_seg = jnp.pad(segments, ((0, 0), (lag, 0)), constant_values=-1)[:, :length]
        keep = (moved_seg == segments).astype(proj.dtype)[..., None]
        summed = summed + conv_w[taps - 1 - lag] * moved * keep
    active = jax.nn.silu(summed).reshape(count, length, heads, inner_width)
    query = active[..., :key_dim]
    key = active[..., key_dim:2 * key_dim]
    value = active[..., 2 * key_dim:]
    query = query * lax.rsqrt(lax.optimization_barrier(jnp.sum(query * query, axis=-1, keepdims=True)) + 1e-06) * key_dim ** (-0.5)
    key = key * lax.rsqrt(lax.optimization_barrier(jnp.sum(key * key, axis=-1, keepdims=True)) + 1e-06)
    paired = decay_in.reshape(count, length, heads, 2)
    beta = jax.nn.sigmoid(paired[..., 0])
    decay = -jnp.exp(decay_log) * jax.nn.softplus(paired[..., 1] + decay_bias)
    prior = jnp.pad(segments, ((0, 0), (1, 0)), constant_values=-1)[:, :length]
    starts = jnp.broadcast_to((prior != segments).astype(proj.dtype)[..., None], (count, length, heads))
    blocks = length // BLOCK

    def to_blocks(values):
        values = values.reshape((count, blocks, BLOCK) + values.shape[2:])
        values = jnp.moveaxis(values, 1, 0)
        return jnp.moveaxis(values, 3, 2)
    inputs = (to_blocks(query), to_blocks(key), to_blocks(value), to_blocks(beta), to_blocks(decay), to_blocks(starts))
    state = jnp.zeros((count, heads, key_dim, value_dim), proj.dtype)
    state, outputs = lax.scan(jax.checkpoint(block_step), state, inputs)
    outputs = jnp.moveaxis(jnp.moveaxis(outputs, 3, 2), 0, 1).reshape(count, length, heads, value_dim)
    normed = outputs * lax.rsqrt(lax.optimization_barrier(jnp.mean(outputs * outputs, axis=-1, keepdims=True)) + 1e-05)
    normed = normed * out_gain * jax.nn.silu(gate_out)
    return normed.reshape(count, length, heads * value_dim)

def rms_norm(values, gain):
    return values * lax.rsqrt(lax.optimization_barrier(jnp.mean(values * values, axis=-1, keepdims=True)) + 1e-05) * gain

def layer_forward(segments, block_x, attn_gain, mix_weight, decay_weight, conv_weight, decay_log, decay_bias, out_gain, out_weight, ffn_gain, gate_weight, up_weight, down_weight):
    highest = lax.Precision.HIGHEST
    tokens = block_x.shape[0]
    first = low(rms_norm(block_x, attn_gain))
    proj = low_back(jnp.dot(first, mix_weight, precision=highest))
    decay_in = low_back(jnp.dot(first, decay_weight, precision=highest))
    count = segments.shape[0]
    mixed = mix_core(proj.reshape(count, SEQ, -1), decay_in.reshape(count, SEQ, -1), conv_weight, decay_log, decay_bias, out_gain, segments)
    mixed = low(mixed.reshape(tokens, -1))
    residual = block_x + low_back(jnp.dot(mixed, out_weight, precision=highest))
    second = low(rms_norm(residual, ffn_gain))
    gate = low_back(jnp.dot(second, gate_weight, precision=highest))
    up_values = low_back(jnp.dot(second, up_weight, precision=highest))
    hidden = low(jax.nn.silu(gate) * up_values)
    return residual + low_back(jnp.dot(hidden, down_weight, precision=highest))

def reference(block_input, segment_ids, attn_gain, mix_weight, decay_weight, conv_weight, decay_log, decay_bias, out_gain, out_weight, ffn_gain, gate_weight, up_weight, down_weight, cotangent):
    params = tuple((p.astype(jnp.float32) for p in (attn_gain, mix_weight, decay_weight, conv_weight, decay_log, decay_bias, out_gain, out_weight, ffn_gain, gate_weight, up_weight, down_weight)))
    group = 4 * SEQ
    groups = block_input.shape[0] // group
    items = (block_input.reshape(groups, group, -1), segment_ids.reshape(groups, 4, SEQ), cotangent.reshape(groups, group, -1))

    def one_group(totals, item):
        block_x, segments, grad_out = item
        result, backward = jax.vjp(partial(layer_forward, segments), block_x.astype(jnp.float32), *params)
        grads = backward(grad_out.astype(jnp.float32))
        totals = tuple((a + b for a, b in zip(totals, grads[1:])))
        return (totals, (result.astype(jnp.bfloat16), grads[0].astype(jnp.bfloat16)))
    start = tuple((jnp.zeros_like(p) for p in params))
    totals, (outputs, input_grads) = lax.scan(one_group, start, items)
    return (outputs.reshape(block_input.shape), input_grads.reshape(block_input.shape), totals[0], totals[1], totals[2], totals[3], totals[4], totals[5], totals[6], totals[7], totals[8], totals[9], totals[10], totals[11])
```

```python
import functools
import jax
import jax.numpy as jnp
from jax import lax
from jax.experimental import pallas as pl
from jax.experimental.pallas import tpu as pltpu
from jax.sharding import Mesh
from jax.sharding import PartitionSpec as P

F32, BF16 = jnp.float32, jnp.bfloat16
DK, DV, TAPS = 128, 256, 4
INNER = 2 * DK + DV
PER_HEAD = INNER + DV
NN = (((1,), (0,)), ((), ()))
NT = (((1,), (1,)), ((), ()))
TN = (((0,), (0,)), ((), ()))


def mm(left, right, dims=NN):
    return lax.dot_general(left.astype(BF16), right.astype(BF16), dims, preferred_element_type=F32)


def sigmoid(values):
    return 1.0 / (1.0 + jnp.exp(-values))


def softplus(values):
    return jnp.maximum(values, 0.0) + jnp.log(1.0 + jnp.exp(-jnp.abs(values)))


def shift_down(values, lag):
    return jnp.concatenate([jnp.zeros_like(values[:lag]), values[: values.shape[0] - lag]], axis=0)


def shift_up(values, lag):
    return jnp.concatenate([values[lag:], jnp.zeros_like(values[:lag])], axis=0)


def cumsum_rows(values):
    step = 1
    while step < values.shape[0]:
        values = values + shift_down(values, step)
        step *= 2
    return values


def reverse_cumsum_rows(values):
    step = 1
    while step < values.shape[0]:
        values = values + shift_up(values, step)
        step *= 2
    return values


def prepare(head, proj, extra, seg_col, seg_row, conv, log_ref, bias_ref):
    length = proj.shape[0]
    summed = conv[TAPS - 1 : TAPS] * proj[:, :INNER]
    keeps = []
    for lag in range(1, TAPS):
        keep = (shift_down(seg_col + 1.0, lag) == seg_col + 1.0).astype(F32)
        keeps.append(keep)
        summed = summed + conv[TAPS - 1 - lag : TAPS - lag] * (shift_down(proj[:, :INNER], lag) * keep)
    gate_conv = sigmoid(summed)
    active = summed * gate_conv
    lane = lax.broadcasted_iota(jnp.int32, extra.shape, 1)
    write = jnp.sum(jnp.where(lane == 2 * head, extra, 0.0), axis=1, keepdims=True)
    drive = jnp.sum(jnp.where(lane == 2 * head + 1, extra, 0.0), axis=1, keepdims=True)
    beta = sigmoid(write)
    drive = drive + bias_ref[head]
    rate = jnp.exp(jnp.full((1, 1), log_ref[head], F32))
    decay = -rate * softplus(drive)
    total = cumsum_rows(decay)
    rows = lax.broadcasted_iota(jnp.int32, (length, length), 0)
    cols = lax.broadcasted_iota(jnp.int32, (length, length), 1)
    total_row = jnp.sum(jnp.where(rows == cols, total, 0.0), axis=0, keepdims=True)
    weight = jnp.exp(jnp.where((rows >= cols) & (seg_col == seg_row), total - total_row, -1e30))
    raw_q, raw_k, value = active[:, :DK], active[:, DK : 2 * DK], active[:, 2 * DK :]
    scale_q = lax.rsqrt(jnp.sum(raw_q * raw_q, axis=1, keepdims=True) + 1e-06)
    scale_k = lax.rsqrt(jnp.sum(raw_k * raw_k, axis=1, keepdims=True) + 1e-06)
    query = (raw_q * scale_q * DK ** (-0.5)).astype(BF16)
    key = (raw_k * scale_k).astype(BF16)
    inner = mm(key, key, NT)
    strict = jnp.where(rows > cols, weight, 0.0)
    return dict(
        summed=summed, keeps=keeps, gate_conv=gate_conv, raw_q=raw_q, raw_k=raw_k, value=value,
        scale_q=scale_q, scale_k=scale_k, query=query, key=key, inner=inner, weight=weight,
        strict=strict, beta=beta, drive=drive, rate=rate, decay=decay, rows=rows, cols=cols,
    )


def forward_kernel(head, proj_ref, extra_ref, segc_ref, segr_ref, conv_ref, log_ref, bias_ref, gain_ref,
                   mixed_ref, solve_ref, work):
    length = proj_ref.shape[0]
    size = work.shape[0]
    p = prepare(head, proj_ref[...], extra_ref[...], segc_ref[...], segr_ref[0], conv_ref[...], log_ref, bias_ref)
    lower = p["beta"] * p["strict"] * p["inner"]
    if size != length:
        work[...] = jnp.zeros_like(work)
    work[0:length, 0:length] = lower
    tile = min(128, size)
    blocks = size // tile
    r = lax.broadcasted_iota(jnp.int32, (tile, tile), 0)
    c = lax.broadcasted_iota(jnp.int32, (tile, tile), 1)
    parts = [work[b * tile : (b + 1) * tile, b * tile : (b + 1) * tile] for b in range(blocks)]
    eye = (r == c).astype(F32)
    inv = [eye - jnp.where((r // 2 == c // 2), part, 0.0) for part in parts]
    step = 2
    while step < tile:
        pick = (r // (2 * step) == c // (2 * step)) & (r // step != c // step)
        lows = [mm(jnp.where(pick, part, 0.0), x) for part, x in zip(parts, inv)]
        inv = [x - mm(x, low) for x, low in zip(inv, lows)]
        step *= 2
    for b in range(blocks):
        work[b * tile : (b + 1) * tile, b * tile : (b + 1) * tile] = inv[b]
    step = tile
    while step < size:
        for start in range(0, size, 2 * step):
            mid, end = start + step, start + 2 * step
            low = mm(work[mid:end, start:mid], work[start:mid, start:mid])
            work[mid:end, start:mid] = -mm(work[mid:end, mid:end], low)
        step *= 2
    solve = work[0:length, 0:length].astype(BF16)
    solve_ref[0] = solve
    fresh = mm(solve, p["beta"] * p["value"])
    out = mm(mm(p["query"], p["key"], NT) * p["weight"], fresh)
    scale = lax.rsqrt(jnp.sum(out * out, axis=1, keepdims=True) * (1.0 / DV) + 1e-05)
    gate = proj_ref[:, INNER:]
    mixed_ref[...] = (out * scale * gain_ref[...] * (gate * sigmoid(gate))).astype(BF16)


def backward_kernel(head, last, *refs):
    if last:
        (proj_ref, extra_ref, segc_ref, segr_ref, conv_ref, log_ref, bias_ref, gain_ref, solve_ref, grad_ref,
         other_ref, gproj_ref, gconv_ref, gsmall_ref) = refs
    else:
        (proj_ref, extra_ref, segc_ref, segr_ref, conv_ref, log_ref, bias_ref, gain_ref, solve_ref, grad_ref,
         gproj_ref, gextra_ref, gconv_ref, gsmall_ref) = refs
    conv = conv_ref[...]
    p = prepare(head, proj_ref[...], extra_ref[...], segc_ref[...], segr_ref[0], conv, log_ref, bias_ref)
    weight, strict, inner, beta, value = p["weight"], p["strict"], p["inner"], p["beta"], p["value"]
    query, key = p["query"], p["key"]
    solve = solve_ref[0]
    fresh = mm(solve, beta * value).astype(BF16)
    scores = mm(query, key, NT)
    probs = (scores * weight).astype(BF16)
    out = mm(probs, fresh)
    scale = lax.rsqrt(jnp.sum(out * out, axis=1, keepdims=True) * (1.0 / DV) + 1e-05)
    normed = out * scale
    gate = proj_ref[:, INNER:]
    gate_sig = sigmoid(gate)
    grad = grad_ref[...].astype(F32)
    gain = gain_ref[...]
    through = grad * normed
    ggate = through * gain * (gate_sig * (1.0 + gate * (1.0 - gate_sig)))
    ggain = jnp.sum(through * (gate * gate_sig), axis=0, keepdims=True)
    gnormed = grad * gain * (gate * gate_sig)
    gout = scale * (gnormed - normed * (jnp.sum(gnormed * normed, axis=1, keepdims=True) * (1.0 / DV)))
    gout = gout.astype(BF16)
    gprobs = mm(gout, fresh, NT)
    gfresh = mm(probs, gout, TN)
    gtarget = mm(solve, gfresh, TN)
    glower = -mm(gtarget, fresh, NT) * strict
    gscores = gprobs * weight
    tilt = glower * inner
    flow = gscores * scores + beta * tilt
    gbeta = jnp.sum(tilt, axis=1, keepdims=True) + jnp.sum(gtarget * value, axis=1, keepdims=True)
    gscores = gscores.astype(BF16)
    ginner = (beta * glower).astype(BF16)
    gquery = mm(gscores, key)
    gkey = mm(gscores, query, TN) + mm(ginner, key) + mm(ginner, key, TN)
    col_flow = jnp.sum(flow, axis=0, keepdims=True)
    col_flow = jnp.sum(jnp.where(p["rows"] == p["cols"], col_flow, 0.0), axis=1, keepdims=True)
    gdecay = reverse_cumsum_rows(jnp.sum(flow, axis=1, keepdims=True) - col_flow)
    raw_q, raw_k, scale_q, scale_k = p["raw_q"], p["raw_k"], p["scale_q"], p["scale_k"]
    gq = (DK ** (-0.5)) * scale_q * (
        gquery - raw_q * (scale_q * scale_q * jnp.sum(gquery * raw_q, axis=1, keepdims=True)))
    gk = scale_k * (gkey - raw_k * (scale_k * scale_k * jnp.sum(gkey * raw_k, axis=1, keepdims=True)))
    gactive = jnp.concatenate([gq, gk, beta * gtarget], axis=1)
    gsummed = gactive * (p["gate_conv"] * (1.0 + p["summed"] * (1.0 - p["gate_conv"])))
    source = proj_ref[:, :INNER]
    gsource = conv[TAPS - 1 : TAPS] * gsummed
    gconv_ref[0, TAPS - 1 : TAPS, :] = jnp.sum(gsummed * source, axis=0, keepdims=True)
    for lag in range(1, TAPS):
        kept = gsummed * p["keeps"][lag - 1]
        gsource = gsource + conv[TAPS - 1 - lag : TAPS - lag] * shift_up(kept, lag)
        gconv_ref[0, TAPS - 1 - lag : TAPS - lag, :] = jnp.sum(kept * shift_down(source, lag), axis=0, keepdims=True)
    gdrive = -p["rate"] * gdecay * sigmoid(p["drive"])
    gwrite = gbeta * beta * (1.0 - beta)
    lane = lax.broadcasted_iota(jnp.int32, extra_ref.shape, 1)
    gextra = jnp.where(lane == 2 * head, gwrite, jnp.where(lane == 2 * head + 1, gdrive, 0.0))
    gproj_ref[:, :INNER] = gsource.astype(BF16)
    gproj_ref[:, INNER:PER_HEAD] = ggate.astype(BF16)
    if last:
        gproj_ref[:, PER_HEAD:] = (gextra + other_ref[...].astype(F32)).astype(BF16)
    else:
        gextra_ref[...] = gextra.astype(BF16)
    glog = jnp.sum(gdecay * p["decay"], axis=0, keepdims=True)
    gbias = jnp.sum(gdrive, axis=0, keepdims=True)
    lane = lax.broadcasted_iota(jnp.int32, (1, 128), 1)
    gsmall_ref[0, :, 0:DV] = ggain
    gsmall_ref[0, :, DV:] = jnp.where(lane == 0, glog, jnp.where(lane == 1, gbias, 0.0))


def common_specs(length, heads, head, extra_block):
    smem = pl.BlockSpec(memory_space=pltpu.SMEM)
    return [
        pl.BlockSpec((length, PER_HEAD), lambda s: (s, 0)),
        pl.BlockSpec((length, 128), lambda s: (s, extra_block)),
        pl.BlockSpec((length, 1), lambda s: (s, 0)),
        pl.BlockSpec((1, 1, length), lambda s: (s, 0, 0)),
        pl.BlockSpec((TAPS, INNER), lambda s: (0, head)),
        smem,
        smem,
        pl.BlockSpec((1, DV), lambda s: (0, 0)),
    ]


def mixer_forward(head, heads, proj, extra, extra_block, seg_col, seg_row, conv, log, bias, gain):
    count, _, length = seg_row.shape
    tokens = count * length
    size = 64
    while size < length:
        size *= 2
    return pl.pallas_call(
        functools.partial(forward_kernel, head),
        grid=(count,),
        in_specs=common_specs(length, heads, head, extra_block),
        out_specs=[
            pl.BlockSpec((length, DV), lambda s: (s, 0)),
            pl.BlockSpec((1, length, length), lambda s: (s, 0, 0)),
        ],
        out_shape=[
            jax.ShapeDtypeStruct((tokens, DV), BF16),
            jax.ShapeDtypeStruct((count, length, length), BF16),
        ],
        scratch_shapes=[pltpu.VMEM((size, size), F32)],
        compiler_params=pltpu.CompilerParams(vmem_limit_bytes=56 << 20),
        name="mixer_forward",
    )(proj, extra, seg_col, seg_row, conv, log, bias, gain)


def mixer_backward(head, heads, proj, extra, extra_block, seg_col, seg_row, conv, log, bias, gain, solve, grad, other):
    count, _, length = seg_row.shape
    tokens = count * length
    last = other is not None
    in_specs = common_specs(length, heads, head, extra_block) + [
        pl.BlockSpec((1, length, length), lambda s: (s, 0, 0)),
        pl.BlockSpec((length, DV), lambda s: (s, head)),
    ]
    args = [proj, extra, seg_col, seg_row, conv, log, bias, gain, solve, grad]
    width = PER_HEAD
    tail_specs = [
        pl.BlockSpec((1, TAPS, INNER), lambda s: (s, 0, 0)),
        pl.BlockSpec((1, 1, DV + 128), lambda s: (s, 0, 0)),
    ]
    tail_shapes = [
        jax.ShapeDtypeStruct((count, TAPS, INNER), F32),
        jax.ShapeDtypeStruct((count, 1, DV + 128), F32),
    ]
    mid_specs, mid_shapes = [], []
    if last:
        width += 128
        in_specs.append(pl.BlockSpec((length, 128), lambda s: (s, 0)))
        args.append(other)
    else:
        mid_specs = [pl.BlockSpec((length, 128), lambda s: (s, 0))]
        mid_shapes = [jax.ShapeDtypeStruct((tokens, 128), BF16)]
    return pl.pallas_call(
        functools.partial(backward_kernel, head, last),
        grid=(count,),
        in_specs=in_specs,
        out_specs=[pl.BlockSpec((length, width), lambda s: (s, 0))] + mid_specs + tail_specs,
        out_shape=[jax.ShapeDtypeStruct((tokens, width), BF16)] + mid_shapes + tail_shapes,
        compiler_params=pltpu.CompilerParams(vmem_limit_bytes=60 << 20),
        name="mixer_backward",
    )(*args)


MESH_ID = pl.DeviceIdType.MESH
ANY_SPEC = pl.BlockSpec(memory_space=pl.ANY)


def meet(targets):
    barrier = pltpu.get_barrier_semaphore()
    for target in targets:
        pl.semaphore_signal(barrier, inc=1, device_id=target, device_id_type=MESH_ID)
    pl.semaphore_wait(barrier, len(targets))


def remote(source, dest, send, recv, index, target):
    return pltpu.make_async_remote_copy(
        src_ref=source,
        dst_ref=dest,
        send_sem=send.at[index],
        recv_sem=recv.at[index],
        device_id=target,
        device_id_type=MESH_ID,
    )


def team_places(part_name):
    part, col = lax.axis_index(part_name), lax.axis_index("col")
    across, twin, other = lax.rem(part + 2, 4), part + 1 - 2 * lax.rem(part, 2), 1 - col
    targets = {
        "x": {part_name: across, "col": col},
        "y": {part_name: part, "col": other},
        "core": {part_name: twin, "col": col},
    }
    slots = [across * 2 + other, across * 2 + col, part * 2 + other, part * 2 + col]
    far = lax.rem(twin + 2, 4)
    twin_slots = [far * 2 + other, far * 2 + col, twin * 2 + other, twin * 2 + col]
    return targets, slots, twin_slots


def gather_kernel(part_name, src, out, keep, send, recv):
    targets, (diag, across, other, own), _ = team_places(part_name)
    half = src.shape[0] // 2
    first, second = pl.ds(0, half), pl.ds(half, half)
    meet(list(targets.values()))
    local = pltpu.make_async_copy(src, out.at[own], keep)
    local.start()
    x_first = remote(src.at[first], out.at[own, first], send, recv, 0, targets["x"])
    x_second = remote(src.at[second], out.at[own, second], send, recv, 1, targets["x"])
    y_second = remote(src.at[second], out.at[own, second], send, recv, 2, targets["y"])
    y_first = remote(src.at[first], out.at[own, first], send, recv, 3, targets["y"])
    core_own = remote(src, out.at[own], send, recv, 4, targets["core"])
    for copy in (x_first, y_second, core_own, x_second, y_first):
        copy.start()
    y_pass = remote(out.at[across, first], out.at[across, first], send, recv, 5, targets["y"])
    x_pass = remote(out.at[other, second], out.at[other, second], send, recv, 6, targets["x"])
    core_x = remote(out.at[across], out.at[across], send, recv, 7, targets["core"])
    core_y = remote(out.at[other], out.at[other], send, recv, 8, targets["core"])
    core_first = remote(out.at[diag, first], out.at[diag, first], send, recv, 9, targets["core"])
    core_second = remote(out.at[diag, second], out.at[diag, second], send, recv, 10, targets["core"])
    x_first.wait_recv()
    y_pass.start()
    y_second.wait_recv()
    x_pass.start()
    x_second.wait_recv()
    core_x.start()
    y_first.wait_recv()
    core_y.start()
    y_pass.wait_recv()
    core_first.start()
    x_pass.wait_recv()
    core_second.start()
    for copy in (core_own, core_x, core_y, core_first, core_second):
        copy.wait_recv()
    for copy in (x_first, x_second, y_second, y_first, core_own, y_pass, x_pass, core_x, core_y, core_first, core_second):
        copy.wait_send()
    local.wait()


def team_gather_kernel(part_name, values, ident):
    rows, width = values.shape
    return pl.pallas_call(
        functools.partial(gather_kernel, part_name),
        in_specs=[ANY_SPEC],
        out_specs=ANY_SPEC,
        out_shape=jax.ShapeDtypeStruct((8, rows, width), values.dtype),
        scratch_shapes=[
            pltpu.SemaphoreType.DMA,
            pltpu.SemaphoreType.DMA((11,)),
            pltpu.SemaphoreType.DMA((11,)),
        ],
        compiler_params=pltpu.CompilerParams(collective_id=ident, has_side_effects=True),
        name="team_gather",
    )(values).reshape(8 * rows, width)


def add_rows(dest, sources, start, count):
    @pl.loop(0, count // 16)
    def _(step):
        rows = pl.ds(pl.multiple_of(start + step * 16, 16), 16)
        total = sources[0][0][rows if sources[0][1] else pl.ds(pl.multiple_of(step * 16, 16), 16), :].astype(F32)
        for ref, whole in sources[1:]:
            total = total + ref[rows if whole else pl.ds(pl.multiple_of(step * 16, 16), 16), :].astype(F32)
        dest[rows, :] = total.astype(dest.dtype)


def scatter_kernel(part_name, src, out, mine, twin, sent, relay, final, keep, send, recv):
    targets, slots, twin_slots = team_places(part_name)
    rows = out.shape[0]
    half = rows // 2
    first, second = pl.ds(0, half), pl.ds(half, half)
    meet(list(targets.values()))
    swaps, loads = [], []
    for item in range(4):
        swaps.append(remote(src.at[twin_slots[item]], twin.at[item], send, recv, item, targets["core"]))
        loads.append(pltpu.make_async_copy(src.at[slots[item]], mine.at[item], keep.at[item]))
        swaps[item].start()
        loads[item].start()

    def arrive(item):
        loads[item].wait()
        swaps[item].wait_recv()

    def both(item):
        return [(mine.at[item], True), (twin.at[item], True)]

    relay_x = remote(sent.at[0, first], relay.at[0], send, recv, 4, targets["x"])
    relay_y = remote(sent.at[0, second], relay.at[1], send, recv, 5, targets["y"])
    x_first = remote(sent.at[1, first], final.at[0, first], send, recv, 6, targets["x"])
    x_second = remote(sent.at[1, second], final.at[0, second], send, recv, 7, targets["x"])
    y_second = remote(sent.at[2, second], final.at[1, second], send, recv, 8, targets["y"])
    y_first = remote(sent.at[2, first], final.at[1, first], send, recv, 9, targets["y"])
    arrive(0)
    add_rows(sent.at[0], both(0), 0, half)
    relay_x.start()
    add_rows(sent.at[0], both(0), half, half)
    relay_y.start()
    arrive(1)
    add_rows(sent.at[1], both(1), 0, half)
    x_first.start()
    arrive(2)
    add_rows(sent.at[2], both(2), half, half)
    y_second.start()
    relay_y.wait_recv()
    add_rows(sent.at[1], both(1) + [(relay.at[1], False)], half, half)
    x_second.start()
    relay_x.wait_recv()
    add_rows(sent.at[2], both(2) + [(relay.at[0], False)], 0, half)
    y_first.start()
    arrive(3)
    x_first.wait_recv()
    y_first.wait_recv()
    ends = both(3) + [(final.at[0], True), (final.at[1], True)]
    add_rows(out, ends, 0, half)
    x_second.wait_recv()
    y_second.wait_recv()
    add_rows(out, ends, half, half)
    for copy in swaps + [relay_x, relay_y, x_first, x_second, y_second, y_first]:
        copy.wait_send()


def team_scatter_kernel(part_name, values, ident):
    rows, width = values.shape[0] // 8, values.shape[1]
    return pl.pallas_call(
        functools.partial(scatter_kernel, part_name),
        in_specs=[ANY_SPEC],
        out_specs=pl.BlockSpec(memory_space=pltpu.VMEM),
        out_shape=jax.ShapeDtypeStruct((rows, width), F32),
        scratch_shapes=[
            pltpu.VMEM((4, rows, width), BF16),
            pltpu.VMEM((4, rows, width), BF16),
            pltpu.VMEM((3, rows, width), BF16),
            pltpu.VMEM((2, rows // 2, width), BF16),
            pltpu.VMEM((2, rows, width), BF16),
            pltpu.SemaphoreType.DMA((4,)),
            pltpu.SemaphoreType.DMA((10,)),
            pltpu.SemaphoreType.DMA((10,)),
        ],
        compiler_params=pltpu.CompilerParams(collective_id=ident, has_side_effects=True, vmem_limit_bytes=40 << 20),
        name="team_scatter",
    )(values.reshape(8, rows, width))


def spread_kernel(src, out, middle, keep, send, recv):
    row, col = lax.axis_index("row"), lax.axis_index("col")
    meet([{"col": 1 - col}] + [{"row": lax.rem(row + hop, 4)} for hop in range(1, 4)])
    hops = []
    for item in range(2):
        hops.append(remote(src.at[2 * item + 1 - col], middle.at[item], send, recv, item, {"col": 1 - col}))
        hops[item].start()

    def pieces(wait_first):
        for side in range(2):
            home = col if side == 0 else 1 - col
            for item in range(2):
                if side == 1 and wait_first:
                    hops[item].wait_recv()
                source = src.at[2 * item + col] if side == 0 else middle.at[item]
                to_row = 2 * home + item
                copy = pltpu.make_async_remote_copy(
                    src_ref=source,
                    dst_ref=out.at[row],
                    send_sem=send.at[2 + 2 * side + item],
                    recv_sem=recv.at[2 + row],
                    device_id={"row": to_row},
                    device_id_type=MESH_ID,
                )
                yield to_row == row, copy, pltpu.make_async_copy(source, out.at[row], keep)

    for here, far, near in pieces(True):
        pl.when(here)(near.start)
        pl.when(jnp.logical_not(here))(far.start)
    for hop in range(1, 4):
        index = lax.rem(row + hop, 4)
        pltpu.make_async_remote_copy(
            src_ref=src.at[0],
            dst_ref=out.at[index],
            send_sem=send.at[0],
            recv_sem=recv.at[2 + index],
            device_id={"row": index},
            device_id_type=MESH_ID,
        ).wait_recv()
    for here, far, near in pieces(False):
        pl.when(here)(near.wait)
        pl.when(jnp.logical_not(here))(far.wait_send)
    for hop in hops:
        hop.wait_send()


def spread_call(values, ident):
    tokens, width = values.shape[0] // 4, values.shape[1]
    return pl.pallas_call(
        spread_kernel,
        in_specs=[ANY_SPEC],
        out_specs=ANY_SPEC,
        out_shape=jax.ShapeDtypeStruct((4, tokens, width), values.dtype),
        scratch_shapes=[
            pltpu.VMEM((2, tokens, width), values.dtype),
            pltpu.SemaphoreType.DMA,
            pltpu.SemaphoreType.DMA((6,)),
            pltpu.SemaphoreType.DMA((6,)),
        ],
        compiler_params=pltpu.CompilerParams(collective_id=ident, has_side_effects=True),
        name="spread",
    )(values.reshape(4, tokens, width))


def deal(count, inward, part_name, rows_n, cols_n, refs):
    srcs, outs = refs[:count], refs[count : 2 * count]
    keep, send, recv = refs[2 * count :]
    row, col = lax.axis_index("row"), lax.axis_index("col")
    spot = row * cols_n + col

    def holder(index):
        return index, spot // rows_n

    def owner(index):
        place = col * rows_n + index
        return place // cols_n, lax.rem(place, cols_n)

    give, take = (owner, holder) if inward else (holder, owner)
    mark = row if inward else lax.rem(spot, rows_n)
    barrier = pltpu.get_barrier_semaphore()
    for index in range(rows_n):
        to_row, to_col = take(index)

        @pl.when((to_row != row) | (to_col != col))
        def _():
            pl.semaphore_signal(barrier, inc=1, device_id={"row": to_row, "col": to_col}, device_id_type=MESH_ID)

    kept = jnp.int32(0)
    for index in range(rows_n):
        to_row, to_col = give(index)
        kept = kept + ((to_row == row) & (to_col == col)).astype(jnp.int32)
    pl.semaphore_wait(barrier, rows_n - kept)

    def each(act_local, act_remote):
        for item in range(count):
            for index in range(rows_n):
                to_row, to_col = give(index)
                here = (to_row == row) & (to_col == col)

                @pl.when(here)
                def _():
                    act_local(pltpu.make_async_copy(srcs[item].at[index], outs[item].at[mark], keep.at[item]))

                @pl.when(jnp.logical_not(here))
                def _():
                    act_remote(
                        pltpu.make_async_remote_copy(
                            src_ref=srcs[item].at[index],
                            dst_ref=outs[item].at[mark],
                            send_sem=send.at[item, index],
                            recv_sem=recv.at[item, mark],
                            device_id={"row": to_row, "col": to_col},
                            device_id_type=MESH_ID,
                        )
                    )

    each(lambda copy: copy.start(), lambda copy: copy.start())
    for item in range(count):
        for index in range(rows_n):
            from_row, from_col = take(index)

            @pl.when((from_row != row) | (from_col != col))
            def _():
                pltpu.make_async_remote_copy(
                    src_ref=srcs[item].at[0],
                    dst_ref=outs[item].at[index],
                    send_sem=send.at[item, 0],
                    recv_sem=recv.at[item, index],
                    device_id={"row": from_row, "col": from_col},
                    device_id_type=MESH_ID,
                ).wait_recv()

    each(lambda copy: copy.wait(), lambda copy: copy.wait_send())


def deal_kernel(lay, inward, values, ident):
    count = len(values)
    shapes = [jax.ShapeDtypeStruct(v.shape, v.dtype) for v in values]

    def body(*refs):
        deal(count, inward, lay.part, lay.rows, lay.cols, refs)

    return pl.pallas_call(
        body,
        in_specs=[ANY_SPEC] * count,
        out_specs=[ANY_SPEC] * count,
        out_shape=shapes,
        scratch_shapes=[
            pltpu.SemaphoreType.DMA((count,)),
            pltpu.SemaphoreType.DMA((count, lay.rows)),
            pltpu.SemaphoreType.DMA((count, lay.rows)),
        ],
        compiler_params=pltpu.CompilerParams(collective_id=ident, has_side_effects=True),
        name="deal",
    )(*values)


SEQ = 448


def project(left, right):
    return jnp.dot(left, right, preferred_element_type=F32)


def project_back(left, right):
    return lax.dot_general(left, right, NT, preferred_element_type=F32)


def weight_grad(left, right):
    return lax.dot_general(left, right, TN, preferred_element_type=F32).astype(BF16)


class Layout:
    def __init__(self, mesh, heads):
        dp, self.rows, self.cols = (mesh.shape[name] for name in ("dp", "row", "col"))
        ways = dp
        while dp % ways or (heads // self.cols) % ways:
            ways -= 1
        self.ways = ways
        if ways == dp:
            self.mesh, self.shared, self.part = mesh, (), "dp"
        else:
            devices = mesh.devices.reshape(dp // ways, ways, self.rows, self.cols)
            self.mesh = Mesh(devices, ("group", "part", "row", "col"))
            self.shared, self.part = ("group",), "part"
        self.data = self.shared + (self.part,)
        self.team = (self.part, "col")
        self.native = (ways, self.rows, self.cols) == (4, 4, 2)
        self.next_id = 0

    def fresh_id(self):
        self.next_id += 1
        return self.next_id


def spread(lay, values):
    if lay.native:
        moved = spread_call(values, lay.fresh_id())
        return jnp.moveaxis(moved, 0, 1).reshape(moved.shape[1], -1)
    local = values.shape[0]
    whole = lax.all_gather(values, "col", axis=0, tiled=True)
    whole = lax.all_to_all(whole, "row", split_axis=0, concat_axis=1, tiled=True)
    mine = local // lay.rows
    return lax.dynamic_slice_in_dim(whole, lax.axis_index("col") * mine, mine, 0)


def unspread(lay, values):
    if lay.native:
        pieces = [jnp.moveaxis(v.reshape(v.shape[0], lay.rows, -1), 1, 0) for v in values]
        return [v.reshape(-1, v.shape[2]) for v in deal_kernel(lay, False, pieces, lay.fresh_id())]
    results = []
    for value in values:
        local = value.shape[0] * lay.rows
        whole = lax.all_gather(value, "col", axis=0, tiled=True)
        whole = lax.all_to_all(whole, "row", split_axis=1, concat_axis=0, tiled=True)
        results.append(lax.dynamic_slice_in_dim(whole, lax.axis_index("col") * local, local, 0))
    return results


def team_gather(lay, values):
    if lay.native:
        return team_gather_kernel(lay.part, values, lay.fresh_id())
    return lax.all_gather(values, lay.team, axis=0, tiled=True)


def team_scatter(lay, values):
    if lay.native:
        return team_scatter_kernel(lay.part, values.astype(BF16), lay.fresh_id())
    return lax.psum_scatter(values.astype(BF16), lay.team, scatter_dimension=0, tiled=True).astype(F32)


def norm_forward(values):
    scale = lax.rsqrt(jnp.mean(values * values, axis=1, keepdims=True) + 1e-05)
    return values * scale, scale


def norm_backward(grad, normed, scale, gain):
    scaled = grad * gain
    inner = jnp.mean(scaled * normed, axis=1, keepdims=True)
    return scale * (scaled - normed * inner), jnp.sum(grad * normed, axis=0)


def on_device(
    lay,
    block_input,
    segment_ids,
    attn_gain,
    mix_weight,
    decay_weight,
    conv_weight,
    decay_log,
    decay_bias,
    out_gain,
    out_weight,
    ffn_gain,
    gate_weight,
    up_weight,
    down_weight,
    cotangent,
):
    part = lax.axis_index(lay.part)
    heads = decay_log.shape[0] // lay.ways
    units = gate_weight.shape[1] // lay.ways
    width = mix_weight.shape[0]

    def mine(values, dim, size):
        return lax.dynamic_slice_in_dim(values, part * size, size, dim)

    def gather_rows(values):
        return lax.all_gather(values, "row", axis=0, tiled=False)

    mix_mine = mine(mix_weight, 1, heads * PER_HEAD)
    decay_mine = mine(decay_weight, 1, heads * 2)
    decay_pad = jnp.pad(decay_mine, ((0, 0), (0, 128 - heads * 2)))
    head_weights = []
    for head in range(heads):
        piece = mix_mine[:, head * PER_HEAD : (head + 1) * PER_HEAD]
        if head == 0:
            piece = jnp.concatenate([piece, decay_pad], axis=1)
        head_weights.append(gather_rows(piece).reshape(lay.rows * width, -1))
    out_all = gather_rows(mine(out_weight, 0, heads * DV))
    pair = jnp.concatenate([mine(gate_weight, 1, units), mine(up_weight, 1, units)], axis=1)
    pair_all = gather_rows(pair).reshape(lay.rows * width, -1)
    down_all = gather_rows(mine(down_weight, 0, units))
    gains = lax.all_gather(jnp.stack([attn_gain, ffn_gain]), "row", axis=1, tiled=True)
    gain_one, gain_two = gains[0], gains[1]
    segments = lax.all_gather(segment_ids, lay.part, axis=0, tiled=True).astype(F32)
    sequences = segments.shape[0] // SEQ
    seg_col = segments.reshape(-1, 1)
    seg_row = segments.reshape(sequences, 1, SEQ)
    conv_mine = mine(conv_weight, 1, heads * INNER)
    log_mine, bias_mine = mine(decay_log, 0, heads), mine(decay_bias, 0, heads)
    gain_row = out_gain.reshape(1, -1)

    stored = spread(lay, block_input).astype(F32)
    normed_one, scale_one = norm_forward(stored)
    attn_all = team_gather(lay, (normed_one * gain_one).astype(BF16))
    projs = [project(attn_all, weight) for weight in head_weights]
    shared = (projs[0], PER_HEAD // 128, seg_col, seg_row, conv_mine, log_mine, bias_mine, gain_row)
    mixed, solves = [], []
    for head in range(heads):
        values, solve = mixer_forward(head, heads, projs[head], *shared)
        mixed.append(values)
        solves.append(solve)
    mixed = jnp.concatenate(mixed, axis=1)
    tokens = mixed.shape[0]

    def wide(left, stack):
        return jnp.einsum("tk,rkn->trn", left, stack, preferred_element_type=F32).reshape(tokens, -1)

    def wide_back(left, stack):
        left = left.reshape(tokens, lay.rows, -1)
        return jnp.einsum("trn,rkn->tk", left, stack, preferred_element_type=F32)

    def wide_grad(left, right):
        right = right.reshape(tokens, lay.rows, -1)
        return jnp.einsum("tk,trn->rkn", left, right, preferred_element_type=F32).astype(BF16)

    def sum_rows(grads):
        grads = lax.psum_scatter(grads, "row", scatter_dimension=0, tiled=False)
        return lax.psum(grads, lay.shared) if lay.shared else grads

    residual = stored + team_scatter(lay, wide(mixed, out_all))

    normed_two, scale_two = norm_forward(residual)
    ffn_all = team_gather(lay, (normed_two * gain_two).astype(BF16))
    both = project(ffn_all, pair_all)
    gate, up_values = both[:, :units], both[:, units:]
    gate_sig = jax.nn.sigmoid(gate)
    hidden = (gate * gate_sig * up_values).astype(BF16)
    block_output = (residual + team_scatter(lay, wide(hidden, down_all))).astype(BF16)

    out_grads = spread(lay, cotangent)
    out_grads_all = team_gather(lay, out_grads)
    grad_hidden = wide_back(out_grads_all, down_all)
    grad_gate = grad_hidden * up_values * gate_sig * (1.0 + gate * (1.0 - gate_sig))
    grad_up = grad_hidden * gate * gate_sig
    grad_both = jnp.concatenate([grad_gate.astype(BF16), grad_up.astype(BF16)], axis=1)
    grad_ffn = team_scatter(lay, project_back(grad_both, pair_all))
    pair_grad = sum_rows(weight_grad(ffn_all, grad_both).reshape(lay.rows, width, -1))
    down_grad = sum_rows(wide_grad(hidden, out_grads_all))
    grad_norm, ffn_gain_part = norm_backward(grad_ffn, normed_two, scale_two, gain_two)
    grad_residual = out_grads.astype(F32) + grad_norm
    branch_all = team_gather(lay, grad_residual.astype(BF16))
    grad_mixed = wide_back(branch_all, out_all)
    out_grad = sum_rows(wide_grad(mixed, branch_all))
    other = jnp.zeros((tokens, 128), BF16)
    proj_grads, mix_grads, conv_parts, small_parts = [], [], [], []
    for head in reversed(range(heads)):
        common = (head, heads, projs[head], *shared, solves[head], grad_mixed)
        if head:
            grad, extra, conv_part, small_part = mixer_backward(*common, None)
            other = other + extra
        else:
            grad, conv_part, small_part = mixer_backward(*common, other)
        proj_grads.insert(0, grad)
        conv_parts.insert(0, conv_part.sum(0))
        small_parts.insert(0, small_part.sum(0)[0])
        mix_grads.insert(0, sum_rows(weight_grad(attn_all, grad).reshape(lay.rows, width, -1)))
    grad_attn = sum(project_back(grad, weight) for grad, weight in zip(proj_grads, head_weights))
    grad_attn = team_scatter(lay, grad_attn)
    grad_norm, attn_gain_part = norm_backward(grad_attn, normed_one, scale_one, gain_one)
    input_grad = (grad_residual + grad_norm).astype(BF16)
    block_output, input_grad = unspread(lay, [block_output, input_grad])

    def join(grads):
        return lax.all_gather(grads, lay.part, axis=0, tiled=False)

    def columns(stack):
        return jnp.moveaxis(stack, 0, 1).reshape(stack.shape[1], -1).astype(F32)

    mix_stack = [join(grads) for grads in mix_grads]
    decay_grad = columns(mix_stack[0][:, :, PER_HEAD : PER_HEAD + 2 * heads])
    mix_grad = columns(jnp.concatenate([stack[:, :, :PER_HEAD] for stack in mix_stack], axis=2))
    pair_stack = join(pair_grad)
    gate_grad, up_grad = columns(pair_stack[:, :, :units]), columns(pair_stack[:, :, units:])
    out_weight_grad = join(out_grad).reshape(-1, width).astype(F32)
    down_weight_grad = join(down_grad).reshape(-1, width).astype(F32)

    everyone = lay.data + ("row", "col")
    place = part * lay.cols + lax.axis_index("col")
    slots = lay.ways * lay.cols
    pick = (jnp.arange(slots) == place).astype(F32)[:, None]
    own = jnp.concatenate(
        [jnp.concatenate(conv_parts, axis=1).reshape(-1)]
        + [jnp.stack([part_of[DV + item] for part_of in small_parts]) for item in range(2)]
    )
    sums, gain_sum, ffn_sum, attn_sum = lax.psum(
        (
            pick * own[None, :],
            sum(part_of[:DV] for part_of in small_parts),
            ffn_gain_part,
            attn_gain_part,
        ),
        everyone,
    )
    sums = sums.reshape(lay.ways, lay.cols, -1)
    sums = lax.dynamic_index_in_dim(sums, lax.axis_index("col"), 1, keepdims=False)
    split = TAPS * heads * INNER
    conv_grad = jnp.moveaxis(sums[:, :split].reshape(lay.ways, TAPS, -1), 0, 1).reshape(TAPS, -1)
    log_grad = sums[:, split : split + heads].reshape(-1)
    bias_grad = sums[:, split + heads :].reshape(-1)
    row = lax.axis_index("row")
    attn_gain_grad = lax.dynamic_slice_in_dim(attn_sum, row * width, width, 0)
    ffn_gain_grad = lax.dynamic_slice_in_dim(ffn_sum, row * width, width, 0)
    return (
        block_output,
        input_grad,
        attn_gain_grad,
        mix_grad,
        decay_grad,
        conv_grad,
        log_grad,
        bias_grad,
        gain_sum,
        out_weight_grad,
        ffn_gain_grad,
        gate_grad,
        up_grad,
        down_weight_grad,
    )


def solution(mesh):
    def run(*args):
        lay = Layout(mesh, args[6].shape[0])
        tokens, grid = P(lay.data + ("col",), "row"), P("row", "col")
        turned, features, inner = P("col", "row"), P("row"), P("col")
        conv = P(None, "col")
        return jax.shard_map(
            functools.partial(on_device, lay),
            mesh=lay.mesh,
            in_specs=(
                tokens, P(lay.data + ("row",)), features, grid, grid, conv, inner, inner, P(),
                turned, features, grid, grid, turned, tokens,
            ),
            out_specs=(
                tokens, tokens, features, grid, grid, conv, inner, inner, P(),
                turned, features, grid, grid, turned,
            ),
            check_vma=False,
        )(*args)

    return run
```

```python
import functools
import jax
import jax.numpy as jnp
from jax import lax
from jax.experimental import pallas as pl
from jax.experimental.pallas import tpu as pltpu
from jax.sharding import Mesh
from jax.sharding import PartitionSpec as P

F32, BF16 = jnp.float32, jnp.bfloat16
DK, DV, TAPS = 128, 256, 4
INNER = 2 * DK + DV
PER_HEAD = INNER + DV
NN = (((1,), (0,)), ((), ()))
NT = (((1,), (1,)), ((), ()))
TN = (((0,), (0,)), ((), ()))


def mm(left, right, dims=NN):
    return lax.dot_general(left.astype(BF16), right.astype(BF16), dims, preferred_element_type=F32)


def sigmoid(values):
    return 1.0 / (1.0 + jnp.exp(-values))


def softplus(values):
    return jnp.maximum(values, 0.0) + jnp.log(1.0 + jnp.exp(-jnp.abs(values)))


def shift_down(values, lag):
    return jnp.concatenate([jnp.zeros_like(values[:lag]), values[: values.shape[0] - lag]], axis=0)


def shift_up(values, lag):
    return jnp.concatenate([values[lag:], jnp.zeros_like(values[:lag])], axis=0)


def cumsum_rows(values):
    step = 1
    while step < values.shape[0]:
        values = values + shift_down(values, step)
        step *= 2
    return values


def reverse_cumsum_rows(values):
    step = 1
    while step < values.shape[0]:
        values = values + shift_up(values, step)
        step *= 2
    return values


def prepare(head, proj, extra, seg_col, seg_row, conv, log_ref, bias_ref):
    length = proj.shape[0]
    summed = conv[TAPS - 1 : TAPS] * proj[:, :INNER]
    keeps = []
    for lag in range(1, TAPS):
        keep = (shift_down(seg_col + 1.0, lag) == seg_col + 1.0).astype(F32)
        keeps.append(keep)
        summed = summed + conv[TAPS - 1 - lag : TAPS - lag] * (shift_down(proj[:, :INNER], lag) * keep)
    gate_conv = sigmoid(summed)
    active = summed * gate_conv
    lane = lax.broadcasted_iota(jnp.int32, extra.shape, 1)
    write = jnp.sum(jnp.where(lane == 2 * head, extra, 0.0), axis=1, keepdims=True)
    drive = jnp.sum(jnp.where(lane == 2 * head + 1, extra, 0.0), axis=1, keepdims=True)
    beta = sigmoid(write)
    drive = drive + bias_ref[head]
    rate = jnp.exp(jnp.full((1, 1), log_ref[head], F32))
    decay = -rate * softplus(drive)
    total = cumsum_rows(decay)
    rows = lax.broadcasted_iota(jnp.int32, (length, length), 0)
    cols = lax.broadcasted_iota(jnp.int32, (length, length), 1)
    total_row = jnp.sum(jnp.where(rows == cols, total, 0.0), axis=0, keepdims=True)
    weight = jnp.exp(jnp.where((rows >= cols) & (seg_col == seg_row), total - total_row, -1e30))
    raw_q, raw_k, value = active[:, :DK], active[:, DK : 2 * DK], active[:, 2 * DK :]
    scale_q = lax.rsqrt(jnp.sum(raw_q * raw_q, axis=1, keepdims=True) + 1e-06)
    scale_k = lax.rsqrt(jnp.sum(raw_k * raw_k, axis=1, keepdims=True) + 1e-06)
    query = (raw_q * scale_q * DK ** (-0.5)).astype(BF16)
    key = (raw_k * scale_k).astype(BF16)
    inner = mm(key, key, NT)
    strict = jnp.where(rows > cols, weight, 0.0)
    return dict(
        summed=summed, keeps=keeps, gate_conv=gate_conv, raw_q=raw_q, raw_k=raw_k, value=value,
        scale_q=scale_q, scale_k=scale_k, query=query, key=key, inner=inner, weight=weight,
        strict=strict, beta=beta, drive=drive, rate=rate, decay=decay, rows=rows, cols=cols,
    )


def forward_kernel(head, proj_ref, extra_ref, segc_ref, segr_ref, conv_ref, log_ref, bias_ref, gain_ref,
                   mixed_ref, solve_ref, work):
    length = proj_ref.shape[0]
    size = work.shape[0]
    p = prepare(head, proj_ref[...], extra_ref[...], segc_ref[...], segr_ref[0], conv_ref[...], log_ref, bias_ref)
    lower = p["beta"] * p["strict"] * p["inner"]
    if size != length:
        work[...] = jnp.zeros_like(work)
    work[0:length, 0:length] = lower
    tile = min(128, size)
    blocks = size // tile
    r = lax.broadcasted_iota(jnp.int32, (tile, tile), 0)
    c = lax.broadcasted_iota(jnp.int32, (tile, tile), 1)
    parts = [work[b * tile : (b + 1) * tile, b * tile : (b + 1) * tile] for b in range(blocks)]
    eye = (r == c).astype(F32)
    inv = [eye - jnp.where((r // 2 == c // 2), part, 0.0) for part in parts]
    step = 2
    while step < tile:
        pick = (r // (2 * step) == c // (2 * step)) & (r // step != c // step)
        lows = [mm(jnp.where(pick, part, 0.0), x) for part, x in zip(parts, inv)]
        inv = [x - mm(x, low) for x, low in zip(inv, lows)]
        step *= 2
    for b in range(blocks):
        work[b * tile : (b + 1) * tile, b * tile : (b + 1) * tile] = inv[b]
    step = tile
    while step < size:
        for start in range(0, size, 2 * step):
            mid, end = start + step, start + 2 * step
            low = mm(work[mid:end, start:mid], work[start:mid, start:mid])
            work[mid:end, start:mid] = -mm(work[mid:end, mid:end], low)
        step *= 2
    solve = work[0:length, 0:length].astype(BF16)
    solve_ref[0] = solve
    fresh = mm(solve, p["beta"] * p["value"])
    out = mm(mm(p["query"], p["key"], NT) * p["weight"], fresh)
    scale = lax.rsqrt(jnp.sum(out * out, axis=1, keepdims=True) * (1.0 / DV) + 1e-05)
    gate = proj_ref[:, INNER:]
    mixed_ref[...] = (out * scale * gain_ref[...] * (gate * sigmoid(gate))).astype(BF16)


def backward_kernel(head, last, *refs):
    if last:
        (proj_ref, extra_ref, segc_ref, segr_ref, conv_ref, log_ref, bias_ref, gain_ref, solve_ref, grad_ref,
         turn_ref, other_ref, gproj_ref, gconv_ref, gsmall_ref) = refs
    else:
        (proj_ref, extra_ref, segc_ref, segr_ref, conv_ref, log_ref, bias_ref, gain_ref, solve_ref, grad_ref,
         turn_ref, gproj_ref, gextra_ref, gconv_ref, gsmall_ref) = refs
    conv = conv_ref[...]
    p = prepare(head, proj_ref[...], extra_ref[...], segc_ref[...], segr_ref[0], conv, log_ref, bias_ref)
    weight, strict, inner, beta, value = p["weight"], p["strict"], p["inner"], p["beta"], p["value"]
    query, key = p["query"], p["key"]
    solve = solve_ref[0]
    fresh = mm(solve, beta * value).astype(BF16)
    scores = mm(query, key, NT)
    probs = (scores * weight).astype(BF16)
    out = mm(probs, fresh)
    scale = lax.rsqrt(jnp.sum(out * out, axis=1, keepdims=True) * (1.0 / DV) + 1e-05)
    normed = out * scale
    gate = proj_ref[:, INNER:]
    gate_sig = sigmoid(gate)
    grad, width = 0.0, turn_ref.shape[2]
    for index in range(turn_ref.shape[0]):
        grad = grad + mm(grad_ref[:, index * width : (index + 1) * width], turn_ref[index], NT)
    gain = gain_ref[...]
    through = grad * normed
    ggate = through * gain * (gate_sig * (1.0 + gate * (1.0 - gate_sig)))
    ggain = jnp.sum(through * (gate * gate_sig), axis=0, keepdims=True)
    gnormed = grad * gain * (gate * gate_sig)
    gout = scale * (gnormed - normed * (jnp.sum(gnormed * normed, axis=1, keepdims=True) * (1.0 / DV)))
    gout = gout.astype(BF16)
    gprobs = mm(gout, fresh, NT)
    gfresh = mm(probs, gout, TN)
    gtarget = mm(solve, gfresh, TN)
    glower = -mm(gtarget, fresh, NT) * strict
    gscores = gprobs * weight
    tilt = glower * inner
    flow = gscores * scores + beta * tilt
    gbeta = jnp.sum(tilt, axis=1, keepdims=True) + jnp.sum(gtarget * value, axis=1, keepdims=True)
    gscores = gscores.astype(BF16)
    ginner = (beta * glower).astype(BF16)
    gquery = mm(gscores, key)
    gkey = mm(gscores, query, TN) + mm(ginner, key) + mm(ginner, key, TN)
    col_flow = jnp.sum(flow, axis=0, keepdims=True)
    col_flow = jnp.sum(jnp.where(p["rows"] == p["cols"], col_flow, 0.0), axis=1, keepdims=True)
    gdecay = reverse_cumsum_rows(jnp.sum(flow, axis=1, keepdims=True) - col_flow)
    raw_q, raw_k, scale_q, scale_k = p["raw_q"], p["raw_k"], p["scale_q"], p["scale_k"]
    gq = (DK ** (-0.5)) * scale_q * (
        gquery - raw_q * (scale_q * scale_q * jnp.sum(gquery * raw_q, axis=1, keepdims=True)))
    gk = scale_k * (gkey - raw_k * (scale_k * scale_k * jnp.sum(gkey * raw_k, axis=1, keepdims=True)))
    gactive = jnp.concatenate([gq, gk, beta * gtarget], axis=1)
    gsummed = gactive * (p["gate_conv"] * (1.0 + p["summed"] * (1.0 - p["gate_conv"])))
    source = proj_ref[:, :INNER]
    gsource = conv[TAPS - 1 : TAPS] * gsummed
    gconv_ref[0, TAPS - 1 : TAPS, :] = jnp.sum(gsummed * source, axis=0, keepdims=True)
    for lag in range(1, TAPS):
        kept = gsummed * p["keeps"][lag - 1]
        gsource = gsource + conv[TAPS - 1 - lag : TAPS - lag] * shift_up(kept, lag)
        gconv_ref[0, TAPS - 1 - lag : TAPS - lag, :] = jnp.sum(kept * shift_down(source, lag), axis=0, keepdims=True)
    gdrive = -p["rate"] * gdecay * sigmoid(p["drive"])
    gwrite = gbeta * beta * (1.0 - beta)
    lane = lax.broadcasted_iota(jnp.int32, extra_ref.shape, 1)
    gextra = jnp.where(lane == 2 * head, gwrite, jnp.where(lane == 2 * head + 1, gdrive, 0.0))
    gproj_ref[:, :INNER] = gsource.astype(BF16)
    gproj_ref[:, INNER:PER_HEAD] = ggate.astype(BF16)
    if last:
        gproj_ref[:, PER_HEAD:] = (gextra + other_ref[...].astype(F32)).astype(BF16)
    else:
        gextra_ref[...] = gextra.astype(BF16)
    glog = jnp.sum(gdecay * p["decay"], axis=0, keepdims=True)
    gbias = jnp.sum(gdrive, axis=0, keepdims=True)
    lane = lax.broadcasted_iota(jnp.int32, (1, 128), 1)
    gsmall_ref[0, :, 0:DV] = ggain
    gsmall_ref[0, :, DV:] = jnp.where(lane == 0, glog, jnp.where(lane == 1, gbias, 0.0))


def common_specs(length, heads, head, extra_block):
    smem = pl.BlockSpec(memory_space=pltpu.SMEM)
    return [
        pl.BlockSpec((length, PER_HEAD), lambda s: (s, 0)),
        pl.BlockSpec((length, 128), lambda s: (s, extra_block)),
        pl.BlockSpec((length, 1), lambda s: (s, 0)),
        pl.BlockSpec((1, 1, length), lambda s: (s, 0, 0)),
        pl.BlockSpec((TAPS, INNER), lambda s: (0, head)),
        smem,
        smem,
        pl.BlockSpec((1, DV), lambda s: (0, 0)),
    ]


def mixer_forward(head, heads, proj, extra, extra_block, seg_col, seg_row, conv, log, bias, gain):
    count, _, length = seg_row.shape
    tokens = count * length
    size = 64
    while size < length:
        size *= 2
    return pl.pallas_call(
        functools.partial(forward_kernel, head),
        grid=(count,),
        in_specs=common_specs(length, heads, head, extra_block),
        out_specs=[
            pl.BlockSpec((length, DV), lambda s: (s, 0)),
            pl.BlockSpec((1, length, length), lambda s: (s, 0, 0)),
        ],
        out_shape=[
            jax.ShapeDtypeStruct((tokens, DV), BF16),
            jax.ShapeDtypeStruct((count, length, length), BF16),
        ],
        scratch_shapes=[pltpu.VMEM((size, size), F32)],
        compiler_params=pltpu.CompilerParams(vmem_limit_bytes=56 << 20),
        name="mixer_forward",
    )(proj, extra, seg_col, seg_row, conv, log, bias, gain)


def mixer_backward(head, heads, proj, extra, extra_block, seg_col, seg_row, conv, log, bias, gain, solve, grad, turned, other):
    count, _, length = seg_row.shape
    tokens = count * length
    last = other is not None
    in_specs = common_specs(length, heads, head, extra_block) + [
        pl.BlockSpec((1, length, length), lambda s: (s, 0, 0)),
        pl.BlockSpec((length, grad.shape[1]), lambda s: (s, 0)),
        pl.BlockSpec((turned.shape[0], DV, turned.shape[2]), lambda s: (0, head, 0)),
    ]
    args = [proj, extra, seg_col, seg_row, conv, log, bias, gain, solve, grad, turned]
    width = PER_HEAD
    tail_specs = [
        pl.BlockSpec((1, TAPS, INNER), lambda s: (s, 0, 0)),
        pl.BlockSpec((1, 1, DV + 128), lambda s: (s, 0, 0)),
    ]
    tail_shapes = [
        jax.ShapeDtypeStruct((count, TAPS, INNER), F32),
        jax.ShapeDtypeStruct((count, 1, DV + 128), F32),
    ]
    mid_specs, mid_shapes = [], []
    if last:
        width += 128
        in_specs.append(pl.BlockSpec((length, 128), lambda s: (s, 0)))
        args.append(other)
    else:
        mid_specs = [pl.BlockSpec((length, 128), lambda s: (s, 0))]
        mid_shapes = [jax.ShapeDtypeStruct((tokens, 128), BF16)]
    return pl.pallas_call(
        functools.partial(backward_kernel, head, last),
        grid=(count,),
        in_specs=in_specs,
        out_specs=[pl.BlockSpec((length, width), lambda s: (s, 0))] + mid_specs + tail_specs,
        out_shape=[jax.ShapeDtypeStruct((tokens, width), BF16)] + mid_shapes + tail_shapes,
        compiler_params=pltpu.CompilerParams(vmem_limit_bytes=60 << 20),
        name="mixer_backward",
    )(*args)


MESH_ID = pl.DeviceIdType.MESH
ANY_SPEC = pl.BlockSpec(memory_space=pl.ANY)
VMEM_SPEC = pl.BlockSpec(memory_space=pltpu.VMEM)
STRIP = 16
DECAY_ROWS = 16


def meet(targets):
    barrier = pltpu.get_barrier_semaphore()
    for target in targets:
        pl.semaphore_signal(barrier, inc=1, device_id=target, device_id_type=MESH_ID)
    pl.semaphore_wait(barrier, len(targets))


def remote(source, dest, send, recv, index, target):
    return pltpu.make_async_remote_copy(
        src_ref=source,
        dst_ref=dest,
        send_sem=send.at[index],
        recv_sem=recv.at[index],
        device_id=target,
        device_id_type=MESH_ID,
    )


class Team:
    def __init__(self, name):
        self.name, self.part, self.col = name, lax.axis_index(name), lax.axis_index("col")
        self.across, self.twin = lax.rem(self.part + 2, 4), self.part + 1 - 2 * lax.rem(self.part, 2)
        self.far, self.other = lax.rem(self.twin + 2, 4), 1 - self.col
        self.x, self.y, self.core = {name: self.across}, {"col": self.other}, {name: self.twin}

    def partners(self):
        return [self.x, self.y, self.core]


def gather_phase(team, src, out, keep, send, recv):
    half = src.shape[0] // 2
    first, second = pl.ds(0, half), pl.ds(half, half)
    own, across = team.part * 2 + team.col, team.across * 2 + team.col
    other, diag = team.part * 2 + team.other, team.across * 2 + team.other
    local = pltpu.make_async_copy(src, out.at[own], keep)
    local.start()
    x_first = remote(src.at[first], out.at[own, first], send, recv, 0, team.x)
    x_second = remote(src.at[second], out.at[own, second], send, recv, 1, team.x)
    y_second = remote(src.at[second], out.at[own, second], send, recv, 2, team.y)
    y_first = remote(src.at[first], out.at[own, first], send, recv, 3, team.y)
    core_own = remote(src, out.at[own], send, recv, 4, team.core)
    for copy in (x_first, y_second, core_own, x_second, y_first):
        copy.start()
    y_pass = remote(out.at[across, first], out.at[across, first], send, recv, 5, team.y)
    x_pass = remote(out.at[other, second], out.at[other, second], send, recv, 6, team.x)
    core_x = remote(out.at[across], out.at[across], send, recv, 7, team.core)
    core_y = remote(out.at[other], out.at[other], send, recv, 8, team.core)
    core_first = remote(out.at[diag, first], out.at[diag, first], send, recv, 9, team.core)
    core_second = remote(out.at[diag, second], out.at[diag, second], send, recv, 10, team.core)
    x_first.wait_recv()
    y_pass.start()
    y_second.wait_recv()
    x_pass.start()
    x_second.wait_recv()
    core_x.start()
    y_first.wait_recv()
    core_y.start()
    y_pass.wait_recv()
    core_first.start()
    x_pass.wait_recv()
    core_second.start()
    for copy in (core_own, core_x, core_y, core_first, core_second):
        copy.wait_recv()
    for copy in (
        x_first, x_second, y_second, y_first, core_own, y_pass, x_pass, core_x, core_y, core_first, core_second,
    ):
        copy.wait_send()
    local.wait()


GATHER_SEMS = [pltpu.SemaphoreType.DMA, pltpu.SemaphoreType.DMA((11,)), pltpu.SemaphoreType.DMA((11,))]


def spread_phase(src, out, middle, keep, send, recv):
    row, col = lax.axis_index("row"), lax.axis_index("col")
    hops = []
    for item in range(2):
        hops.append(remote(src.at[2 * item + 1 - col], middle.at[item], send, recv, item, {"col": 1 - col}))
        hops[item].start()

    def pieces(wait_first):
        for side in range(2):
            home = col if side == 0 else 1 - col
            for item in range(2):
                if side == 1 and wait_first:
                    hops[item].wait_recv()
                source = src.at[2 * item + col] if side == 0 else middle.at[item]
                to_row = 2 * home + item
                copy = pltpu.make_async_remote_copy(
                    src_ref=source,
                    dst_ref=out.at[row],
                    send_sem=send.at[2 + 2 * side + item],
                    recv_sem=recv.at[2 + row],
                    device_id={"row": to_row},
                    device_id_type=MESH_ID,
                )
                yield to_row == row, copy, pltpu.make_async_copy(source, out.at[row], keep)

    for here, far, near in pieces(True):
        pl.when(here)(near.start)
        pl.when(jnp.logical_not(here))(far.start)
    for hop in range(1, 4):
        index = lax.rem(row + hop, 4)
        pltpu.make_async_remote_copy(
            src_ref=src.at[0],
            dst_ref=out.at[index],
            send_sem=send.at[0],
            recv_sem=recv.at[2 + index],
            device_id={"row": index},
            device_id_type=MESH_ID,
        ).wait_recv()
    for here, far, near in pieces(False):
        pl.when(here)(near.wait)
        pl.when(jnp.logical_not(here))(far.wait_send)
    for hop in hops:
        hop.wait_send()


def share(source, dest, mark, others, keep, send, recv):
    near = pltpu.make_async_copy(source, dest.at[mark], keep)
    near.start()
    copies = []
    for item, (target, _) in enumerate(others):
        copies.append(
            pltpu.make_async_remote_copy(
                src_ref=source,
                dst_ref=dest.at[mark],
                send_sem=send.at[item],
                recv_sem=recv.at[mark],
                device_id=target,
                device_id_type=MESH_ID,
            )
        )
        copies[item].start()

    def finish():
        near.wait()
        for target, index in others:
            pltpu.make_async_remote_copy(
                src_ref=source,
                dst_ref=dest.at[index],
                send_sem=send.at[0],
                recv_sem=recv.at[index],
                device_id=target,
                device_id_type=MESH_ID,
            ).wait_recv()
        for copy in copies:
            copy.wait_send()

    return finish


def enter_kernel(part_name, normed, *refs):
    if normed:
        (src, gains, segs, tok, everyone, gains_all, segs_all, stage, middle, ready, spread_keep, spread_send,
         spread_recv, keep, send, recv, small_keep, gain_send, gain_recv, seg_send, seg_recv) = refs
    else:
        (src, tok, everyone, stage, middle, ready, spread_keep, spread_send, spread_recv, keep, send, recv) = refs
    team = Team(part_name)
    row = lax.axis_index("row")
    rows = [({"row": lax.rem(row + hop, 4)}, lax.rem(row + hop, 4)) for hop in range(1, 4)]
    targets = team.partners() + [target for target, _ in rows]
    if normed:
        targets.append({part_name: team.far})
    meet(targets)
    if normed:
        done_gains = share(gains, gains_all, row, rows, small_keep.at[0], gain_send, gain_recv)
        parts = [({part_name: index}, index) for index in (team.across, team.twin, team.far)]
        done_segs = share(segs, segs_all, team.part, parts, small_keep.at[1], seg_send, seg_recv)
    spread_phase(src, stage, middle, spread_keep, spread_send, spread_recv)
    if normed:
        done_gains()
        done_segs()
    tokens, width = src.shape[1], src.shape[2]

    @pl.loop(0, tokens // STRIP)
    def _(step):
        strip = pl.ds(pl.multiple_of(step * STRIP, STRIP), STRIP)
        pieces = [stage[index, strip, :] for index in range(4)]
        if normed:
            wides = [piece.astype(F32) for piece in pieces]
            square = sum(jnp.sum(wide * wide, axis=1, keepdims=True) for wide in wides)
            scale = lax.rsqrt(square * (1.0 / (4 * width)) + 1e-05)
        for index in range(4):
            cols = slice(index * width, (index + 1) * width)
            tok[strip, cols] = pieces[index]
            if normed:
                ready[strip, cols] = (wides[index] * scale * gains_all[index, 0:1, :]).astype(BF16)
            else:
                ready[strip, cols] = pieces[index]

    gather_phase(team, ready, everyone, keep, send, recv)


def enter_call(lay, values, gains, segs):
    tokens, width = values.shape[0] // 4, values.shape[1]
    wide = 4 * width
    normed = gains is not None
    args = [values.reshape(4, tokens, width)]
    in_specs, out_specs = [ANY_SPEC], [VMEM_SPEC, ANY_SPEC]
    out_shape = [jax.ShapeDtypeStruct((tokens, wide), BF16), jax.ShapeDtypeStruct((8, tokens, wide), BF16)]
    scratch = [
        pltpu.VMEM((4, tokens, width), BF16),
        pltpu.VMEM((2, tokens, width), BF16),
        pltpu.VMEM((tokens, wide), BF16),
        pltpu.SemaphoreType.DMA,
        pltpu.SemaphoreType.DMA((6,)),
        pltpu.SemaphoreType.DMA((6,)),
    ] + GATHER_SEMS
    if normed:
        args += [gains, segs]
        in_specs += [VMEM_SPEC, VMEM_SPEC]
        out_specs += [VMEM_SPEC, VMEM_SPEC]
        out_shape += [
            jax.ShapeDtypeStruct((4,) + gains.shape, gains.dtype),
            jax.ShapeDtypeStruct((4,) + segs.shape, segs.dtype),
        ]
        scratch += [
            pltpu.SemaphoreType.DMA((2,)),
            pltpu.SemaphoreType.DMA((3,)),
            pltpu.SemaphoreType.DMA((4,)),
            pltpu.SemaphoreType.DMA((3,)),
            pltpu.SemaphoreType.DMA((4,)),
        ]
    results = list(pl.pallas_call(
        functools.partial(enter_kernel, lay.part, normed),
        in_specs=in_specs,
        out_specs=out_specs,
        out_shape=out_shape,
        scratch_shapes=scratch,
        compiler_params=pltpu.CompilerParams(
            collective_id=lay.fresh_id(), has_side_effects=True, vmem_limit_bytes=16 << 20
        ),
        name="enter",
    )(*args))
    results[1] = results[1].reshape(8 * tokens, wide)
    return results


def strips(start, count, body):
    @pl.loop(0, count // STRIP)
    def _(step):
        body(pl.ds(pl.multiple_of(start + step * STRIP, STRIP), STRIP), pl.ds(pl.multiple_of(step * STRIP, STRIP), STRIP))


def scatter_phase(team, dots, finish, work, twin, sent, relay, final, send, recv):
    rows, chunk_size = twin.shape[1], twin.shape[2] // 4
    half = rows // 2
    first, second = pl.ds(0, half), pl.ds(half, half)

    def swap(item):
        return remote(work.at[item, 0], twin.at[item], send, recv, item, team.core)

    relay_x = remote(sent.at[0, first], relay.at[0], send, recv, 4, team.x)
    relay_y = remote(sent.at[0, second], relay.at[1], send, recv, 5, team.y)
    x_first = remote(sent.at[1, first], final.at[0, first], send, recv, 6, team.x)
    x_second = remote(sent.at[1, second], final.at[0, second], send, recv, 7, team.x)
    y_second = remote(sent.at[2, second], final.at[1, second], send, recv, 8, team.y)
    y_first = remote(sent.at[2, first], final.at[1, first], send, recv, 9, team.y)

    def total(item, start, passed=None):
        def add(rows, local):
            value = work[item, 1, rows, :].astype(F32) + twin[item, rows, :].astype(F32)
            if passed is not None:
                value = value + relay[passed, local, :].astype(F32)
            sent[item, rows, :] = value.astype(BF16)

        strips(start, half, add)

    @pl.loop(0, 4)
    def _(item):
        @pl.loop(0, 8)
        def _(step):
            which, chunk = step // 4, lax.rem(step, 4)
            base = team.part * which + team.twin * (1 - which)
            slot = lax.rem(base + 2 * (1 - item // 2), 4) * 2 + lax.rem(team.col + 1 + item, 2)
            columns = pl.ds(pl.multiple_of(chunk * chunk_size, chunk_size), chunk_size)
            work[item, which, :, columns] = dots(
                pl.ds(pl.multiple_of(slot * rows, STRIP), rows), chunk, columns
            ).astype(BF16)

        swap(item).start()

        @pl.when(item == 1)
        def _():
            swap(0).wait_recv()
            total(0, 0)
            relay_x.start()
            total(0, half)
            relay_y.start()

        @pl.when(item == 2)
        def _():
            swap(1).wait_recv()
            total(1, 0)
            x_first.start()

        @pl.when(item == 3)
        def _():
            swap(2).wait_recv()
            total(2, half)
            y_second.start()

    relay_y.wait_recv()
    total(1, half, 1)
    x_second.start()
    relay_x.wait_recv()
    total(2, 0, 0)
    y_first.start()
    swap(3).wait_recv()

    def last(rows, _):
        value = work[3, 1, rows, :].astype(F32) + twin[3, rows, :].astype(F32)
        finish(rows, value + final[0, rows, :].astype(F32) + final[1, rows, :].astype(F32))

    x_first.wait_recv()
    y_first.wait_recv()
    strips(0, half, last)
    x_second.wait_recv()
    y_second.wait_recv()
    strips(half, half, last)
    for copy in [swap(item) for item in range(4)] + [relay_x, relay_y, x_first, x_second, y_second, y_first]:
        copy.wait_send()


def team_kernel(part_name, kind, starts, *refs):
    extras, outs = {"mid": (2, 2), "end": (1, 1), "branch": (3, 3), "input": (3, 2)}[kind]
    count = len(starts)
    lefts, right, refs = refs[:count], refs[count], refs[count + 1 :]
    extra, out, scratch = refs[:extras], refs[extras : extras + outs], refs[extras + outs :]
    scatter_refs, scratch = scratch[:7], scratch[7:]
    team = Team(part_name)
    meet(team.partners())

    def dots(rows, chunk, columns):
        value = 0.0
        for left, start in zip(lefts, starts):
            depth = slice(start, start + left.shape[1])
            if len(right.shape) == 3:
                value = value + lax.dot_general(left[rows, :], right[chunk, depth, :], NN, preferred_element_type=F32)
            else:
                value = value + lax.dot_general(left[rows, :], right[columns, depth], NT, preferred_element_type=F32)
        return value

    if kind in ("branch", "input"):
        gain_sum, scratch = scratch[0], scratch[1:]
        gain_sum[...] = jnp.zeros_like(gain_sum)
    if kind in ("mid", "branch"):
        ready, scratch = scratch[0], scratch[1:]

    def deal_out(rows, value):
        width = value.shape[1] // 4
        for index in range(4):
            out[0][index, rows, :] = value[:, index * width : (index + 1) * width].astype(BF16)

    def finish(rows, total):
        width = total.shape[1]
        if kind == "mid":
            stored, gain = extra
            value = stored[rows, :].astype(F32) + total
            out[0][rows, :] = value
            scale = lax.rsqrt(jnp.sum(value * value, axis=1, keepdims=True) * (1.0 / width) + 1e-05)
            ready[rows, :] = (value * scale * gain[...]).astype(BF16)
        elif kind == "end":
            deal_out(rows, extra[0][rows, :] + total)
        else:
            before, through, gain = extra
            value = before[rows, :].astype(F32)
            scale = lax.rsqrt(jnp.sum(value * value, axis=1, keepdims=True) * (1.0 / width) + 1e-05)
            normed = value * scale
            gain_sum[...] += total * normed
            scaled = total * gain[...]
            inner = jnp.sum(scaled * normed, axis=1, keepdims=True) * (1.0 / width)
            value = through[rows, :].astype(F32) + scale * (scaled - normed * inner)
            if kind == "branch":
                out[0][rows, :] = value
                ready[rows, :] = value.astype(BF16)
            else:
                deal_out(rows, value)

    scatter_phase(team, dots, finish, *scatter_refs)
    if kind == "branch":
        out[2][...] = jnp.sum(gain_sum[...], axis=0, keepdims=True)
    if kind == "input":
        out[1][...] = jnp.sum(gain_sum[...], axis=0, keepdims=True)
    if kind in ("mid", "branch"):
        gather_phase(team, ready, out[1], *scratch)


def team_call(lay, kind, lefts, right, starts, extra):
    tokens = lefts[0].shape[0] // 8
    wide = extra[0].shape[1]
    whole = jax.ShapeDtypeStruct((tokens, wide), F32)
    if kind in ("end", "input"):
        whole = jax.ShapeDtypeStruct((4, tokens, wide // 4), BF16)
    everyone = jax.ShapeDtypeStruct((8, tokens, wide), BF16)
    gain = jax.ShapeDtypeStruct((1, wide), F32)
    shapes = {"mid": [whole, everyone], "end": [whole], "branch": [whole, everyone, gain], "input": [whole, gain]}[kind]
    specs = [VMEM_SPEC if shape is not everyone else ANY_SPEC for shape in shapes]
    scratch = [
        pltpu.VMEM((4, 2, tokens, wide), BF16),
        pltpu.VMEM((4, tokens, wide), BF16),
        pltpu.VMEM((3, tokens, wide), BF16),
        pltpu.VMEM((2, tokens // 2, wide), BF16),
        pltpu.VMEM((2, tokens, wide), BF16),
        pltpu.SemaphoreType.DMA((10,)),
        pltpu.SemaphoreType.DMA((10,)),
    ]
    if kind in ("branch", "input"):
        scratch.append(pltpu.VMEM((STRIP, wide), F32))
    if kind in ("mid", "branch"):
        scratch.append(pltpu.VMEM((tokens, wide), BF16))
        scratch += GATHER_SEMS
    flops = 2 * 8 * tokens * wide * sum(left.shape[1] for left in lefts)
    results = list(pl.pallas_call(
        functools.partial(team_kernel, lay.part, kind, tuple(starts)),
        in_specs=[VMEM_SPEC] * (len(lefts) + 1 + len(extra)),
        out_specs=specs,
        out_shape=shapes,
        scratch_shapes=scratch,
        compiler_params=pltpu.CompilerParams(
            collective_id=lay.fresh_id(), has_side_effects=True, vmem_limit_bytes=56 << 20
        ),
        cost_estimate=pl.CostEstimate(flops=flops, bytes_accessed=200 << 20, transcendentals=0),
        name="team_" + kind,
    )(*lefts, right, *extra))
    if kind in ("mid", "branch"):
        results[1] = results[1].reshape(8 * tokens, wide)
    return results


def leave_kernel(part_name, rows_n, cols_n, count, *refs):
    srcs, src = refs[:count], refs[count]
    outs, out = refs[count + 1 : 2 * count + 1], refs[2 * count + 1]
    keep, send, recv, rows_in, summed, near, row_send, row_recv, team_send, team_recv = refs[2 * count + 2 :]
    team = Team(part_name)
    row, col = lax.axis_index("row"), lax.axis_index("col")
    rows = [({"row": lax.rem(row + hop, 4)}, lax.rem(row + hop, 4)) for hop in range(1, 4)]
    mates = []
    for part in (team.part, team.across, team.twin, team.far):
        for side in (team.col, team.other):
            mates.append(({part_name: part, "col": side}, part * 2 + side))
    mates = mates[1:]
    spot = row * cols_n + col
    mark = lax.rem(spot, rows_n)
    home = spot // rows_n

    def owner(index):
        place = col * rows_n + index
        return place // cols_n, lax.rem(place, cols_n)

    barrier = pltpu.get_barrier_semaphore()
    for target, _ in rows + mates:
        pl.semaphore_signal(barrier, inc=1, device_id=target, device_id_type=MESH_ID)
    for index in range(rows_n):
        from_row, from_col = owner(index)

        @pl.when((from_row != row) | (from_col != col))
        def _():
            pl.semaphore_signal(barrier, inc=1, device_id={"row": from_row, "col": from_col}, device_id_type=MESH_ID)

    pl.semaphore_wait(barrier, len(rows + mates) + rows_n - (home == col).astype(jnp.int32))
    finish_rows = share(src, rows_in, row, rows, near.at[0], row_send, row_recv)

    def each(act_local, act_remote):
        for item in range(count):
            for index in range(rows_n):
                here = (row == index) & (home == col)

                @pl.when(here)
                def _():
                    act_local(pltpu.make_async_copy(srcs[item].at[index], outs[item].at[mark], keep.at[item]))

                @pl.when(jnp.logical_not(here))
                def _():
                    act_remote(
                        pltpu.make_async_remote_copy(
                            src_ref=srcs[item].at[index],
                            dst_ref=outs[item].at[mark],
                            send_sem=send.at[item, index],
                            recv_sem=recv.at[item, mark],
                            device_id={"row": index, "col": home},
                            device_id_type=MESH_ID,
                        )
                    )

    each(lambda copy: copy.start(), lambda copy: copy.start())
    finish_rows()
    summed[...] = (rows_in[0] + rows_in[1]) + (rows_in[2] + rows_in[3])
    finish_team = share(summed, out, team.part * 2 + team.col, mates, near.at[1], team_send, team_recv)
    for item in range(count):
        for index in range(rows_n):
            from_row, from_col = owner(index)

            @pl.when((from_row != row) | (from_col != col))
            def _():
                pltpu.make_async_remote_copy(
                    src_ref=srcs[item].at[0],
                    dst_ref=outs[item].at[index],
                    send_sem=send.at[item, 0],
                    recv_sem=recv.at[item, index],
                    device_id={"row": from_row, "col": from_col},
                    device_id_type=MESH_ID,
                ).wait_recv()

    each(lambda copy: copy.wait(), lambda copy: copy.wait_send())
    finish_team()


def leave_call(lay, values, small):
    count = len(values)
    return pl.pallas_call(
        functools.partial(leave_kernel, lay.part, lay.rows, lay.cols, count),
        in_specs=[ANY_SPEC] * count + [VMEM_SPEC],
        out_specs=[ANY_SPEC] * count + [VMEM_SPEC],
        out_shape=[jax.ShapeDtypeStruct(value.shape, value.dtype) for value in values]
        + [jax.ShapeDtypeStruct((8,) + small.shape, F32)],
        scratch_shapes=[
            pltpu.SemaphoreType.DMA((count,)),
            pltpu.SemaphoreType.DMA((count, lay.rows)),
            pltpu.SemaphoreType.DMA((count, lay.rows)),
            pltpu.VMEM((4,) + small.shape, F32),
            pltpu.VMEM(small.shape, F32),
            pltpu.SemaphoreType.DMA((2,)),
            pltpu.SemaphoreType.DMA((3,)),
            pltpu.SemaphoreType.DMA((4,)),
            pltpu.SemaphoreType.DMA((7,)),
            pltpu.SemaphoreType.DMA((8,)),
        ],
        compiler_params=pltpu.CompilerParams(collective_id=lay.fresh_id(), has_side_effects=True),
        name="leave",
    )(*values, small)


def permute_join(lay, value):
    across = lax.ppermute(value, lay.part, [(0, 2), (2, 0), (1, 3), (3, 1)])
    pairs = [(0, 1), (1, 0), (2, 3), (3, 2)]
    return [value, across, lax.ppermute(value, lay.part, pairs), lax.ppermute(across, lay.part, pairs)]


def part_order(lay):
    part = lax.axis_index(lay.part)
    twin = part + 1 - 2 * (part % 2)
    return jnp.stack([part, (part + 2) % 4, twin, (twin + 2) % 4]).astype(jnp.int32)


def rows_kernel(order, *refs):
    for index, ref in enumerate(refs[:4]):

        @pl.when(pl.program_id(0) == index)
        def _():
            refs[4][...] = ref[...].astype(F32)


def place_rows(order, pieces, start, rows):
    width = pieces[0].shape[1]
    return pl.pallas_call(
        rows_kernel,
        grid_spec=pltpu.PrefetchScalarGridSpec(
            num_scalar_prefetch=1,
            grid=(4,),
            in_specs=[pl.BlockSpec((rows, width), lambda i, order: (start // rows, 0))] * 4,
            out_specs=pl.BlockSpec((rows, width), lambda i, order: (order[i], 0)),
        ),
        out_shape=jax.ShapeDtypeStruct((4 * rows, width), F32),
        compiler_params=pltpu.CompilerParams(vmem_limit_bytes=24 << 20),
        name="place_rows",
    )(order, *pieces)


def heads_kernel(heads, order, *refs):
    ins, decays, (out, decay) = refs[: 4 * heads], refs[4 * heads : -2], refs[-2:]
    for index in range(4):
        for head in range(heads):
            start = pl.multiple_of((order[index] * heads + head) * PER_HEAD, 128)
            out[:, pl.ds(start, PER_HEAD)] = ins[head * 4 + index][...].astype(F32).T
        small = decays[index][...].astype(F32).T[:, : 2 * heads]
        for part in range(4):

            @pl.when(order[index] == part)
            def _():
                decay[:, part * 2 * heads : (part + 1) * 2 * heads] = small


def place_heads(order, pieces):
    heads = len(pieces)
    flat = [piece for group in pieces for piece in group]
    features = flat[0].shape[1]
    wide = 4 * heads * PER_HEAD
    return pl.pallas_call(
        functools.partial(heads_kernel, heads),
        grid_spec=pltpu.PrefetchScalarGridSpec(
            num_scalar_prefetch=1,
            grid=(features // 128,),
            in_specs=[pl.BlockSpec((PER_HEAD, 128), lambda i, order: (0, i))] * len(flat)
            + [pl.BlockSpec((DECAY_ROWS, 128), lambda i, order: (PER_HEAD // DECAY_ROWS, i))] * 4,
            out_specs=[
                pl.BlockSpec((128, wide), lambda i, order: (i, 0)),
                pl.BlockSpec((128, 8 * heads), lambda i, order: (i, 0)),
            ],
        ),
        out_shape=[
            jax.ShapeDtypeStruct((features, wide), F32),
            jax.ShapeDtypeStruct((features, 8 * heads), F32),
        ],
        compiler_params=pltpu.CompilerParams(vmem_limit_bytes=40 << 20),
        name="place_heads",
    )(order, *flat, *pieces[0])


def pair_kernel(units, order, *refs):
    srcs, gate, up = refs[:4], refs[4], refs[5]
    for index in range(4):
        gate_part = srcs[index][:units, :].astype(F32).T
        up_part = srcs[index][units:, :].astype(F32).T
        for part in range(4):

            @pl.when(order[index] == part)
            def _():
                gate[:, part * units : (part + 1) * units] = gate_part
                up[:, part * units : (part + 1) * units] = up_part


def place_pair(order, pieces, units):
    features = pieces[0].shape[1]
    shape = jax.ShapeDtypeStruct((features, 4 * units), F32)
    return pl.pallas_call(
        functools.partial(pair_kernel, units),
        grid_spec=pltpu.PrefetchScalarGridSpec(
            num_scalar_prefetch=1,
            grid=(features // 128,),
            in_specs=[pl.BlockSpec((2 * units, 128), lambda i, order: (0, i))] * 4,
            out_specs=[pl.BlockSpec((128, 4 * units), lambda i, order: (i, 0))] * 2,
        ),
        out_shape=[shape, shape],
        compiler_params=pltpu.CompilerParams(vmem_limit_bytes=24 << 20),
        name="place_pair",
    )(order, *pieces)


def stack_kernel(counts, *refs):
    grads, values, out = refs[: len(counts)], refs[len(counts) : -1], refs[-1]
    base = 0
    for grad, value, count in zip(grads, values, counts):
        for start in range(0, count, 256):
            size = min(256, grad.shape[1] - start)
            part = lax.dot_general(grad[:, start : start + size], value[...], TN, preferred_element_type=F32)
            size = min(size, count - start)
            out[0, base + start : base + start + size, :] = part[:size].astype(BF16)
        base += count


def stack_call(rows_n, pairs, counts):
    tokens, wide = pairs[0][1].shape
    width = wide // rows_n
    total = sum(counts)
    flops = 2 * tokens * wide * sum(grad.shape[1] for grad, _ in pairs)
    return pl.pallas_call(
        functools.partial(stack_kernel, counts),
        grid=(rows_n,),
        in_specs=[
            pl.BlockSpec(grad.shape, lambda i: (0, 0), pipeline_mode=pl.Buffered(1)) for grad, _ in pairs
        ]
        + [pl.BlockSpec((tokens, width), lambda i: (0, i)) for _ in pairs],
        out_specs=pl.BlockSpec((1, total, width), lambda i: (i, 0, 0)),
        out_shape=jax.ShapeDtypeStruct((rows_n, total, width), BF16),
        compiler_params=pltpu.CompilerParams(vmem_limit_bytes=48 << 20),
        cost_estimate=pl.CostEstimate(flops=flops, bytes_accessed=40 << 20, transcendentals=0),
        name="weight_grads",
    )(*[grad for grad, _ in pairs], *[value for _, value in pairs])


def ffn_kernel(start, values, grads, pair, turned, hidden, both_grad):
    units = hidden.shape[1]
    both = lax.dot_general(values[...], pair[...], NN, preferred_element_type=F32)
    grad, width = 0.0, turned.shape[2]
    for index in range(turned.shape[0]):
        left = grads[:, index * width : (index + 1) * width]
        grad = grad + lax.dot_general(left, turned[index, start : start + units, :], NT, preferred_element_type=F32)
    gate, up = both[:, :units], both[:, units:]
    sig = sigmoid(gate)
    act = gate * sig
    hidden[...] = (act * up).astype(BF16)
    both_grad[:, :units] = (grad * up * (sig + act * (1.0 - sig))).astype(BF16)
    both_grad[:, units:] = (grad * act).astype(BF16)


def ffn_call(values, grads, pair, turned, start):
    tokens, width = values.shape
    units = pair.shape[1] // 2
    block = 256
    while tokens % block:
        block //= 2
    row = pl.BlockSpec((block, width), lambda i: (i, 0))
    return pl.pallas_call(
        functools.partial(ffn_kernel, start),
        grid=(tokens // block,),
        in_specs=[
            row,
            row,
            pl.BlockSpec(pair.shape, lambda i: (0, 0)),
            pl.BlockSpec(turned.shape, lambda i: (0, 0, 0)),
        ],
        out_specs=[
            pl.BlockSpec((block, units), lambda i: (i, 0)),
            pl.BlockSpec((block, 2 * units), lambda i: (i, 0)),
        ],
        out_shape=[
            jax.ShapeDtypeStruct((tokens, units), BF16),
            jax.ShapeDtypeStruct((tokens, 2 * units), BF16),
        ],
        compiler_params=pltpu.CompilerParams(vmem_limit_bytes=48 << 20),
        cost_estimate=pl.CostEstimate(
            flops=6 * tokens * width * units, bytes_accessed=30 << 20, transcendentals=tokens * units
        ),
        name="ffn",
    )(values, grads, pair, turned)


SEQ = 448


def project(left, right):
    return jnp.dot(left, right, preferred_element_type=F32)


def project_back(left, right):
    return lax.dot_general(left, right, NT, preferred_element_type=F32)


def weight_grads(lay, *pairs):
    if lay.native:
        return stack_call(lay.rows, [pair[:2] for pair in pairs], [count for _, _, count in pairs])
    stacks = []
    for grad, value, count in pairs:
        whole = lax.dot_general(grad, value, TN, preferred_element_type=F32)[:count].astype(BF16)
        stacks.append(jnp.moveaxis(whole.reshape(count, lay.rows, -1), 1, 0))
    return jnp.concatenate(stacks, axis=1)


def after(value, *others):
    return lax.optimization_barrier((value,) + others)[0]


class Layout:
    def __init__(self, mesh, heads):
        dp, self.rows, self.cols = (mesh.shape[name] for name in ("dp", "row", "col"))
        ways = dp
        while dp % ways or (heads // self.cols) % ways:
            ways -= 1
        self.ways = ways
        if ways == dp:
            self.mesh, self.shared, self.part = mesh, (), "dp"
        else:
            devices = mesh.devices.reshape(dp // ways, ways, self.rows, self.cols)
            self.mesh = Mesh(devices, ("group", "part", "row", "col"))
            self.shared, self.part = ("group",), "part"
        self.data = self.shared + (self.part,)
        self.team = (self.part, "col")
        self.native = (ways, self.rows, self.cols) == (4, 4, 2)
        self.next_id = 0

    def fresh_id(self):
        self.next_id += 1
        return self.next_id


def spread(lay, values):
    local = values.shape[0]
    whole = lax.all_gather(values, "col", axis=0, tiled=True)
    whole = lax.all_to_all(whole, "row", split_axis=0, concat_axis=1, tiled=True)
    mine = local // lay.rows
    return lax.dynamic_slice_in_dim(whole, lax.axis_index("col") * mine, mine, 0)


def unspread(lay, value):
    local = value.shape[0] * lay.rows
    whole = lax.all_gather(value, "col", axis=0, tiled=True)
    whole = lax.all_to_all(whole, "row", split_axis=1, concat_axis=0, tiled=True)
    return lax.dynamic_slice_in_dim(whole, lax.axis_index("col") * local, local, 0)


def team_gather(lay, values):
    return lax.all_gather(values, lay.team, axis=0, tiled=True)


def team_scatter(lay, values):
    return lax.psum_scatter(values.astype(BF16), lay.team, scatter_dimension=0, tiled=True).astype(F32)


def norm_forward(values):
    scale = lax.rsqrt(jnp.mean(values * values, axis=1, keepdims=True) + 1e-05)
    return values * scale, scale


def norm_backward(grad, values, gain):
    normed, scale = norm_forward(values)
    scaled = grad * gain
    inner = jnp.mean(scaled * normed, axis=1, keepdims=True)
    return scale * (scaled - normed * inner), jnp.sum(grad * normed, axis=0, keepdims=True)


def enter(lay, values, gains, segments):
    if lay.native:
        return enter_call(lay, values, gains, segments)
    mine = spread(lay, values)
    if gains is None:
        return mine, team_gather(lay, mine)
    gains = lax.all_gather(gains, "row", axis=0, tiled=False)
    segments = lax.all_gather(segments, lay.part, axis=0, tiled=False)
    normed, _ = norm_forward(mine.astype(F32))
    everyone = team_gather(lay, (normed * gains[:, 0].reshape(1, -1)).astype(BF16))
    return mine, everyone, gains, segments


def beside(stack, start, size):
    return jnp.moveaxis(stack[:, start : start + size], 0, 1).reshape(size, -1)


def mid_step(lay, mixed, turned, stored, gain):
    starts = [head * DV for head in range(len(mixed))]
    if lay.native:
        return team_call(lay, "mid", mixed, turned, starts, [stored, gain])
    total = sum(project(left, beside(turned, start, DV)) for left, start in zip(mixed, starts))
    residual = stored.astype(F32) + team_scatter(lay, total)
    normed, _ = norm_forward(residual)
    return residual, team_gather(lay, (normed * gain).astype(BF16))


def feed_forward(lay, values, grads, pair, turned, start):
    if lay.native:
        return ffn_call(values, grads, pair, turned, start)
    units = pair.shape[1] // 2
    both = project(values, pair)
    gate, up = both[:, :units], both[:, units:]
    sig = jax.nn.sigmoid(gate)
    grad = project_back(grads, beside(turned, start, units))
    grad_gate = grad * up * sig * (1.0 + gate * (1.0 - sig))
    both = jnp.concatenate([grad_gate.astype(BF16), (grad * gate * sig).astype(BF16)], axis=1)
    return (gate * sig * up).astype(BF16), both


def end_step(lay, hidden, turned, start, residual):
    if lay.native:
        return team_call(lay, "end", [hidden], turned, [start], [residual])[0]
    total = project(hidden, beside(turned, start, hidden.shape[1]))
    return (residual + team_scatter(lay, total)).astype(BF16)


def branch_step(lay, left, right, residual, out_grads, gain):
    if lay.native:
        return team_call(lay, "branch", [left], right, [0], [residual, out_grads, gain])
    grad, gain_part = norm_backward(team_scatter(lay, project_back(left, right)), residual, gain)
    grad = out_grads.astype(F32) + grad
    return grad, team_gather(lay, grad.astype(BF16)), gain_part


def input_step(lay, lefts, right, starts, stored, grad_residual, gain):
    if lay.native:
        return team_call(lay, "input", lefts, right, starts, [stored, grad_residual, gain])
    total = sum(project_back(left, right[:, start : start + left.shape[1]]) for left, start in zip(lefts, starts))
    grad, gain_part = norm_backward(team_scatter(lay, total), stored.astype(F32), gain)
    return (grad_residual + grad).astype(BF16), gain_part


def columns(stack):
    return jnp.moveaxis(stack, 2, 0).reshape(stack.shape[2], -1).astype(F32)


def on_device(
    lay,
    block_input,
    segment_ids,
    attn_gain,
    mix_weight,
    decay_weight,
    conv_weight,
    decay_log,
    decay_bias,
    out_gain,
    out_weight,
    ffn_gain,
    gate_weight,
    up_weight,
    down_weight,
    cotangent,
):
    part = lax.axis_index(lay.part)
    heads = decay_log.shape[0] // lay.ways
    units = gate_weight.shape[1] // lay.ways
    width = mix_weight.shape[0]

    def mine(values, dim, size):
        return lax.dynamic_slice_in_dim(values, part * size, size, dim)

    def gather_rows(values):
        return lax.all_gather(values, "row", axis=0, tiled=False)

    mix_mine = mine(mix_weight, 1, heads * PER_HEAD)
    decay_mine = mine(decay_weight, 1, heads * 2)
    decay_pad = jnp.pad(decay_mine, ((0, 0), (0, 128 - heads * 2)))
    splits = [0, PER_HEAD + 128]
    for head in range(1, heads):
        splits.append(splits[-1] + PER_HEAD)
    mix_pad = jnp.concatenate([mix_mine[:, :PER_HEAD], decay_pad, mix_mine[:, PER_HEAD:]], axis=1)
    mix_all = gather_rows(mix_pad).reshape(lay.rows * width, -1)
    turned = jnp.concatenate([mine(out_weight, 0, heads * DV), mine(down_weight, 0, units)], axis=0)
    turned_all = gather_rows(turned)
    pair = jnp.concatenate([mine(gate_weight, 1, units), mine(up_weight, 1, units)], axis=1)
    pair_all = gather_rows(pair).reshape(lay.rows * width, -1)
    conv_mine = mine(conv_weight, 1, heads * INNER)
    log_mine, bias_mine = mine(decay_log, 0, heads), mine(decay_bias, 0, heads)

    gains = jnp.stack([attn_gain, ffn_gain])
    stored, attn_all, gains, segments = enter(lay, block_input, gains, segment_ids.reshape(1, -1))
    gain_one, gain_two = gains[:, 0].reshape(1, -1), gains[:, 1].reshape(1, -1)
    segments = segments.astype(F32)
    seg_col, seg_row = segments.reshape(-1, 1), segments.reshape(-1, 1, SEQ)
    tokens = attn_all.shape[0]
    head_weights = [mix_all[:, start:end] for start, end in zip(splits[:-1], splits[1:])]
    shared, mixed, solves, projs = (), [], [], []
    for head in range(heads):
        projs.append(project(attn_all, head_weights[head]))
        if not head:
            shared = (
                projs[0], PER_HEAD // 128, seg_col, seg_row, conv_mine, log_mine, bias_mine, out_gain.reshape(1, -1),
            )
        values, solve = mixer_forward(head, heads, projs[head], *shared)
        mixed.append(values)
        solves.append(solve)
    out_grads, out_grads_all = enter(lay, after(cotangent, *mixed), None, None)
    mixed[0] = after(mixed[0], out_grads)
    residual, ffn_all = mid_step(lay, mixed, turned_all, stored, gain_two)

    hidden, grad_both = feed_forward(lay, ffn_all, out_grads_all, pair_all, turned_all, heads * DV)

    def sum_rows(grads):
        grads = lax.psum_scatter(grads, "row", scatter_dimension=0, tiled=False)
        return lax.psum(grads, lay.shared) if lay.shared else grads

    ffn_part = weight_grads(lay, (grad_both, ffn_all, 2 * units), (hidden, out_grads_all, units))
    grad_both, hidden = lax.optimization_barrier((grad_both, hidden, ffn_part))[:2]
    ffn_grad = sum_rows(ffn_part)
    grad_residual, branch_all, ffn_gain_part = branch_step(lay, grad_both, pair_all, residual, out_grads, gain_two)

    branch = branch_all
    other = jnp.zeros((tokens, 128), BF16)
    proj_grads, mix_grads, conv_parts, small_parts = [], [], [], []
    for head in reversed(range(heads)):
        common = (head, heads, projs[head], *shared, solves[head], branch, turned_all)
        if head:
            grad, extra, conv_part, small_part = mixer_backward(*common, None)
            other = other + extra
        else:
            grad, conv_part, small_part = mixer_backward(*common, other)
        triples = [(grad, attn_all, PER_HEAD if head else PER_HEAD + DECAY_ROWS)]
        if head == heads - 1:
            triples += [(values, branch_all, DV) for values in mixed]
        mix_part = weight_grads(lay, *triples)
        branch, grad = lax.optimization_barrier((branch, grad, mix_part))[:2]
        proj_grads.insert(0, grad)
        conv_parts.insert(0, conv_part.sum(0))
        small_parts.insert(0, small_part.sum(0)[0])
        mix_grads.insert(0, sum_rows(mix_part))
    input_grad, attn_gain_part = input_step(lay, proj_grads, mix_all, splits[:-1], stored, grad_residual, gain_one)
    hidden, ffn_grad = lax.optimization_barrier((hidden, ffn_grad, input_grad))[:2]
    block_output = end_step(lay, hidden, turned_all, heads * DV, residual)
    own = jnp.concatenate(
        [jnp.concatenate(conv_parts, axis=1).reshape(-1)]
        + [jnp.stack([part_of[DV + item] for part_of in small_parts]) for item in range(2)]
    )
    split = TAPS * heads * INNER
    gain_part = sum(part_of[:DV] for part_of in small_parts)
    col = lax.axis_index("col")
    if lay.native:
        flat = jnp.concatenate([own, gain_part, attn_gain_part[0], ffn_gain_part[0]])
        size = flat.shape[0]
        flat = jnp.pad(flat, (0, -size % 1024)).reshape(-1, 128)
        block_output, input_grad, sums = leave_call(lay, [block_output, input_grad], flat)
        block_output, input_grad = (value.reshape(-1, value.shape[2]) for value in (block_output, input_grad))
        sums = sums.reshape(8, -1)
        gain_sum, attn_sum, ffn_sum = jnp.split(
            jnp.sum(sums[:, own.shape[0] : size], axis=0), [DV, DV + lay.rows * width]
        )
        sums = sums[:, : own.shape[0]].reshape(lay.ways, lay.cols, -1)
    else:
        block_output, input_grad = unspread(lay, block_output), unspread(lay, input_grad)
        slots = lay.ways * lay.cols
        pick = (jnp.arange(slots) == part * lay.cols + col).astype(F32)[:, None]
        sums, gain_sum, ffn_sum, attn_sum = lax.psum(
            (pick * own[None, :], gain_part, ffn_gain_part[0], attn_gain_part[0]), lay.data + ("row", "col")
        )
        sums = sums.reshape(lay.ways, lay.cols, -1)
    sums = lax.dynamic_index_in_dim(sums, col, 1, keepdims=False)
    conv_grad = jnp.moveaxis(sums[:, :split].reshape(lay.ways, TAPS, -1), 0, 1).reshape(TAPS, -1)
    log_grad = sums[:, split : split + heads].reshape(-1)
    bias_grad = sums[:, split + heads :].reshape(-1)
    row = lax.axis_index("row")
    attn_gain_grad = lax.dynamic_slice_in_dim(attn_sum, row * width, width, 0)
    ffn_gain_grad = lax.dynamic_slice_in_dim(ffn_sum, row * width, width, 0)

    out_start = PER_HEAD if heads > 1 else PER_HEAD + DECAY_ROWS
    if lay.native:
        order = part_order(lay)
        pieces = [permute_join(lay, ffn_grad)]
        for grads in reversed(mix_grads):
            pieces.append(permute_join(lay, after(grads, input_grad)))
        gate_grad, up_grad = place_pair(order, pieces[0], units)
        down_weight_grad = place_rows(order, pieces[0], 2 * units, units)
        mix_grad, decay_grad = place_heads(order, pieces[:0:-1])
        out_weight_grad = place_rows(order, [piece[out_start:] for piece in pieces[1]], 0, heads * DV)
    else:
        ffn_stack, *mix_stacks = (
            lax.all_gather(value, lay.part, axis=0, tiled=False) for value in [ffn_grad] + mix_grads
        )
        decay_grad = columns(mix_stacks[0][:, PER_HEAD : PER_HEAD + 2 * heads])
        mix_grad = columns(jnp.concatenate([stack[:, :PER_HEAD] for stack in mix_stacks], axis=1))
        gate_grad, up_grad = columns(ffn_stack[:, :units]), columns(ffn_stack[:, units : 2 * units])
        down_weight_grad = ffn_stack[:, 2 * units :].reshape(-1, width).astype(F32)
        out_weight_grad = mix_stacks[-1][:, out_start : out_start + heads * DV].reshape(-1, width).astype(F32)
    return (
        block_output,
        input_grad,
        attn_gain_grad,
        mix_grad,
        decay_grad,
        conv_grad,
        log_grad,
        bias_grad,
        gain_sum,
        out_weight_grad,
        ffn_gain_grad,
        gate_grad,
        up_grad,
        down_weight_grad,
    )


def solution(mesh):
    def run(*args):
        lay = Layout(mesh, args[6].shape[0])
        tokens, grid = P(lay.data + ("col",), "row"), P("row", "col")
        turned, features, inner = P("col", "row"), P("row"), P("col")
        conv = P(None, "col")
        return jax.shard_map(
            functools.partial(on_device, lay),
            mesh=lay.mesh,
            in_specs=(
                tokens, P(lay.data + ("row",)), features, grid, grid, conv, inner, inner, P(),
                turned, features, grid, grid, turned, tokens,
            ),
            out_specs=(
                tokens, tokens, features, grid, grid, conv, inner, inner, P(),
                turned, features, grid, grid, turned,
            ),
            check_vma=False,
        )(*args)

    return run
```

```python
import functools
import jax
import jax.numpy as jnp
from jax import lax
from jax.experimental import pallas as pl
from jax.experimental.pallas import tpu as pltpu
from jax.sharding import Mesh
from jax.sharding import PartitionSpec as P

F32, BF16 = jnp.float32, jnp.bfloat16
DK, DV, TAPS = 128, 256, 4
INNER = 2 * DK + DV
PER_HEAD = INNER + DV
NN = (((1,), (0,)), ((), ()))
NT = (((1,), (1,)), ((), ()))
TN = (((0,), (0,)), ((), ()))


def mm(left, right, dims=NN):
    return lax.dot_general(left.astype(BF16), right.astype(BF16), dims, preferred_element_type=F32)


def sigmoid(values):
    return 1.0 / (1.0 + jnp.exp(-values))


def softplus(values):
    return jnp.maximum(values, 0.0) + jnp.log(1.0 + jnp.exp(-jnp.abs(values)))


def shift_down(values, lag):
    return jnp.concatenate([jnp.zeros_like(values[:lag]), values[: values.shape[0] - lag]], axis=0)


def shift_up(values, lag):
    return jnp.concatenate([values[lag:], jnp.zeros_like(values[:lag])], axis=0)


def cumsum_rows(values):
    step = 1
    while step < values.shape[0]:
        values = values + shift_down(values, step)
        step *= 2
    return values


def reverse_cumsum_rows(values):
    step = 1
    while step < values.shape[0]:
        values = values + shift_up(values, step)
        step *= 2
    return values


def prepare(head, proj, extra, seg_col, seg_row, conv, log_ref, bias_ref):
    length = proj.shape[0]
    summed = conv[TAPS - 1 : TAPS] * proj[:, :INNER]
    keeps = []
    for lag in range(1, TAPS):
        keep = (shift_down(seg_col + 1.0, lag) == seg_col + 1.0).astype(F32)
        keeps.append(keep)
        summed = summed + conv[TAPS - 1 - lag : TAPS - lag] * (shift_down(proj[:, :INNER], lag) * keep)
    gate_conv = sigmoid(summed)
    active = summed * gate_conv
    lane = lax.broadcasted_iota(jnp.int32, extra.shape, 1)
    write = jnp.sum(jnp.where(lane == 2 * head, extra, 0.0), axis=1, keepdims=True)
    drive = jnp.sum(jnp.where(lane == 2 * head + 1, extra, 0.0), axis=1, keepdims=True)
    beta = sigmoid(write)
    drive = drive + bias_ref[head]
    rate = jnp.exp(jnp.full((1, 1), log_ref[head], F32))
    decay = -rate * softplus(drive)
    total = cumsum_rows(decay)
    rows = lax.broadcasted_iota(jnp.int32, (length, length), 0)
    cols = lax.broadcasted_iota(jnp.int32, (length, length), 1)
    total_row = jnp.sum(jnp.where(rows == cols, total, 0.0), axis=0, keepdims=True)
    weight = jnp.exp(jnp.where((rows >= cols) & (seg_col == seg_row), total - total_row, -1e30))
    raw_q, raw_k, value = active[:, :DK], active[:, DK : 2 * DK], active[:, 2 * DK :]
    scale_q = lax.rsqrt(jnp.sum(raw_q * raw_q, axis=1, keepdims=True) + 1e-06)
    scale_k = lax.rsqrt(jnp.sum(raw_k * raw_k, axis=1, keepdims=True) + 1e-06)
    query = (raw_q * scale_q * DK ** (-0.5)).astype(BF16)
    key = (raw_k * scale_k).astype(BF16)
    inner = mm(key, key, NT)
    strict = jnp.where(rows > cols, weight, 0.0)
    return dict(
        summed=summed, keeps=keeps, gate_conv=gate_conv, raw_q=raw_q, raw_k=raw_k, value=value,
        scale_q=scale_q, scale_k=scale_k, query=query, key=key, inner=inner, weight=weight,
        strict=strict, beta=beta, drive=drive, rate=rate, decay=decay, rows=rows, cols=cols,
    )


def forward_kernel(head, proj_ref, extra_ref, segc_ref, segr_ref, conv_ref, log_ref, bias_ref, gain_ref,
                   mixed_ref, solve_ref, work):
    length = proj_ref.shape[0]
    size = work.shape[0]
    p = prepare(head, proj_ref[...], extra_ref[...], segc_ref[...], segr_ref[0], conv_ref[...], log_ref, bias_ref)
    lower = p["beta"] * p["strict"] * p["inner"]
    if size != length:
        work[...] = jnp.zeros_like(work)
    work[0:length, 0:length] = lower
    tile = min(128, size)
    blocks = size // tile
    r = lax.broadcasted_iota(jnp.int32, (tile, tile), 0)
    c = lax.broadcasted_iota(jnp.int32, (tile, tile), 1)
    parts = [work[b * tile : (b + 1) * tile, b * tile : (b + 1) * tile] for b in range(blocks)]
    eye = (r == c).astype(F32)
    inv = [eye - jnp.where((r // 2 == c // 2), part, 0.0) for part in parts]
    step = 2
    while step < tile:
        pick = (r // (2 * step) == c // (2 * step)) & (r // step != c // step)
        lows = [mm(jnp.where(pick, part, 0.0), x) for part, x in zip(parts, inv)]
        inv = [x - mm(x, low) for x, low in zip(inv, lows)]
        step *= 2
    for b in range(blocks):
        work[b * tile : (b + 1) * tile, b * tile : (b + 1) * tile] = inv[b]
    step = tile
    while step < size:
        for start in range(0, size, 2 * step):
            mid, end = start + step, start + 2 * step
            low = mm(work[mid:end, start:mid], work[start:mid, start:mid])
            work[mid:end, start:mid] = -mm(work[mid:end, mid:end], low)
        step *= 2
    solve = work[0:length, 0:length].astype(BF16)
    solve_ref[0] = solve
    fresh = mm(solve, p["beta"] * p["value"])
    out = mm(mm(p["query"], p["key"], NT) * p["weight"], fresh)
    scale = lax.rsqrt(jnp.sum(out * out, axis=1, keepdims=True) * (1.0 / DV) + 1e-05)
    gate = proj_ref[:, INNER:]
    mixed_ref[...] = (out * scale * gain_ref[...] * (gate * sigmoid(gate))).astype(BF16)


def backward_kernel(head, last, *refs):
    if last:
        (proj_ref, extra_ref, segc_ref, segr_ref, conv_ref, log_ref, bias_ref, gain_ref, solve_ref, grad_ref,
         turn_ref, other_ref, gproj_ref, gconv_ref, gsmall_ref) = refs
    else:
        (proj_ref, extra_ref, segc_ref, segr_ref, conv_ref, log_ref, bias_ref, gain_ref, solve_ref, grad_ref,
         turn_ref, gproj_ref, gextra_ref, gconv_ref, gsmall_ref) = refs
    conv = conv_ref[...]
    p = prepare(head, proj_ref[...], extra_ref[...], segc_ref[...], segr_ref[0], conv, log_ref, bias_ref)
    weight, strict, inner, beta, value = p["weight"], p["strict"], p["inner"], p["beta"], p["value"]
    query, key = p["query"], p["key"]
    solve = solve_ref[0]
    fresh = mm(solve, beta * value).astype(BF16)
    scores = mm(query, key, NT)
    probs = (scores * weight).astype(BF16)
    out = mm(probs, fresh)
    scale = lax.rsqrt(jnp.sum(out * out, axis=1, keepdims=True) * (1.0 / DV) + 1e-05)
    normed = out * scale
    gate = proj_ref[:, INNER:]
    gate_sig = sigmoid(gate)
    grad, width = 0.0, turn_ref.shape[2]
    for index in range(turn_ref.shape[0]):
        grad = grad + mm(grad_ref[:, index * width : (index + 1) * width], turn_ref[index], NT)
    gain = gain_ref[...]
    through = grad * normed
    ggate = through * gain * (gate_sig * (1.0 + gate * (1.0 - gate_sig)))
    ggain = jnp.sum(through * (gate * gate_sig), axis=0, keepdims=True)
    gnormed = grad * gain * (gate * gate_sig)
    gout = scale * (gnormed - normed * (jnp.sum(gnormed * normed, axis=1, keepdims=True) * (1.0 / DV)))
    gout = gout.astype(BF16)
    gprobs = mm(gout, fresh, NT)
    gfresh = mm(probs, gout, TN)
    gtarget = mm(solve, gfresh, TN)
    glower = -mm(gtarget, fresh, NT) * strict
    gscores = gprobs * weight
    tilt = glower * inner
    flow = gscores * scores + beta * tilt
    gbeta = jnp.sum(tilt, axis=1, keepdims=True) + jnp.sum(gtarget * value, axis=1, keepdims=True)
    gscores = gscores.astype(BF16)
    ginner = (beta * glower).astype(BF16)
    gquery = mm(gscores, key)
    gkey = mm(gscores, query, TN) + mm(ginner, key) + mm(ginner, key, TN)
    col_flow = jnp.sum(flow, axis=0, keepdims=True)
    col_flow = jnp.sum(jnp.where(p["rows"] == p["cols"], col_flow, 0.0), axis=1, keepdims=True)
    gdecay = reverse_cumsum_rows(jnp.sum(flow, axis=1, keepdims=True) - col_flow)
    raw_q, raw_k, scale_q, scale_k = p["raw_q"], p["raw_k"], p["scale_q"], p["scale_k"]
    gq = (DK ** (-0.5)) * scale_q * (
        gquery - raw_q * (scale_q * scale_q * jnp.sum(gquery * raw_q, axis=1, keepdims=True)))
    gk = scale_k * (gkey - raw_k * (scale_k * scale_k * jnp.sum(gkey * raw_k, axis=1, keepdims=True)))
    gactive = jnp.concatenate([gq, gk, beta * gtarget], axis=1)
    gsummed = gactive * (p["gate_conv"] * (1.0 + p["summed"] * (1.0 - p["gate_conv"])))
    source = proj_ref[:, :INNER]
    gsource = conv[TAPS - 1 : TAPS] * gsummed
    gconv_ref[0, TAPS - 1 : TAPS, :] = jnp.sum(gsummed * source, axis=0, keepdims=True)
    for lag in range(1, TAPS):
        kept = gsummed * p["keeps"][lag - 1]
        gsource = gsource + conv[TAPS - 1 - lag : TAPS - lag] * shift_up(kept, lag)
        gconv_ref[0, TAPS - 1 - lag : TAPS - lag, :] = jnp.sum(kept * shift_down(source, lag), axis=0, keepdims=True)
    gdrive = -p["rate"] * gdecay * sigmoid(p["drive"])
    gwrite = gbeta * beta * (1.0 - beta)
    lane = lax.broadcasted_iota(jnp.int32, extra_ref.shape, 1)
    gextra = jnp.where(lane == 2 * head, gwrite, jnp.where(lane == 2 * head + 1, gdrive, 0.0))
    gproj_ref[:, :INNER] = gsource.astype(BF16)
    gproj_ref[:, INNER:PER_HEAD] = ggate.astype(BF16)
    if last:
        gproj_ref[:, PER_HEAD:] = (gextra + other_ref[...].astype(F32)).astype(BF16)
    else:
        gextra_ref[...] = gextra.astype(BF16)
    glog = jnp.sum(gdecay * p["decay"], axis=0, keepdims=True)
    gbias = jnp.sum(gdrive, axis=0, keepdims=True)
    lane = lax.broadcasted_iota(jnp.int32, (1, 128), 1)
    gsmall_ref[0, :, 0:DV] = ggain
    gsmall_ref[0, :, DV:] = jnp.where(lane == 0, glog, jnp.where(lane == 1, gbias, 0.0))


def common_specs(length, heads, head, extra_block):
    smem = pl.BlockSpec(memory_space=pltpu.SMEM)
    return [
        pl.BlockSpec((length, PER_HEAD), lambda s: (s, 0)),
        pl.BlockSpec((length, 128), lambda s: (s, extra_block)),
        pl.BlockSpec((length, 1), lambda s: (s, 0)),
        pl.BlockSpec((1, 1, length), lambda s: (s, 0, 0)),
        pl.BlockSpec((TAPS, INNER), lambda s: (0, head)),
        smem,
        smem,
        pl.BlockSpec((1, DV), lambda s: (0, 0)),
    ]


def mixer_cost(count, passes):
    return pl.CostEstimate(flops=passes * count * (3 << 30), bytes_accessed=passes * count << 23, transcendentals=0)


def mixer_forward(head, heads, proj, extra, extra_block, seg_col, seg_row, conv, log, bias, gain):
    count, _, length = seg_row.shape
    tokens = count * length
    size = 64
    while size < length:
        size *= 2
    return pl.pallas_call(
        functools.partial(forward_kernel, head),
        grid=(count,),
        in_specs=common_specs(length, heads, head, extra_block),
        out_specs=[
            pl.BlockSpec((length, DV), lambda s: (s, 0)),
            pl.BlockSpec((1, length, length), lambda s: (s, 0, 0)),
        ],
        out_shape=[
            jax.ShapeDtypeStruct((tokens, DV), BF16),
            jax.ShapeDtypeStruct((count, length, length), BF16),
        ],
        scratch_shapes=[pltpu.VMEM((size, size), F32)],
        compiler_params=pltpu.CompilerParams(vmem_limit_bytes=56 << 20),
        cost_estimate=mixer_cost(count, 1),
        name="mixer_forward",
    )(proj, extra, seg_col, seg_row, conv, log, bias, gain)


def mixer_backward(head, heads, proj, extra, extra_block, seg_col, seg_row, conv, log, bias, gain, solve, grad, turned, other):
    count, _, length = seg_row.shape
    tokens = count * length
    last = other is not None
    in_specs = common_specs(length, heads, head, extra_block) + [
        pl.BlockSpec((1, length, length), lambda s: (s, 0, 0)),
        pl.BlockSpec((length, grad.shape[1]), lambda s: (s, 0)),
        pl.BlockSpec((turned.shape[0], DV, turned.shape[2]), lambda s: (0, head, 0)),
    ]
    args = [proj, extra, seg_col, seg_row, conv, log, bias, gain, solve, grad, turned]
    width = PER_HEAD
    tail_specs = [
        pl.BlockSpec((1, TAPS, INNER), lambda s: (s, 0, 0)),
        pl.BlockSpec((1, 1, DV + 128), lambda s: (s, 0, 0)),
    ]
    tail_shapes = [
        jax.ShapeDtypeStruct((count, TAPS, INNER), F32),
        jax.ShapeDtypeStruct((count, 1, DV + 128), F32),
    ]
    mid_specs, mid_shapes = [], []
    if last:
        width += 128
        in_specs.append(pl.BlockSpec((length, 128), lambda s: (s, 0)))
        args.append(other)
    else:
        mid_specs = [pl.BlockSpec((length, 128), lambda s: (s, 0))]
        mid_shapes = [jax.ShapeDtypeStruct((tokens, 128), BF16)]
    return pl.pallas_call(
        functools.partial(backward_kernel, head, last),
        grid=(count,),
        in_specs=in_specs,
        out_specs=[pl.BlockSpec((length, width), lambda s: (s, 0))] + mid_specs + tail_specs,
        out_shape=[jax.ShapeDtypeStruct((tokens, width), BF16)] + mid_shapes + tail_shapes,
        compiler_params=pltpu.CompilerParams(vmem_limit_bytes=60 << 20),
        cost_estimate=mixer_cost(count, 2),
        name="mixer_backward",
    )(*args)


MESH_ID = pl.DeviceIdType.MESH
HBM_SPEC = pl.BlockSpec(memory_space=pltpu.HBM)
VMEM_SPEC = pl.BlockSpec(memory_space=pltpu.VMEM)
STRIP = 16
DECAY_ROWS = 16


def meet(targets):
    barrier = pltpu.get_barrier_semaphore()
    for target in targets:
        pl.semaphore_signal(barrier, inc=1, device_id=target, device_id_type=MESH_ID)
    pl.semaphore_wait(barrier, len(targets))


def remote(source, dest, send, recv, index, target):
    return pltpu.make_async_remote_copy(
        src_ref=source,
        dst_ref=dest,
        send_sem=send.at[index],
        recv_sem=recv.at[index],
        device_id=target,
        device_id_type=MESH_ID,
    )


class Team:
    def __init__(self, name):
        self.name, self.part, self.col = name, lax.axis_index(name), lax.axis_index("col")
        self.across, self.twin = lax.rem(self.part + 2, 4), self.part + 1 - 2 * lax.rem(self.part, 2)
        self.far, self.other = lax.rem(self.twin + 2, 4), 1 - self.col
        self.x, self.y, self.core = {name: self.across}, {"col": self.other}, {name: self.twin}

    def partners(self):
        return [self.x, self.y, self.core]


def gather_phase(team, src, out, keep, send, recv):
    half = src.shape[0] // 2
    first, second = pl.ds(0, half), pl.ds(half, half)
    own, across = team.part * 2 + team.col, team.across * 2 + team.col
    other, diag = team.part * 2 + team.other, team.across * 2 + team.other
    local = pltpu.make_async_copy(src, out.at[own], keep)
    local.start()
    x_first = remote(src.at[first], out.at[own, first], send, recv, 0, team.x)
    x_second = remote(src.at[second], out.at[own, second], send, recv, 1, team.x)
    y_second = remote(src.at[second], out.at[own, second], send, recv, 2, team.y)
    y_first = remote(src.at[first], out.at[own, first], send, recv, 3, team.y)
    core_own = remote(src, out.at[own], send, recv, 4, team.core)
    for copy in (x_first, y_second, core_own, x_second, y_first):
        copy.start()
    y_pass = remote(out.at[across, first], out.at[across, first], send, recv, 5, team.y)
    x_pass = remote(out.at[other, second], out.at[other, second], send, recv, 6, team.x)
    core_x = remote(out.at[across], out.at[across], send, recv, 7, team.core)
    core_y = remote(out.at[other], out.at[other], send, recv, 8, team.core)
    core_first = remote(out.at[diag, first], out.at[diag, first], send, recv, 9, team.core)
    core_second = remote(out.at[diag, second], out.at[diag, second], send, recv, 10, team.core)
    x_first.wait_recv()
    y_pass.start()
    y_second.wait_recv()
    x_pass.start()
    x_second.wait_recv()
    core_x.start()
    y_first.wait_recv()
    core_y.start()
    y_pass.wait_recv()
    core_first.start()
    x_pass.wait_recv()
    core_second.start()
    for copy in (core_own, core_x, core_y, core_first, core_second):
        copy.wait_recv()
    for copy in (
        x_first, x_second, y_second, y_first, core_own, y_pass, x_pass, core_x, core_y, core_first, core_second,
    ):
        copy.wait_send()
    local.wait()


GATHER_SEMS = [pltpu.SemaphoreType.DMA, pltpu.SemaphoreType.DMA((11,)), pltpu.SemaphoreType.DMA((11,))]


class Spread:
    def __init__(self, src, out, middle, keep, send, recv):
        self.src, self.out, self.middle, self.keep, self.send, self.recv = src, out, middle, keep, send, recv
        self.row, self.col = lax.axis_index("row"), lax.axis_index("col")
        self.hops = [
            remote(src.at[2 * item + 1 - self.col], middle.at[item], send, recv, item, {"col": 1 - self.col})
            for item in range(2)
        ]

    def pieces(self, side):
        home = self.col if side == 0 else 1 - self.col
        for item in range(2):
            source = self.src.at[2 * item + self.col] if side == 0 else self.middle.at[item]
            to_row = 2 * home + item
            copy = pltpu.make_async_remote_copy(
                src_ref=source,
                dst_ref=self.out.at[self.row],
                send_sem=self.send.at[2 + 2 * side + item],
                recv_sem=self.recv.at[2 + self.row],
                device_id={"row": to_row},
                device_id_type=MESH_ID,
            )
            yield to_row == self.row, copy, pltpu.make_async_copy(source, self.out.at[self.row], self.keep)

    def start(self):
        for hop in self.hops:
            hop.start()
        self.send_side(0)

    def send_side(self, side):
        for here, far, near in self.pieces(side):
            pl.when(here)(near.start)
            pl.when(jnp.logical_not(here))(far.start)

    def turn(self):
        for hop in self.hops:
            hop.wait_recv()
        self.send_side(1)

    def finish(self):
        for hop in range(1, 4):
            index = lax.rem(self.row + hop, 4)
            pltpu.make_async_remote_copy(
                src_ref=self.src.at[0],
                dst_ref=self.out.at[index],
                send_sem=self.send.at[0],
                recv_sem=self.recv.at[2 + index],
                device_id={"row": index},
                device_id_type=MESH_ID,
            ).wait_recv()
        for side in range(2):
            for here, far, near in self.pieces(side):
                pl.when(here)(near.wait)
                pl.when(jnp.logical_not(here))(far.wait_send)
        for hop in self.hops:
            hop.wait_send()


class Line:
    def __init__(self, src, out, keep, send, recv):
        self.src, self.out, self.send, self.recv = src, out, send, recv
        self.row = lax.axis_index("row")
        self.near = pltpu.make_async_copy(src, out.at[self.row], keep)

    def copy(self, hops, up):
        step = 1 if up else -1
        mark = self.row - hops * step
        return pltpu.make_async_remote_copy(
            src_ref=self.src if hops == 0 else self.out.at[mark],
            dst_ref=self.out.at[mark],
            send_sem=self.send.at[hops if up else 3 + hops],
            recv_sem=self.recv.at[mark],
            device_id={"row": self.row + step},
            device_id_type=MESH_ID,
        )

    def sends(self, hops, up):
        return (self.row >= hops) & (self.row < 3) if up else (self.row + hops <= 3) & (self.row > 0)

    def start(self):
        self.near.start()
        for up in (True, False):
            pl.when(self.sends(0, up))(lambda: self.copy(0, up).start())

    def arrive(self, hops):
        for up in (True, False):
            mark = self.row - hops if up else self.row + hops

            @pl.when((self.row >= hops) if up else (self.row + hops <= 3))
            def _():
                pltpu.make_async_remote_copy(
                    src_ref=self.src,
                    dst_ref=self.out.at[mark],
                    send_sem=self.send.at[0],
                    recv_sem=self.recv.at[mark],
                    device_id={"row": self.row - 1 if up else self.row + 1},
                    device_id_type=MESH_ID,
                ).wait_recv()

    def pass_on(self, hops):
        self.arrive(hops)
        for up in (True, False):
            pl.when(self.sends(hops, up))(lambda: self.copy(hops, up).start())

    def finish(self):
        self.arrive(3)
        for hops in range(3):
            for up in (True, False):
                pl.when(self.sends(hops, up))(lambda: self.copy(hops, up).wait_send())
        self.near.wait()


def share(source, dest, mark, others, keep, send, recv):
    near = pltpu.make_async_copy(source, dest.at[mark], keep)
    near.start()
    copies = []
    for item, (target, _) in enumerate(others):
        copies.append(
            pltpu.make_async_remote_copy(
                src_ref=source,
                dst_ref=dest.at[mark],
                send_sem=send.at[item],
                recv_sem=recv.at[mark],
                device_id=target,
                device_id_type=MESH_ID,
            )
        )
        copies[item].start()

    def finish():
        near.wait()
        for target, index in others:
            pltpu.make_async_remote_copy(
                src_ref=source,
                dst_ref=dest.at[index],
                send_sem=send.at[0],
                recv_sem=recv.at[index],
                device_id=target,
                device_id_type=MESH_ID,
            ).wait_recv()
        for copy in copies:
            copy.wait_send()

    return finish


def enter_kernel(part_name, *refs):
    sources, outs, scratch = refs[:5], refs[5:12], refs[12:]
    first, second, gains, segs, weight = sources
    first_tok, first_all, second_tok, second_all, gains_all, segs_all, weight_all = outs
    (stage_one, middle_one, stage_two, middle_two, ready_one, ready_two, line_keep, line_send, line_recv, small_keep,
     gain_send, gain_recv, seg_send, seg_recv) = scratch[:14]
    spread_one, spread_two, gather_one, gather_two = (scratch[14 + 3 * index : 17 + 3 * index] for index in range(4))
    team = Team(part_name)
    row = lax.axis_index("row")
    rows = [({"row": lax.rem(row + hop, 4)}, lax.rem(row + hop, 4)) for hop in range(1, 4)]
    meet(team.partners() + [target for target, _ in rows] + [{part_name: team.far}])
    one = Spread(first, stage_one, middle_one, *spread_one)
    two = Spread(second, stage_two, middle_two, *spread_two)
    line = Line(weight, weight_all, line_keep, line_send, line_recv)
    one.start()
    done_gains = share(gains, gains_all, row, rows, small_keep.at[0], gain_send, gain_recv)
    parts = [({part_name: index}, index) for index in (team.across, team.twin, team.far)]
    done_segs = share(segs, segs_all, team.part, parts, small_keep.at[1], seg_send, seg_recv)
    line.start()
    one.turn()
    two.start()
    one.finish()
    done_gains()
    done_segs()
    tokens, width = first.shape[1], first.shape[2]

    def norm(rows, _):
        wides = [stage_one[index, rows, :].astype(F32) for index in range(4)]
        square = sum(jnp.sum(wide * wide, axis=1, keepdims=True) for wide in wides)
        scale = lax.rsqrt(square * (1.0 / (4 * width)) + 1e-05)
        for index in range(4):
            cols = slice(index * width, (index + 1) * width)
            first_tok[rows, cols] = stage_one[index, rows, :]
            ready_one[rows, cols] = (wides[index] * scale * gains_all[index, 0:1, :]).astype(BF16)

    strips(0, tokens, norm)
    two.turn()
    line.pass_on(1)
    gather_phase(team, ready_one, first_all, *gather_one)
    two.finish()

    def join_blocks(rows, _):
        for index in range(4):
            cols = slice(index * width, (index + 1) * width)
            second_tok[rows, cols] = stage_two[index, rows, :]
            ready_two[rows, cols] = stage_two[index, rows, :]

    strips(0, tokens, join_blocks)
    line.pass_on(2)
    gather_phase(team, ready_two, second_all, *gather_two)
    line.finish()


def enter_call(lay, first, second, gains, segs, weight):
    tokens, width = first.shape[0] // 4, first.shape[1]
    wide = 4 * width
    tok, everyone = jax.ShapeDtypeStruct((tokens, wide), BF16), jax.ShapeDtypeStruct((8, tokens, wide), BF16)
    stage = [pltpu.VMEM((4, tokens, width), BF16), pltpu.VMEM((2, tokens, width), BF16)]
    line_sems = [pltpu.SemaphoreType.DMA, pltpu.SemaphoreType.DMA((6,)), pltpu.SemaphoreType.DMA((4,))]
    small_sems = [pltpu.SemaphoreType.DMA((count,)) for count in (2, 3, 4, 3, 4)]
    spread_sems = [pltpu.SemaphoreType.DMA, pltpu.SemaphoreType.DMA((6,)), pltpu.SemaphoreType.DMA((6,))]
    results = pl.pallas_call(
        functools.partial(enter_kernel, lay.part),
        in_specs=[HBM_SPEC, HBM_SPEC, VMEM_SPEC, VMEM_SPEC, HBM_SPEC],
        out_specs=[VMEM_SPEC, HBM_SPEC, VMEM_SPEC, HBM_SPEC, VMEM_SPEC, VMEM_SPEC, HBM_SPEC],
        out_shape=[
            tok,
            everyone,
            tok,
            everyone,
            jax.ShapeDtypeStruct((4,) + gains.shape, gains.dtype),
            jax.ShapeDtypeStruct((4,) + segs.shape, segs.dtype),
            jax.ShapeDtypeStruct((4,) + weight.shape, weight.dtype),
        ],
        scratch_shapes=stage
        + stage
        + [pltpu.VMEM((tokens, wide), BF16)] * 2
        + line_sems
        + small_sems
        + spread_sems
        + spread_sems
        + GATHER_SEMS
        + GATHER_SEMS,
        compiler_params=pltpu.CompilerParams(
            collective_id=lay.fresh_id(), has_side_effects=True, vmem_limit_bytes=60 << 20
        ),
        cost_estimate=pl.CostEstimate(flops=1 << 30, bytes_accessed=400 << 20, transcendentals=0),
        name="enter",
    )(first.reshape(4, tokens, width), second.reshape(4, tokens, width), gains, segs, weight)
    first_tok, first_all, second_tok, second_all, gains, segs, weight = results
    return (
        first_tok, first_all.reshape(-1, wide), second_tok, second_all.reshape(-1, wide), gains, segs, weight,
    )


def strips(start, count, body):
    @pl.loop(0, count // STRIP)
    def _(step):
        body(pl.ds(pl.multiple_of(start + step * STRIP, STRIP), STRIP), pl.ds(pl.multiple_of(step * STRIP, STRIP), STRIP))


class Scatter:
    def __init__(self, team, dots, finish, refs):
        self.team, self.dots, self.finish = team, dots, finish
        self.work, self.twin, self.sent, self.relay, self.final, self.send, self.recv = refs
        self.rows, self.chunk = self.twin.shape[1], self.twin.shape[2] // 4
        self.half = self.rows // 2
        first, second = pl.ds(0, self.half), pl.ds(self.half, self.half)
        sent, relay, final = self.sent, self.relay, self.final
        self.relay_x = self.copy(sent.at[0, first], relay.at[0], 4, team.x)
        self.relay_y = self.copy(sent.at[0, second], relay.at[1], 5, team.y)
        self.x_first = self.copy(sent.at[1, first], final.at[0, first], 6, team.x)
        self.x_second = self.copy(sent.at[1, second], final.at[0, second], 7, team.x)
        self.y_second = self.copy(sent.at[2, second], final.at[1, second], 8, team.y)
        self.y_first = self.copy(sent.at[2, first], final.at[1, first], 9, team.y)

    def copy(self, source, dest, index, target):
        return remote(source, dest, self.send, self.recv, index, target)

    def swap(self, item):
        return self.copy(self.work.at[item, 0], self.twin.at[item], item, self.team.core)

    def total(self, item, start, passed=None):
        def add(rows, local):
            value = self.work[item, 1, rows, :].astype(F32) + self.twin[item, rows, :].astype(F32)
            if passed is not None:
                value = value + self.relay[passed, local, :].astype(F32)
            self.sent[item, rows, :] = value.astype(BF16)

        strips(start, self.half, add)

    def begin(self):
        team = self.team

        @pl.loop(0, 4)
        def _(item):
            @pl.loop(0, 8)
            def _(step):
                which, chunk = step // 4, lax.rem(step, 4)
                base = team.part * which + team.twin * (1 - which)
                slot = lax.rem(base + 2 * (1 - item // 2), 4) * 2 + lax.rem(team.col + 1 + item, 2)
                columns = pl.ds(pl.multiple_of(chunk * self.chunk, self.chunk), self.chunk)
                rows = pl.ds(pl.multiple_of(slot * self.rows, STRIP), self.rows)
                self.work[item, which, :, columns] = self.dots(rows, chunk, columns).astype(BF16)

            self.swap(item).start()

            @pl.when(item == 1)
            def _():
                self.swap(0).wait_recv()
                self.total(0, 0)
                self.relay_x.start()
                self.total(0, self.half)
                self.relay_y.start()

            @pl.when(item == 2)
            def _():
                self.swap(1).wait_recv()
                self.total(1, 0)
                self.x_first.start()

            @pl.when(item == 3)
            def _():
                self.swap(2).wait_recv()
                self.total(2, self.half)
                self.y_second.start()

    def pass_on(self):
        self.relay_y.wait_recv()
        self.total(1, self.half, 1)
        self.x_second.start()
        self.relay_x.wait_recv()
        self.total(2, 0, 0)
        self.y_first.start()

    def conclude(self):
        self.swap(3).wait_recv()

        def last(rows, _):
            value = self.work[3, 1, rows, :].astype(F32) + self.twin[3, rows, :].astype(F32)
            self.finish(rows, value + self.final[0, rows, :].astype(F32) + self.final[1, rows, :].astype(F32))

        self.x_first.wait_recv()
        self.y_first.wait_recv()
        strips(0, self.half, last)
        self.x_second.wait_recv()
        self.y_second.wait_recv()
        strips(self.half, self.half, last)
        for copy in [self.swap(item) for item in range(4)]:
            copy.wait_send()
        for copy in (self.relay_x, self.relay_y, self.x_first, self.x_second, self.y_second, self.y_first):
            copy.wait_send()


def scatter_scratch(tokens, wide):
    return [
        pltpu.VMEM((4, 2, tokens, wide), BF16),
        pltpu.VMEM((4, tokens, wide), BF16),
        pltpu.VMEM((3, tokens, wide), BF16),
        pltpu.VMEM((2, tokens // 2, wide), BF16),
        pltpu.VMEM((2, tokens, wide), BF16),
        pltpu.SemaphoreType.DMA((10,)),
        pltpu.SemaphoreType.DMA((10,)),
    ]


def make_dots(lefts, rights, starts):
    def dots(rows, chunk, columns):
        value = 0.0
        for left, (index, start) in zip(lefts, starts):
            right, depth = rights[index], slice(start, start + left.shape[1])
            if len(right.shape) == 3:
                value = value + lax.dot_general(left[rows, :], right[chunk, depth, :], NN, preferred_element_type=F32)
            else:
                value = value + lax.dot_general(left[rows, :], right[columns, depth], NT, preferred_element_type=F32)
        return value

    return dots


def norm_back(value, total, gain, gain_sum):
    scale = lax.rsqrt(jnp.sum(value * value, axis=1, keepdims=True) * (1.0 / value.shape[1]) + 1e-05)
    normed = value * scale
    gain_sum[...] += total * normed
    scaled = total * gain
    inner = jnp.sum(scaled * normed, axis=1, keepdims=True) * (1.0 / value.shape[1])
    return scale * (scaled - normed * inner)


def deal_out(out, rows, value):
    width = value.shape[1] // 4
    for index in range(4):
        out[index, rows, :] = value[:, index * width : (index + 1) * width].astype(BF16)


def fetch(sources, places, sems):
    copies = []
    for index, (source, place) in enumerate(zip(sources, places)):
        if isinstance(source, tuple):
            ref, start = source
            source = ref.at[:, pl.ds(start, place.shape[1]), :]
        copies.append(pltpu.make_async_copy(source, place, sems.at[index]))
        copies[index].start()
    return copies


def fetched(shapes):
    return [pltpu.VMEM(shape, dtype) for shape, dtype in shapes] + [pltpu.SemaphoreType.DMA((len(shapes),))]


def whole(values):
    return values.shape, values.dtype


def mid_kernel(part_name, starts, *refs):
    count = len(starts)
    sources, (out, everyone), scratch = refs[: count + 3], refs[count + 3 : count + 5], refs[count + 5 :]
    places, sems, scratch = scratch[: count + 3], scratch[count + 3], scratch[count + 4 :]
    loads = fetch(sources, places, sems)
    lefts, (right, stored, gain) = places[:count], places[count:]
    ready = scratch[7]
    team = Team(part_name)
    meet(team.partners())
    for load in loads:
        load.wait()

    def finish(rows, total):
        value = stored[rows, :].astype(F32) + total
        out[rows, :] = value
        scale = lax.rsqrt(jnp.sum(value * value, axis=1, keepdims=True) * (1.0 / value.shape[1]) + 1e-05)
        ready[rows, :] = (value * scale * gain[...]).astype(BF16)

    scatter = Scatter(team, make_dots(lefts, [right], starts), finish, scratch[:7])
    scatter.begin()
    scatter.pass_on()
    scatter.conclude()
    gather_phase(team, ready, everyone, *scratch[8:])


def mid_call(lay, lefts, right, starts, stored, gain):
    tokens, wide = stored.shape
    residual, everyone = pl.pallas_call(
        functools.partial(mid_kernel, lay.part, starts),
        in_specs=[HBM_SPEC] * (len(lefts) + 3),
        out_specs=[VMEM_SPEC, HBM_SPEC],
        out_shape=[jax.ShapeDtypeStruct((tokens, wide), F32), jax.ShapeDtypeStruct((8, tokens, wide), BF16)],
        scratch_shapes=fetched([whole(values) for values in (*lefts, right, stored, gain)])
        + scatter_scratch(tokens, wide) + [pltpu.VMEM((tokens, wide), BF16)] + GATHER_SEMS,
        compiler_params=pltpu.CompilerParams(
            collective_id=lay.fresh_id(), has_side_effects=True, vmem_limit_bytes=60 << 20
        ),
        cost_estimate=pl.CostEstimate(flops=1 << 35, bytes_accessed=200 << 20, transcendentals=0),
        name="team_mid",
    )(*lefts, right, stored, gain)
    return residual, everyone.reshape(8 * tokens, wide)


def branch_kernel(part_name, count, *refs):
    total = 2 * count + 3
    sources, (out, everyone, gain_out), scratch = refs[:total], refs[total : total + 3], refs[total + 3 :]
    places, sems, scratch = scratch[:total], scratch[total], scratch[total + 1 :]
    sources = [(ref, 0) if count <= index < 2 * count else ref for index, ref in enumerate(sources)]
    loads = fetch(sources, places, sems)
    lefts, rights, (residual, through, gain) = places[:count], places[count : 2 * count], places[2 * count :]
    gain_sum, ready = scratch[7:9]
    team = Team(part_name)
    meet(team.partners())
    for load in loads:
        load.wait()
    gain_sum[...] = jnp.zeros_like(gain_sum)

    def finish(rows, total):
        value = through[rows, :].astype(F32) + norm_back(residual[rows, :], total, gain[...], gain_sum)
        out[rows, :] = value
        ready[rows, :] = value.astype(BF16)

    scatter = Scatter(team, make_dots(lefts, rights, [(index, 0) for index in range(count)]), finish, scratch[:7])
    scatter.begin()
    scatter.pass_on()
    scatter.conclude()
    gain_out[...] = jnp.sum(gain_sum[...], axis=0, keepdims=True)
    gather_phase(team, ready, everyone, *scratch[9:])


def branch_call(lay, lefts, rights, residual, through, gain):
    tokens, wide = residual.shape
    width = rights[0].shape[2]
    out, everyone, gain_part = pl.pallas_call(
        functools.partial(branch_kernel, lay.part, len(lefts)),
        in_specs=[HBM_SPEC] * (2 * len(lefts) + 3),
        out_specs=[VMEM_SPEC, HBM_SPEC, VMEM_SPEC],
        out_shape=[
            jax.ShapeDtypeStruct((tokens, wide), F32),
            jax.ShapeDtypeStruct((8, tokens, wide), BF16),
            jax.ShapeDtypeStruct((1, wide), F32),
        ],
        scratch_shapes=fetched(
            [whole(left) for left in lefts]
            + [((4, left.shape[1], width), BF16) for left in lefts]
            + [whole(values) for values in (residual, through, gain)]
        )
        + scatter_scratch(tokens, wide)
        + [pltpu.VMEM((STRIP, wide), F32), pltpu.VMEM((tokens, wide), BF16)]
        + GATHER_SEMS,
        compiler_params=pltpu.CompilerParams(
            collective_id=lay.fresh_id(), has_side_effects=True, vmem_limit_bytes=60 << 20
        ),
        cost_estimate=pl.CostEstimate(flops=1 << 35, bytes_accessed=250 << 20, transcendentals=0),
        name="team_branch",
    )(*lefts, *rights, residual, through, gain)
    return out, everyone.reshape(8 * tokens, wide), gain_part


def finish_kernel(part_name, count, starts, *refs):
    total = 2 * count + len(starts) + 5
    sources, (block_out, input_out, gain_out), scratch = refs[:total], refs[total : total + 3], refs[total + 3 :]
    places, sems, scratch = scratch[:total], scratch[total], scratch[total + 1 :]
    hidden, downs, grads = places[:count], places[count : 2 * count], places[2 * count : -5]
    mix, residual, stored, through, gain = places[-5:]
    downs_from = [(ref, 2 * values.shape[1]) for ref, values in zip(sources[count : 2 * count], hidden)]
    loads = fetch([*sources[:count], *downs_from, *sources[2 * count :]], places, sems)
    gain_sum = scratch[14]
    team = Team(part_name)
    meet(team.partners())
    for load in loads[: 2 * count]:
        load.wait()
    gain_sum[...] = jnp.zeros_like(gain_sum)

    def finish_block(rows, total):
        deal_out(block_out, rows, residual[rows, :] + total)

    def finish_input(rows, total):
        value = norm_back(stored[rows, :].astype(F32), total, gain[...], gain_sum)
        deal_out(input_out, rows, through[rows, :] + value)

    block = Scatter(
        team, make_dots(hidden, downs, [(index, 0) for index in range(count)]), finish_block, scratch[:7]
    )
    inputs = Scatter(team, make_dots(grads, [mix], [(0, start) for start in starts]), finish_input, scratch[7:14])
    block.begin()
    for load in loads[2 * count :]:
        load.wait()
    inputs.begin()
    block.pass_on()
    inputs.pass_on()
    block.conclude()
    inputs.conclude()
    gain_out[...] = jnp.sum(gain_sum[...], axis=0, keepdims=True)


def finish_call(lay, hidden, stacks, grads, mix, starts, residual, stored, through, gain):
    tokens, wide = residual.shape
    width = stacks[0].shape[2]
    pieces = jax.ShapeDtypeStruct((4, tokens, width), BF16)
    return pl.pallas_call(
        functools.partial(finish_kernel, lay.part, len(hidden), starts),
        in_specs=[HBM_SPEC] * (2 * len(hidden) + len(grads) + 5),
        out_specs=[VMEM_SPEC] * 3,
        out_shape=[pieces, pieces, jax.ShapeDtypeStruct((1, wide), F32)],
        scratch_shapes=fetched(
            [whole(values) for values in hidden]
            + [((4, values.shape[1], width), BF16) for values in hidden]
            + [whole(values) for values in (*grads, mix, residual, stored, through, gain)]
        )
        + scatter_scratch(tokens, wide)
        + scatter_scratch(tokens, wide)
        + [pltpu.VMEM((STRIP, wide), F32)],
        compiler_params=pltpu.CompilerParams(
            collective_id=lay.fresh_id(), has_side_effects=True, vmem_limit_bytes=60 << 20
        ),
        cost_estimate=pl.CostEstimate(flops=1 << 35, bytes_accessed=250 << 20, transcendentals=0),
        name="team_finish",
    )(*hidden, *stacks, *grads, mix, residual, stored, through, gain)


class Deal:
    def __init__(self, src, out, keep, send, recv):
        self.src, self.out, self.keep, self.send, self.recv = src, out, keep, send, recv
        self.row, self.col = lax.axis_index("row"), lax.axis_index("col")
        spot = self.row * 2 + self.col
        self.mark, self.home = lax.rem(spot, 4), spot // 4

    def owner(self, index):
        place = self.col * 4 + index
        return {"row": place // 2, "col": lax.rem(place, 2)}

    def apart(self, index):
        owner = self.owner(index)
        return (owner["row"] != self.row) | (owner["col"] != self.col)

    def greet(self, barrier):
        for index in range(4):

            @pl.when(self.apart(index))
            def _():
                pl.semaphore_signal(barrier, inc=1, device_id=self.owner(index), device_id_type=MESH_ID)

        return 4 - (self.home == self.col).astype(jnp.int32)

    def each(self, act_near, act_far):
        for index in range(4):
            here = (self.row == index) & (self.home == self.col)

            @pl.when(here)
            def _():
                act_near(pltpu.make_async_copy(self.src.at[index], self.out.at[self.mark], self.keep))

            @pl.when(jnp.logical_not(here))
            def _():
                act_far(
                    pltpu.make_async_remote_copy(
                        src_ref=self.src.at[index],
                        dst_ref=self.out.at[self.mark],
                        send_sem=self.send.at[index],
                        recv_sem=self.recv.at[self.mark],
                        device_id={"row": index, "col": self.home},
                        device_id_type=MESH_ID,
                    )
                )

    def start(self):
        self.each(lambda copy: copy.start(), lambda copy: copy.start())

    def finish(self):
        for index in range(4):

            @pl.when(self.apart(index))
            def _():
                pltpu.make_async_remote_copy(
                    src_ref=self.src.at[0],
                    dst_ref=self.out.at[index],
                    send_sem=self.send.at[0],
                    recv_sem=self.recv.at[index],
                    device_id=self.owner(index),
                    device_id_type=MESH_ID,
                ).wait_recv()

        self.each(lambda copy: copy.wait(), lambda copy: copy.wait_send())


DEAL_SEMS = [pltpu.SemaphoreType.DMA, pltpu.SemaphoreType.DMA((4,)), pltpu.SemaphoreType.DMA((4,))]


def leave_kernel(part_name, *refs):
    first, second, block, src, first_out, second_out, blocks, out = refs[:8]
    deals = [Deal(first, first_out, *refs[8:11]), Deal(second, second_out, *refs[11:14])]
    rows_in, summed, near, row_send, row_recv, team_send, team_recv, join_send, join_recv = refs[14:]
    team = Team(part_name)
    row = lax.axis_index("row")
    rows = [({"row": lax.rem(row + hop, 4)}, lax.rem(row + hop, 4)) for hop in range(1, 4)]
    mates = []
    for part in (team.part, team.across, team.twin, team.far):
        for side in (team.col, team.other):
            mates.append(({part_name: part, "col": side}, part * 2 + side))
    mates = mates[1:]
    barrier = pltpu.get_barrier_semaphore()
    for target, _ in rows + mates:
        pl.semaphore_signal(barrier, inc=1, device_id=target, device_id_type=MESH_ID)
    pl.semaphore_wait(barrier, len(rows + mates) + deals[0].greet(barrier))
    own, across = blocks.at[team.part], blocks.at[team.across]
    join_x = remote(block, own, join_send, join_recv, 0, team.x)
    join_core = remote(block, own, join_send, join_recv, 1, team.core)
    join_pass = remote(across, across, join_send, join_recv, 2, team.core)
    join_near = pltpu.make_async_copy(block, own, near.at[2])
    finish_rows = share(src, rows_in, row, rows, near.at[0], row_send, row_recv)
    for copy in (join_x, join_core, join_near):
        copy.start()
    for deal in deals:
        deal.start()
    finish_rows()
    summed[...] = (rows_in[0] + rows_in[1]) + (rows_in[2] + rows_in[3])
    finish_team = share(summed, out, team.part * 2 + team.col, mates, near.at[1], team_send, team_recv)
    join_x.wait_recv()
    join_pass.start()
    for deal in deals:
        deal.finish()
    finish_team()
    join_core.wait_recv()
    join_pass.wait_recv()
    for copy in (join_x, join_core, join_pass):
        copy.wait_send()
    join_near.wait()


def leave_call(lay, first, second, block, small):
    whole_array = jax.ShapeDtypeStruct(first.shape, first.dtype)
    return pl.pallas_call(
        functools.partial(leave_kernel, lay.part),
        in_specs=[HBM_SPEC, HBM_SPEC, HBM_SPEC, VMEM_SPEC],
        out_specs=[HBM_SPEC, HBM_SPEC, HBM_SPEC, VMEM_SPEC],
        out_shape=[
            whole_array,
            whole_array,
            jax.ShapeDtypeStruct((4,) + block.shape, block.dtype),
            jax.ShapeDtypeStruct((8,) + small.shape, F32),
        ],
        scratch_shapes=DEAL_SEMS
        + DEAL_SEMS
        + [pltpu.VMEM((4,) + small.shape, F32), pltpu.VMEM(small.shape, F32)]
        + [pltpu.SemaphoreType.DMA((count,)) for count in (3, 3, 4, 7, 8, 3, 3)],
        compiler_params=pltpu.CompilerParams(
            collective_id=lay.fresh_id(), has_side_effects=True, vmem_limit_bytes=60 << 20
        ),
        cost_estimate=pl.CostEstimate(flops=1 << 30, bytes_accessed=120 << 20, transcendentals=0),
        name="leave",
    )(first, second, block, small)


def cross(lay, value):
    return lax.ppermute(value, lay.part, [(0, 2), (2, 0), (1, 3), (3, 1)])


def link(lay, value):
    return lax.ppermute(value, lay.part, [(0, 1), (1, 0), (2, 3), (3, 2)])


def part_order(lay):
    part = lax.axis_index(lay.part)
    twin = part + 1 - 2 * (part % 2)
    return jnp.stack([part, (part + 2) % 4, twin, (twin + 2) % 4]).astype(jnp.int32)


def rows_kernel(order, *refs):
    for index, ref in enumerate(refs[:4]):

        @pl.when(pl.program_id(1) == index)
        def _():
            refs[4][...] = ref[...].astype(F32)


def place_rows(order, pieces, start, rows):
    width = pieces[0].shape[1]
    block = rows
    while start % block:
        block //= 2
    steps = rows // block
    return pl.pallas_call(
        rows_kernel,
        grid_spec=pltpu.PrefetchScalarGridSpec(
            num_scalar_prefetch=1,
            grid=(steps, 4),
            in_specs=[pl.BlockSpec((block, width), lambda j, i, order: (start // block + j, 0))] * 4,
            out_specs=pl.BlockSpec((block, width), lambda j, i, order: (order[i] * steps + j, 0)),
        ),
        out_shape=jax.ShapeDtypeStruct((4 * rows, width), F32),
        compiler_params=pltpu.CompilerParams(vmem_limit_bytes=60 << 20),
        name="place_rows",
    )(order, *pieces)


def late_head_kernel(order, *refs):
    for index, ref in enumerate(refs[:4]):

        @pl.when(pl.program_id(0) == index)
        def _():
            refs[4][...] = ref[...].T.astype(F32)


def place_late_head(order, heads, head, pieces):
    features = pieces[0].shape[1]
    return pl.pallas_call(
        late_head_kernel,
        grid_spec=pltpu.PrefetchScalarGridSpec(
            num_scalar_prefetch=1,
            grid=(4,),
            in_specs=[pl.BlockSpec((PER_HEAD, features), lambda i, order: (0, 0))] * 4,
            out_specs=pl.BlockSpec((features, PER_HEAD), lambda i, order: (0, order[i] * heads + head)),
        ),
        out_shape=jax.ShapeDtypeStruct((features, 4 * heads * PER_HEAD), F32),
        compiler_params=pltpu.CompilerParams(vmem_limit_bytes=60 << 20),
        name="place_late_head",
    )(order, *pieces)


def first_head_kernel(heads, src, tail, _, out, decay):
    out[...] = src[0].T.astype(F32)
    small = tail[0].astype(F32).T[:, : 2 * heads]
    for part in range(4):

        @pl.when(pl.program_id(0) == part)
        def _():
            decay[:, part * 2 * heads : (part + 1) * 2 * heads] = small


def place_first_head(heads, stack, whole_grad):
    features = stack.shape[2]
    return pl.pallas_call(
        functools.partial(first_head_kernel, heads),
        grid=(4,),
        in_specs=[
            pl.BlockSpec((1, PER_HEAD, features), lambda i: (i, 0, 0)),
            pl.BlockSpec((1, DECAY_ROWS, features), lambda i: (i, PER_HEAD // DECAY_ROWS, 0)),
            HBM_SPEC,
        ],
        out_specs=[
            pl.BlockSpec((features, PER_HEAD), lambda i: (0, i * heads)),
            pl.BlockSpec((features, 8 * heads), lambda i: (0, 0)),
        ],
        out_shape=[
            jax.ShapeDtypeStruct((features, 4 * heads * PER_HEAD), F32),
            jax.ShapeDtypeStruct((features, 8 * heads), F32),
        ],
        input_output_aliases={2: 0},
        compiler_params=pltpu.CompilerParams(vmem_limit_bytes=60 << 20),
        name="place_first_head",
    )(stack, stack, whole_grad)


def place_ffn_kernel(counts, order, *refs):
    units = sum(counts)
    blocks = len(counts)
    pairs, downs = refs[: 4 * blocks], refs[4 * blocks : 8 * blocks]
    gate, up, down = refs[8 * blocks : 8 * blocks + 3]
    turned = refs[8 * blocks + 3 :]
    base = 0
    for block, count in enumerate(counts):
        for index in range(4):
            turned[block][order[index]] = pairs[4 * block + index][...].T.astype(F32)
            start = pl.multiple_of(order[index] * units + base, 64)
            down[pl.ds(start, count), :] = downs[4 * block + index][...].astype(F32)
        for part in range(4):
            place = slice(part * units + base, part * units + base + count)
            gate[:, place] = turned[block][part, :, :count]
            up[:, place] = turned[block][part, :, count:]
        base += count


def place_ffn(order, pieces):
    counts = [group[0].shape[0] // 3 for group in pieces]
    flat = [piece for group in pieces for piece in group]
    features, units = flat[0].shape[1], sum(counts)
    wide = jax.ShapeDtypeStruct((features, 4 * units), F32)
    return pl.pallas_call(
        functools.partial(place_ffn_kernel, counts),
        grid_spec=pltpu.PrefetchScalarGridSpec(
            num_scalar_prefetch=1,
            grid=(features // 128,),
            in_specs=[pl.BlockSpec((2 * (p.shape[0] // 3), 128), lambda i, order: (0, i)) for p in flat]
            + [pl.BlockSpec((p.shape[0] // 3, 128), lambda i, order: (2, i)) for p in flat],
            out_specs=[
                pl.BlockSpec((128, 4 * units), lambda i, order: (i, 0)),
                pl.BlockSpec((128, 4 * units), lambda i, order: (i, 0)),
                pl.BlockSpec((4 * units, 128), lambda i, order: (0, i)),
            ],
            scratch_shapes=[pltpu.VMEM((4, 128, 2 * count), F32) for count in counts],
        ),
        out_shape=[wide, wide, jax.ShapeDtypeStruct((4 * units, features), F32)],
        compiler_params=pltpu.CompilerParams(vmem_limit_bytes=60 << 20),
        cost_estimate=pl.CostEstimate(flops=1 << 30, bytes_accessed=30 << 20, transcendentals=0),
        name="place_ffn",
    )(order, *flat, *flat)


def stack_kernel(counts, *refs):
    grads, values, out = refs[: len(counts)], refs[len(counts) : -1], refs[-1]
    base = 0
    for grad, value, count in zip(grads, values, counts):
        for start in range(0, count, 256):
            size = min(256, grad.shape[1] - start)
            part = lax.dot_general(grad[:, start : start + size], value[...], TN, preferred_element_type=F32)
            size = min(size, count - start)
            out[0, base + start : base + start + size, :] = part[:size].astype(BF16)
        base += count


def stack_call(rows_n, pairs, counts):
    tokens, wide = pairs[0][1].shape
    width = wide // rows_n
    total = sum(counts)
    flops = 2 * tokens * wide * sum(grad.shape[1] for grad, _ in pairs)
    return pl.pallas_call(
        functools.partial(stack_kernel, counts),
        grid=(rows_n,),
        in_specs=[
            pl.BlockSpec(grad.shape, lambda i: (0, 0), pipeline_mode=pl.Buffered(1)) for grad, _ in pairs
        ]
        + [pl.BlockSpec((tokens, width), lambda i: (0, i)) for _ in pairs],
        out_specs=pl.BlockSpec((1, total, width), lambda i: (i, 0, 0)),
        out_shape=jax.ShapeDtypeStruct((rows_n, total, width), BF16),
        compiler_params=pltpu.CompilerParams(vmem_limit_bytes=60 << 20),
        cost_estimate=pl.CostEstimate(flops=flops, bytes_accessed=40 << 20, transcendentals=0),
        name="weight_grads",
    )(*[grad for grad, _ in pairs], *[value for _, value in pairs])


def units_kernel(part_name, cuts, gate, up, down, *outs):
    part, units = lax.axis_index(part_name), cuts[-1]
    for index in range(gate.shape[1] // units):

        @pl.when(part == index)
        def _():
            base = index * units
            for which, ref in enumerate((gate, up)):
                turned = ref[:, base : base + units].T
                for out, start, end in zip(outs, cuts[:-1], cuts[1:]):
                    out[which * (end - start) : (which + 1) * (end - start), :] = turned[start:end]
            for out, start, end in zip(outs, cuts[:-1], cuts[1:]):
                out[2 * (end - start) :, :] = down[base + start : base + end, :]


def units_call(lay, cuts, gate, up, down):
    features, wide = gate.shape
    rows = [3 * (end - start) for start, end in zip(cuts[:-1], cuts[1:])]
    return pl.pallas_call(
        functools.partial(units_kernel, lay.part, cuts),
        grid=(features // 128,),
        in_specs=[pl.BlockSpec((128, wide), lambda i: (i, 0))] * 2 + [pl.BlockSpec((wide, 128), lambda i: (0, i))],
        out_specs=[pl.BlockSpec((count, 128), lambda i: (0, i)) for count in rows],
        out_shape=[jax.ShapeDtypeStruct((count, features), BF16) for count in rows],
        compiler_params=pltpu.CompilerParams(vmem_limit_bytes=60 << 20),
        name="own_units",
    )(gate, up, down)


def ffn_kernel(values, grads, stack, hidden, both_grad):
    units, width = hidden.shape[1], stack.shape[2]
    both, grad = 0.0, 0.0
    for index in range(stack.shape[0]):
        cols = slice(index * width, (index + 1) * width)
        both = both + lax.dot_general(
            values[:, cols], stack[index, : 2 * units, :], NT, preferred_element_type=F32
        )
        grad = grad + lax.dot_general(grads[:, cols], stack[index, 2 * units :, :], NT, preferred_element_type=F32)
    gate, up = both[:, :units], both[:, units:]
    sig = sigmoid(gate)
    act = gate * sig
    hidden[...] = (act * up).astype(BF16)
    both_grad[:, :units] = (grad * up * (sig + act * (1.0 - sig))).astype(BF16)
    both_grad[:, units:] = (grad * act).astype(BF16)


def ffn_call(values, grads, stack):
    tokens, width = values.shape
    units = stack.shape[1] // 3
    block = 256
    while tokens % block:
        block //= 2
    row = pl.BlockSpec((block, width), lambda i: (i, 0))
    return pl.pallas_call(
        ffn_kernel,
        grid=(tokens // block,),
        in_specs=[row, row, pl.BlockSpec(stack.shape, lambda i: (0, 0, 0))],
        out_specs=[
            pl.BlockSpec((block, units), lambda i: (i, 0)),
            pl.BlockSpec((block, 2 * units), lambda i: (i, 0)),
        ],
        out_shape=[
            jax.ShapeDtypeStruct((tokens, units), BF16),
            jax.ShapeDtypeStruct((tokens, 2 * units), BF16),
        ],
        compiler_params=pltpu.CompilerParams(vmem_limit_bytes=60 << 20),
        cost_estimate=pl.CostEstimate(
            flops=6 * tokens * width * units, bytes_accessed=30 << 20, transcendentals=tokens * units
        ),
        name="ffn",
    )(values, grads, stack)


SEQ = 448


def project(left, right):
    return jnp.dot(left, right, preferred_element_type=F32)


def project_back(left, right):
    return lax.dot_general(left, right, NT, preferred_element_type=F32)


def weight_grads(lay, *pairs):
    if lay.native:
        return stack_call(lay.rows, [pair[:2] for pair in pairs], [count for _, _, count in pairs])
    stacks = []
    for grad, value, count in pairs:
        whole = lax.dot_general(grad, value, TN, preferred_element_type=F32)[:count].astype(BF16)
        stacks.append(jnp.moveaxis(whole.reshape(count, lay.rows, -1), 1, 0))
    return jnp.concatenate(stacks, axis=1)


def after(value, *others):
    return lax.optimization_barrier((value,) + others)[0]


class Plan:
    def __init__(self, mesh, heads):
        dp, self.rows, self.cols = (mesh.shape[name] for name in ("dp", "row", "col"))
        ways = dp
        while dp % ways or (heads // self.cols) % ways:
            ways -= 1
        self.ways = ways
        if ways == dp:
            self.mesh, self.shared, self.part = mesh, (), "dp"
        else:
            devices = mesh.devices.reshape(dp // ways, ways, self.rows, self.cols)
            self.mesh = Mesh(devices, ("group", "part", "row", "col"))
            self.shared, self.part = ("group",), "part"
        self.data = self.shared + (self.part,)
        self.team = (self.part, "col")
        self.native = (ways, self.rows, self.cols) == (4, 4, 2) and heads == 2 * ways * self.cols
        self.next_id = 0

    def fresh_id(self):
        self.next_id += 1
        return self.next_id


def spread(lay, values):
    local = values.shape[0]
    whole = lax.all_gather(values, "col", axis=0, tiled=True)
    whole = lax.all_to_all(whole, "row", split_axis=0, concat_axis=1, tiled=True)
    mine = local // lay.rows
    return lax.dynamic_slice_in_dim(whole, lax.axis_index("col") * mine, mine, 0)


def unspread(lay, value):
    local = value.shape[0] * lay.rows
    whole = lax.all_gather(value, "col", axis=0, tiled=True)
    whole = lax.all_to_all(whole, "row", split_axis=1, concat_axis=0, tiled=True)
    return lax.dynamic_slice_in_dim(whole, lax.axis_index("col") * local, local, 0)


def team_gather(lay, values):
    return lax.all_gather(values, lay.team, axis=0, tiled=True)


def team_scatter(lay, values):
    return lax.psum_scatter(values.astype(BF16), lay.team, scatter_dimension=0, tiled=True).astype(F32)


def norm_forward(values):
    scale = lax.rsqrt(jnp.mean(values * values, axis=1, keepdims=True) + 1e-05)
    return values * scale, scale


def norm_backward(grad, values, gain):
    normed, scale = norm_forward(values)
    scaled = grad * gain
    inner = jnp.mean(scaled * normed, axis=1, keepdims=True)
    return scale * (scaled - normed * inner), jnp.sum(grad * normed, axis=0, keepdims=True)


def enter(lay, values, grads, gains, segments, weight):
    if lay.native:
        return enter_call(lay, values, grads, gains, segments, weight)
    mine, grads = spread(lay, values), spread(lay, grads)
    gains, weight = (lax.all_gather(value, "row", axis=0, tiled=False) for value in (gains, weight))
    segments = lax.all_gather(segments, lay.part, axis=0, tiled=False)
    normed, _ = norm_forward(mine.astype(F32))
    everyone = team_gather(lay, (normed * gains[:, 0].reshape(1, -1)).astype(BF16))
    return mine, everyone, grads, team_gather(lay, grads), gains, segments, weight


def beside(stack, start, size):
    return jnp.moveaxis(stack[:, start : start + size], 0, 1).reshape(size, -1)


def own_units(lay, cuts, gate, up, down):
    if lay.native:
        return units_call(lay, cuts, gate, up, down)
    start, size = lax.axis_index(lay.part) * cuts[-1], cuts[-1]
    gate, up = (lax.dynamic_slice_in_dim(values, start, size, 1).T for values in (gate, up))
    down = lax.dynamic_slice_in_dim(down, start, size, 0)
    return [
        jnp.concatenate([values[first:last] for values in (gate, up, down)], axis=0)
        for first, last in zip(cuts[:-1], cuts[1:])
    ]


def mid_step(lay, mixed, out_all, stored, gain):
    starts = [head * DV for head in range(len(mixed))]
    if lay.native:
        return mid_call(lay, mixed, out_all, [(0, start) for start in starts], stored, gain)
    total = sum(project(left, beside(out_all, start, DV)) for left, start in zip(mixed, starts))
    residual = stored.astype(F32) + team_scatter(lay, total)
    normed, _ = norm_forward(residual)
    return residual, team_gather(lay, (normed * gain).astype(BF16))


def feed_forward(lay, values, grads, stack):
    if lay.native:
        return ffn_call(values, grads, stack)
    units = stack.shape[1] // 3
    gate, up = (project_back(values, beside(stack, start, units)) for start in (0, units))
    sig = jax.nn.sigmoid(gate)
    grad = project_back(grads, beside(stack, 2 * units, units))
    grad_gate = grad * up * sig * (1.0 + gate * (1.0 - sig))
    both = jnp.concatenate([grad_gate.astype(BF16), (grad * gate * sig).astype(BF16)], axis=1)
    return (gate * sig * up).astype(BF16), both


def branch_step(lay, lefts, stacks, residual, out_grads, gain):
    if lay.native:
        return branch_call(lay, lefts, stacks, residual, out_grads, gain)
    total = sum(project(left, beside(stack, 0, left.shape[1])) for left, stack in zip(lefts, stacks))
    grad, gain_part = norm_backward(team_scatter(lay, total), residual, gain)
    grad = out_grads.astype(F32) + grad
    return grad, team_gather(lay, grad.astype(BF16)), gain_part


def finish_step(lay, hidden, stacks, grads, mix, starts, residual, stored, grad_residual, gain):
    if lay.native:
        return finish_call(lay, hidden, stacks, grads, mix, starts, residual, stored, grad_residual, gain)
    total = sum(
        project(left, beside(stack, 2 * left.shape[1], left.shape[1])) for left, stack in zip(hidden, stacks)
    )
    block_output = (residual + team_scatter(lay, total)).astype(BF16)
    total = sum(project_back(left, mix[:, start : start + left.shape[1]]) for left, start in zip(grads, starts))
    grad, gain_part = norm_backward(team_scatter(lay, total), stored.astype(F32), gain)
    return block_output, (grad_residual + grad).astype(BF16), gain_part


def columns(stack):
    return jnp.moveaxis(stack, 2, 0).reshape(stack.shape[2], -1).astype(F32)


def on_device(
    lay,
    block_input,
    segment_ids,
    attn_gain,
    mix_weight,
    decay_weight,
    conv_weight,
    decay_log,
    decay_bias,
    out_gain,
    out_weight,
    ffn_gain,
    gate_weight,
    up_weight,
    down_weight,
    cotangent,
):
    part = lax.axis_index(lay.part)
    heads = decay_log.shape[0] // lay.ways
    units = gate_weight.shape[1] // lay.ways
    width = mix_weight.shape[0]

    def mine(values, dim, size):
        return lax.dynamic_slice_in_dim(values, part * size, size, dim)

    def gather_rows(values):
        return lax.all_gather(values, "row", axis=0, tiled=False)

    mix_mine = mine(mix_weight, 1, heads * PER_HEAD)
    decay_mine = mine(decay_weight, 1, heads * 2)
    decay_pad = jnp.pad(decay_mine, ((0, 0), (0, 128 - heads * 2)))
    splits = [0, PER_HEAD + 128]
    for head in range(1, heads):
        splits.append(splits[-1] + PER_HEAD)
    mix_pad = jnp.concatenate([mix_mine[:, :PER_HEAD], decay_pad, mix_mine[:, PER_HEAD:]], axis=1)
    out_all = gather_rows(mine(out_weight, 0, heads * DV))
    cuts = [0, min(units, -(-units // 256) * 128), units]
    unit_blocks = own_units(lay, cuts, gate_weight, up_weight, down_weight)
    conv_mine = mine(conv_weight, 1, heads * INNER)
    log_mine, bias_mine = mine(decay_log, 0, heads), mine(decay_bias, 0, heads)

    gains = jnp.stack([attn_gain, ffn_gain])
    stored, attn_all, out_grads, out_grads_all, gains, segments, mix_all = enter(
        lay, block_input, cotangent, gains, segment_ids.reshape(1, -1), after(mix_pad, *unit_blocks)
    )
    mix_all = mix_all.reshape(lay.rows * width, -1)
    gain_one, gain_two = gains[:, 0].reshape(1, -1), gains[:, 1].reshape(1, -1)
    segments = segments.astype(F32)
    seg_col, seg_row = segments.reshape(-1, 1), segments.reshape(-1, 1, SEQ)
    waiting = lax.optimization_barrier((*unit_blocks, attn_all))[:-1]
    stacks = [gather_rows(values) for values in waiting]
    tokens = attn_all.shape[0]
    head_weights = [mix_all[:, start:end] for start, end in zip(splits[:-1], splits[1:])]
    shared, mixed, solves, projs = (), [], [], []
    for head in range(heads):
        projs.append(project(after(attn_all, *mixed), head_weights[head]))
        if not head:
            shared = (
                projs[0], PER_HEAD // 128, seg_col, seg_row, conv_mine, log_mine, bias_mine, out_gain.reshape(1, -1),
            )
        values, solve = mixer_forward(head, heads, projs[head], *shared)
        mixed.append(values)
        solves.append(solve)
    residual, ffn_all = mid_step(lay, mixed, out_all, stored, gain_two)

    def sum_rows(grads):
        grads = lax.psum_scatter(grads, "row", scatter_dimension=0, tiled=False)
        return lax.psum(grads, lay.shared) if lay.shared else grads

    hidden, grad_both, ffn_grads = [], [], []
    for stack in stacks:
        values, grads = feed_forward(lay, ffn_all, out_grads_all, stack)
        count = values.shape[1]
        ffn_part = weight_grads(lay, (grads, ffn_all, 2 * count), (values, out_grads_all, count))
        ffn_all, values, grads = lax.optimization_barrier((ffn_all, values, grads, ffn_part))[:3]
        hidden.append(values)
        grad_both.append(grads)
        ffn_grads.append(sum_rows(ffn_part))
    grad_residual, branch_all, ffn_gain_part = branch_step(lay, grad_both, stacks, residual, out_grads, gain_two)

    branch = branch_all
    if lay.native:
        branch = after(branch, ffn_grads[0])
        crossed = [cross(lay, grads) for grads in ffn_grads]
    other = jnp.zeros((tokens, 128), BF16)
    proj_grads, mix_grads, conv_parts, small_parts = [], [], [], []
    for head in reversed(range(heads)):
        common = (head, heads, projs[head], *shared, solves[head], branch, out_all)
        if head:
            grad, extra, conv_part, small_part = mixer_backward(*common, None)
            if lay.native:
                grad = after(grad, crossed[0])
            other = other + extra
        else:
            grad, conv_part, small_part = mixer_backward(*common, other)
            if lay.native:
                grad = after(grad, *crossed)
        triples = [(grad, attn_all, PER_HEAD if head else PER_HEAD + DECAY_ROWS)]
        if head == heads - 1:
            triples += [(values, branch_all, DV) for values in mixed]
        mix_part = weight_grads(lay, *triples)
        branch, grad = lax.optimization_barrier((branch, grad, mix_part))[:2]
        if lay.native:
            branch = after(branch, *ffn_grads[1:])
        proj_grads.insert(0, grad)
        conv_parts.insert(0, conv_part.sum(0))
        small_parts.insert(0, small_part.sum(0)[0])
        mix_grads.insert(0, sum_rows(mix_part))
    if lay.native:
        ffn_pieces = [[ffn_grads[0], crossed[0], link(lay, ffn_grads[0]), link(lay, crossed[0])]]
        hidden[0] = after(hidden[0], *ffn_pieces[0])
    block_output, input_grad, attn_gain_part = finish_step(
        lay, hidden, stacks, proj_grads, mix_all, splits[:-1], residual, stored, grad_residual, gain_one
    )

    own = jnp.concatenate(
        [jnp.concatenate(conv_parts, axis=1).reshape(-1)]
        + [jnp.stack([part_of[DV + item] for part_of in small_parts]) for item in range(2)]
    )
    split = TAPS * heads * INNER
    gain_part = sum(part_of[:DV] for part_of in small_parts)
    col = lax.axis_index("col")
    if lay.native:
        flat = jnp.concatenate([own, gain_part, attn_gain_part[0], ffn_gain_part[0]])
        size = flat.shape[0]
        flat = jnp.pad(flat, (0, -size % 1024)).reshape(-1, 128)
        order = part_order(lay)
        for grads, passed in zip(ffn_grads[1:], crossed[1:]):
            ffn_pieces.append([grads, passed, link(lay, grads), link(lay, passed)])
        late = after(mix_grads[1], block_output)
        late_passed = cross(lay, late)
        ffn_pieces[0][0] = after(ffn_pieces[0][0], block_output)
        gate_grad, up_grad, down_weight_grad = place_ffn(order, ffn_pieces)
        passed = after(late_passed, gate_grad)
        late_pieces = [late, passed, link(lay, late), link(lay, passed)]
        out_weight_grad = place_rows(order, late_pieces, PER_HEAD, heads * DV)
        mix_grad = place_late_head(order, heads, 1, late_pieces)
        first = after(mix_grads[0], mix_grad)
        flat = after(flat, mix_grad, out_weight_grad)
        block_output, input_grad, first_stack, sums = leave_call(lay, block_output, input_grad, first, flat)
        mix_grad, decay_grad = place_first_head(heads, first_stack, mix_grad)
        block_output, input_grad = (value.reshape(-1, value.shape[2]) for value in (block_output, input_grad))
        sums = sums.reshape(8, -1)
        gain_sum, attn_sum, ffn_sum = jnp.split(
            jnp.sum(sums[:, own.shape[0] : size], axis=0), [DV, DV + lay.rows * width]
        )
        sums = sums[:, : own.shape[0]].reshape(lay.ways, lay.cols, -1)
    else:
        block_output, input_grad = unspread(lay, block_output), unspread(lay, input_grad)
        slots = lay.ways * lay.cols
        pick = (jnp.arange(slots) == part * lay.cols + col).astype(F32)[:, None]
        sums, gain_sum, ffn_sum, attn_sum = lax.psum(
            (pick * own[None, :], gain_part, ffn_gain_part[0], attn_gain_part[0]), lay.data + ("row", "col")
        )
        sums = sums.reshape(lay.ways, lay.cols, -1)
    sums = lax.dynamic_index_in_dim(sums, col, 1, keepdims=False)
    conv_grad = jnp.moveaxis(sums[:, :split].reshape(lay.ways, TAPS, -1), 0, 1).reshape(TAPS, -1)
    log_grad = sums[:, split : split + heads].reshape(-1)
    bias_grad = sums[:, split + heads :].reshape(-1)
    row = lax.axis_index("row")
    attn_gain_grad = lax.dynamic_slice_in_dim(attn_sum, row * width, width, 0)
    ffn_gain_grad = lax.dynamic_slice_in_dim(ffn_sum, row * width, width, 0)

    out_start = PER_HEAD if heads > 1 else PER_HEAD + DECAY_ROWS
    if not lay.native:
        mix_stacks = [lax.all_gather(value, lay.part, axis=0, tiled=False) for value in mix_grads]
        ffn_stacks = [lax.all_gather(value, lay.part, axis=0, tiled=False) for value in ffn_grads]
        decay_grad = columns(mix_stacks[0][:, PER_HEAD : PER_HEAD + 2 * heads])
        mix_grad = columns(jnp.concatenate([stack[:, :PER_HEAD] for stack in mix_stacks], axis=1))
        gate_grad, up_grad, down_weight_grad = (
            jnp.concatenate([jnp.split(stack, 3, axis=1)[item] for stack in ffn_stacks], axis=1) for item in range(3)
        )
        gate_grad, up_grad = columns(gate_grad), columns(up_grad)
        down_weight_grad = down_weight_grad.reshape(-1, width).astype(F32)
        out_weight_grad = mix_stacks[-1][:, out_start : out_start + heads * DV].reshape(-1, width).astype(F32)
    return (
        block_output,
        input_grad,
        attn_gain_grad,
        mix_grad,
        decay_grad,
        conv_grad,
        log_grad,
        bias_grad,
        gain_sum,
        out_weight_grad,
        ffn_gain_grad,
        gate_grad,
        up_grad,
        down_weight_grad,
    )


def solution(mesh):
    def run(*args):
        lay = Plan(mesh, args[6].shape[0])
        tokens, grid = P(lay.data + ("col",), "row"), P("row", "col")
        turned, features, inner = P("col", "row"), P("row"), P("col")
        conv = P(None, "col")
        return jax.shard_map(
            functools.partial(on_device, lay),
            mesh=lay.mesh,
            in_specs=(
                tokens, P(lay.data + ("row",)), features, grid, grid, conv, inner, inner, P(),
                turned, features, grid, grid, turned, tokens,
            ),
            out_specs=(
                tokens, tokens, features, grid, grid, conv, inner, inner, P(),
                turned, features, grid, grid, turned,
            ),
            check_vma=False,
        )(*args)

    return run
```

```python
import functools
import jax
import jax.numpy as jnp
from jax import lax
from jax.experimental import pallas as pl
from jax.experimental.pallas import tpu as pltpu
from jax.sharding import Mesh
from jax.sharding import PartitionSpec as P

F32, BF16 = jnp.float32, jnp.bfloat16
DK, DV, TAPS = 128, 256, 4
INNER = 2 * DK + DV
PER_HEAD = INNER + DV
NN = (((1,), (0,)), ((), ()))
NT = (((1,), (1,)), ((), ()))
TN = (((0,), (0,)), ((), ()))


def mm(left, right, dims=NN):
    return lax.dot_general(left.astype(BF16), right.astype(BF16), dims, preferred_element_type=F32)


def sigmoid(values):
    return 1.0 / (1.0 + jnp.exp(-values))


def softplus(values):
    return jnp.maximum(values, 0.0) + jnp.log(1.0 + jnp.exp(-jnp.abs(values)))


def shift_down(values, lag):
    return jnp.concatenate([jnp.zeros_like(values[:lag]), values[: values.shape[0] - lag]], axis=0)


def shift_up(values, lag):
    return jnp.concatenate([values[lag:], jnp.zeros_like(values[:lag])], axis=0)


def cumsum_rows(values):
    step = 1
    while step < values.shape[0]:
        values = values + shift_down(values, step)
        step *= 2
    return values


def reverse_cumsum_rows(values):
    step = 1
    while step < values.shape[0]:
        values = values + shift_up(values, step)
        step *= 2
    return values


def prepare(head, proj, extra, seg_row, conv, log_ref, bias_ref):
    length = proj.shape[0]
    seg_row = seg_row.astype(F32)
    rows = lax.broadcasted_iota(jnp.int32, (length, length), 0)
    cols = lax.broadcasted_iota(jnp.int32, (length, length), 1)
    seg_col = jnp.sum(jnp.where(rows == cols, seg_row, 0.0), axis=1, keepdims=True)
    summed = conv[TAPS - 1 : TAPS] * proj[:, :INNER]
    keeps = []
    for lag in range(1, TAPS):
        keep = (shift_down(seg_col + 1.0, lag) == seg_col + 1.0).astype(F32)
        keeps.append(keep)
        summed = summed + conv[TAPS - 1 - lag : TAPS - lag] * (shift_down(proj[:, :INNER], lag) * keep)
    gate_conv = sigmoid(summed)
    active = summed * gate_conv
    lane = lax.broadcasted_iota(jnp.int32, extra.shape, 1)
    write = jnp.sum(jnp.where(lane == 2 * head, extra, 0.0), axis=1, keepdims=True)
    drive = jnp.sum(jnp.where(lane == 2 * head + 1, extra, 0.0), axis=1, keepdims=True)
    beta = sigmoid(write)
    drive = drive + bias_ref[head]
    rate = jnp.exp(jnp.full((1, 1), log_ref[head], F32))
    decay = -rate * softplus(drive)
    total = cumsum_rows(decay)
    total_row = jnp.sum(jnp.where(rows == cols, total, 0.0), axis=0, keepdims=True)
    weight = jnp.exp(jnp.where((rows >= cols) & (seg_col == seg_row), total - total_row, -1e30))
    raw_q, raw_k, value = active[:, :DK], active[:, DK : 2 * DK], active[:, 2 * DK :]
    scale_q = lax.rsqrt(jnp.sum(raw_q * raw_q, axis=1, keepdims=True) + 1e-06)
    scale_k = lax.rsqrt(jnp.sum(raw_k * raw_k, axis=1, keepdims=True) + 1e-06)
    query = (raw_q * scale_q * DK ** (-0.5)).astype(BF16)
    key = (raw_k * scale_k).astype(BF16)
    inner = mm(key, key, NT)
    strict = jnp.where(rows > cols, weight, 0.0)
    return dict(
        summed=summed, keeps=keeps, gate_conv=gate_conv, raw_q=raw_q, raw_k=raw_k, value=value,
        scale_q=scale_q, scale_k=scale_k, query=query, key=key, inner=inner, weight=weight,
        strict=strict, beta=beta, drive=drive, rate=rate, decay=decay, rows=rows, cols=cols,
    )


def forward_kernel(head, proj_ref, extra_ref, segr_ref, conv_ref, log_ref, bias_ref, gain_ref,
                   mixed_ref, solve_ref, work):
    count, size = work.shape[:2]
    length = proj_ref.shape[0] // count
    spans = [slice(item * length, (item + 1) * length) for item in range(count)]
    tile = min(128, size)
    starts = range(0, size, tile)
    r = lax.broadcasted_iota(jnp.int32, (tile, tile), 0)
    c = lax.broadcasted_iota(jnp.int32, (tile, tile), 1)
    eye = (r == c).astype(F32)
    ready, parts = [], []
    for item, span in enumerate(spans):
        p = prepare(
            head, proj_ref[span, :], extra_ref[span, :], segr_ref[item], conv_ref[...], log_ref, bias_ref
        )
        if size != length:
            work[item] = jnp.zeros(work.shape[1:], F32)
        work[item, 0:length, 0:length] = p["beta"] * p["strict"] * p["inner"]
        scores = (mm(p["query"], p["key"], NT) * p["weight"]).astype(BF16)
        ready.append((scores, (p["beta"] * p["value"]).astype(BF16)))
        parts += [work[item, start : start + tile, start : start + tile] for start in starts]
    inv = [eye - jnp.where((r // 2 == c // 2), part, 0.0) for part in parts]
    step = 2
    while step < tile:
        pick = (r // (2 * step) == c // (2 * step)) & (r // step != c // step)
        lows = [mm(jnp.where(pick, part, 0.0), x) for part, x in zip(parts, inv)]
        inv = [x - mm(x, low) for x, low in zip(inv, lows)]
        step *= 2
    for index, values in enumerate(inv):
        item, start = index // len(starts), starts[index % len(starts)]
        work[item, start : start + tile, start : start + tile] = values
    step = tile
    while step < size:
        places = [(item, start) for item in range(count) for start in range(0, size, 2 * step)]
        lows = [
            mm(work[item, start + step : start + 2 * step, start : start + step],
               work[item, start : start + step, start : start + step])
            for item, start in places
        ]
        for (item, start), low in zip(places, lows):
            mid, end = start + step, start + 2 * step
            work[item, mid:end, start:mid] = -mm(work[item, mid:end, mid:end], low)
        step *= 2
    for item, span in enumerate(spans):
        solve = work[item, 0:length, 0:length].astype(BF16)
        solve_ref[item] = solve
        scores, target = ready[item]
        out = mm(scores, mm(solve, target))
        scale = lax.rsqrt(jnp.sum(out * out, axis=1, keepdims=True) * (1.0 / DV) + 1e-05)
        gate = proj_ref[span, INNER:PER_HEAD]
        mixed_ref[span, :] = (out * scale * gain_ref[...] * (gate * sigmoid(gate))).astype(BF16)


def backward_kernel(head, last, *refs):
    if last:
        (proj_ref, extra_ref, segr_ref, conv_ref, log_ref, bias_ref, gain_ref, solve_ref, grad_ref,
         turn_ref, other_ref, gproj_ref, gconv_ref, gsmall_ref) = refs
    else:
        (proj_ref, extra_ref, segr_ref, conv_ref, log_ref, bias_ref, gain_ref, solve_ref, grad_ref,
         turn_ref, gproj_ref, gextra_ref, gconv_ref, gsmall_ref) = refs
    conv = conv_ref[...]
    p = prepare(head, proj_ref[...], extra_ref[...], segr_ref[0], conv, log_ref, bias_ref)
    weight, strict, inner, beta, value = p["weight"], p["strict"], p["inner"], p["beta"], p["value"]
    query, key = p["query"], p["key"]
    solve = solve_ref[0]
    fresh = mm(solve, beta * value).astype(BF16)
    scores = mm(query, key, NT)
    probs = (scores * weight).astype(BF16)
    out = mm(probs, fresh)
    scale = lax.rsqrt(jnp.sum(out * out, axis=1, keepdims=True) * (1.0 / DV) + 1e-05)
    normed = out * scale
    gate = proj_ref[:, INNER:]
    gate_sig = sigmoid(gate)
    grad, width = 0.0, turn_ref.shape[2]
    for index in range(turn_ref.shape[0]):
        grad = grad + mm(grad_ref[:, index * width : (index + 1) * width], turn_ref[index], NT)
    gain = gain_ref[...]
    through = grad * normed
    ggate = through * gain * (gate_sig * (1.0 + gate * (1.0 - gate_sig)))
    ggain = jnp.sum(through * (gate * gate_sig), axis=0, keepdims=True)
    gnormed = grad * gain * (gate * gate_sig)
    gout = scale * (gnormed - normed * (jnp.sum(gnormed * normed, axis=1, keepdims=True) * (1.0 / DV)))
    gout = gout.astype(BF16)
    gprobs = mm(gout, fresh, NT)
    gfresh = mm(probs, gout, TN)
    gtarget = mm(solve, gfresh, TN)
    glower = -mm(gtarget, fresh, NT) * strict
    gscores = gprobs * weight
    tilt = glower * inner
    flow = gscores * scores + beta * tilt
    gbeta = jnp.sum(tilt, axis=1, keepdims=True) + jnp.sum(gtarget * value, axis=1, keepdims=True)
    gscores = gscores.astype(BF16)
    ginner = (beta * glower).astype(BF16)
    gquery = mm(gscores, key)
    gkey = mm(gscores, query, TN) + mm(ginner, key) + mm(ginner, key, TN)
    col_flow = jnp.sum(flow, axis=0, keepdims=True)
    col_flow = jnp.sum(jnp.where(p["rows"] == p["cols"], col_flow, 0.0), axis=1, keepdims=True)
    gdecay = reverse_cumsum_rows(jnp.sum(flow, axis=1, keepdims=True) - col_flow)
    raw_q, raw_k, scale_q, scale_k = p["raw_q"], p["raw_k"], p["scale_q"], p["scale_k"]
    gq = (DK ** (-0.5)) * scale_q * (
        gquery - raw_q * (scale_q * scale_q * jnp.sum(gquery * raw_q, axis=1, keepdims=True)))
    gk = scale_k * (gkey - raw_k * (scale_k * scale_k * jnp.sum(gkey * raw_k, axis=1, keepdims=True)))
    gactive = jnp.concatenate([gq, gk, beta * gtarget], axis=1)
    gsummed = gactive * (p["gate_conv"] * (1.0 + p["summed"] * (1.0 - p["gate_conv"])))
    source = proj_ref[:, :INNER]
    gsource = conv[TAPS - 1 : TAPS] * gsummed
    gconv_ref[0, TAPS - 1 : TAPS, :] = jnp.sum(gsummed * source, axis=0, keepdims=True)
    for lag in range(1, TAPS):
        kept = gsummed * p["keeps"][lag - 1]
        gsource = gsource + conv[TAPS - 1 - lag : TAPS - lag] * shift_up(kept, lag)
        gconv_ref[0, TAPS - 1 - lag : TAPS - lag, :] = jnp.sum(kept * shift_down(source, lag), axis=0, keepdims=True)
    gdrive = -p["rate"] * gdecay * sigmoid(p["drive"])
    gwrite = gbeta * beta * (1.0 - beta)
    lane = lax.broadcasted_iota(jnp.int32, extra_ref.shape, 1)
    gextra = jnp.where(lane == 2 * head, gwrite, jnp.where(lane == 2 * head + 1, gdrive, 0.0))
    gproj_ref[:, :INNER] = gsource.astype(BF16)
    gproj_ref[:, INNER:PER_HEAD] = ggate.astype(BF16)
    if last:
        gproj_ref[:, PER_HEAD:] = (gextra + other_ref[...].astype(F32)).astype(BF16)
    else:
        gextra_ref[...] = gextra.astype(BF16)
    glog = jnp.sum(gdecay * p["decay"], axis=0, keepdims=True)
    gbias = jnp.sum(gdrive, axis=0, keepdims=True)
    lane = lax.broadcasted_iota(jnp.int32, (1, 128), 1)
    gsmall_ref[0, :, 0:DV] = ggain
    gsmall_ref[0, :, DV:] = jnp.where(lane == 0, glog, jnp.where(lane == 1, gbias, 0.0))


def common_specs(length, head, extra_block, group):
    smem = pl.BlockSpec(memory_space=pltpu.SMEM)
    rows = length * group
    return [
        pl.BlockSpec((rows, PER_HEAD), lambda s: (s, 0)),
        pl.BlockSpec((rows, 128), lambda s: (s, extra_block)),
        pl.BlockSpec((group, 1, length), lambda s: (s, 0, 0)),
        pl.BlockSpec((TAPS, INNER), lambda s: (0, head)),
        smem,
        smem,
        pl.BlockSpec((1, DV), lambda s: (0, 0)),
    ]


def mixer_cost(count, passes):
    return pl.CostEstimate(flops=passes * count * (3 << 30), bytes_accessed=passes * count << 23, transcendentals=0)


def mixer_forward(head, heads, proj, extra, extra_block, seg_row, conv, log, bias, gain):
    count, _, length = seg_row.shape
    tokens = count * length
    size = 64
    while size < length:
        size *= 2
    group = 2 if count % 2 == 0 else 1
    return pl.pallas_call(
        functools.partial(forward_kernel, head),
        grid=(count // group,),
        in_specs=common_specs(length, head, extra_block, group),
        out_specs=[
            pl.BlockSpec((group * length, DV), lambda s: (s, 0)),
            pl.BlockSpec((group, length, length), lambda s: (s, 0, 0)),
        ],
        out_shape=[
            jax.ShapeDtypeStruct((tokens, DV), BF16),
            jax.ShapeDtypeStruct((count, length, length), BF16),
        ],
        scratch_shapes=[pltpu.VMEM((group, size, size), F32)],
        compiler_params=pltpu.CompilerParams(vmem_limit_bytes=56 << 20),
        cost_estimate=mixer_cost(count, 1),
        name="mixer_forward",
    )(proj, extra, seg_row, conv, log, bias, gain)


def mixer_backward(head, heads, proj, extra, extra_block, seg_row, conv, log, bias, gain, solve, grad, turned, other):
    count, _, length = seg_row.shape
    tokens = count * length
    last = other is not None
    in_specs = common_specs(length, head, extra_block, 1) + [
        pl.BlockSpec((1, length, length), lambda s: (s, 0, 0)),
        pl.BlockSpec((length, grad.shape[1]), lambda s: (s, 0)),
        pl.BlockSpec((turned.shape[0], DV, turned.shape[2]), lambda s: (0, head, 0)),
    ]
    args = [proj, extra, seg_row, conv, log, bias, gain, solve, grad, turned]
    width = PER_HEAD
    tail_specs = [
        pl.BlockSpec((1, TAPS, INNER), lambda s: (s, 0, 0)),
        pl.BlockSpec((1, 1, DV + 128), lambda s: (s, 0, 0)),
    ]
    tail_shapes = [
        jax.ShapeDtypeStruct((count, TAPS, INNER), F32),
        jax.ShapeDtypeStruct((count, 1, DV + 128), F32),
    ]
    mid_specs, mid_shapes = [], []
    if last:
        width += 128
        in_specs.append(pl.BlockSpec((length, 128), lambda s: (s, 0)))
        args.append(other)
    else:
        mid_specs = [pl.BlockSpec((length, 128), lambda s: (s, 0))]
        mid_shapes = [jax.ShapeDtypeStruct((tokens, 128), BF16)]
    return pl.pallas_call(
        functools.partial(backward_kernel, head, last),
        grid=(count,),
        in_specs=in_specs,
        out_specs=[pl.BlockSpec((length, width), lambda s: (s, 0))] + mid_specs + tail_specs,
        out_shape=[jax.ShapeDtypeStruct((tokens, width), BF16)] + mid_shapes + tail_shapes,
        compiler_params=pltpu.CompilerParams(vmem_limit_bytes=60 << 20),
        cost_estimate=mixer_cost(count, 2),
        name="mixer_backward",
    )(*args)


MESH_ID = pl.DeviceIdType.MESH
HBM_SPEC = pl.BlockSpec(memory_space=pltpu.HBM)
VMEM_SPEC = pl.BlockSpec(memory_space=pltpu.VMEM)
STRIP = 16
DECAY_ROWS = 16
GAIN_ROW, ATTN_ROW, FFN_ROW, REST_ROW, SMALL_ROWS = 32, 34, 50, 66, 72


def meet(targets):
    barrier = pltpu.get_barrier_semaphore()
    for target in targets:
        pl.semaphore_signal(barrier, inc=1, device_id=target, device_id_type=MESH_ID)
    pl.semaphore_wait(barrier, len(targets))


def remote(source, dest, send, recv, index, target):
    return pltpu.make_async_remote_copy(
        src_ref=source,
        dst_ref=dest,
        send_sem=send.at[index],
        recv_sem=recv.at[index],
        device_id=target,
        device_id_type=MESH_ID,
    )


class Team:
    def __init__(self, name):
        self.name, self.part, self.col = name, lax.axis_index(name), lax.axis_index("col")
        self.across, self.twin = lax.rem(self.part + 2, 4), self.part + 1 - 2 * lax.rem(self.part, 2)
        self.far, self.other = lax.rem(self.twin + 2, 4), 1 - self.col
        self.x, self.y, self.core = {name: self.across}, {"col": self.other}, {name: self.twin}

    def partners(self):
        return [self.x, self.y, self.core]


class Gather:
    def __init__(self, team, src, out, keep, send, recv):
        self.out, self.send, self.recv = out, send, recv
        half = src.shape[0] // 2
        first, second = pl.ds(0, half), pl.ds(half, half)
        own, across = team.part * 2 + team.col, team.across * 2 + team.col
        other, diag = team.part * 2 + team.other, team.across * 2 + team.other
        self.local = pltpu.make_async_copy(src, out.at[own], keep)
        self.x_first = self.copy(src.at[first], out.at[own, first], 0, team.x)
        self.x_second = self.copy(src.at[second], out.at[own, second], 1, team.x)
        self.y_second = self.copy(src.at[second], out.at[own, second], 2, team.y)
        self.y_first = self.copy(src.at[first], out.at[own, first], 3, team.y)
        self.core_own = self.copy(src, out.at[own], 4, team.core)
        self.y_pass = self.copy(out.at[across, first], out.at[across, first], 5, team.y)
        self.x_pass = self.copy(out.at[other, second], out.at[other, second], 6, team.x)
        self.core_x = self.copy(out.at[across], out.at[across], 7, team.core)
        self.core_y = self.copy(out.at[other], out.at[other], 8, team.core)
        self.core_first = self.copy(out.at[diag, first], out.at[diag, first], 9, team.core)
        self.core_second = self.copy(out.at[diag, second], out.at[diag, second], 10, team.core)

    def copy(self, source, dest, index, target):
        return remote(source, dest, self.send, self.recv, index, target)

    def start_first(self):
        self.x_first.start()
        self.y_first.start()

    def start_second(self):
        for copy in (self.y_second, self.x_second, self.core_own, self.local):
            copy.start()

    def finish(self):
        self.x_first.wait_recv()
        self.y_pass.start()
        self.y_first.wait_recv()
        self.y_second.wait_recv()
        self.x_pass.start()
        self.core_y.start()
        self.x_second.wait_recv()
        self.core_x.start()
        self.y_pass.wait_recv()
        self.core_first.start()
        self.x_pass.wait_recv()
        self.core_second.start()
        cores = (self.core_own, self.core_x, self.core_y, self.core_first, self.core_second)
        for copy in cores:
            copy.wait_recv()
        for copy in (self.x_first, self.x_second, self.y_second, self.y_first, self.y_pass, self.x_pass) + cores:
            copy.wait_send()
        self.local.wait()


def gather_phase(team, src, out, *sems):
    gather = Gather(team, src, out, *sems)
    gather.start_first()
    gather.start_second()
    gather.finish()


GATHER_SEMS = [pltpu.SemaphoreType.DMA, pltpu.SemaphoreType.DMA((11,)), pltpu.SemaphoreType.DMA((11,))]


class Spread:
    def __init__(self, src, out, middle, keep, send, recv):
        self.src, self.out, self.middle, self.keep, self.send, self.recv = src, out, middle, keep, send, recv
        self.row, self.col = lax.axis_index("row"), lax.axis_index("col")
        self.hops = [
            remote(src.at[2 * item + 1 - self.col], middle.at[item], send, recv, item, {"col": 1 - self.col})
            for item in range(2)
        ]

    def pieces(self, side):
        home = self.col if side == 0 else 1 - self.col
        for item in range(2):
            source = self.src.at[2 * item + self.col] if side == 0 else self.middle.at[item]
            to_row = 2 * home + item
            copy = pltpu.make_async_remote_copy(
                src_ref=source,
                dst_ref=self.out.at[self.row],
                send_sem=self.send.at[2 + 2 * side + item],
                recv_sem=self.recv.at[2 + self.row],
                device_id={"row": to_row},
                device_id_type=MESH_ID,
            )
            yield to_row == self.row, copy, pltpu.make_async_copy(source, self.out.at[self.row], self.keep)

    def start(self):
        for hop in self.hops:
            hop.start()
        self.send_side(0)

    def send_side(self, side):
        for here, far, near in self.pieces(side):
            pl.when(here)(near.start)
            pl.when(jnp.logical_not(here))(far.start)

    def turn(self):
        for hop in self.hops:
            hop.wait_recv()
        self.send_side(1)

    def finish(self):
        for hop in range(1, 4):
            index = lax.rem(self.row + hop, 4)
            pltpu.make_async_remote_copy(
                src_ref=self.src.at[0],
                dst_ref=self.out.at[index],
                send_sem=self.send.at[0],
                recv_sem=self.recv.at[2 + index],
                device_id={"row": index},
                device_id_type=MESH_ID,
            ).wait_recv()
        for side in range(2):
            for here, far, near in self.pieces(side):
                pl.when(here)(near.wait)
                pl.when(jnp.logical_not(here))(far.wait_send)
        for hop in self.hops:
            hop.wait_send()


class Line:
    def __init__(self, src, out, keep, send, recv):
        self.src, self.out, self.send, self.recv = src, out, send, recv
        self.row = lax.axis_index("row")
        self.near = pltpu.make_async_copy(src, out.at[self.row], keep)

    def copy(self, hops, up):
        step = 1 if up else -1
        mark = self.row - hops * step
        return pltpu.make_async_remote_copy(
            src_ref=self.src if hops == 0 else self.out.at[mark],
            dst_ref=self.out.at[mark],
            send_sem=self.send.at[hops if up else 3 + hops],
            recv_sem=self.recv.at[mark],
            device_id={"row": self.row + step},
            device_id_type=MESH_ID,
        )

    def sends(self, hops, up):
        return (self.row >= hops) & (self.row < 3) if up else (self.row + hops <= 3) & (self.row > 0)

    def start(self):
        self.near.start()
        for up in (True, False):
            pl.when(self.sends(0, up))(lambda: self.copy(0, up).start())

    def arrive(self, hops):
        for up in (True, False):
            mark = self.row - hops if up else self.row + hops

            @pl.when((self.row >= hops) if up else (self.row + hops <= 3))
            def _():
                pltpu.make_async_remote_copy(
                    src_ref=self.src,
                    dst_ref=self.out.at[mark],
                    send_sem=self.send.at[0],
                    recv_sem=self.recv.at[mark],
                    device_id={"row": self.row - 1 if up else self.row + 1},
                    device_id_type=MESH_ID,
                ).wait_recv()

    def pass_on(self, hops):
        self.arrive(hops)
        for up in (True, False):
            pl.when(self.sends(hops, up))(lambda: self.copy(hops, up).start())

    def finish(self):
        self.arrive(3)
        for hops in range(3):
            for up in (True, False):
                pl.when(self.sends(hops, up))(lambda: self.copy(hops, up).wait_send())
        self.near.wait()


def share(source, dest, mark, others, keep, send, recv):
    near = pltpu.make_async_copy(source, dest.at[mark], keep)
    near.start()
    copies = []
    for item, (target, _) in enumerate(others):
        copies.append(
            pltpu.make_async_remote_copy(
                src_ref=source,
                dst_ref=dest.at[mark],
                send_sem=send.at[item],
                recv_sem=recv.at[mark],
                device_id=target,
                device_id_type=MESH_ID,
            )
        )
        copies[item].start()

    def finish():
        near.wait()
        for target, index in others:
            pltpu.make_async_remote_copy(
                src_ref=source,
                dst_ref=dest.at[index],
                send_sem=send.at[0],
                recv_sem=recv.at[index],
                device_id=target,
                device_id_type=MESH_ID,
            ).wait_recv()
        for copy in copies:
            copy.wait_send()

    return finish


def enter_kernel(part_name, *refs):
    sources, outs, scratch = refs[:5], refs[5:12], refs[12:]
    first, second, gains, segs, weight = sources
    first_tok, first_all, second_tok, second_all, gains_all, segs_all, weight_all = outs
    (stage_one, middle_one, stage_two, middle_two, ready_one, ready_two, line_keep, line_send, line_recv, small_keep,
     gain_send, gain_recv, seg_send, seg_recv) = scratch[:14]
    spread_one, spread_two, gather_one, gather_two = (scratch[14 + 3 * index : 17 + 3 * index] for index in range(4))
    team = Team(part_name)
    row = lax.axis_index("row")
    rows = [({"row": lax.rem(row + hop, 4)}, lax.rem(row + hop, 4)) for hop in range(1, 4)]
    meet(team.partners() + [target for target, _ in rows] + [{part_name: team.far}])
    one = Spread(first, stage_one, middle_one, *spread_one)
    two = Spread(second, stage_two, middle_two, *spread_two)
    line = Line(weight, weight_all, line_keep, line_send, line_recv)
    one.start()
    done_gains = share(gains, gains_all, row, rows, small_keep.at[0], gain_send, gain_recv)
    parts = [({part_name: index}, index) for index in (team.across, team.twin, team.far)]
    done_segs = share(segs, segs_all, team.part, parts, small_keep.at[1], seg_send, seg_recv)
    line.start()
    one.turn()
    two.start()
    one.finish()
    done_gains()
    done_segs()
    tokens, width = first.shape[1], first.shape[2]

    def norm(rows, _):
        wides = [stage_one[index, rows, :].astype(F32) for index in range(4)]
        square = sum(jnp.sum(wide * wide, axis=1, keepdims=True) for wide in wides)
        scale = lax.rsqrt(square * (1.0 / (4 * width)) + 1e-05)
        for index in range(4):
            cols = slice(index * width, (index + 1) * width)
            first_tok[rows, cols] = stage_one[index, rows, :]
            ready_one[rows, cols] = (wides[index] * scale * gains_all[index, 0:1, :]).astype(BF16)

    strips(0, tokens, norm)
    two.turn()
    line.pass_on(1)
    gather_phase(team, ready_one, first_all, *gather_one)
    two.finish()

    def join_blocks(rows, _):
        for index in range(4):
            cols = slice(index * width, (index + 1) * width)
            second_tok[rows, cols] = stage_two[index, rows, :]
            ready_two[rows, cols] = stage_two[index, rows, :]

    strips(0, tokens, join_blocks)
    line.pass_on(2)
    gather_phase(team, ready_two, second_all, *gather_two)
    line.finish()


def enter_call(lay, first, second, gains, segs, weight):
    tokens, width = first.shape[0] // 4, first.shape[1]
    wide = 4 * width
    tok, everyone = jax.ShapeDtypeStruct((tokens, wide), BF16), jax.ShapeDtypeStruct((8, tokens, wide), BF16)
    stage = [pltpu.VMEM((4, tokens, width), BF16), pltpu.VMEM((2, tokens, width), BF16)]
    line_sems = [pltpu.SemaphoreType.DMA, pltpu.SemaphoreType.DMA((6,)), pltpu.SemaphoreType.DMA((4,))]
    small_sems = [pltpu.SemaphoreType.DMA((count,)) for count in (2, 3, 4, 3, 4)]
    spread_sems = [pltpu.SemaphoreType.DMA, pltpu.SemaphoreType.DMA((6,)), pltpu.SemaphoreType.DMA((6,))]
    results = pl.pallas_call(
        functools.partial(enter_kernel, lay.part),
        in_specs=[VMEM_SPEC] * 5,
        out_specs=[VMEM_SPEC, HBM_SPEC, VMEM_SPEC, HBM_SPEC, VMEM_SPEC, VMEM_SPEC, HBM_SPEC],
        out_shape=[
            tok,
            everyone,
            tok,
            everyone,
            jax.ShapeDtypeStruct((4,) + gains.shape, gains.dtype),
            jax.ShapeDtypeStruct((4,) + segs.shape, segs.dtype),
            jax.ShapeDtypeStruct((4,) + weight.shape, weight.dtype),
        ],
        scratch_shapes=stage
        + stage
        + [pltpu.VMEM((tokens, wide), BF16)] * 2
        + line_sems
        + small_sems
        + spread_sems
        + spread_sems
        + GATHER_SEMS
        + GATHER_SEMS,
        compiler_params=pltpu.CompilerParams(
            collective_id=lay.fresh_id(), has_side_effects=True, vmem_limit_bytes=60 << 20
        ),
        cost_estimate=pl.CostEstimate(flops=1 << 30, bytes_accessed=400 << 20, transcendentals=0),
        name="enter",
    )(first.reshape(4, tokens, width), second.reshape(4, tokens, width), gains, segs, weight)
    first_tok, first_all, second_tok, second_all, gains, segs, weight = results
    return (
        first_tok, first_all.reshape(-1, wide), second_tok, second_all.reshape(-1, wide), gains, segs, weight,
    )


def strips(start, count, body):
    @pl.loop(0, count // STRIP)
    def _(step):
        body(pl.ds(pl.multiple_of(start + step * STRIP, STRIP), STRIP), pl.ds(pl.multiple_of(step * STRIP, STRIP), STRIP))


class Scatter:
    def __init__(self, team, dots, finish, refs):
        self.team, self.dots, self.finish = team, dots, finish
        self.work, self.twin, self.sent, self.relay, self.final, self.send, self.recv = refs
        self.rows, self.chunk = self.twin.shape[1], self.twin.shape[2] // 4
        self.half = self.rows // 2
        first, second = pl.ds(0, self.half), pl.ds(self.half, self.half)
        sent, relay, final = self.sent, self.relay, self.final
        self.relay_x = self.copy(sent.at[0, first], relay.at[0], 4, team.x)
        self.relay_y = self.copy(sent.at[0, second], relay.at[1], 5, team.y)
        self.x_first = self.copy(sent.at[1, first], final.at[0, first], 6, team.x)
        self.x_second = self.copy(sent.at[1, second], final.at[0, second], 7, team.x)
        self.y_second = self.copy(sent.at[2, second], final.at[1, second], 8, team.y)
        self.y_first = self.copy(sent.at[2, first], final.at[1, first], 9, team.y)

    def copy(self, source, dest, index, target):
        return remote(source, dest, self.send, self.recv, index, target)

    def swap(self, item):
        return self.copy(self.work.at[item, 0], self.twin.at[item], item, self.team.core)

    def total(self, item, start, passed=None):
        def add(rows, local):
            value = self.work[item, 1, rows, :].astype(F32) + self.twin[item, rows, :].astype(F32)
            if passed is not None:
                value = value + self.relay[passed, local, :].astype(F32)
            self.sent[item, rows, :] = value.astype(BF16)

        strips(start, self.half, add)

    def begin(self):
        team = self.team

        @pl.loop(0, 4)
        def _(item):
            @pl.loop(0, 8)
            def _(step):
                which, chunk = step // 4, lax.rem(step, 4)
                base = team.part * which + team.twin * (1 - which)
                slot = lax.rem(base + 2 * (1 - item // 2), 4) * 2 + lax.rem(team.col + 1 + item, 2)
                columns = pl.ds(pl.multiple_of(chunk * self.chunk, self.chunk), self.chunk)
                rows = pl.ds(pl.multiple_of(slot * self.rows, STRIP), self.rows)
                self.work[item, which, :, columns] = self.dots(rows, chunk, columns).astype(BF16)

            self.swap(item).start()

            @pl.when(item == 1)
            def _():
                self.swap(0).wait_recv()
                self.total(0, 0)
                self.relay_x.start()
                self.total(0, self.half)
                self.relay_y.start()

            @pl.when(item == 2)
            def _():
                self.swap(1).wait_recv()
                self.total(1, 0)
                self.x_first.start()

            @pl.when(item == 3)
            def _():
                self.swap(2).wait_recv()
                self.total(2, self.half)
                self.y_second.start()

    def pass_on(self):
        self.relay_y.wait_recv()
        self.total(1, self.half, 1)
        self.x_second.start()
        self.relay_x.wait_recv()
        self.total(2, 0, 0)
        self.y_first.start()

    def last(self, rows, _):
        value = self.work[3, 1, rows, :].astype(F32) + self.twin[3, rows, :].astype(F32)
        self.finish(rows, value + self.final[0, rows, :].astype(F32) + self.final[1, rows, :].astype(F32))

    def conclude(self, between=None):
        self.swap(3).wait_recv()
        self.x_first.wait_recv()
        self.y_first.wait_recv()
        strips(0, self.half, self.last)
        if between:
            between()
        self.x_second.wait_recv()
        self.y_second.wait_recv()
        strips(self.half, self.half, self.last)
        for copy in [self.swap(item) for item in range(4)]:
            copy.wait_send()
        for copy in (self.relay_x, self.relay_y, self.x_first, self.x_second, self.y_second, self.y_first):
            copy.wait_send()


def scatter_scratch(tokens, wide):
    return [
        pltpu.VMEM((4, 2, tokens, wide), BF16),
        pltpu.VMEM((4, tokens, wide), BF16),
        pltpu.VMEM((3, tokens, wide), BF16),
        pltpu.VMEM((2, tokens // 2, wide), BF16),
        pltpu.VMEM((2, tokens, wide), BF16),
        pltpu.SemaphoreType.DMA((10,)),
        pltpu.SemaphoreType.DMA((10,)),
    ]


def make_dots(lefts, rights, starts):
    def dots(rows, chunk, columns):
        value = 0.0
        for left, (index, start) in zip(lefts, starts):
            right, depth = rights[index], slice(start, start + left.shape[1])
            if len(right.shape) == 3:
                value = value + lax.dot_general(left[rows, :], right[chunk, depth, :], NN, preferred_element_type=F32)
            else:
                value = value + lax.dot_general(left[rows, :], right[columns, depth], NT, preferred_element_type=F32)
        return value

    return dots


def norm_back(value, total, gain, gain_sum):
    scale = lax.rsqrt(jnp.sum(value * value, axis=1, keepdims=True) * (1.0 / value.shape[1]) + 1e-05)
    normed = value * scale
    gain_sum[...] += total * normed
    scaled = total * gain
    inner = jnp.sum(scaled * normed, axis=1, keepdims=True) * (1.0 / value.shape[1])
    return scale * (scaled - normed * inner)


def deal_out(out, rows, value):
    width = value.shape[1] // 4
    for index in range(4):
        out[index, rows, :] = value[:, index * width : (index + 1) * width].astype(BF16)


def fetch(sources, places, sems):
    copies = []
    for index, (source, place) in enumerate(zip(sources, places)):
        if isinstance(source, tuple):
            ref, start = source
            source = ref.at[:, pl.ds(start, place.shape[1]), :]
        copies.append(pltpu.make_async_copy(source, place, sems.at[index]))
        copies[index].start()
    return copies


def fetched(shapes):
    return [pltpu.VMEM(shape, dtype) for shape, dtype in shapes] + [pltpu.SemaphoreType.DMA((len(shapes),))]


def whole(values):
    return values.shape, values.dtype


def mid_kernel(part_name, starts, *refs):
    count = len(starts)
    sources, (out, everyone), scratch = refs[: count + 3], refs[count + 3 : count + 5], refs[count + 5 :]
    places, sems, scratch = scratch[: count + 3], scratch[count + 3], scratch[count + 4 :]
    loads = fetch(sources, places, sems)
    lefts, (right, stored, gain) = places[:count], places[count:]
    ready = scratch[7]
    team = Team(part_name)
    meet(team.partners())
    for load in loads:
        load.wait()

    def finish(rows, total):
        value = stored[rows, :].astype(F32) + total
        out[rows, :] = value
        scale = lax.rsqrt(jnp.sum(value * value, axis=1, keepdims=True) * (1.0 / value.shape[1]) + 1e-05)
        ready[rows, :] = (value * scale * gain[...]).astype(BF16)

    scatter = Scatter(team, make_dots(lefts, [right], starts), finish, scratch[:7])
    scatter.begin()
    scatter.pass_on()
    gather = Gather(team, ready, everyone, *scratch[8:])
    scatter.conclude(gather.start_first)
    gather.start_second()
    gather.finish()


def mid_call(lay, lefts, right, starts, stored, gain):
    tokens, wide = stored.shape
    residual, everyone = pl.pallas_call(
        functools.partial(mid_kernel, lay.part, starts),
        in_specs=[HBM_SPEC] * (len(lefts) + 3),
        out_specs=[VMEM_SPEC, HBM_SPEC],
        out_shape=[jax.ShapeDtypeStruct((tokens, wide), F32), jax.ShapeDtypeStruct((8, tokens, wide), BF16)],
        scratch_shapes=fetched([whole(values) for values in (*lefts, right, stored, gain)])
        + scatter_scratch(tokens, wide) + [pltpu.VMEM((tokens, wide), BF16)] + GATHER_SEMS,
        compiler_params=pltpu.CompilerParams(
            collective_id=lay.fresh_id(), has_side_effects=True, vmem_limit_bytes=60 << 20
        ),
        cost_estimate=pl.CostEstimate(flops=1 << 35, bytes_accessed=200 << 20, transcendentals=0),
        name="team_mid",
    )(*lefts, right, stored, gain)
    return residual, everyone.reshape(8 * tokens, wide)


def branch_kernel(part_name, count, *refs):
    total = 2 * count + 3
    sources, (out, everyone, gain_out), scratch = refs[:total], refs[total : total + 3], refs[total + 3 :]
    places, sems, scratch = scratch[:total], scratch[total], scratch[total + 1 :]
    sources = [(ref, 0) if count <= index < 2 * count else ref for index, ref in enumerate(sources)]
    loads = fetch(sources, places, sems)
    lefts, rights, (residual, through, gain) = places[:count], places[count : 2 * count], places[2 * count :]
    gain_sum, ready = scratch[7:9]
    team = Team(part_name)
    meet(team.partners())
    for load in loads:
        load.wait()
    gain_sum[...] = jnp.zeros_like(gain_sum)

    def finish(rows, total):
        value = through[rows, :].astype(F32) + norm_back(residual[rows, :], total, gain[...], gain_sum)
        out[rows, :] = value
        ready[rows, :] = value.astype(BF16)

    scatter = Scatter(team, make_dots(lefts, rights, [(index, 0) for index in range(count)]), finish, scratch[:7])
    scatter.begin()
    scatter.pass_on()
    gather = Gather(team, ready, everyone, *scratch[9:])
    scatter.conclude(gather.start_first)
    gather.start_second()
    gain_out[...] = jnp.sum(gain_sum[...], axis=0, keepdims=True)
    gather.finish()


def branch_call(lay, lefts, rights, residual, through, gain):
    tokens, wide = residual.shape
    width = rights[0].shape[2]
    out, everyone, gain_part = pl.pallas_call(
        functools.partial(branch_kernel, lay.part, len(lefts)),
        in_specs=[HBM_SPEC] * (2 * len(lefts) + 3),
        out_specs=[VMEM_SPEC, HBM_SPEC, VMEM_SPEC],
        out_shape=[
            jax.ShapeDtypeStruct((tokens, wide), F32),
            jax.ShapeDtypeStruct((8, tokens, wide), BF16),
            jax.ShapeDtypeStruct((1, wide), F32),
        ],
        scratch_shapes=fetched(
            [whole(left) for left in lefts]
            + [((4, left.shape[1], width), BF16) for left in lefts]
            + [whole(values) for values in (residual, through, gain)]
        )
        + scatter_scratch(tokens, wide)
        + [pltpu.VMEM((STRIP, wide), F32), pltpu.VMEM((tokens, wide), BF16)]
        + GATHER_SEMS,
        compiler_params=pltpu.CompilerParams(
            collective_id=lay.fresh_id(), has_side_effects=True, vmem_limit_bytes=60 << 20
        ),
        cost_estimate=pl.CostEstimate(flops=1 << 35, bytes_accessed=250 << 20, transcendentals=0),
        name="team_branch",
    )(*lefts, *rights, residual, through, gain)
    return out, everyone.reshape(8 * tokens, wide), gain_part


def finish_kernel(part_name, count, starts, *refs):
    total = 2 * count + len(starts) + 5
    sources, (block_out, input_out, gain_out), scratch = refs[:total], refs[total : total + 3], refs[total + 3 :]
    places, sems, scratch = scratch[:total], scratch[total], scratch[total + 1 :]
    hidden, downs, grads = places[:count], places[count : 2 * count], places[2 * count : -5]
    mix, residual, stored, through, gain = places[-5:]
    downs_from = [(ref, 2 * values.shape[1]) for ref, values in zip(sources[count : 2 * count], hidden)]
    loads = fetch([*sources[:count], *downs_from, *sources[2 * count :]], places, sems)
    gain_sum = scratch[14]
    team = Team(part_name)
    meet(team.partners())
    for load in loads[: 2 * count]:
        load.wait()
    gain_sum[...] = jnp.zeros_like(gain_sum)

    def finish_block(rows, total):
        deal_out(block_out, rows, residual[rows, :] + total)

    def finish_input(rows, total):
        value = norm_back(stored[rows, :].astype(F32), total, gain[...], gain_sum)
        deal_out(input_out, rows, through[rows, :] + value)

    block = Scatter(
        team, make_dots(hidden, downs, [(index, 0) for index in range(count)]), finish_block, scratch[:7]
    )
    inputs = Scatter(team, make_dots(grads, [mix], [(0, start) for start in starts]), finish_input, scratch[7:14])
    block.begin()
    for load in loads[2 * count :]:
        load.wait()
    inputs.begin()
    block.pass_on()
    inputs.pass_on()
    block.conclude()
    inputs.conclude()
    gain_out[...] = jnp.sum(gain_sum[...], axis=0, keepdims=True)


def finish_call(lay, hidden, stacks, grads, mix, starts, residual, stored, through, gain):
    tokens, wide = residual.shape
    width = stacks[0].shape[2]
    pieces = jax.ShapeDtypeStruct((4, tokens, width), BF16)
    return pl.pallas_call(
        functools.partial(finish_kernel, lay.part, len(hidden), starts),
        in_specs=[HBM_SPEC] * (2 * len(hidden) + len(grads) + 5),
        out_specs=[VMEM_SPEC] * 3,
        out_shape=[pieces, pieces, jax.ShapeDtypeStruct((1, wide), F32)],
        scratch_shapes=fetched(
            [whole(values) for values in hidden]
            + [((4, values.shape[1], width), BF16) for values in hidden]
            + [whole(values) for values in (*grads, mix, residual, stored, through, gain)]
        )
        + scatter_scratch(tokens, wide)
        + scatter_scratch(tokens, wide)
        + [pltpu.VMEM((STRIP, wide), F32)],
        compiler_params=pltpu.CompilerParams(
            collective_id=lay.fresh_id(), has_side_effects=True, vmem_limit_bytes=60 << 20
        ),
        cost_estimate=pl.CostEstimate(flops=1 << 35, bytes_accessed=250 << 20, transcendentals=0),
        name="team_finish",
    )(*hidden, *stacks, *grads, mix, residual, stored, through, gain)


class Deal:
    def __init__(self, src, out, keep, send, recv):
        self.src, self.out, self.keep, self.send, self.recv = src, out, keep, send, recv
        self.row, self.col = lax.axis_index("row"), lax.axis_index("col")
        spot = self.row * 2 + self.col
        self.mark, self.home = lax.rem(spot, 4), spot // 4

    def owner(self, index):
        place = self.col * 4 + index
        return {"row": place // 2, "col": lax.rem(place, 2)}

    def apart(self, index):
        owner = self.owner(index)
        return (owner["row"] != self.row) | (owner["col"] != self.col)

    def greet(self, barrier):
        for index in range(4):

            @pl.when(self.apart(index))
            def _():
                pl.semaphore_signal(barrier, inc=1, device_id=self.owner(index), device_id_type=MESH_ID)

        return 4 - (self.home == self.col).astype(jnp.int32)

    def each(self, act_near, act_far):
        for index in range(4):
            here = (self.row == index) & (self.home == self.col)

            @pl.when(here)
            def _():
                act_near(pltpu.make_async_copy(self.src.at[index], self.out.at[self.mark], self.keep))

            @pl.when(jnp.logical_not(here))
            def _():
                act_far(
                    pltpu.make_async_remote_copy(
                        src_ref=self.src.at[index],
                        dst_ref=self.out.at[self.mark],
                        send_sem=self.send.at[index],
                        recv_sem=self.recv.at[self.mark],
                        device_id={"row": index, "col": self.home},
                        device_id_type=MESH_ID,
                    )
                )

    def start(self):
        self.each(lambda copy: copy.start(), lambda copy: copy.start())

    def finish(self):
        for index in range(4):

            @pl.when(self.apart(index))
            def _():
                pltpu.make_async_remote_copy(
                    src_ref=self.src.at[0],
                    dst_ref=self.out.at[index],
                    send_sem=self.send.at[0],
                    recv_sem=self.recv.at[index],
                    device_id=self.owner(index),
                    device_id_type=MESH_ID,
                ).wait_recv()

        self.each(lambda copy: copy.wait(), lambda copy: copy.wait_send())


DEAL_SEMS = [pltpu.SemaphoreType.DMA, pltpu.SemaphoreType.DMA((4,)), pltpu.SemaphoreType.DMA((4,))]


def leave_kernel(part_name, *refs):
    first, second, block, src, first_out, second_out, blocks, out = refs[:8]
    deals = [Deal(first, first_out, *refs[8:11]), Deal(second, second_out, *refs[11:14])]
    rows_in, summed, near, row_send, row_recv, team_send, team_recv, join_send, join_recv = refs[14:]
    team = Team(part_name)
    row = lax.axis_index("row")
    rows = [({"row": lax.rem(row + hop, 4)}, lax.rem(row + hop, 4)) for hop in range(1, 4)]
    mates = []
    for part in (team.part, team.across, team.twin, team.far):
        for side in (team.col, team.other):
            mates.append(({part_name: part, "col": side}, part * 2 + side))
    mates = mates[1:]
    barrier = pltpu.get_barrier_semaphore()
    for target, _ in rows + mates:
        pl.semaphore_signal(barrier, inc=1, device_id=target, device_id_type=MESH_ID)
    pl.semaphore_wait(barrier, len(rows + mates) + deals[0].greet(barrier))
    own, across = blocks.at[team.part], blocks.at[team.across]
    join_x = remote(block, own, join_send, join_recv, 0, team.x)
    join_core = remote(block, own, join_send, join_recv, 1, team.core)
    join_pass = remote(across, across, join_send, join_recv, 2, team.core)
    join_near = pltpu.make_async_copy(block, own, near.at[2])
    finish_rows = share(src, rows_in, row, rows, near.at[0], row_send, row_recv)
    for copy in (join_x, join_core, join_near):
        copy.start()
    for deal in deals:
        deal.start()
    finish_rows()
    summed[...] = (rows_in[0] + rows_in[1]) + (rows_in[2] + rows_in[3])
    finish_team = share(summed, out, team.part * 2 + team.col, mates, near.at[1], team_send, team_recv)
    join_x.wait_recv()
    join_pass.start()
    for deal in deals:
        deal.finish()
    finish_team()
    join_core.wait_recv()
    join_pass.wait_recv()
    for copy in (join_x, join_core, join_pass):
        copy.wait_send()
    join_near.wait()


def leave_call(lay, first, second, block, small):
    whole_array = jax.ShapeDtypeStruct(first.shape, first.dtype)
    return pl.pallas_call(
        functools.partial(leave_kernel, lay.part),
        in_specs=[VMEM_SPEC] * 4,
        out_specs=[HBM_SPEC, HBM_SPEC, HBM_SPEC, VMEM_SPEC],
        out_shape=[
            whole_array,
            whole_array,
            jax.ShapeDtypeStruct((4,) + block.shape, block.dtype),
            jax.ShapeDtypeStruct((8,) + small.shape, F32),
        ],
        scratch_shapes=DEAL_SEMS
        + DEAL_SEMS
        + [pltpu.VMEM((4,) + small.shape, F32), pltpu.VMEM(small.shape, F32)]
        + [pltpu.SemaphoreType.DMA((count,)) for count in (3, 3, 4, 7, 8, 3, 3)],
        compiler_params=pltpu.CompilerParams(
            collective_id=lay.fresh_id(), has_side_effects=True, vmem_limit_bytes=60 << 20
        ),
        cost_estimate=pl.CostEstimate(flops=1 << 30, bytes_accessed=120 << 20, transcendentals=0),
        name="leave",
    )(first, second, block, small)


def cross(lay, value):
    return lax.ppermute(value, lay.part, [(0, 2), (2, 0), (1, 3), (3, 1)])


def link(lay, value):
    return lax.ppermute(value, lay.part, [(0, 1), (1, 0), (2, 3), (3, 2)])


def part_order(lay):
    part = lax.axis_index(lay.part)
    twin = part + 1 - 2 * (part % 2)
    return jnp.stack([part, (part + 2) % 4, twin, (twin + 2) % 4]).astype(jnp.int32)


def rows_kernel(order, *refs):
    for index, ref in enumerate(refs[:4]):

        @pl.when(pl.program_id(1) == index)
        def _():
            refs[4][...] = ref[...].astype(F32)


def place_rows(order, pieces, start, rows):
    width = pieces[0].shape[1]
    block = rows
    while start % block:
        block //= 2
    steps = rows // block
    return pl.pallas_call(
        rows_kernel,
        grid_spec=pltpu.PrefetchScalarGridSpec(
            num_scalar_prefetch=1,
            grid=(steps, 4),
            in_specs=[pl.BlockSpec((block, width), lambda j, i, order: (start // block + j, 0))] * 4,
            out_specs=pl.BlockSpec((block, width), lambda j, i, order: (order[i] * steps + j, 0)),
        ),
        out_shape=jax.ShapeDtypeStruct((4 * rows, width), F32),
        compiler_params=pltpu.CompilerParams(vmem_limit_bytes=60 << 20),
        name="place_rows",
    )(order, *pieces)


def late_head_kernel(order, *refs):
    for index, ref in enumerate(refs[:4]):

        @pl.when(pl.program_id(0) == index)
        def _():
            refs[4][...] = ref[...].T.astype(F32)


def place_late_head(order, heads, head, pieces):
    features = pieces[0].shape[1]
    return pl.pallas_call(
        late_head_kernel,
        grid_spec=pltpu.PrefetchScalarGridSpec(
            num_scalar_prefetch=1,
            grid=(4,),
            in_specs=[pl.BlockSpec((PER_HEAD, features), lambda i, order: (0, 0))] * 4,
            out_specs=pl.BlockSpec((features, PER_HEAD), lambda i, order: (0, order[i] * heads + head)),
        ),
        out_shape=jax.ShapeDtypeStruct((features, 4 * heads * PER_HEAD), F32),
        compiler_params=pltpu.CompilerParams(vmem_limit_bytes=60 << 20),
        name="place_late_head",
    )(order, *pieces)


def close_kernel(heads, src, tail, _, sums, first, second, out, decay, conv, gain, attn, ffn, rest, first_out,
                 second_out):
    step = pl.program_id(0)
    first_out[...] = first[...]
    second_out[...] = second[...]
    out[...] = src[0].T.astype(F32)
    for part in range(4):

        @pl.when(step == part)
        def _():
            decay[part * 2 * heads : (part + 1) * 2 * heads, :] = tail[0, : 2 * heads, :].astype(F32)

    @pl.when(step == 1)
    def _():
        row, col = lax.axis_index("row"), lax.axis_index("col")
        blocks = conv.shape[1] // 512
        for part in range(4):
            own = sums[2 * part + col]
            for tap in range(TAPS):
                for block in range(blocks):
                    start = (part * blocks + block) * 128
                    conv[tap : tap + 1, start : start + 128] = own[tap * blocks + block : tap * blocks + block + 1]
            rest[part : part + 1, :] = own[REST_ROW : REST_ROW + 1]
        total = sums[0]
        for slot in range(1, 8):
            total = total + sums[slot]
        gain[...] = total[GAIN_ROW:ATTN_ROW]
        for index in range(4):

            @pl.when(row == index)
            def _():
                attn[...] = total[ATTN_ROW + 4 * index : ATTN_ROW + 4 * index + 4]
                ffn[...] = total[FFN_ROW + 4 * index : FFN_ROW + 4 * index + 4]


def close_call(heads, stack, whole_grad, sums, first, second):
    features = stack.shape[2]
    channels = 4 * heads * INNER

    def fixed(*shape):
        return pl.BlockSpec(shape, lambda i: (0,) * len(shape))

    piece = pl.BlockSpec((1,) + first.shape[1:], lambda i: (i, 0, 0))
    return pl.pallas_call(
        functools.partial(close_kernel, heads),
        grid=(4,),
        in_specs=[
            pl.BlockSpec((1, PER_HEAD, features), lambda i: (i, 0, 0)),
            pl.BlockSpec((1, DECAY_ROWS, features), lambda i: (i, PER_HEAD // DECAY_ROWS, 0)),
            HBM_SPEC,
            fixed(*sums.shape),
            piece,
            piece,
        ],
        out_specs=[
            pl.BlockSpec((features, PER_HEAD), lambda i: (0, i * heads)),
            fixed(8 * heads, features),
            fixed(TAPS, channels),
            fixed(DV // 128, 128),
            fixed(4, 128),
            fixed(4, 128),
            fixed(4, 128),
            piece,
            piece,
        ],
        out_shape=[
            jax.ShapeDtypeStruct((features, 4 * heads * PER_HEAD), F32),
            jax.ShapeDtypeStruct((8 * heads, features), F32),
            jax.ShapeDtypeStruct((TAPS, channels), F32),
            jax.ShapeDtypeStruct((DV // 128, 128), F32),
            jax.ShapeDtypeStruct((4, 128), F32),
            jax.ShapeDtypeStruct((4, 128), F32),
            jax.ShapeDtypeStruct((4, 128), F32),
            jax.ShapeDtypeStruct(first.shape, first.dtype),
            jax.ShapeDtypeStruct(second.shape, second.dtype),
        ],
        input_output_aliases={2: 0},
        compiler_params=pltpu.CompilerParams(vmem_limit_bytes=60 << 20),
        name="close",
    )(stack, stack, whole_grad, sums, first, second)


def place_ffn_kernel(counts, order, *refs):
    units = sum(counts)
    blocks = len(counts)
    pairs, downs = refs[: 4 * blocks], refs[4 * blocks : 8 * blocks]
    gate, up, down = refs[8 * blocks : 8 * blocks + 3]
    turned = refs[8 * blocks + 3 :]
    base = 0
    for block, count in enumerate(counts):
        for index in range(4):
            turned[block][order[index]] = pairs[4 * block + index][...].T.astype(F32)
            start = pl.multiple_of(order[index] * units + base, 64)
            down[pl.ds(start, count), :] = downs[4 * block + index][...].astype(F32)
        for part in range(4):
            place = slice(part * units + base, part * units + base + count)
            gate[:, place] = turned[block][part, :, :count]
            up[:, place] = turned[block][part, :, count:]
        base += count


def place_ffn(order, pieces):
    counts = [group[0].shape[0] // 3 for group in pieces]
    flat = [piece for group in pieces for piece in group]
    features, units = flat[0].shape[1], sum(counts)
    wide = jax.ShapeDtypeStruct((features, 4 * units), F32)
    return pl.pallas_call(
        functools.partial(place_ffn_kernel, counts),
        grid_spec=pltpu.PrefetchScalarGridSpec(
            num_scalar_prefetch=1,
            grid=(features // 128,),
            in_specs=[pl.BlockSpec((2 * (p.shape[0] // 3), 128), lambda i, order: (0, i)) for p in flat]
            + [pl.BlockSpec((p.shape[0] // 3, 128), lambda i, order: (2, i)) for p in flat],
            out_specs=[
                pl.BlockSpec((128, 4 * units), lambda i, order: (i, 0)),
                pl.BlockSpec((128, 4 * units), lambda i, order: (i, 0)),
                pl.BlockSpec((4 * units, 128), lambda i, order: (0, i)),
            ],
            scratch_shapes=[pltpu.VMEM((4, 128, 2 * count), F32) for count in counts],
        ),
        out_shape=[wide, wide, jax.ShapeDtypeStruct((4 * units, features), F32)],
        compiler_params=pltpu.CompilerParams(vmem_limit_bytes=60 << 20),
        cost_estimate=pl.CostEstimate(flops=1 << 30, bytes_accessed=30 << 20, transcendentals=0),
        name="place_ffn",
    )(order, *flat, *flat)


def stack_kernel(counts, *refs):
    grads, values, out = refs[: len(counts)], refs[len(counts) : -1], refs[-1]
    base = 0
    for grad, value, count in zip(grads, values, counts):
        for start in range(0, count, 256):
            size = min(256, grad.shape[1] - start)
            part = lax.dot_general(grad[:, start : start + size], value[...], TN, preferred_element_type=F32)
            size = min(size, count - start)
            out[0, base + start : base + start + size, :] = part[:size].astype(BF16)
        base += count


def stack_call(rows_n, pairs, counts):
    tokens, wide = pairs[0][1].shape
    width = wide // rows_n
    total = sum(counts)
    flops = 2 * tokens * wide * sum(grad.shape[1] for grad, _ in pairs)
    return pl.pallas_call(
        functools.partial(stack_kernel, counts),
        grid=(rows_n,),
        in_specs=[
            pl.BlockSpec(grad.shape, lambda i: (0, 0), pipeline_mode=pl.Buffered(1)) for grad, _ in pairs
        ]
        + [pl.BlockSpec((tokens, width), lambda i: (0, i)) for _ in pairs],
        out_specs=pl.BlockSpec((1, total, width), lambda i: (i, 0, 0)),
        out_shape=jax.ShapeDtypeStruct((rows_n, total, width), BF16),
        compiler_params=pltpu.CompilerParams(vmem_limit_bytes=60 << 20),
        cost_estimate=pl.CostEstimate(flops=flops, bytes_accessed=40 << 20, transcendentals=0),
        name="weight_grads",
    )(*[grad for grad, _ in pairs], *[value for _, value in pairs])


def units_kernel(part_name, cuts, gate, up, down, *outs):
    part, units = lax.axis_index(part_name), cuts[-1]
    for index in range(gate.shape[1] // units):

        @pl.when(part == index)
        def _():
            base = index * units
            for which, ref in enumerate((gate, up)):
                turned = ref[:, base : base + units].T
                for out, start, end in zip(outs, cuts[:-1], cuts[1:]):
                    out[which * (end - start) : (which + 1) * (end - start), :] = turned[start:end]
            for out, start, end in zip(outs, cuts[:-1], cuts[1:]):
                out[2 * (end - start) :, :] = down[base + start : base + end, :]


def units_call(lay, cuts, gate, up, down):
    features, wide = gate.shape
    rows = [3 * (end - start) for start, end in zip(cuts[:-1], cuts[1:])]
    return pl.pallas_call(
        functools.partial(units_kernel, lay.part, cuts),
        grid=(features // 128,),
        in_specs=[pl.BlockSpec((128, wide), lambda i: (i, 0))] * 2 + [pl.BlockSpec((wide, 128), lambda i: (0, i))],
        out_specs=[pl.BlockSpec((count, 128), lambda i: (0, i)) for count in rows],
        out_shape=[jax.ShapeDtypeStruct((count, features), BF16) for count in rows],
        compiler_params=pltpu.CompilerParams(vmem_limit_bytes=60 << 20),
        name="own_units",
    )(gate, up, down)


def ffn_kernel(values, grads, stack, hidden, both_grad):
    units, width = hidden.shape[1], stack.shape[2]
    both, grad = 0.0, 0.0
    for index in range(stack.shape[0]):
        cols = slice(index * width, (index + 1) * width)
        both = both + lax.dot_general(
            values[:, cols], stack[index, : 2 * units, :], NT, preferred_element_type=F32
        )
        grad = grad + lax.dot_general(grads[:, cols], stack[index, 2 * units :, :], NT, preferred_element_type=F32)
    gate, up = both[:, :units], both[:, units:]
    sig = sigmoid(gate)
    act = gate * sig
    hidden[...] = (act * up).astype(BF16)
    both_grad[:, :units] = (grad * up * (sig + act * (1.0 - sig))).astype(BF16)
    both_grad[:, units:] = (grad * act).astype(BF16)


def ffn_call(values, grads, stack):
    tokens, width = values.shape
    units = stack.shape[1] // 3
    block = 256
    while tokens % block:
        block //= 2
    row = pl.BlockSpec((block, width), lambda i: (i, 0))
    return pl.pallas_call(
        ffn_kernel,
        grid=(tokens // block,),
        in_specs=[row, row, pl.BlockSpec(stack.shape, lambda i: (0, 0, 0))],
        out_specs=[
            pl.BlockSpec((block, units), lambda i: (i, 0)),
            pl.BlockSpec((block, 2 * units), lambda i: (i, 0)),
        ],
        out_shape=[
            jax.ShapeDtypeStruct((tokens, units), BF16),
            jax.ShapeDtypeStruct((tokens, 2 * units), BF16),
        ],
        compiler_params=pltpu.CompilerParams(vmem_limit_bytes=60 << 20),
        cost_estimate=pl.CostEstimate(
            flops=6 * tokens * width * units, bytes_accessed=30 << 20, transcendentals=tokens * units
        ),
        name="ffn",
    )(values, grads, stack)


SEQ = 448


def project(left, right):
    return jnp.dot(left, right, preferred_element_type=F32)


def project_back(left, right):
    return lax.dot_general(left, right, NT, preferred_element_type=F32)


def weight_grads(lay, *pairs):
    if lay.native:
        return stack_call(lay.rows, [pair[:2] for pair in pairs], [count for _, _, count in pairs])
    stacks = []
    for grad, value, count in pairs:
        whole = lax.dot_general(grad, value, TN, preferred_element_type=F32)[:count].astype(BF16)
        stacks.append(jnp.moveaxis(whole.reshape(count, lay.rows, -1), 1, 0))
    return jnp.concatenate(stacks, axis=1)


def after(value, *others):
    return lax.optimization_barrier((value,) + others)[0]


class Plan:
    def __init__(self, mesh, heads):
        dp, self.rows, self.cols = (mesh.shape[name] for name in ("dp", "row", "col"))
        ways = dp
        while dp % ways or (heads // self.cols) % ways:
            ways -= 1
        self.ways = ways
        if ways == dp:
            self.mesh, self.shared, self.part = mesh, (), "dp"
        else:
            devices = mesh.devices.reshape(dp // ways, ways, self.rows, self.cols)
            self.mesh = Mesh(devices, ("group", "part", "row", "col"))
            self.shared, self.part = ("group",), "part"
        self.data = self.shared + (self.part,)
        self.team = (self.part, "col")
        self.native = (ways, self.rows, self.cols) == (4, 4, 2) and heads == 2 * ways * self.cols
        self.next_id = 0

    def fresh_id(self):
        self.next_id += 1
        return self.next_id


def spread(lay, values):
    local = values.shape[0]
    whole = lax.all_gather(values, "col", axis=0, tiled=True)
    whole = lax.all_to_all(whole, "row", split_axis=0, concat_axis=1, tiled=True)
    mine = local // lay.rows
    return lax.dynamic_slice_in_dim(whole, lax.axis_index("col") * mine, mine, 0)


def unspread(lay, value):
    local = value.shape[0] * lay.rows
    whole = lax.all_gather(value, "col", axis=0, tiled=True)
    whole = lax.all_to_all(whole, "row", split_axis=1, concat_axis=0, tiled=True)
    return lax.dynamic_slice_in_dim(whole, lax.axis_index("col") * local, local, 0)


def team_gather(lay, values):
    return lax.all_gather(values, lay.team, axis=0, tiled=True)


def team_scatter(lay, values):
    return lax.psum_scatter(values.astype(BF16), lay.team, scatter_dimension=0, tiled=True).astype(F32)


def norm_forward(values):
    scale = lax.rsqrt(jnp.mean(values * values, axis=1, keepdims=True) + 1e-05)
    return values * scale, scale


def norm_backward(grad, values, gain):
    normed, scale = norm_forward(values)
    scaled = grad * gain
    inner = jnp.mean(scaled * normed, axis=1, keepdims=True)
    return scale * (scaled - normed * inner), jnp.sum(grad * normed, axis=0, keepdims=True)


def enter(lay, values, grads, gains, segments, weight):
    if lay.native:
        return enter_call(lay, values, grads, gains, segments, weight)
    mine, grads = spread(lay, values), spread(lay, grads)
    gains, weight = (lax.all_gather(value, "row", axis=0, tiled=False) for value in (gains, weight))
    segments = lax.all_gather(segments, lay.part, axis=0, tiled=False)
    normed, _ = norm_forward(mine.astype(F32))
    everyone = team_gather(lay, (normed * gains[:, 0].reshape(1, -1)).astype(BF16))
    return mine, everyone, grads, team_gather(lay, grads), gains, segments, weight


def beside(stack, start, size):
    return jnp.moveaxis(stack[:, start : start + size], 0, 1).reshape(size, -1)


def own_units(lay, cuts, gate, up, down):
    if lay.native:
        return units_call(lay, cuts, gate, up, down)
    start, size = lax.axis_index(lay.part) * cuts[-1], cuts[-1]
    gate, up = (lax.dynamic_slice_in_dim(values, start, size, 1).T for values in (gate, up))
    down = lax.dynamic_slice_in_dim(down, start, size, 0)
    return [
        jnp.concatenate([values[first:last] for values in (gate, up, down)], axis=0)
        for first, last in zip(cuts[:-1], cuts[1:])
    ]


def mid_step(lay, mixed, out_all, stored, gain):
    starts = [head * DV for head in range(len(mixed))]
    if lay.native:
        return mid_call(lay, mixed, out_all, [(0, start) for start in starts], stored, gain)
    total = sum(project(left, beside(out_all, start, DV)) for left, start in zip(mixed, starts))
    residual = stored.astype(F32) + team_scatter(lay, total)
    normed, _ = norm_forward(residual)
    return residual, team_gather(lay, (normed * gain).astype(BF16))


def feed_forward(lay, values, grads, stack):
    if lay.native:
        return ffn_call(values, grads, stack)
    units = stack.shape[1] // 3
    gate, up = (project_back(values, beside(stack, start, units)) for start in (0, units))
    sig = jax.nn.sigmoid(gate)
    grad = project_back(grads, beside(stack, 2 * units, units))
    grad_gate = grad * up * sig * (1.0 + gate * (1.0 - sig))
    both = jnp.concatenate([grad_gate.astype(BF16), (grad * gate * sig).astype(BF16)], axis=1)
    return (gate * sig * up).astype(BF16), both


def branch_step(lay, lefts, stacks, residual, out_grads, gain):
    if lay.native:
        return branch_call(lay, lefts, stacks, residual, out_grads, gain)
    total = sum(project(left, beside(stack, 0, left.shape[1])) for left, stack in zip(lefts, stacks))
    grad, gain_part = norm_backward(team_scatter(lay, total), residual, gain)
    grad = out_grads.astype(F32) + grad
    return grad, team_gather(lay, grad.astype(BF16)), gain_part


def finish_step(lay, hidden, stacks, grads, mix, starts, residual, stored, grad_residual, gain):
    if lay.native:
        return finish_call(lay, hidden, stacks, grads, mix, starts, residual, stored, grad_residual, gain)
    total = sum(
        project(left, beside(stack, 2 * left.shape[1], left.shape[1])) for left, stack in zip(hidden, stacks)
    )
    block_output = (residual + team_scatter(lay, total)).astype(BF16)
    total = sum(project_back(left, mix[:, start : start + left.shape[1]]) for left, start in zip(grads, starts))
    grad, gain_part = norm_backward(team_scatter(lay, total), stored.astype(F32), gain)
    return block_output, (grad_residual + grad).astype(BF16), gain_part


def columns(stack):
    return jnp.moveaxis(stack, 2, 0).reshape(stack.shape[2], -1).astype(F32)


def on_device(
    lay,
    block_input,
    segment_ids,
    attn_gain,
    mix_weight,
    decay_weight,
    conv_weight,
    decay_log,
    decay_bias,
    out_gain,
    out_weight,
    ffn_gain,
    gate_weight,
    up_weight,
    down_weight,
    cotangent,
):
    part = lax.axis_index(lay.part)
    heads = decay_log.shape[0] // lay.ways
    units = gate_weight.shape[1] // lay.ways
    width = mix_weight.shape[0]

    def mine(values, dim, size):
        return lax.dynamic_slice_in_dim(values, part * size, size, dim)

    def gather_rows(values):
        return lax.all_gather(values, "row", axis=0, tiled=False)

    mix_mine = mine(mix_weight, 1, heads * PER_HEAD)
    decay_mine = mine(decay_weight, 1, heads * 2)
    decay_pad = jnp.pad(decay_mine, ((0, 0), (0, 128 - heads * 2)))
    splits = [0, PER_HEAD + 128]
    for head in range(1, heads):
        splits.append(splits[-1] + PER_HEAD)
    mix_pad = jnp.concatenate([mix_mine[:, :PER_HEAD], decay_pad, mix_mine[:, PER_HEAD:]], axis=1)
    out_all = gather_rows(mine(out_weight, 0, heads * DV))
    cuts = [0, min(units, 320), units]
    unit_blocks = own_units(lay, cuts, gate_weight, up_weight, down_weight)
    conv_mine = mine(conv_weight, 1, heads * INNER)
    log_mine, bias_mine = mine(decay_log, 0, heads), mine(decay_bias, 0, heads)

    gains = jnp.stack([attn_gain, ffn_gain])
    stored, attn_all, out_grads, out_grads_all, gains, segments, mix_all = enter(
        lay, block_input, cotangent, gains, segment_ids.reshape(1, -1), after(mix_pad, *unit_blocks)
    )
    mix_all = mix_all.reshape(lay.rows * width, -1)
    gain_one, gain_two = gains[:, 0].reshape(1, -1), gains[:, 1].reshape(1, -1)
    seg_row = segments.reshape(-1, 1, SEQ)
    waiting = lax.optimization_barrier((*unit_blocks, attn_all))[:-1]
    stacks = [gather_rows(values) for values in waiting]
    tokens = attn_all.shape[0]
    head_weights = [mix_all[:, start:end] for start, end in zip(splits[:-1], splits[1:])]
    shared, mixed, solves, projs = (), [], [], []
    for head in range(heads):
        projs.append(project(after(attn_all, *mixed), head_weights[head]))
        if not head:
            shared = (
                projs[0], PER_HEAD // 128, seg_row, conv_mine, log_mine, bias_mine, out_gain.reshape(1, -1),
            )
        values, solve = mixer_forward(head, heads, projs[head], *shared)
        mixed.append(values)
        solves.append(solve)
    residual, ffn_all = mid_step(lay, mixed, out_all, stored, gain_two)

    def sum_rows(grads):
        grads = lax.psum_scatter(grads, "row", scatter_dimension=0, tiled=False)
        return lax.psum(grads, lay.shared) if lay.shared else grads

    hidden, grad_both, ffn_grads = [], [], []
    for stack in stacks:
        values, grads = feed_forward(lay, ffn_all, out_grads_all, stack)
        count = values.shape[1]
        ffn_part = weight_grads(lay, (grads, ffn_all, 2 * count), (values, out_grads_all, count))
        ffn_all, values, grads = lax.optimization_barrier((ffn_all, values, grads, ffn_part))[:3]
        hidden.append(values)
        grad_both.append(grads)
        ffn_grads.append(sum_rows(ffn_part))
    grad_residual, branch_all, ffn_gain_part = branch_step(lay, grad_both, stacks, residual, out_grads, gain_two)

    branch = branch_all
    if lay.native:
        branch = after(branch, ffn_grads[0])
        crossed = [cross(lay, grads) for grads in ffn_grads]
    other = jnp.zeros((tokens, 128), BF16)
    proj_grads, mix_grads, conv_parts, small_parts = [], [], [], []
    for head in reversed(range(heads)):
        common = (head, heads, projs[head], *shared, solves[head], branch, out_all)
        if head:
            grad, extra, conv_part, small_part = mixer_backward(*common, None)
            if lay.native:
                grad = after(grad, crossed[0])
            other = other + extra
        else:
            grad, conv_part, small_part = mixer_backward(*common, other)
            if lay.native:
                grad = after(grad, *crossed)
        triples = [(grad, attn_all, PER_HEAD if head else PER_HEAD + DECAY_ROWS)]
        if head == heads - 1:
            triples += [(values, branch_all, DV) for values in mixed]
        mix_part = weight_grads(lay, *triples)
        branch, grad = lax.optimization_barrier((branch, grad, mix_part))[:2]
        if lay.native:
            branch = after(branch, *ffn_grads[1:])
        proj_grads.insert(0, grad)
        conv_parts.insert(0, conv_part.sum(0))
        small_parts.insert(0, small_part.sum(0)[0])
        mix_grads.insert(0, sum_rows(mix_part))
    if lay.native:
        ffn_pieces = [[ffn_grads[0], crossed[0], link(lay, ffn_grads[0]), link(lay, crossed[0])]]
        hidden[0] = after(hidden[0], *ffn_pieces[0])
    block_output, input_grad, attn_gain_part = finish_step(
        lay, hidden, stacks, proj_grads, mix_all, splits[:-1], residual, stored, grad_residual, gain_one
    )

    conv_part = jnp.concatenate(conv_parts, axis=1)
    rest_part = jnp.concatenate([part_of[DV + item : DV + item + 1] for item in range(2) for part_of in small_parts])
    gain_part = sum(part_of[:DV] for part_of in small_parts)
    row, col = lax.axis_index("row"), lax.axis_index("col")
    if lay.native:
        lines = [conv_part, gain_part, attn_gain_part, ffn_gain_part, jnp.pad(rest_part, (0, 128 - rest_part.size))]
        flat = jnp.concatenate([values.reshape(-1, 128) for values in lines])
        flat = jnp.pad(flat, ((0, SMALL_ROWS - flat.shape[0]), (0, 0)))
        order = part_order(lay)
        for grads, passed in zip(ffn_grads[1:], crossed[1:]):
            ffn_pieces.append([grads, passed, link(lay, grads), link(lay, passed)])
        late = after(mix_grads[1], block_output)
        late_passed = cross(lay, late)
        ffn_pieces[0][0] = after(ffn_pieces[0][0], block_output)
        gate_grad, up_grad, down_weight_grad = place_ffn(order, ffn_pieces)
        passed = after(late_passed, gate_grad)
        late_pieces = [late, passed, link(lay, late), link(lay, passed)]
        out_weight_grad = place_rows(order, late_pieces, PER_HEAD, heads * DV)
        mix_grad = place_late_head(order, heads, 1, late_pieces)
        first = after(mix_grads[0], mix_grad)
        flat = after(flat, mix_grad, out_weight_grad)
        block_output, input_grad, first_stack, sums = leave_call(lay, block_output, input_grad, first, flat)
        mix_grad, decay_grad, conv_grad, gain_sum, attn_sum, ffn_sum, rest, block_output, input_grad = close_call(
            heads, first_stack, mix_grad, sums, block_output, input_grad
        )
        block_output, input_grad = (value.reshape(-1, value.shape[2]) for value in (block_output, input_grad))
        decay_grad, gain_sum = decay_grad.T, gain_sum.reshape(-1)
        attn_gain_grad, ffn_gain_grad = attn_sum.reshape(-1), ffn_sum.reshape(-1)
        log_grad, bias_grad = rest[:, :heads].reshape(-1), rest[:, heads : 2 * heads].reshape(-1)
    else:
        block_output, input_grad = unspread(lay, block_output), unspread(lay, input_grad)
        own = jnp.concatenate([conv_part.reshape(-1), rest_part])
        pick = (jnp.arange(lay.ways * lay.cols) == part * lay.cols + col).astype(F32)[:, None]
        sums, gain_sum, ffn_sum, attn_sum = lax.psum(
            (pick * own[None, :], gain_part, ffn_gain_part[0], attn_gain_part[0]), lay.data + ("row", "col")
        )
        sums = lax.dynamic_index_in_dim(sums.reshape(lay.ways, lay.cols, -1), col, 1, keepdims=False)
        split = conv_part.size
        conv_grad = jnp.moveaxis(sums[:, :split].reshape(lay.ways, TAPS, -1), 0, 1).reshape(TAPS, -1)
        log_grad = sums[:, split : split + heads].reshape(-1)
        bias_grad = sums[:, split + heads :].reshape(-1)
        attn_gain_grad = lax.dynamic_slice_in_dim(attn_sum, row * width, width, 0)
        ffn_gain_grad = lax.dynamic_slice_in_dim(ffn_sum, row * width, width, 0)

    out_start = PER_HEAD if heads > 1 else PER_HEAD + DECAY_ROWS
    if not lay.native:
        mix_stacks = [lax.all_gather(value, lay.part, axis=0, tiled=False) for value in mix_grads]
        ffn_stacks = [lax.all_gather(value, lay.part, axis=0, tiled=False) for value in ffn_grads]
        decay_grad = columns(mix_stacks[0][:, PER_HEAD : PER_HEAD + 2 * heads])
        mix_grad = columns(jnp.concatenate([stack[:, :PER_HEAD] for stack in mix_stacks], axis=1))
        gate_grad, up_grad, down_weight_grad = (
            jnp.concatenate([jnp.split(stack, 3, axis=1)[item] for stack in ffn_stacks], axis=1) for item in range(3)
        )
        gate_grad, up_grad = columns(gate_grad), columns(up_grad)
        down_weight_grad = down_weight_grad.reshape(-1, width).astype(F32)
        out_weight_grad = mix_stacks[-1][:, out_start : out_start + heads * DV].reshape(-1, width).astype(F32)
    return (
        block_output,
        input_grad,
        attn_gain_grad,
        mix_grad,
        decay_grad,
        conv_grad,
        log_grad,
        bias_grad,
        gain_sum,
        out_weight_grad,
        ffn_gain_grad,
        gate_grad,
        up_grad,
        down_weight_grad,
    )


def solution(mesh):
    def run(*args):
        lay = Plan(mesh, args[6].shape[0])
        tokens, grid = P(lay.data + ("col",), "row"), P("row", "col")
        turned, features, inner = P("col", "row"), P("row"), P("col")
        conv = P(None, "col")
        return jax.shard_map(
            functools.partial(on_device, lay),
            mesh=lay.mesh,
            in_specs=(
                tokens, P(lay.data + ("row",)), features, grid, grid, conv, inner, inner, P(),
                turned, features, grid, grid, turned, tokens,
            ),
            out_specs=(
                tokens, tokens, features, grid, grid, conv, inner, inner, P(),
                turned, features, grid, grid, turned,
            ),
            check_vma=False,
        )(*args)

    return run
```

```python
import functools
import jax
import jax.numpy as jnp
from jax import lax
from jax.experimental import pallas as pl
from jax.experimental.pallas import tpu as pltpu
from jax.sharding import Mesh
from jax.sharding import PartitionSpec as P

F32, BF16 = jnp.float32, jnp.bfloat16
DK, DV, TAPS = 128, 256, 4
DECAY_ROWS = 16
INNER = 2 * DK + DV
PER_HEAD = INNER + DV
NN = (((1,), (0,)), ((), ()))
NT = (((1,), (1,)), ((), ()))
TN = (((0,), (0,)), ((), ()))


def mm(left, right, dims=NN):
    return lax.dot_general(left.astype(BF16), right.astype(BF16), dims, preferred_element_type=F32)


def sigmoid(values):
    return 1.0 / (1.0 + jnp.exp(-values))


def softplus(values):
    return jnp.maximum(values, 0.0) + jnp.log1p(jnp.exp(-jnp.abs(values)))


def shift_down(values, lag):
    return jnp.concatenate([jnp.zeros_like(values[:lag]), values[: values.shape[0] - lag]], axis=0)


def shift_up(values, lag):
    return jnp.concatenate([values[lag:], jnp.zeros_like(values[:lag])], axis=0)


def cumsum_rows(values):
    step = 1
    while step < values.shape[0]:
        values = values + shift_down(values, step)
        step *= 2
    return values


def reverse_cumsum_rows(values):
    step = 1
    while step < values.shape[0]:
        values = values + shift_up(values, step)
        step *= 2
    return values


def prepare(head, proj, extra, seg_row, conv, log_ref, bias_ref):
    length = proj.shape[0]
    seg_row = seg_row.astype(F32)
    rows = lax.broadcasted_iota(jnp.int32, (length, length), 0)
    cols = lax.broadcasted_iota(jnp.int32, (length, length), 1)
    seg_col = jnp.sum(jnp.where(rows == cols, seg_row, 0.0), axis=1, keepdims=True)
    summed = conv[TAPS - 1 : TAPS] * proj[:, :INNER]
    keeps = []
    for lag in range(1, TAPS):
        keep = (shift_down(seg_col + 1.0, lag) == seg_col + 1.0).astype(F32)
        keeps.append(keep)
        summed = summed + conv[TAPS - 1 - lag : TAPS - lag] * (shift_down(proj[:, :INNER], lag) * keep)
    gate_conv = sigmoid(summed)
    active = summed * gate_conv
    lane = lax.broadcasted_iota(jnp.int32, extra.shape, 1)
    write = jnp.sum(jnp.where(lane == 2 * head, extra, 0.0), axis=1, keepdims=True)
    drive = jnp.sum(jnp.where(lane == 2 * head + 1, extra, 0.0), axis=1, keepdims=True)
    beta = sigmoid(write)
    drive = drive + bias_ref[head]
    rate = jnp.exp(jnp.full((1, 1), log_ref[head], F32))
    decay = -rate * softplus(drive)
    total = cumsum_rows(decay)
    total_row = jnp.sum(jnp.where(rows == cols, total, 0.0), axis=0, keepdims=True)
    weight = jnp.exp(jnp.where((rows >= cols) & (seg_col == seg_row), total - total_row, -1e30))
    raw_q, raw_k, value = active[:, :DK], active[:, DK : 2 * DK], active[:, 2 * DK :]
    scale_q = lax.rsqrt(jnp.sum(raw_q * raw_q, axis=1, keepdims=True) + 1e-06)
    scale_k = lax.rsqrt(jnp.sum(raw_k * raw_k, axis=1, keepdims=True) + 1e-06)
    query = (raw_q * scale_q * DK ** (-0.5)).astype(BF16)
    key = (raw_k * scale_k).astype(BF16)
    inner = mm(key, key, NT)
    strict = jnp.where(rows > cols, weight, 0.0)
    return dict(
        summed=summed, keeps=keeps, gate_conv=gate_conv, raw_q=raw_q, raw_k=raw_k, value=value,
        scale_q=scale_q, scale_k=scale_k, query=query, key=key, inner=inner, weight=weight,
        strict=strict, beta=beta, drive=drive, rate=rate, decay=decay, rows=rows, cols=cols,
    )


def forward_kernel(head, start, *refs):
    if head:
        (attn_ref, stack_ref, extra_ref, segr_ref, conv_ref, log_ref, bias_ref, gain_ref, mixed_ref, solve_ref,
         proj_ref, work) = refs
    else:
        (attn_ref, stack_ref, segr_ref, conv_ref, log_ref, bias_ref, gain_ref, mixed_ref, solve_ref, proj_ref,
         extra_ref, work) = refs
    count, size = work.shape[:2]
    length, width = proj_ref.shape[0] // count, stack_ref.shape[2]
    spans = [slice(item * length, (item + 1) * length) for item in range(count)]
    tile = min(128, size)
    starts = range(0, size, tile)
    r = lax.broadcasted_iota(jnp.int32, (tile, tile), 0)
    c = lax.broadcasted_iota(jnp.int32, (tile, tile), 1)
    eye = (r == c).astype(F32)
    ready, parts = [], []

    def product(span, first, rows):
        value = 0.0
        for index in range(stack_ref.shape[0]):
            left = attn_ref[span, index * width : (index + 1) * width]
            value = value + mm(left, stack_ref[index, first : first + rows, :], NT)
        return value

    for span in spans:
        proj_ref[span, :] = product(span, start, PER_HEAD)
        if not head:
            extra_ref[span, :] = product(span, start + PER_HEAD, DECAY_ROWS)
    for item, span in enumerate(spans):
        p = prepare(
            head, proj_ref[span, :], extra_ref[span, :], segr_ref[item], conv_ref[...], log_ref, bias_ref
        )
        if size != length:
            work[item] = jnp.zeros(work.shape[1:], F32)
        work[item, 0:length, 0:length] = p["beta"] * p["strict"] * p["inner"]
        scores = (mm(p["query"], p["key"], NT) * p["weight"]).astype(BF16)
        ready.append((scores, (p["beta"] * p["value"]).astype(BF16)))
        parts += [work[item, start : start + tile, start : start + tile] for start in starts]
    inv = [eye - jnp.where((r // 2 == c // 2), part, 0.0) for part in parts]
    step = 2
    while step < tile:
        pick = (r // (2 * step) == c // (2 * step)) & (r // step != c // step)
        lows = [mm(jnp.where(pick, part, 0.0), x) for part, x in zip(parts, inv)]
        inv = [x - mm(x, low) for x, low in zip(inv, lows)]
        step *= 2
    for index, values in enumerate(inv):
        item, start = index // len(starts), starts[index % len(starts)]
        work[item, start : start + tile, start : start + tile] = values
    step = tile
    while step < size:
        places = [(item, start) for item in range(count) for start in range(0, size, 2 * step)]
        lows = [
            mm(work[item, start + step : start + 2 * step, start : start + step],
               work[item, start : start + step, start : start + step])
            for item, start in places
        ]
        for (item, start), low in zip(places, lows):
            mid, end = start + step, start + 2 * step
            work[item, mid:end, start:mid] = -mm(work[item, mid:end, mid:end], low)
        step *= 2
    for item, span in enumerate(spans):
        solve = work[item, 0:length, 0:length].astype(BF16)
        solve_ref[item] = solve
        scores, target = ready[item]
        out = mm(scores, mm(solve, target))
        scale = lax.rsqrt(jnp.sum(out * out, axis=1, keepdims=True) * (1.0 / DV) + 1e-05)
        gate = proj_ref[span, INNER:]
        mixed_ref[span, :] = (out * scale * gain_ref[...] * (gate * sigmoid(gate))).astype(BF16)


def backward_kernel(head, last, *refs):
    if last:
        (proj_ref, extra_ref, segr_ref, conv_ref, log_ref, bias_ref, gain_ref, solve_ref, grad_ref,
         turn_ref, other_ref, gproj_ref, gconv_ref, gsmall_ref) = refs
    else:
        (proj_ref, extra_ref, segr_ref, conv_ref, log_ref, bias_ref, gain_ref, solve_ref, grad_ref,
         turn_ref, gproj_ref, gextra_ref, gconv_ref, gsmall_ref) = refs
    conv = conv_ref[...]
    p = prepare(head, proj_ref[...], extra_ref[...], segr_ref[0], conv, log_ref, bias_ref)
    weight, strict, inner, beta, value = p["weight"], p["strict"], p["inner"], p["beta"], p["value"]
    query, key = p["query"], p["key"]
    solve = solve_ref[0]
    fresh = mm(solve, beta * value).astype(BF16)
    scores = mm(query, key, NT)
    probs = (scores * weight).astype(BF16)
    out = mm(probs, fresh)
    scale = lax.rsqrt(jnp.sum(out * out, axis=1, keepdims=True) * (1.0 / DV) + 1e-05)
    normed = out * scale
    gate = proj_ref[:, INNER:]
    gate_sig = sigmoid(gate)
    grad, width = 0.0, turn_ref.shape[2]
    for index in range(turn_ref.shape[0]):
        grad = grad + mm(grad_ref[:, index * width : (index + 1) * width], turn_ref[index], NT)
    gain = gain_ref[...]
    through = grad * normed
    ggate = through * gain * (gate_sig * (1.0 + gate * (1.0 - gate_sig)))
    ggain = jnp.sum(through * (gate * gate_sig), axis=0, keepdims=True)
    gnormed = grad * gain * (gate * gate_sig)
    gout = scale * (gnormed - normed * (jnp.sum(gnormed * normed, axis=1, keepdims=True) * (1.0 / DV)))
    gout = gout.astype(BF16)
    gprobs = mm(gout, fresh, NT)
    gfresh = mm(probs, gout, TN)
    gtarget = mm(solve, gfresh, TN)
    glower = -mm(gtarget, fresh, NT) * strict
    gscores = gprobs * weight
    tilt = glower * inner
    flow = gscores * scores + beta * tilt
    gbeta = jnp.sum(tilt, axis=1, keepdims=True) + jnp.sum(gtarget * value, axis=1, keepdims=True)
    gscores = gscores.astype(BF16)
    ginner = (beta * glower).astype(BF16)
    gquery = mm(gscores, key)
    gkey = mm(gscores, query, TN) + mm(ginner, key) + mm(ginner, key, TN)
    col_flow = jnp.sum(flow, axis=0, keepdims=True)
    col_flow = jnp.sum(jnp.where(p["rows"] == p["cols"], col_flow, 0.0), axis=1, keepdims=True)
    gdecay = reverse_cumsum_rows(jnp.sum(flow, axis=1, keepdims=True) - col_flow)
    raw_q, raw_k, scale_q, scale_k = p["raw_q"], p["raw_k"], p["scale_q"], p["scale_k"]
    gq = (DK ** (-0.5)) * scale_q * (
        gquery - raw_q * (scale_q * scale_q * jnp.sum(gquery * raw_q, axis=1, keepdims=True)))
    gk = scale_k * (gkey - raw_k * (scale_k * scale_k * jnp.sum(gkey * raw_k, axis=1, keepdims=True)))
    gactive = jnp.concatenate([gq, gk, beta * gtarget], axis=1)
    gsummed = gactive * (p["gate_conv"] * (1.0 + p["summed"] * (1.0 - p["gate_conv"])))
    source = proj_ref[:, :INNER]
    gsource = conv[TAPS - 1 : TAPS] * gsummed
    gconv_ref[0, TAPS - 1 : TAPS, :] = jnp.sum(gsummed * source, axis=0, keepdims=True)
    for lag in range(1, TAPS):
        kept = gsummed * p["keeps"][lag - 1]
        gsource = gsource + conv[TAPS - 1 - lag : TAPS - lag] * shift_up(kept, lag)
        gconv_ref[0, TAPS - 1 - lag : TAPS - lag, :] = jnp.sum(kept * shift_down(source, lag), axis=0, keepdims=True)
    gdrive = -p["rate"] * gdecay * sigmoid(p["drive"])
    gwrite = gbeta * beta * (1.0 - beta)
    lane = lax.broadcasted_iota(jnp.int32, (extra_ref.shape[0], 128), 1)
    gextra = jnp.where(lane == 2 * head, gwrite, jnp.where(lane == 2 * head + 1, gdrive, 0.0))
    gproj_ref[:, :INNER] = gsource.astype(BF16)
    gproj_ref[:, INNER:PER_HEAD] = ggate.astype(BF16)
    if last:
        gproj_ref[:, PER_HEAD:] = (gextra + other_ref[...].astype(F32)).astype(BF16)
    else:
        gextra_ref[...] = gextra.astype(BF16)
    glog = jnp.sum(gdecay * p["decay"], axis=0, keepdims=True)
    gbias = jnp.sum(gdrive, axis=0, keepdims=True)
    lane = lax.broadcasted_iota(jnp.int32, (1, 128), 1)
    gsmall_ref[0, :, 0:DV] = ggain
    gsmall_ref[0, :, DV:] = jnp.where(lane == 0, glog, jnp.where(lane == 1, gbias, 0.0))


def small_specs(length, head, group):
    smem = pl.BlockSpec(memory_space=pltpu.SMEM)
    return [
        pl.BlockSpec((group, 1, length), lambda s: (s, 0, 0)),
        pl.BlockSpec((TAPS, INNER), lambda s: (0, head)),
        smem,
        smem,
        pl.BlockSpec((1, DV), lambda s: (0, 0)),
    ]


def mixer_cost(count, passes):
    return pl.CostEstimate(flops=passes * count * (3 << 30), bytes_accessed=passes * count << 23, transcendentals=0)


def mixer_forward(head, start, attn, stack, extra, seg_row, conv, log, bias, gain):
    count, _, length = seg_row.shape
    tokens = count * length
    size = 64
    while size < length:
        size *= 2
    group = 2 if count % 2 == 0 else 1
    extra_spec = pl.BlockSpec((group * length, DECAY_ROWS), lambda s: (s, 0))
    extra_shape = jax.ShapeDtypeStruct((tokens, DECAY_ROWS), F32)
    return pl.pallas_call(
        functools.partial(forward_kernel, head, start),
        grid=(count // group,),
        in_specs=[
            pl.BlockSpec((group * length, attn.shape[1]), lambda s: (s, 0)),
            pl.BlockSpec(stack.shape, lambda s: (0, 0, 0), pipeline_mode=pl.Buffered(1)),
        ]
        + ([extra_spec] if head else [])
        + small_specs(length, head, group),
        out_specs=[
            pl.BlockSpec((group * length, DV), lambda s: (s, 0)),
            pl.BlockSpec((group, length, length), lambda s: (s, 0, 0)),
            pl.BlockSpec((group * length, PER_HEAD), lambda s: (s, 0)),
        ]
        + ([] if head else [extra_spec]),
        out_shape=[
            jax.ShapeDtypeStruct((tokens, DV), BF16),
            jax.ShapeDtypeStruct((count, length, length), BF16),
            jax.ShapeDtypeStruct((tokens, PER_HEAD), F32),
        ]
        + ([] if head else [extra_shape]),
        scratch_shapes=[pltpu.VMEM((group, size, size), F32)],
        compiler_params=pltpu.CompilerParams(vmem_limit_bytes=60 << 20),
        cost_estimate=mixer_cost(count, 1),
        name="mixer_forward",
    )(attn, stack, *([extra] if head else []), seg_row, conv, log, bias, gain)


def mixer_backward(head, proj, extra, seg_row, conv, log, bias, gain, solve, grad, turned, other):
    count, _, length = seg_row.shape
    tokens = count * length
    last = other is not None
    in_specs = [
        pl.BlockSpec((length, PER_HEAD), lambda s: (s, 0)),
        pl.BlockSpec((length, DECAY_ROWS), lambda s: (s, 0)),
        *small_specs(length, head, 1),
        pl.BlockSpec((1, length, length), lambda s: (s, 0, 0)),
        pl.BlockSpec((length, grad.shape[1]), lambda s: (s, 0)),
        pl.BlockSpec((turned.shape[0], DV, turned.shape[2]), lambda s: (0, head, 0)),
    ]
    args = [proj, extra, seg_row, conv, log, bias, gain, solve, grad, turned]
    width = PER_HEAD
    tail_specs = [
        pl.BlockSpec((1, TAPS, INNER), lambda s: (s, 0, 0)),
        pl.BlockSpec((1, 1, DV + 128), lambda s: (s, 0, 0)),
    ]
    tail_shapes = [
        jax.ShapeDtypeStruct((count, TAPS, INNER), F32),
        jax.ShapeDtypeStruct((count, 1, DV + 128), F32),
    ]
    mid_specs, mid_shapes = [], []
    if last:
        width += 128
        in_specs.append(pl.BlockSpec((length, 128), lambda s: (s, 0)))
        args.append(other)
    else:
        mid_specs = [pl.BlockSpec((length, 128), lambda s: (s, 0))]
        mid_shapes = [jax.ShapeDtypeStruct((tokens, 128), BF16)]
    return pl.pallas_call(
        functools.partial(backward_kernel, head, last),
        grid=(count,),
        in_specs=in_specs,
        out_specs=[pl.BlockSpec((length, width), lambda s: (s, 0))] + mid_specs + tail_specs,
        out_shape=[jax.ShapeDtypeStruct((tokens, width), BF16)] + mid_shapes + tail_shapes,
        compiler_params=pltpu.CompilerParams(vmem_limit_bytes=60 << 20),
        cost_estimate=mixer_cost(count, 2),
        name="mixer_backward",
    )(*args)


MESH_ID = pl.DeviceIdType.MESH
HBM_SPEC = pl.BlockSpec(memory_space=pltpu.HBM)
VMEM_SPEC = pl.BlockSpec(memory_space=pltpu.VMEM)
STRIP = 16
GAIN_ROW, ATTN_ROW, FFN_ROW, REST_ROW, SMALL_ROWS = 32, 34, 50, 66, 72


def meet(targets):
    barrier = pltpu.get_barrier_semaphore()
    for target in targets:
        pl.semaphore_signal(barrier, inc=1, device_id=target, device_id_type=MESH_ID)
    pl.semaphore_wait(barrier, len(targets))


def remote(source, dest, send, recv, index, target):
    return pltpu.make_async_remote_copy(
        src_ref=source,
        dst_ref=dest,
        send_sem=send.at[index],
        recv_sem=recv.at[index],
        device_id=target,
        device_id_type=MESH_ID,
    )


class Team:
    def __init__(self, name):
        self.name, self.part, self.col = name, lax.axis_index(name), lax.axis_index("col")
        self.across, self.twin = lax.rem(self.part + 2, 4), self.part + 1 - 2 * lax.rem(self.part, 2)
        self.far, self.other = lax.rem(self.twin + 2, 4), 1 - self.col
        self.x, self.y, self.core = {name: self.across}, {"col": self.other}, {name: self.twin}

    def partners(self):
        return [self.x, self.y, self.core]


class Gather:
    def __init__(self, team, src, out, keep, send, recv):
        self.out, self.send, self.recv = out, send, recv
        half = src.shape[0] // 2
        first, second = pl.ds(0, half), pl.ds(half, half)
        own, across = team.part * 2 + team.col, team.across * 2 + team.col
        other, diag = team.part * 2 + team.other, team.across * 2 + team.other
        self.local = pltpu.make_async_copy(src, out.at[own], keep)
        self.x_first = self.copy(src.at[first], out.at[own, first], 0, team.x)
        self.x_second = self.copy(src.at[second], out.at[own, second], 1, team.x)
        self.y_second = self.copy(src.at[second], out.at[own, second], 2, team.y)
        self.y_first = self.copy(src.at[first], out.at[own, first], 3, team.y)
        self.core_own = self.copy(src, out.at[own], 4, team.core)
        self.y_pass = self.copy(out.at[across, first], out.at[across, first], 5, team.y)
        self.x_pass = self.copy(out.at[other, second], out.at[other, second], 6, team.x)
        self.core_x = self.copy(out.at[across], out.at[across], 7, team.core)
        self.core_y = self.copy(out.at[other], out.at[other], 8, team.core)
        self.core_first = self.copy(out.at[diag, first], out.at[diag, first], 9, team.core)
        self.core_second = self.copy(out.at[diag, second], out.at[diag, second], 10, team.core)

    def copy(self, source, dest, index, target):
        return remote(source, dest, self.send, self.recv, index, target)

    def start_first(self):
        self.x_first.start()
        self.y_first.start()

    def start_second(self):
        for copy in (self.y_second, self.x_second, self.core_own, self.local):
            copy.start()

    def finish(self):
        self.x_first.wait_recv()
        self.y_pass.start()
        self.y_first.wait_recv()
        self.y_second.wait_recv()
        self.x_pass.start()
        self.core_y.start()
        self.x_second.wait_recv()
        self.core_x.start()
        self.y_pass.wait_recv()
        self.core_first.start()
        self.x_pass.wait_recv()
        self.core_second.start()
        cores = (self.core_own, self.core_x, self.core_y, self.core_first, self.core_second)
        for copy in cores:
            copy.wait_recv()
        for copy in (self.x_first, self.x_second, self.y_second, self.y_first, self.y_pass, self.x_pass) + cores:
            copy.wait_send()
        self.local.wait()


def gather_phase(team, src, out, *sems):
    gather = Gather(team, src, out, *sems)
    gather.start_first()
    gather.start_second()
    gather.finish()


GATHER_SEMS = [pltpu.SemaphoreType.DMA, pltpu.SemaphoreType.DMA((11,)), pltpu.SemaphoreType.DMA((11,))]


class Spread:
    def __init__(self, src, out, middle, keep, send, recv):
        self.src, self.out, self.middle, self.keep, self.send, self.recv = src, out, middle, keep, send, recv
        self.row, self.col = lax.axis_index("row"), lax.axis_index("col")
        self.hops = [
            remote(src.at[2 * item + 1 - self.col], middle.at[item], send, recv, item, {"col": 1 - self.col})
            for item in range(2)
        ]

    def pieces(self, side):
        home = self.col if side == 0 else 1 - self.col
        for item in range(2):
            source = self.src.at[2 * item + self.col] if side == 0 else self.middle.at[item]
            to_row = 2 * home + item
            copy = pltpu.make_async_remote_copy(
                src_ref=source,
                dst_ref=self.out.at[self.row],
                send_sem=self.send.at[2 + 2 * side + item],
                recv_sem=self.recv.at[2 + self.row],
                device_id={"row": to_row},
                device_id_type=MESH_ID,
            )
            yield to_row == self.row, copy, pltpu.make_async_copy(source, self.out.at[self.row], self.keep)

    def start(self):
        for hop in self.hops:
            hop.start()
        self.send_side(0)

    def send_side(self, side):
        for here, far, near in self.pieces(side):
            pl.when(here)(near.start)
            pl.when(jnp.logical_not(here))(far.start)

    def turn(self):
        for hop in self.hops:
            hop.wait_recv()
        self.send_side(1)

    def finish(self):
        for hop in range(1, 4):
            index = lax.rem(self.row + hop, 4)
            pltpu.make_async_remote_copy(
                src_ref=self.src.at[0],
                dst_ref=self.out.at[index],
                send_sem=self.send.at[0],
                recv_sem=self.recv.at[2 + index],
                device_id={"row": index},
                device_id_type=MESH_ID,
            ).wait_recv()
        for side in range(2):
            for here, far, near in self.pieces(side):
                pl.when(here)(near.wait)
                pl.when(jnp.logical_not(here))(far.wait_send)
        for hop in self.hops:
            hop.wait_send()


class Line:
    def __init__(self, src, out, keep, send, recv):
        self.src, self.out, self.send, self.recv = src, out, send, recv
        self.row = lax.axis_index("row")
        self.near = pltpu.make_async_copy(src, out.at[self.row], keep)

    def copy(self, hops, up):
        step = 1 if up else -1
        mark = self.row - hops * step
        return pltpu.make_async_remote_copy(
            src_ref=self.src if hops == 0 else self.out.at[mark],
            dst_ref=self.out.at[mark],
            send_sem=self.send.at[hops if up else 3 + hops],
            recv_sem=self.recv.at[mark],
            device_id={"row": self.row + step},
            device_id_type=MESH_ID,
        )

    def sends(self, hops, up):
        return (self.row >= hops) & (self.row < 3) if up else (self.row + hops <= 3) & (self.row > 0)

    def start(self):
        self.near.start()
        for up in (True, False):
            pl.when(self.sends(0, up))(lambda: self.copy(0, up).start())

    def arrive(self, hops):
        for up in (True, False):
            mark = self.row - hops if up else self.row + hops

            @pl.when((self.row >= hops) if up else (self.row + hops <= 3))
            def _():
                pltpu.make_async_remote_copy(
                    src_ref=self.src,
                    dst_ref=self.out.at[mark],
                    send_sem=self.send.at[0],
                    recv_sem=self.recv.at[mark],
                    device_id={"row": self.row - 1 if up else self.row + 1},
                    device_id_type=MESH_ID,
                ).wait_recv()

    def pass_on(self, hops):
        self.arrive(hops)
        for up in (True, False):
            pl.when(self.sends(hops, up))(lambda: self.copy(hops, up).start())

    def finish(self):
        self.arrive(3)
        for hops in range(3):
            for up in (True, False):
                pl.when(self.sends(hops, up))(lambda: self.copy(hops, up).wait_send())
        self.near.wait()


def share(source, dest, mark, others, keep, send, recv):
    near = pltpu.make_async_copy(source, dest.at[mark], keep)
    near.start()
    copies = []
    for item, (target, _) in enumerate(others):
        copies.append(
            pltpu.make_async_remote_copy(
                src_ref=source,
                dst_ref=dest.at[mark],
                send_sem=send.at[item],
                recv_sem=recv.at[mark],
                device_id=target,
                device_id_type=MESH_ID,
            )
        )
        copies[item].start()

    def finish():
        near.wait()
        for target, index in others:
            pltpu.make_async_remote_copy(
                src_ref=source,
                dst_ref=dest.at[index],
                send_sem=send.at[0],
                recv_sem=recv.at[index],
                device_id=target,
                device_id_type=MESH_ID,
            ).wait_recv()
        for copy in copies:
            copy.wait_send()

    return finish


def enter_kernel(part_name, *refs):
    sources, outs, scratch = refs[:5], refs[5:12], refs[12:]
    first, second, gains, segs, weight = sources
    first_tok, first_all, second_tok, second_all, gains_all, segs_all, weight_all = outs
    (stage_one, middle_one, stage_two, middle_two, ready_one, ready_two, line_keep, line_send, line_recv, small_keep,
     gain_send, gain_recv, seg_send, seg_recv) = scratch[:14]
    spread_one, spread_two, gather_one, gather_two = (scratch[14 + 3 * index : 17 + 3 * index] for index in range(4))
    team = Team(part_name)
    row = lax.axis_index("row")
    rows = [({"row": lax.rem(row + hop, 4)}, lax.rem(row + hop, 4)) for hop in range(1, 4)]
    meet(team.partners() + [target for target, _ in rows] + [{part_name: team.far}])
    one = Spread(first, stage_one, middle_one, *spread_one)
    two = Spread(second, stage_two, middle_two, *spread_two)
    line = Line(weight, weight_all, line_keep, line_send, line_recv)
    one.start()
    done_gains = share(gains, gains_all, row, rows, small_keep.at[0], gain_send, gain_recv)
    parts = [({part_name: index}, index) for index in (team.across, team.twin, team.far)]
    done_segs = share(segs, segs_all, team.part, parts, small_keep.at[1], seg_send, seg_recv)
    line.start()
    one.turn()
    two.start()
    one.finish()
    done_gains()
    done_segs()
    tokens, width = first.shape[1], first.shape[2]

    def norm(rows, _):
        wides = [stage_one[index, rows, :].astype(F32) for index in range(4)]
        square = sum(jnp.sum(wide * wide, axis=1, keepdims=True) for wide in wides)
        scale = lax.rsqrt(square * (1.0 / (4 * width)) + 1e-05)
        for index in range(4):
            cols = slice(index * width, (index + 1) * width)
            first_tok[rows, cols] = stage_one[index, rows, :]
            ready_one[rows, cols] = (wides[index] * scale * gains_all[index, 0:1, :]).astype(BF16)

    strips(0, tokens, norm)
    two.turn()
    line.pass_on(1)
    gather_phase(team, ready_one, first_all, *gather_one)
    two.finish()

    def join_blocks(rows, _):
        for index in range(4):
            cols = slice(index * width, (index + 1) * width)
            second_tok[rows, cols] = stage_two[index, rows, :]
            ready_two[rows, cols] = stage_two[index, rows, :]

    strips(0, tokens, join_blocks)
    line.pass_on(2)
    gather_phase(team, ready_two, second_all, *gather_two)
    line.finish()


def enter_call(lay, first, second, gains, segs, weight):
    tokens, width = first.shape[0] // 4, first.shape[1]
    wide = 4 * width
    tok, everyone = jax.ShapeDtypeStruct((tokens, wide), BF16), jax.ShapeDtypeStruct((8, tokens, wide), BF16)
    stage = [pltpu.VMEM((4, tokens, width), BF16), pltpu.VMEM((2, tokens, width), BF16)]
    line_sems = [pltpu.SemaphoreType.DMA, pltpu.SemaphoreType.DMA((6,)), pltpu.SemaphoreType.DMA((4,))]
    small_sems = [pltpu.SemaphoreType.DMA((count,)) for count in (2, 3, 4, 3, 4)]
    spread_sems = [pltpu.SemaphoreType.DMA, pltpu.SemaphoreType.DMA((6,)), pltpu.SemaphoreType.DMA((6,))]
    results = pl.pallas_call(
        functools.partial(enter_kernel, lay.part),
        in_specs=[VMEM_SPEC] * 5,
        out_specs=[VMEM_SPEC, HBM_SPEC, VMEM_SPEC, HBM_SPEC, VMEM_SPEC, VMEM_SPEC, HBM_SPEC],
        out_shape=[
            tok,
            everyone,
            tok,
            everyone,
            jax.ShapeDtypeStruct((4,) + gains.shape, gains.dtype),
            jax.ShapeDtypeStruct((4,) + segs.shape, segs.dtype),
            jax.ShapeDtypeStruct((4,) + weight.shape, weight.dtype),
        ],
        scratch_shapes=stage
        + stage
        + [pltpu.VMEM((tokens, wide), BF16)] * 2
        + line_sems
        + small_sems
        + spread_sems
        + spread_sems
        + GATHER_SEMS
        + GATHER_SEMS,
        compiler_params=pltpu.CompilerParams(
            collective_id=lay.fresh_id(), has_side_effects=True, vmem_limit_bytes=60 << 20
        ),
        cost_estimate=pl.CostEstimate(flops=1 << 30, bytes_accessed=400 << 20, transcendentals=0),
        name="enter",
    )(first.reshape(4, tokens, width), second.reshape(4, tokens, width), gains, segs, weight)
    first_tok, first_all, second_tok, second_all, gains, segs, weight = results
    return (
        first_tok, first_all.reshape(-1, wide), second_tok, second_all.reshape(-1, wide), gains, segs, weight,
    )


def strips(start, count, body):
    @pl.loop(0, count // STRIP)
    def _(step):
        body(pl.ds(pl.multiple_of(start + step * STRIP, STRIP), STRIP), pl.ds(pl.multiple_of(step * STRIP, STRIP), STRIP))


class Scatter:
    def __init__(self, team, dots, finish, refs):
        self.team, self.dots, self.finish = team, dots, finish
        self.work, self.twin, self.sent, self.relay, self.final, self.send, self.recv = refs
        self.rows, self.chunk = self.twin.shape[1], self.twin.shape[2] // 4
        self.half = self.rows // 2
        first, second = pl.ds(0, self.half), pl.ds(self.half, self.half)
        sent, relay, final = self.sent, self.relay, self.final
        self.relay_x = self.copy(sent.at[0, first], relay.at[0], 4, team.x)
        self.relay_y = self.copy(sent.at[0, second], relay.at[1], 5, team.y)
        self.x_first = self.copy(sent.at[1, first], final.at[0, first], 6, team.x)
        self.x_second = self.copy(sent.at[1, second], final.at[0, second], 7, team.x)
        self.y_second = self.copy(sent.at[2, second], final.at[1, second], 8, team.y)
        self.y_first = self.copy(sent.at[2, first], final.at[1, first], 9, team.y)

    def copy(self, source, dest, index, target):
        return remote(source, dest, self.send, self.recv, index, target)

    def swap(self, item):
        return self.copy(self.work.at[item, 0], self.twin.at[item], item, self.team.core)

    def total(self, item, start, passed=None):
        def add(rows, local):
            value = self.work[item, 1, rows, :].astype(F32) + self.twin[item, rows, :].astype(F32)
            if passed is not None:
                value = value + self.relay[passed, local, :].astype(F32)
            self.sent[item, rows, :] = value.astype(BF16)

        strips(start, self.half, add)

    def begin(self):
        team = self.team

        @pl.loop(0, 4)
        def _(item):
            @pl.loop(0, 8)
            def _(step):
                which, chunk = step // 4, lax.rem(step, 4)
                base = team.part * which + team.twin * (1 - which)
                slot = lax.rem(base + 2 * (1 - item // 2), 4) * 2 + lax.rem(team.col + 1 + item, 2)
                columns = pl.ds(pl.multiple_of(chunk * self.chunk, self.chunk), self.chunk)
                rows = pl.ds(pl.multiple_of(slot * self.rows, STRIP), self.rows)
                self.work[item, which, :, columns] = self.dots(rows, chunk).astype(BF16)

            self.swap(item).start()

            @pl.when(item == 1)
            def _():
                self.swap(0).wait_recv()
                self.total(0, 0)
                self.relay_x.start()
                self.total(0, self.half)
                self.relay_y.start()

            @pl.when(item == 2)
            def _():
                self.swap(1).wait_recv()
                self.total(1, 0)
                self.x_first.start()

            @pl.when(item == 3)
            def _():
                self.swap(2).wait_recv()
                self.total(2, self.half)
                self.y_second.start()

    def pass_on(self):
        self.relay_y.wait_recv()
        self.total(1, self.half, 1)
        self.x_second.start()
        self.relay_x.wait_recv()
        self.total(2, 0, 0)
        self.y_first.start()

    def last(self, rows, _):
        value = self.work[3, 1, rows, :].astype(F32) + self.twin[3, rows, :].astype(F32)
        self.finish(rows, value + self.final[0, rows, :].astype(F32) + self.final[1, rows, :].astype(F32))

    def conclude(self, between=None):
        self.swap(3).wait_recv()
        self.x_first.wait_recv()
        self.y_first.wait_recv()
        strips(0, self.half, self.last)
        if between:
            between()
        self.x_second.wait_recv()
        self.y_second.wait_recv()
        strips(self.half, self.half, self.last)
        for copy in [self.swap(item) for item in range(4)]:
            copy.wait_send()
        for copy in (self.relay_x, self.relay_y, self.x_first, self.x_second, self.y_second, self.y_first):
            copy.wait_send()


def scatter_scratch(tokens, wide):
    return [
        pltpu.VMEM((4, 2, tokens, wide), BF16),
        pltpu.VMEM((4, tokens, wide), BF16),
        pltpu.VMEM((3, tokens, wide), BF16),
        pltpu.VMEM((2, tokens // 2, wide), BF16),
        pltpu.VMEM((2, tokens, wide), BF16),
        pltpu.SemaphoreType.DMA((10,)),
        pltpu.SemaphoreType.DMA((10,)),
    ]


def whole_rights(rights):
    return [(index, 0, right.shape[1]) for index, right in enumerate(rights)]


def make_dots(lefts, rights, starts):
    def dots(rows, chunk):
        value = 0.0
        for left, (index, start, size) in zip(lefts, starts):
            part = rights[index][chunk, start : start + size, :]
            value = value + lax.dot_general(left[rows, :size], part, NN, preferred_element_type=F32)
        return value

    return dots


def norm_back(value, total, gain, gain_sum):
    scale = lax.rsqrt(jnp.sum(value * value, axis=1, keepdims=True) * (1.0 / value.shape[1]) + 1e-05)
    normed = value * scale
    gain_sum[...] += total * normed
    scaled = total * gain
    inner = jnp.sum(scaled * normed, axis=1, keepdims=True) * (1.0 / value.shape[1])
    return scale * (scaled - normed * inner)


def deal_out(out, rows, value):
    width = value.shape[1] // 4
    for index in range(4):
        out[index, rows, :] = value[:, index * width : (index + 1) * width].astype(BF16)


def fetch(sources, places, sems):
    copies = []
    for index, (source, place) in enumerate(zip(sources, places)):
        if isinstance(source, tuple):
            ref, start = source
            source = ref.at[:, pl.ds(start, place.shape[1]), :]
        copies.append(pltpu.make_async_copy(source, place, sems.at[index]))
        copies[index].start()
    return copies


def fetched(shapes):
    return [pltpu.VMEM(shape, dtype) for shape, dtype in shapes] + [pltpu.SemaphoreType.DMA((len(shapes),))]


def whole(values):
    return values.shape, values.dtype


def mid_kernel(part_name, starts, *refs):
    count = len(starts)
    sources, (out, everyone), scratch = refs[: count + 3], refs[count + 3 : count + 5], refs[count + 5 :]
    places, sems, scratch = scratch[: count + 3], scratch[count + 3], scratch[count + 4 :]
    loads = fetch(sources, places, sems)
    lefts, (right, stored, gain) = places[:count], places[count:]
    ready = scratch[7]
    team = Team(part_name)
    meet(team.partners())
    for load in loads:
        load.wait()

    def finish(rows, total):
        value = stored[rows, :].astype(F32) + total
        out[rows, :] = value
        scale = lax.rsqrt(jnp.sum(value * value, axis=1, keepdims=True) * (1.0 / value.shape[1]) + 1e-05)
        ready[rows, :] = (value * scale * gain[...]).astype(BF16)

    scatter = Scatter(team, make_dots(lefts, [right], [(0, *place) for place in starts]), finish, scratch[:7])
    scatter.begin()
    scatter.pass_on()
    gather = Gather(team, ready, everyone, *scratch[8:])
    scatter.conclude(gather.start_first)
    gather.start_second()
    gather.finish()


def mid_call(lay, lefts, right, starts, stored, gain):
    tokens, wide = stored.shape
    residual, everyone = pl.pallas_call(
        functools.partial(mid_kernel, lay.part, starts),
        in_specs=[HBM_SPEC] * (len(lefts) + 3),
        out_specs=[VMEM_SPEC, HBM_SPEC],
        out_shape=[jax.ShapeDtypeStruct((tokens, wide), F32), jax.ShapeDtypeStruct((8, tokens, wide), BF16)],
        scratch_shapes=fetched([whole(values) for values in (*lefts, right, stored, gain)])
        + scatter_scratch(tokens, wide) + [pltpu.VMEM((tokens, wide), BF16)] + GATHER_SEMS,
        compiler_params=pltpu.CompilerParams(
            collective_id=lay.fresh_id(), has_side_effects=True, vmem_limit_bytes=60 << 20
        ),
        cost_estimate=pl.CostEstimate(flops=1 << 35, bytes_accessed=200 << 20, transcendentals=0),
        name="team_mid",
    )(*lefts, right, stored, gain)
    return residual, everyone.reshape(8 * tokens, wide)


def branch_kernel(part_name, count, *refs):
    total = 2 * count + 3
    sources, (out, everyone, gain_out), scratch = refs[:total], refs[total : total + 3], refs[total + 3 :]
    places, sems, scratch = scratch[:total], scratch[total], scratch[total + 1 :]
    sources = [(ref, 0) if count <= index < 2 * count else ref for index, ref in enumerate(sources)]
    loads = fetch(sources, places, sems)
    lefts, rights, (residual, through, gain) = places[:count], places[count : 2 * count], places[2 * count :]
    gain_sum, ready = scratch[7:9]
    team = Team(part_name)
    meet(team.partners())
    for load in loads:
        load.wait()
    gain_sum[...] = jnp.zeros_like(gain_sum)

    def finish(rows, total):
        value = through[rows, :].astype(F32) + norm_back(residual[rows, :], total, gain[...], gain_sum)
        out[rows, :] = value
        ready[rows, :] = value.astype(BF16)

    scatter = Scatter(team, make_dots(lefts, rights, whole_rights(rights)), finish, scratch[:7])
    scatter.begin()
    scatter.pass_on()
    gather = Gather(team, ready, everyone, *scratch[9:])
    scatter.conclude(gather.start_first)
    gather.start_second()
    gain_out[...] = jnp.sum(gain_sum[...], axis=0, keepdims=True)
    gather.finish()


def branch_call(lay, lefts, rights, residual, through, gain):
    tokens, wide = residual.shape
    width = rights[0].shape[2]
    out, everyone, gain_part = pl.pallas_call(
        functools.partial(branch_kernel, lay.part, len(lefts)),
        in_specs=[HBM_SPEC] * (2 * len(lefts) + 3),
        out_specs=[VMEM_SPEC, HBM_SPEC, VMEM_SPEC],
        out_shape=[
            jax.ShapeDtypeStruct((tokens, wide), F32),
            jax.ShapeDtypeStruct((8, tokens, wide), BF16),
            jax.ShapeDtypeStruct((1, wide), F32),
        ],
        scratch_shapes=fetched(
            [whole(left) for left in lefts]
            + [((4, left.shape[1], width), BF16) for left in lefts]
            + [whole(values) for values in (residual, through, gain)]
        )
        + scatter_scratch(tokens, wide)
        + [pltpu.VMEM((STRIP, wide), F32), pltpu.VMEM((tokens, wide), BF16)]
        + GATHER_SEMS,
        compiler_params=pltpu.CompilerParams(
            collective_id=lay.fresh_id(), has_side_effects=True, vmem_limit_bytes=60 << 20
        ),
        cost_estimate=pl.CostEstimate(flops=1 << 35, bytes_accessed=250 << 20, transcendentals=0),
        name="team_branch",
    )(*lefts, *rights, residual, through, gain)
    return out, everyone.reshape(8 * tokens, wide), gain_part


def finish_kernel(part_name, count, starts, *refs):
    total = 2 * count + len(starts) + 5
    sources, (block_out, input_out, gain_out), scratch = refs[:total], refs[total : total + 3], refs[total + 3 :]
    places, sems, scratch = scratch[:total], scratch[total], scratch[total + 1 :]
    hidden, downs, grads = places[:count], places[count : 2 * count], places[2 * count : -5]
    mix, residual, stored, through, gain = places[-5:]
    downs_from = [(ref, 2 * values.shape[1]) for ref, values in zip(sources[count : 2 * count], hidden)]
    loads = fetch([*sources[:count], *downs_from, *sources[2 * count :]], places, sems)
    gain_sum = scratch[14]
    team = Team(part_name)
    meet(team.partners())
    for load in loads[: 2 * count]:
        load.wait()
    gain_sum[...] = jnp.zeros_like(gain_sum)

    def finish_block(rows, total):
        deal_out(block_out, rows, residual[rows, :] + total)

    def finish_input(rows, total):
        value = norm_back(stored[rows, :].astype(F32), total, gain[...], gain_sum)
        deal_out(input_out, rows, through[rows, :] + value)

    block = Scatter(
        team, make_dots(hidden, downs, whole_rights(downs)), finish_block, scratch[:7]
    )
    inputs = Scatter(team, make_dots(grads, [mix], [(0, *place) for place in starts]), finish_input, scratch[7:14])
    block.begin()
    for load in loads[2 * count :]:
        load.wait()
    inputs.begin()
    block.pass_on()
    inputs.pass_on()
    block.conclude()
    inputs.conclude()
    gain_out[...] = jnp.sum(gain_sum[...], axis=0, keepdims=True)


def finish_call(lay, hidden, stacks, grads, mix, starts, residual, stored, through, gain):
    tokens, wide = residual.shape
    width = stacks[0].shape[2]
    pieces = jax.ShapeDtypeStruct((4, tokens, width), BF16)
    return pl.pallas_call(
        functools.partial(finish_kernel, lay.part, len(hidden), starts),
        in_specs=[HBM_SPEC] * (2 * len(hidden) + len(grads) + 5),
        out_specs=[VMEM_SPEC] * 3,
        out_shape=[pieces, pieces, jax.ShapeDtypeStruct((1, wide), F32)],
        scratch_shapes=fetched(
            [whole(values) for values in hidden]
            + [((4, values.shape[1], width), BF16) for values in hidden]
            + [whole(values) for values in (*grads, mix, residual, stored, through, gain)]
        )
        + scatter_scratch(tokens, wide)
        + scatter_scratch(tokens, wide)
        + [pltpu.VMEM((STRIP, wide), F32)],
        compiler_params=pltpu.CompilerParams(
            collective_id=lay.fresh_id(), has_side_effects=True, vmem_limit_bytes=60 << 20
        ),
        cost_estimate=pl.CostEstimate(flops=1 << 35, bytes_accessed=250 << 20, transcendentals=0),
        name="team_finish",
    )(*hidden, *stacks, *grads, mix, residual, stored, through, gain)


class Deal:
    def __init__(self, src, out, keep, send, recv):
        self.src, self.out, self.keep, self.send, self.recv = src, out, keep, send, recv
        self.row, self.col = lax.axis_index("row"), lax.axis_index("col")
        spot = self.row * 2 + self.col
        self.mark, self.home = lax.rem(spot, 4), spot // 4

    def owner(self, index):
        place = self.col * 4 + index
        return {"row": place // 2, "col": lax.rem(place, 2)}

    def apart(self, index):
        owner = self.owner(index)
        return (owner["row"] != self.row) | (owner["col"] != self.col)

    def greet(self, barrier):
        for index in range(4):

            @pl.when(self.apart(index))
            def _():
                pl.semaphore_signal(barrier, inc=1, device_id=self.owner(index), device_id_type=MESH_ID)

        return 4 - (self.home == self.col).astype(jnp.int32)

    def each(self, act_near, act_far):
        for index in range(4):
            here = (self.row == index) & (self.home == self.col)

            @pl.when(here)
            def _():
                act_near(pltpu.make_async_copy(self.src.at[index], self.out.at[self.mark], self.keep))

            @pl.when(jnp.logical_not(here))
            def _():
                act_far(
                    pltpu.make_async_remote_copy(
                        src_ref=self.src.at[index],
                        dst_ref=self.out.at[self.mark],
                        send_sem=self.send.at[index],
                        recv_sem=self.recv.at[self.mark],
                        device_id={"row": index, "col": self.home},
                        device_id_type=MESH_ID,
                    )
                )

    def start(self):
        self.each(lambda copy: copy.start(), lambda copy: copy.start())

    def finish(self):
        for index in range(4):

            @pl.when(self.apart(index))
            def _():
                pltpu.make_async_remote_copy(
                    src_ref=self.src.at[0],
                    dst_ref=self.out.at[index],
                    send_sem=self.send.at[0],
                    recv_sem=self.recv.at[index],
                    device_id=self.owner(index),
                    device_id_type=MESH_ID,
                ).wait_recv()

        self.each(lambda copy: copy.wait(), lambda copy: copy.wait_send())


DEAL_SEMS = [pltpu.SemaphoreType.DMA, pltpu.SemaphoreType.DMA((4,)), pltpu.SemaphoreType.DMA((4,))]


def leave_kernel(part_name, *refs):
    first, second, block, src, first_out, second_out, blocks, out = refs[:8]
    deals = [Deal(first, first_out, *refs[8:11]), Deal(second, second_out, *refs[11:14])]
    rows_in, summed, near, row_send, row_recv, team_send, team_recv, join_send, join_recv = refs[14:]
    team = Team(part_name)
    row = lax.axis_index("row")
    rows = [({"row": lax.rem(row + hop, 4)}, lax.rem(row + hop, 4)) for hop in range(1, 4)]
    mates = []
    for part in (team.part, team.across, team.twin, team.far):
        for side in (team.col, team.other):
            mates.append(({part_name: part, "col": side}, part * 2 + side))
    mates = mates[1:]
    barrier = pltpu.get_barrier_semaphore()
    for target, _ in rows + mates:
        pl.semaphore_signal(barrier, inc=1, device_id=target, device_id_type=MESH_ID)
    pl.semaphore_wait(barrier, len(rows + mates) + deals[0].greet(barrier))
    own, across = blocks.at[team.part], blocks.at[team.across]
    join_x = remote(block, own, join_send, join_recv, 0, team.x)
    join_core = remote(block, own, join_send, join_recv, 1, team.core)
    join_pass = remote(across, across, join_send, join_recv, 2, team.core)
    join_near = pltpu.make_async_copy(block, own, near.at[2])
    finish_rows = share(src, rows_in, row, rows, near.at[0], row_send, row_recv)
    for copy in (join_x, join_core, join_near):
        copy.start()
    for deal in deals:
        deal.start()
    finish_rows()
    summed[...] = (rows_in[0] + rows_in[1]) + (rows_in[2] + rows_in[3])
    finish_team = share(summed, out, team.part * 2 + team.col, mates, near.at[1], team_send, team_recv)
    join_x.wait_recv()
    join_pass.start()
    for deal in deals:
        deal.finish()
    finish_team()
    join_core.wait_recv()
    join_pass.wait_recv()
    for copy in (join_x, join_core, join_pass):
        copy.wait_send()
    join_near.wait()


def leave_call(lay, first, second, block, small):
    whole_array = jax.ShapeDtypeStruct(first.shape, first.dtype)
    return pl.pallas_call(
        functools.partial(leave_kernel, lay.part),
        in_specs=[VMEM_SPEC] * 4,
        out_specs=[HBM_SPEC, HBM_SPEC, HBM_SPEC, VMEM_SPEC],
        out_shape=[
            whole_array,
            whole_array,
            jax.ShapeDtypeStruct((4,) + block.shape, block.dtype),
            jax.ShapeDtypeStruct((8,) + small.shape, F32),
        ],
        scratch_shapes=DEAL_SEMS
        + DEAL_SEMS
        + [pltpu.VMEM((4,) + small.shape, F32), pltpu.VMEM(small.shape, F32)]
        + [pltpu.SemaphoreType.DMA((count,)) for count in (3, 3, 4, 7, 8, 3, 3)],
        compiler_params=pltpu.CompilerParams(
            collective_id=lay.fresh_id(), has_side_effects=True, vmem_limit_bytes=60 << 20
        ),
        cost_estimate=pl.CostEstimate(flops=1 << 30, bytes_accessed=120 << 20, transcendentals=0),
        name="leave",
    )(first, second, block, small)


def cross(lay, value):
    return lax.ppermute(value, lay.part, [(0, 2), (2, 0), (1, 3), (3, 1)])


def link(lay, value):
    return lax.ppermute(value, lay.part, [(0, 1), (1, 0), (2, 3), (3, 2)])


def part_order(lay):
    part = lax.axis_index(lay.part)
    twin = part + 1 - 2 * (part % 2)
    return jnp.stack([part, (part + 2) % 4, twin, (twin + 2) % 4]).astype(jnp.int32)


def rows_kernel(order, *refs):
    for index, ref in enumerate(refs[:4]):

        @pl.when(pl.program_id(1) == index)
        def _():
            refs[4][...] = ref[...].astype(F32)


def place_rows(order, pieces, start, rows):
    width = pieces[0].shape[1]
    block = rows
    while start % block:
        block //= 2
    steps = rows // block
    return pl.pallas_call(
        rows_kernel,
        grid_spec=pltpu.PrefetchScalarGridSpec(
            num_scalar_prefetch=1,
            grid=(steps, 4),
            in_specs=[pl.BlockSpec((block, width), lambda j, i, order: (start // block + j, 0))] * 4,
            out_specs=pl.BlockSpec((block, width), lambda j, i, order: (order[i] * steps + j, 0)),
        ),
        out_shape=jax.ShapeDtypeStruct((4 * rows, width), F32),
        compiler_params=pltpu.CompilerParams(vmem_limit_bytes=60 << 20),
        name="place_rows",
    )(order, *pieces)


def late_head_kernel(order, *refs):
    for index, ref in enumerate(refs[:4]):

        @pl.when(pl.program_id(0) == index)
        def _():
            refs[4][...] = ref[...].T.astype(F32)


def place_late_head(order, heads, head, pieces):
    features = pieces[0].shape[1]
    return pl.pallas_call(
        late_head_kernel,
        grid_spec=pltpu.PrefetchScalarGridSpec(
            num_scalar_prefetch=1,
            grid=(4,),
            in_specs=[pl.BlockSpec((PER_HEAD, features), lambda i, order: (0, 0))] * 4,
            out_specs=pl.BlockSpec((features, PER_HEAD), lambda i, order: (0, order[i] * heads + head)),
        ),
        out_shape=jax.ShapeDtypeStruct((features, 4 * heads * PER_HEAD), F32),
        compiler_params=pltpu.CompilerParams(vmem_limit_bytes=60 << 20),
        name="place_late_head",
    )(order, *pieces)


def close_kernel(heads, src, tail, _, sums, first, second, out, decay, conv, gain, attn, ffn, rest, first_out,
                 second_out):
    step = pl.program_id(0)
    first_out[...] = first[...]
    second_out[...] = second[...]
    out[...] = src[0].T.astype(F32)
    for part in range(4):

        @pl.when(step == part)
        def _():
            decay[part * 2 * heads : (part + 1) * 2 * heads, :] = tail[0, : 2 * heads, :].astype(F32)

    @pl.when(step == 1)
    def _():
        row, col = lax.axis_index("row"), lax.axis_index("col")
        blocks = conv.shape[1] // 512
        for part in range(4):
            own = sums[2 * part + col]
            for tap in range(TAPS):
                for block in range(blocks):
                    start = (part * blocks + block) * 128
                    conv[tap : tap + 1, start : start + 128] = own[tap * blocks + block : tap * blocks + block + 1]
            rest[part : part + 1, :] = own[REST_ROW : REST_ROW + 1]
        total = sums[0]
        for slot in range(1, 8):
            total = total + sums[slot]
        gain[...] = total[GAIN_ROW:ATTN_ROW]
        for index in range(4):

            @pl.when(row == index)
            def _():
                attn[...] = total[ATTN_ROW + 4 * index : ATTN_ROW + 4 * index + 4]
                ffn[...] = total[FFN_ROW + 4 * index : FFN_ROW + 4 * index + 4]


def close_call(heads, stack, whole_grad, sums, first, second):
    features = stack.shape[2]
    channels = 4 * heads * INNER

    def fixed(*shape):
        return pl.BlockSpec(shape, lambda i: (0,) * len(shape))

    piece = pl.BlockSpec((1,) + first.shape[1:], lambda i: (i, 0, 0))
    return pl.pallas_call(
        functools.partial(close_kernel, heads),
        grid=(4,),
        in_specs=[
            pl.BlockSpec((1, PER_HEAD, features), lambda i: (i, 0, 0)),
            pl.BlockSpec((1, DECAY_ROWS, features), lambda i: (i, PER_HEAD // DECAY_ROWS, 0)),
            HBM_SPEC,
            fixed(*sums.shape),
            piece,
            piece,
        ],
        out_specs=[
            pl.BlockSpec((features, PER_HEAD), lambda i: (0, i * heads)),
            fixed(8 * heads, features),
            fixed(TAPS, channels),
            fixed(DV // 128, 128),
            fixed(4, 128),
            fixed(4, 128),
            fixed(4, 128),
            piece,
            piece,
        ],
        out_shape=[
            jax.ShapeDtypeStruct((features, 4 * heads * PER_HEAD), F32),
            jax.ShapeDtypeStruct((8 * heads, features), F32),
            jax.ShapeDtypeStruct((TAPS, channels), F32),
            jax.ShapeDtypeStruct((DV // 128, 128), F32),
            jax.ShapeDtypeStruct((4, 128), F32),
            jax.ShapeDtypeStruct((4, 128), F32),
            jax.ShapeDtypeStruct((4, 128), F32),
            jax.ShapeDtypeStruct(first.shape, first.dtype),
            jax.ShapeDtypeStruct(second.shape, second.dtype),
        ],
        input_output_aliases={2: 0},
        compiler_params=pltpu.CompilerParams(vmem_limit_bytes=60 << 20),
        name="close",
    )(stack, stack, whole_grad, sums, first, second)


def place_ffn_kernel(counts, order, *refs):
    units = sum(counts)
    blocks = len(counts)
    pairs, downs = refs[: 4 * blocks], refs[4 * blocks : 8 * blocks]
    gate, up, down = refs[8 * blocks : 8 * blocks + 3]
    turned = refs[8 * blocks + 3 :]
    base = 0
    for block, count in enumerate(counts):
        for index in range(4):
            turned[block][order[index]] = pairs[4 * block + index][...].T.astype(F32)
            start = pl.multiple_of(order[index] * units + base, 64)
            down[pl.ds(start, count), :] = downs[4 * block + index][...].astype(F32)
        for part in range(4):
            place = slice(part * units + base, part * units + base + count)
            gate[:, place] = turned[block][part, :, :count]
            up[:, place] = turned[block][part, :, count:]
        base += count


def place_ffn(order, pieces):
    counts = [group[0].shape[0] // 3 for group in pieces]
    flat = [piece for group in pieces for piece in group]
    features, units = flat[0].shape[1], sum(counts)
    wide = jax.ShapeDtypeStruct((features, 4 * units), F32)
    return pl.pallas_call(
        functools.partial(place_ffn_kernel, counts),
        grid_spec=pltpu.PrefetchScalarGridSpec(
            num_scalar_prefetch=1,
            grid=(features // 128,),
            in_specs=[pl.BlockSpec((2 * (p.shape[0] // 3), 128), lambda i, order: (0, i)) for p in flat]
            + [pl.BlockSpec((p.shape[0] // 3, 128), lambda i, order: (2, i)) for p in flat],
            out_specs=[
                pl.BlockSpec((128, 4 * units), lambda i, order: (i, 0)),
                pl.BlockSpec((128, 4 * units), lambda i, order: (i, 0)),
                pl.BlockSpec((4 * units, 128), lambda i, order: (0, i)),
            ],
            scratch_shapes=[pltpu.VMEM((4, 128, 2 * count), F32) for count in counts],
        ),
        out_shape=[wide, wide, jax.ShapeDtypeStruct((4 * units, features), F32)],
        compiler_params=pltpu.CompilerParams(vmem_limit_bytes=60 << 20),
        cost_estimate=pl.CostEstimate(flops=1 << 30, bytes_accessed=30 << 20, transcendentals=0),
        name="place_ffn",
    )(order, *flat, *flat)


def stack_kernel(counts, *refs):
    grads, values, out = refs[: len(counts)], refs[len(counts) : -1], refs[-1]
    base = 0
    for grad, value, count in zip(grads, values, counts):
        for start in range(0, count, 256):
            size = min(256, grad.shape[1] - start)
            part = lax.dot_general(grad[:, start : start + size], value[...], TN, preferred_element_type=F32)
            size = min(size, count - start)
            out[0, base + start : base + start + size, :] = part[:size].astype(BF16)
        base += count


def stack_call(rows_n, pairs, counts):
    tokens, wide = pairs[0][1].shape
    width = wide // rows_n
    total = sum(counts)
    flops = 2 * tokens * wide * sum(grad.shape[1] for grad, _ in pairs)
    return pl.pallas_call(
        functools.partial(stack_kernel, counts),
        grid=(rows_n,),
        in_specs=[
            pl.BlockSpec(grad.shape, lambda i: (0, 0), pipeline_mode=pl.Buffered(1)) for grad, _ in pairs
        ]
        + [pl.BlockSpec((tokens, width), lambda i: (0, i)) for _ in pairs],
        out_specs=pl.BlockSpec((1, total, width), lambda i: (i, 0, 0)),
        out_shape=jax.ShapeDtypeStruct((rows_n, total, width), BF16),
        compiler_params=pltpu.CompilerParams(vmem_limit_bytes=60 << 20),
        cost_estimate=pl.CostEstimate(flops=flops, bytes_accessed=40 << 20, transcendentals=0),
        name="weight_grads",
    )(*[grad for grad, _ in pairs], *[value for _, value in pairs])


def units_kernel(part_name, cuts, gate, up, down, *outs):
    part, units = lax.axis_index(part_name), cuts[-1]
    for index in range(gate.shape[1] // units):

        @pl.when(part == index)
        def _():
            base = index * units
            for which, ref in enumerate((gate, up)):
                turned = ref[:, base : base + units].T
                for out, start, end in zip(outs, cuts[:-1], cuts[1:]):
                    out[which * (end - start) : (which + 1) * (end - start), :] = turned[start:end]
            for out, start, end in zip(outs, cuts[:-1], cuts[1:]):
                out[2 * (end - start) :, :] = down[base + start : base + end, :]


def units_call(lay, cuts, gate, up, down):
    features, wide = gate.shape
    rows = [3 * (end - start) for start, end in zip(cuts[:-1], cuts[1:])]
    return pl.pallas_call(
        functools.partial(units_kernel, lay.part, cuts),
        grid=(features // 128,),
        in_specs=[pl.BlockSpec((128, wide), lambda i: (i, 0))] * 2 + [pl.BlockSpec((wide, 128), lambda i: (0, i))],
        out_specs=[pl.BlockSpec((count, 128), lambda i: (0, i)) for count in rows],
        out_shape=[jax.ShapeDtypeStruct((count, features), BF16) for count in rows],
        compiler_params=pltpu.CompilerParams(vmem_limit_bytes=60 << 20),
        name="own_units",
    )(gate, up, down)


def own_mix_kernel(heads, ways, part, mix, decay, out):
    turned = mix[...].T
    out[:PER_HEAD, :] = turned[:PER_HEAD]
    if heads > 1:
        out[PER_HEAD + DECAY_ROWS :, :] = turned[PER_HEAD:]
    small = decay[...].astype(F32).T
    empty = jnp.zeros((DECAY_ROWS - 2 * heads, small.shape[1]), F32)
    for index in range(ways):

        @pl.when(part[0] == index)
        def _():
            rows = small[index * 2 * heads : (index + 1) * 2 * heads]
            out[PER_HEAD : PER_HEAD + DECAY_ROWS, :] = jnp.concatenate([rows, empty]).astype(BF16)


def own_mix_call(lay, heads, mix, decay):
    features = mix.shape[0]
    rows = heads * PER_HEAD + DECAY_ROWS
    part = lax.axis_index(lay.part).astype(jnp.int32).reshape(1)
    return pl.pallas_call(
        functools.partial(own_mix_kernel, heads, lay.ways),
        grid_spec=pltpu.PrefetchScalarGridSpec(
            num_scalar_prefetch=1,
            grid=(features // 128,),
            in_specs=[
                pl.BlockSpec((128, heads * PER_HEAD), lambda i, part: (i, part[0])),
                pl.BlockSpec((128, decay.shape[1]), lambda i, part: (i, 0)),
            ],
            out_specs=pl.BlockSpec((rows, 128), lambda i, part: (0, i)),
        ),
        out_shape=jax.ShapeDtypeStruct((rows, features), BF16),
        compiler_params=pltpu.CompilerParams(vmem_limit_bytes=60 << 20),
        name="own_mix",
    )(part, mix, decay)


def ffn_kernel(values, grads, stack, hidden, both_grad):
    units, width = hidden.shape[1], stack.shape[2]
    both, grad = 0.0, 0.0
    for index in range(stack.shape[0]):
        cols = slice(index * width, (index + 1) * width)
        both = both + lax.dot_general(
            values[:, cols], stack[index, : 2 * units, :], NT, preferred_element_type=F32
        )
        grad = grad + lax.dot_general(grads[:, cols], stack[index, 2 * units :, :], NT, preferred_element_type=F32)
    gate, up = both[:, :units], both[:, units:]
    sig = sigmoid(gate)
    act = gate * sig
    hidden[...] = (act * up).astype(BF16)
    both_grad[:, :units] = (grad * up * (sig + act * (1.0 - sig))).astype(BF16)
    both_grad[:, units:] = (grad * act).astype(BF16)


def ffn_call(values, grads, stack):
    tokens, width = values.shape
    units = stack.shape[1] // 3
    block = 256
    while tokens % block:
        block //= 2
    row = pl.BlockSpec((block, width), lambda i: (i, 0))
    return pl.pallas_call(
        ffn_kernel,
        grid=(tokens // block,),
        in_specs=[row, row, pl.BlockSpec(stack.shape, lambda i: (0, 0, 0))],
        out_specs=[
            pl.BlockSpec((block, units), lambda i: (i, 0)),
            pl.BlockSpec((block, 2 * units), lambda i: (i, 0)),
        ],
        out_shape=[
            jax.ShapeDtypeStruct((tokens, units), BF16),
            jax.ShapeDtypeStruct((tokens, 2 * units), BF16),
        ],
        compiler_params=pltpu.CompilerParams(vmem_limit_bytes=60 << 20),
        cost_estimate=pl.CostEstimate(
            flops=6 * tokens * width * units, bytes_accessed=30 << 20, transcendentals=tokens * units
        ),
        name="ffn",
    )(values, grads, stack)


SEQ = 448


def project(left, right):
    return jnp.dot(left, right, preferred_element_type=F32)


def project_back(left, right):
    return lax.dot_general(left, right, NT, preferred_element_type=F32)


def weight_grads(lay, *pairs):
    if lay.native:
        return stack_call(lay.rows, [pair[:2] for pair in pairs], [count for _, _, count in pairs])
    stacks = []
    for grad, value, count in pairs:
        whole = lax.dot_general(grad, value, TN, preferred_element_type=F32)[:count].astype(BF16)
        stacks.append(jnp.moveaxis(whole.reshape(count, lay.rows, -1), 1, 0))
    return jnp.concatenate(stacks, axis=1)


def after(value, *others):
    return lax.optimization_barrier((value,) + others)[0]


class Plan:
    def __init__(self, mesh, heads):
        dp, self.rows, self.cols = (mesh.shape[name] for name in ("dp", "row", "col"))
        ways = dp
        while dp % ways or (heads // self.cols) % ways:
            ways -= 1
        self.ways = ways
        if ways == dp:
            self.mesh, self.shared, self.part = mesh, (), "dp"
        else:
            devices = mesh.devices.reshape(dp // ways, ways, self.rows, self.cols)
            self.mesh = Mesh(devices, ("group", "part", "row", "col"))
            self.shared, self.part = ("group",), "part"
        self.data = self.shared + (self.part,)
        self.team = (self.part, "col")
        self.native = (ways, self.rows, self.cols) == (4, 4, 2) and heads == 2 * ways * self.cols
        self.next_id = 0

    def fresh_id(self):
        self.next_id += 1
        return self.next_id


def spread(lay, values):
    local = values.shape[0]
    whole = lax.all_gather(values, "col", axis=0, tiled=True)
    whole = lax.all_to_all(whole, "row", split_axis=0, concat_axis=1, tiled=True)
    mine = local // lay.rows
    return lax.dynamic_slice_in_dim(whole, lax.axis_index("col") * mine, mine, 0)


def unspread(lay, value):
    local = value.shape[0] * lay.rows
    whole = lax.all_gather(value, "col", axis=0, tiled=True)
    whole = lax.all_to_all(whole, "row", split_axis=1, concat_axis=0, tiled=True)
    return lax.dynamic_slice_in_dim(whole, lax.axis_index("col") * local, local, 0)


def team_gather(lay, values):
    return lax.all_gather(values, lay.team, axis=0, tiled=True)


def team_scatter(lay, values):
    return lax.psum_scatter(values.astype(BF16), lay.team, scatter_dimension=0, tiled=True).astype(F32)


def norm_forward(values):
    scale = lax.rsqrt(jnp.mean(values * values, axis=1, keepdims=True) + 1e-05)
    return values * scale, scale


def norm_backward(grad, values, gain):
    normed, scale = norm_forward(values)
    scaled = grad * gain
    inner = jnp.mean(scaled * normed, axis=1, keepdims=True)
    return scale * (scaled - normed * inner), jnp.sum(grad * normed, axis=0, keepdims=True)


def enter(lay, values, grads, gains, segments, weight):
    if lay.native:
        return enter_call(lay, values, grads, gains, segments, weight)
    mine, grads = spread(lay, values), spread(lay, grads)
    gains, weight = (lax.all_gather(value, "row", axis=0, tiled=False) for value in (gains, weight))
    segments = lax.all_gather(segments, lay.part, axis=0, tiled=False)
    normed, _ = norm_forward(mine.astype(F32))
    everyone = team_gather(lay, (normed * gains[:, 0].reshape(1, -1)).astype(BF16))
    return mine, everyone, grads, team_gather(lay, grads), gains, segments, weight


def beside(stack, start, size):
    return jnp.moveaxis(stack[:, start : start + size], 0, 1).reshape(size, -1)


def own_mix(lay, heads, mix, decay):
    if lay.native:
        return own_mix_call(lay, heads, mix, decay)
    part = lax.axis_index(lay.part)
    mix = lax.dynamic_slice_in_dim(mix, part * heads * PER_HEAD, heads * PER_HEAD, 1).T
    decay = lax.dynamic_slice_in_dim(decay, part * 2 * heads, 2 * heads, 1).T
    decay = jnp.pad(decay, ((0, DECAY_ROWS - 2 * heads), (0, 0)))
    return jnp.concatenate([mix[:PER_HEAD], decay, mix[PER_HEAD:]], axis=0)


def own_units(lay, cuts, gate, up, down):
    if lay.native:
        return units_call(lay, cuts, gate, up, down)
    start, size = lax.axis_index(lay.part) * cuts[-1], cuts[-1]
    gate, up = (lax.dynamic_slice_in_dim(values, start, size, 1).T for values in (gate, up))
    down = lax.dynamic_slice_in_dim(down, start, size, 0)
    return [
        jnp.concatenate([values[first:last] for values in (gate, up, down)], axis=0)
        for first, last in zip(cuts[:-1], cuts[1:])
    ]


def mid_step(lay, mixed, out_all, stored, gain):
    starts = [head * DV for head in range(len(mixed))]
    if lay.native:
        return mid_call(lay, mixed, out_all, [(start, DV) for start in starts], stored, gain)
    total = sum(project(left, beside(out_all, start, DV)) for left, start in zip(mixed, starts))
    residual = stored.astype(F32) + team_scatter(lay, total)
    normed, _ = norm_forward(residual)
    return residual, team_gather(lay, (normed * gain).astype(BF16))


def feed_forward(lay, values, grads, stack):
    if lay.native:
        return ffn_call(values, grads, stack)
    units = stack.shape[1] // 3
    gate, up = (project_back(values, beside(stack, start, units)) for start in (0, units))
    sig = jax.nn.sigmoid(gate)
    grad = project_back(grads, beside(stack, 2 * units, units))
    grad_gate = grad * up * sig * (1.0 + gate * (1.0 - sig))
    both = jnp.concatenate([grad_gate.astype(BF16), (grad * gate * sig).astype(BF16)], axis=1)
    return (gate * sig * up).astype(BF16), both


def branch_step(lay, lefts, stacks, residual, out_grads, gain):
    if lay.native:
        return branch_call(lay, lefts, stacks, residual, out_grads, gain)
    total = sum(project(left, beside(stack, 0, left.shape[1])) for left, stack in zip(lefts, stacks))
    grad, gain_part = norm_backward(team_scatter(lay, total), residual, gain)
    grad = out_grads.astype(F32) + grad
    return grad, team_gather(lay, grad.astype(BF16)), gain_part


def finish_step(lay, hidden, stacks, grads, mix, places, residual, stored, grad_residual, gain):
    if lay.native:
        return finish_call(lay, hidden, stacks, grads, mix, places, residual, stored, grad_residual, gain)
    total = sum(
        project(left, beside(stack, 2 * left.shape[1], left.shape[1])) for left, stack in zip(hidden, stacks)
    )
    block_output = (residual + team_scatter(lay, total)).astype(BF16)
    total = sum(project(left[:, :size], beside(mix, start, size)) for left, (start, size) in zip(grads, places))
    grad, gain_part = norm_backward(team_scatter(lay, total), stored.astype(F32), gain)
    return block_output, (grad_residual + grad).astype(BF16), gain_part


def columns(stack):
    return jnp.moveaxis(stack, 2, 0).reshape(stack.shape[2], -1).astype(F32)


def on_device(
    lay,
    block_input,
    segment_ids,
    attn_gain,
    mix_weight,
    decay_weight,
    conv_weight,
    decay_log,
    decay_bias,
    out_gain,
    out_weight,
    ffn_gain,
    gate_weight,
    up_weight,
    down_weight,
    cotangent,
):
    part = lax.axis_index(lay.part)
    heads = decay_log.shape[0] // lay.ways
    units = gate_weight.shape[1] // lay.ways
    width = mix_weight.shape[0]

    def mine(values, dim, size):
        return lax.dynamic_slice_in_dim(values, part * size, size, dim)

    def gather_rows(values):
        return lax.all_gather(values, "row", axis=0, tiled=False)

    places = [(0, PER_HEAD + DECAY_ROWS)]
    for head in range(1, heads):
        places.append((sum(places[-1]), PER_HEAD))
    mix_mine = own_mix(lay, heads, mix_weight, decay_weight)
    out_all = gather_rows(mine(out_weight, 0, heads * DV))
    cuts = [0, min(units, 320), units]
    unit_blocks = own_units(lay, cuts, gate_weight, up_weight, down_weight)
    conv_mine = mine(conv_weight, 1, heads * INNER)
    log_mine, bias_mine = mine(decay_log, 0, heads), mine(decay_bias, 0, heads)

    gains = jnp.stack([attn_gain, ffn_gain])
    stored, attn_all, out_grads, out_grads_all, gains, segments, mix_all = enter(
        lay, block_input, cotangent, gains, segment_ids.reshape(1, -1), after(mix_mine, *unit_blocks)
    )
    gain_one, gain_two = gains[:, 0].reshape(1, -1), gains[:, 1].reshape(1, -1)
    seg_row = segments.reshape(-1, 1, SEQ)
    waiting = lax.optimization_barrier((*unit_blocks, attn_all))[:-1]
    stacks = [gather_rows(values) for values in waiting]
    tokens = attn_all.shape[0]
    shared = (seg_row, conv_mine, log_mine, bias_mine, out_gain.reshape(1, -1))
    mixed, solves, projs, extra = [], [], [], None
    for head in range(heads):
        values, solve, proj, *made = mixer_forward(
            head, places[head][0], after(attn_all, *mixed), mix_all, extra, *shared
        )
        extra = made[0] if made else extra
        mixed.append(values)
        solves.append(solve)
        projs.append(proj)
    residual, ffn_all = mid_step(lay, mixed, out_all, stored, gain_two)

    def sum_rows(grads):
        grads = lax.psum_scatter(grads, "row", scatter_dimension=0, tiled=False)
        return lax.psum(grads, lay.shared) if lay.shared else grads

    hidden, grad_both, ffn_grads = [], [], []
    for stack in stacks:
        values, grads = feed_forward(lay, ffn_all, out_grads_all, stack)
        count = values.shape[1]
        ffn_part = weight_grads(lay, (grads, ffn_all, 2 * count), (values, out_grads_all, count))
        ffn_all, values, grads = lax.optimization_barrier((ffn_all, values, grads, ffn_part))[:3]
        hidden.append(values)
        grad_both.append(grads)
        ffn_grads.append(sum_rows(ffn_part))
    grad_residual, branch_all, ffn_gain_part = branch_step(lay, grad_both, stacks, residual, out_grads, gain_two)

    branch = branch_all
    if lay.native:
        branch = after(branch, ffn_grads[0])
        crossed = [cross(lay, grads) for grads in ffn_grads]
    other = jnp.zeros((tokens, 128), BF16)
    proj_grads, mix_grads, conv_parts, small_parts = [], [], [], []
    for head in reversed(range(heads)):
        common = (head, projs[head], extra, *shared, solves[head], branch, out_all)
        if head:
            grad, passed, conv_part, small_part = mixer_backward(*common, None)
            if lay.native:
                grad = after(grad, crossed[0])
            other = other + passed
        else:
            grad, conv_part, small_part = mixer_backward(*common, other)
            if lay.native:
                grad = after(grad, *crossed)
        triples = [(grad, attn_all, PER_HEAD if head else PER_HEAD + DECAY_ROWS)]
        if head == heads - 1:
            triples += [(values, branch_all, DV) for values in mixed]
        mix_part = weight_grads(lay, *triples)
        branch, grad = lax.optimization_barrier((branch, grad, mix_part))[:2]
        if lay.native:
            branch = after(branch, *ffn_grads[1:])
        proj_grads.insert(0, grad)
        conv_parts.insert(0, conv_part.sum(0))
        small_parts.insert(0, small_part.sum(0)[0])
        mix_grads.insert(0, sum_rows(mix_part))
    if lay.native:
        ffn_pieces = [[ffn_grads[0], crossed[0], link(lay, ffn_grads[0]), link(lay, crossed[0])]]
        hidden[0] = after(hidden[0], *ffn_pieces[0])
    block_output, input_grad, attn_gain_part = finish_step(
        lay, hidden, stacks, proj_grads, mix_all, places, residual, stored, grad_residual, gain_one
    )

    conv_part = jnp.concatenate(conv_parts, axis=1)
    rest_part = jnp.concatenate([part_of[DV + item : DV + item + 1] for item in range(2) for part_of in small_parts])
    gain_part = sum(part_of[:DV] for part_of in small_parts)
    row, col = lax.axis_index("row"), lax.axis_index("col")
    if lay.native:
        lines = [conv_part, gain_part, attn_gain_part, ffn_gain_part, jnp.pad(rest_part, (0, 128 - rest_part.size))]
        flat = jnp.concatenate([values.reshape(-1, 128) for values in lines])
        flat = jnp.pad(flat, ((0, SMALL_ROWS - flat.shape[0]), (0, 0)))
        order = part_order(lay)
        for grads, passed in zip(ffn_grads[1:], crossed[1:]):
            ffn_pieces.append([grads, passed, link(lay, grads), link(lay, passed)])
        late = after(mix_grads[1], block_output)
        late_passed = cross(lay, late)
        ffn_pieces[0][0] = after(ffn_pieces[0][0], block_output)
        gate_grad, up_grad, down_weight_grad = place_ffn(order, ffn_pieces)
        passed = after(late_passed, gate_grad)
        late_pieces = [late, passed, link(lay, late), link(lay, passed)]
        out_weight_grad = place_rows(order, late_pieces, PER_HEAD, heads * DV)
        mix_grad = place_late_head(order, heads, 1, late_pieces)
        first = after(mix_grads[0], mix_grad)
        flat = after(flat, mix_grad, out_weight_grad)
        block_output, input_grad, first_stack, sums = leave_call(lay, block_output, input_grad, first, flat)
        mix_grad, decay_grad, conv_grad, gain_sum, attn_sum, ffn_sum, rest, block_output, input_grad = close_call(
            heads, first_stack, mix_grad, sums, block_output, input_grad
        )
        block_output, input_grad = (value.reshape(-1, value.shape[2]) for value in (block_output, input_grad))
        decay_grad, gain_sum = decay_grad.T, gain_sum.reshape(-1)
        attn_gain_grad, ffn_gain_grad = attn_sum.reshape(-1), ffn_sum.reshape(-1)
        log_grad, bias_grad = rest[:, :heads].reshape(-1), rest[:, heads : 2 * heads].reshape(-1)
    else:
        block_output, input_grad = unspread(lay, block_output), unspread(lay, input_grad)
        own = jnp.concatenate([conv_part.reshape(-1), rest_part])
        pick = (jnp.arange(lay.ways * lay.cols) == part * lay.cols + col).astype(F32)[:, None]
        sums, gain_sum, ffn_sum, attn_sum = lax.psum(
            (pick * own[None, :], gain_part, ffn_gain_part[0], attn_gain_part[0]), lay.data + ("row", "col")
        )
        sums = lax.dynamic_index_in_dim(sums.reshape(lay.ways, lay.cols, -1), col, 1, keepdims=False)
        split = conv_part.size
        conv_grad = jnp.moveaxis(sums[:, :split].reshape(lay.ways, TAPS, -1), 0, 1).reshape(TAPS, -1)
        log_grad = sums[:, split : split + heads].reshape(-1)
        bias_grad = sums[:, split + heads :].reshape(-1)
        attn_gain_grad = lax.dynamic_slice_in_dim(attn_sum, row * width, width, 0)
        ffn_gain_grad = lax.dynamic_slice_in_dim(ffn_sum, row * width, width, 0)

    out_start = PER_HEAD if heads > 1 else PER_HEAD + DECAY_ROWS
    if not lay.native:
        mix_stacks = [lax.all_gather(value, lay.part, axis=0, tiled=False) for value in mix_grads]
        ffn_stacks = [lax.all_gather(value, lay.part, axis=0, tiled=False) for value in ffn_grads]
        decay_grad = columns(mix_stacks[0][:, PER_HEAD : PER_HEAD + 2 * heads])
        mix_grad = columns(jnp.concatenate([stack[:, :PER_HEAD] for stack in mix_stacks], axis=1))
        gate_grad, up_grad, down_weight_grad = (
            jnp.concatenate([jnp.split(stack, 3, axis=1)[item] for stack in ffn_stacks], axis=1) for item in range(3)
        )
        gate_grad, up_grad = columns(gate_grad), columns(up_grad)
        down_weight_grad = down_weight_grad.reshape(-1, width).astype(F32)
        out_weight_grad = mix_stacks[-1][:, out_start : out_start + heads * DV].reshape(-1, width).astype(F32)
    return (
        block_output,
        input_grad,
        attn_gain_grad,
        mix_grad,
        decay_grad,
        conv_grad,
        log_grad,
        bias_grad,
        gain_sum,
        out_weight_grad,
        ffn_gain_grad,
        gate_grad,
        up_grad,
        down_weight_grad,
    )


def solution(mesh):
    def run(*args):
        lay = Plan(mesh, args[6].shape[0])
        tokens, grid = P(lay.data + ("col",), "row"), P("row", "col")
        turned, features, inner = P("col", "row"), P("row"), P("col")
        conv = P(None, "col")
        return jax.shard_map(
            functools.partial(on_device, lay),
            mesh=lay.mesh,
            in_specs=(
                tokens, P(lay.data + ("row",)), features, grid, grid, conv, inner, inner, P(),
                turned, features, grid, grid, turned, tokens,
            ),
            out_specs=(
                tokens, tokens, features, grid, grid, conv, inner, inner, P(),
                turned, features, grid, grid, turned,
            ),
            check_vma=False,
        )(*args)

    return run
```

```python
import functools
import jax
import jax.numpy as jnp
from jax import lax
from jax.experimental import pallas as pl
from jax.experimental.pallas import tpu as pltpu
from jax.sharding import Mesh
from jax.sharding import PartitionSpec as P

F32, BF16 = jnp.float32, jnp.bfloat16
DK, DV, TAPS = 128, 256, 4
DECAY_ROWS = 16
INNER = 2 * DK + DV
PER_HEAD = INNER + DV
NN = (((1,), (0,)), ((), ()))
NT = (((1,), (1,)), ((), ()))
TN = (((0,), (0,)), ((), ()))


def mm(left, right, dims=NN):
    return lax.dot_general(left.astype(BF16), right.astype(BF16), dims, preferred_element_type=F32)


def sigmoid(values):
    return 1.0 / (1.0 + jnp.exp(-values))


def softplus(values):
    return jnp.maximum(values, 0.0) + jnp.log1p(jnp.exp(-jnp.abs(values)))


def shift_down(values, lag):
    return jnp.concatenate([jnp.zeros_like(values[:lag]), values[: values.shape[0] - lag]], axis=0)


def shift_up(values, lag):
    return jnp.concatenate([values[lag:], jnp.zeros_like(values[:lag])], axis=0)


def cumsum_rows(values):
    step = 1
    while step < values.shape[0]:
        values = values + shift_down(values, step)
        step *= 2
    return values


def reverse_cumsum_rows(values):
    step = 1
    while step < values.shape[0]:
        values = values + shift_up(values, step)
        step *= 2
    return values


def prepare(head, proj, extra, seg_row, conv, log_ref, bias_ref):
    length = proj.shape[0]
    seg_row = seg_row.astype(F32)
    rows = lax.broadcasted_iota(jnp.int32, (length, length), 0)
    cols = lax.broadcasted_iota(jnp.int32, (length, length), 1)
    seg_col = jnp.sum(jnp.where(rows == cols, seg_row, 0.0), axis=1, keepdims=True)
    summed = conv[TAPS - 1 : TAPS] * proj[:, :INNER]
    keeps = []
    for lag in range(1, TAPS):
        keep = (shift_down(seg_col + 1.0, lag) == seg_col + 1.0).astype(F32)
        keeps.append(keep)
        summed = summed + conv[TAPS - 1 - lag : TAPS - lag] * (shift_down(proj[:, :INNER], lag) * keep)
    gate_conv = sigmoid(summed)
    active = summed * gate_conv
    lane = lax.broadcasted_iota(jnp.int32, extra.shape, 1)
    write = jnp.sum(jnp.where(lane == 2 * head, extra, 0.0), axis=1, keepdims=True)
    drive = jnp.sum(jnp.where(lane == 2 * head + 1, extra, 0.0), axis=1, keepdims=True)
    beta = sigmoid(write)
    drive = drive + bias_ref[head]
    rate = jnp.exp(jnp.full((1, 1), log_ref[head], F32))
    decay = -rate * softplus(drive)
    total = cumsum_rows(decay)
    total_row = jnp.sum(jnp.where(rows == cols, total, 0.0), axis=0, keepdims=True)
    weight = jnp.exp(jnp.where((rows >= cols) & (seg_col == seg_row), total - total_row, -1e30))
    raw_q, raw_k, value = active[:, :DK], active[:, DK : 2 * DK], active[:, 2 * DK :]
    scale_q = lax.rsqrt(jnp.sum(raw_q * raw_q, axis=1, keepdims=True) + 1e-06)
    scale_k = lax.rsqrt(jnp.sum(raw_k * raw_k, axis=1, keepdims=True) + 1e-06)
    query = (raw_q * scale_q * DK ** (-0.5)).astype(BF16)
    key = (raw_k * scale_k).astype(BF16)
    inner = mm(key, key, NT)
    strict = jnp.where(rows > cols, weight, 0.0)
    return dict(
        summed=summed, keeps=keeps, gate_conv=gate_conv, raw_q=raw_q, raw_k=raw_k, value=value,
        scale_q=scale_q, scale_k=scale_k, query=query, key=key, inner=inner, weight=weight,
        strict=strict, beta=beta, drive=drive, rate=rate, decay=decay, rows=rows, cols=cols,
    )


def forward_kernel(head, start, *refs):
    if head:
        (attn_ref, stack_ref, extra_ref, segr_ref, conv_ref, log_ref, bias_ref, gain_ref, mixed_ref, solve_ref,
         proj_ref, work) = refs
    else:
        (attn_ref, stack_ref, segr_ref, conv_ref, log_ref, bias_ref, gain_ref, mixed_ref, solve_ref, proj_ref,
         extra_ref, work) = refs
    count, size = work.shape[:2]
    length, width = proj_ref.shape[0] // count, stack_ref.shape[2]
    spans = [slice(item * length, (item + 1) * length) for item in range(count)]
    tile = min(128, size)
    starts = range(0, size, tile)
    r = lax.broadcasted_iota(jnp.int32, (tile, tile), 0)
    c = lax.broadcasted_iota(jnp.int32, (tile, tile), 1)
    eye = (r == c).astype(F32)
    ready, parts = [], []

    def product(span, first, rows):
        value = 0.0
        for index in range(stack_ref.shape[0]):
            left = attn_ref[span, index * width : (index + 1) * width]
            value = value + mm(left, stack_ref[index, first : first + rows, :], NT)
        return value

    for span in spans:
        proj_ref[span, :] = product(span, start, PER_HEAD)
        if not head:
            extra_ref[span, :] = product(span, start + PER_HEAD, DECAY_ROWS)
    for item, span in enumerate(spans):
        p = prepare(
            head, proj_ref[span, :], extra_ref[span, :], segr_ref[item], conv_ref[...], log_ref, bias_ref
        )
        if size != length:
            work[item] = jnp.zeros(work.shape[1:], F32)
        work[item, 0:length, 0:length] = p["beta"] * p["strict"] * p["inner"]
        scores = (mm(p["query"], p["key"], NT) * p["weight"]).astype(BF16)
        ready.append((scores, (p["beta"] * p["value"]).astype(BF16)))
        parts += [work[item, start : start + tile, start : start + tile] for start in starts]
    inv = [eye - jnp.where((r // 2 == c // 2), part, 0.0) for part in parts]
    step = 2
    while step < tile:
        pick = (r // (2 * step) == c // (2 * step)) & (r // step != c // step)
        lows = [mm(jnp.where(pick, part, 0.0), x) for part, x in zip(parts, inv)]
        inv = [x - mm(x, low) for x, low in zip(inv, lows)]
        step *= 2
    for index, values in enumerate(inv):
        item, start = index // len(starts), starts[index % len(starts)]
        work[item, start : start + tile, start : start + tile] = values
    step = tile
    while step < size:
        places = [(item, start) for item in range(count) for start in range(0, size, 2 * step)]
        lows = [
            mm(work[item, start + step : start + 2 * step, start : start + step],
               work[item, start : start + step, start : start + step])
            for item, start in places
        ]
        for (item, start), low in zip(places, lows):
            mid, end = start + step, start + 2 * step
            work[item, mid:end, start:mid] = -mm(work[item, mid:end, mid:end], low)
        step *= 2
    for item, span in enumerate(spans):
        solve = work[item, 0:length, 0:length].astype(BF16)
        solve_ref[item] = solve
        scores, target = ready[item]
        out = mm(scores, mm(solve, target))
        scale = lax.rsqrt(jnp.sum(out * out, axis=1, keepdims=True) * (1.0 / DV) + 1e-05)
        gate = proj_ref[span, INNER:]
        mixed_ref[span, :] = (out * scale * gain_ref[...] * (gate * sigmoid(gate))).astype(BF16)


def backward_kernel(head, last, *refs):
    if last:
        (proj_ref, extra_ref, segr_ref, conv_ref, log_ref, bias_ref, gain_ref, solve_ref, grad_ref,
         turn_ref, other_ref, gproj_ref, gconv_ref, gsmall_ref) = refs
    else:
        (proj_ref, extra_ref, segr_ref, conv_ref, log_ref, bias_ref, gain_ref, solve_ref, grad_ref,
         turn_ref, gproj_ref, gextra_ref, gconv_ref, gsmall_ref) = refs
    conv = conv_ref[...]
    p = prepare(head, proj_ref[...], extra_ref[...], segr_ref[0], conv, log_ref, bias_ref)
    weight, strict, inner, beta, value = p["weight"], p["strict"], p["inner"], p["beta"], p["value"]
    query, key = p["query"], p["key"]
    solve = solve_ref[0]
    fresh = mm(solve, beta * value).astype(BF16)
    scores = mm(query, key, NT)
    probs = (scores * weight).astype(BF16)
    out = mm(probs, fresh)
    scale = lax.rsqrt(jnp.sum(out * out, axis=1, keepdims=True) * (1.0 / DV) + 1e-05)
    normed = out * scale
    gate = proj_ref[:, INNER:]
    gate_sig = sigmoid(gate)
    grad, width = 0.0, turn_ref.shape[2]
    for index in range(turn_ref.shape[0]):
        grad = grad + mm(grad_ref[:, index * width : (index + 1) * width], turn_ref[index], NT)
    gain = gain_ref[...]
    through = grad * normed
    ggate = through * gain * (gate_sig * (1.0 + gate * (1.0 - gate_sig)))
    ggain = jnp.sum(through * (gate * gate_sig), axis=0, keepdims=True)
    gnormed = grad * gain * (gate * gate_sig)
    gout = scale * (gnormed - normed * (jnp.sum(gnormed * normed, axis=1, keepdims=True) * (1.0 / DV)))
    gout = gout.astype(BF16)
    gprobs = mm(gout, fresh, NT)
    gfresh = mm(probs, gout, TN)
    gtarget = mm(solve, gfresh, TN)
    glower = -mm(gtarget, fresh, NT) * strict
    gscores = gprobs * weight
    tilt = glower * inner
    flow = gscores * scores + beta * tilt
    gbeta = jnp.sum(tilt, axis=1, keepdims=True) + jnp.sum(gtarget * value, axis=1, keepdims=True)
    gscores = gscores.astype(BF16)
    ginner = (beta * glower).astype(BF16)
    gquery = mm(gscores, key)
    gkey = mm(gscores, query, TN) + mm(ginner, key) + mm(ginner, key, TN)
    col_flow = jnp.sum(flow, axis=0, keepdims=True)
    col_flow = jnp.sum(jnp.where(p["rows"] == p["cols"], col_flow, 0.0), axis=1, keepdims=True)
    gdecay = reverse_cumsum_rows(jnp.sum(flow, axis=1, keepdims=True) - col_flow)
    raw_q, raw_k, scale_q, scale_k = p["raw_q"], p["raw_k"], p["scale_q"], p["scale_k"]
    gq = (DK ** (-0.5)) * scale_q * (
        gquery - raw_q * (scale_q * scale_q * jnp.sum(gquery * raw_q, axis=1, keepdims=True)))
    gk = scale_k * (gkey - raw_k * (scale_k * scale_k * jnp.sum(gkey * raw_k, axis=1, keepdims=True)))
    gactive = jnp.concatenate([gq, gk, beta * gtarget], axis=1)
    gsummed = gactive * (p["gate_conv"] * (1.0 + p["summed"] * (1.0 - p["gate_conv"])))
    source = proj_ref[:, :INNER]
    gsource = conv[TAPS - 1 : TAPS] * gsummed
    gconv_ref[0, TAPS - 1 : TAPS, :] = jnp.sum(gsummed * source, axis=0, keepdims=True)
    for lag in range(1, TAPS):
        kept = gsummed * p["keeps"][lag - 1]
        gsource = gsource + conv[TAPS - 1 - lag : TAPS - lag] * shift_up(kept, lag)
        gconv_ref[0, TAPS - 1 - lag : TAPS - lag, :] = jnp.sum(kept * shift_down(source, lag), axis=0, keepdims=True)
    gdrive = -p["rate"] * gdecay * sigmoid(p["drive"])
    gwrite = gbeta * beta * (1.0 - beta)
    lane = lax.broadcasted_iota(jnp.int32, (extra_ref.shape[0], 128), 1)
    gextra = jnp.where(lane == 2 * head, gwrite, jnp.where(lane == 2 * head + 1, gdrive, 0.0))
    gproj_ref[:, :INNER] = gsource.astype(BF16)
    gproj_ref[:, INNER:PER_HEAD] = ggate.astype(BF16)
    if last:
        gproj_ref[:, PER_HEAD:] = (gextra + other_ref[...].astype(F32)).astype(BF16)
    else:
        gextra_ref[...] = gextra.astype(BF16)
    glog = jnp.sum(gdecay * p["decay"], axis=0, keepdims=True)
    gbias = jnp.sum(gdrive, axis=0, keepdims=True)
    lane = lax.broadcasted_iota(jnp.int32, (1, 128), 1)
    gsmall_ref[0, :, 0:DV] = ggain
    gsmall_ref[0, :, DV:] = jnp.where(lane == 0, glog, jnp.where(lane == 1, gbias, 0.0))


def small_specs(length, head, group):
    smem = pl.BlockSpec(memory_space=pltpu.SMEM)
    return [
        pl.BlockSpec((group, 1, length), lambda s: (s, 0, 0)),
        pl.BlockSpec((TAPS, INNER), lambda s: (0, head)),
        smem,
        smem,
        pl.BlockSpec((1, DV), lambda s: (0, 0)),
    ]


def mixer_cost(count, passes):
    return pl.CostEstimate(flops=passes * count * (3 << 30), bytes_accessed=passes * count << 23, transcendentals=0)


def mixer_forward(head, start, attn, stack, extra, seg_row, conv, log, bias, gain):
    count, _, length = seg_row.shape
    tokens = count * length
    size = 64
    while size < length:
        size *= 2
    group = 1
    extra_spec = pl.BlockSpec((group * length, DECAY_ROWS), lambda s: (s, 0))
    extra_shape = jax.ShapeDtypeStruct((tokens, DECAY_ROWS), F32)
    return pl.pallas_call(
        functools.partial(forward_kernel, head, start),
        grid=(count // group,),
        in_specs=[
            pl.BlockSpec((group * length, attn.shape[1]), lambda s: (s, 0)),
            pl.BlockSpec(stack.shape, lambda s: (0, 0, 0), pipeline_mode=pl.Buffered(1)),
        ]
        + ([extra_spec] if head else [])
        + small_specs(length, head, group),
        out_specs=[
            pl.BlockSpec((group * length, DV), lambda s: (s, 0)),
            pl.BlockSpec((group, length, length), lambda s: (s, 0, 0)),
            pl.BlockSpec((group * length, PER_HEAD), lambda s: (s, 0)),
        ]
        + ([] if head else [extra_spec]),
        out_shape=[
            jax.ShapeDtypeStruct((tokens, DV), BF16),
            jax.ShapeDtypeStruct((count, length, length), BF16),
            jax.ShapeDtypeStruct((tokens, PER_HEAD), F32),
        ]
        + ([] if head else [extra_shape]),
        scratch_shapes=[pltpu.VMEM((group, size, size), F32)],
        compiler_params=pltpu.CompilerParams(vmem_limit_bytes=60 << 20),
        cost_estimate=mixer_cost(count, 1),
        name="mixer_forward",
    )(attn, stack, *([extra] if head else []), seg_row, conv, log, bias, gain)


def mixer_backward(head, proj, extra, seg_row, conv, log, bias, gain, solve, grad, turned, other):
    count, _, length = seg_row.shape
    tokens = count * length
    last = other is not None
    in_specs = [
        pl.BlockSpec((length, PER_HEAD), lambda s: (s, 0)),
        pl.BlockSpec((length, DECAY_ROWS), lambda s: (s, 0)),
        *small_specs(length, head, 1),
        pl.BlockSpec((1, length, length), lambda s: (s, 0, 0)),
        pl.BlockSpec((length, grad.shape[1]), lambda s: (s, 0)),
        pl.BlockSpec((turned.shape[0], DV, turned.shape[2]), lambda s: (0, head, 0)),
    ]
    args = [proj, extra, seg_row, conv, log, bias, gain, solve, grad, turned]
    width = PER_HEAD
    tail_specs = [
        pl.BlockSpec((1, TAPS, INNER), lambda s: (s, 0, 0)),
        pl.BlockSpec((1, 1, DV + 128), lambda s: (s, 0, 0)),
    ]
    tail_shapes = [
        jax.ShapeDtypeStruct((count, TAPS, INNER), F32),
        jax.ShapeDtypeStruct((count, 1, DV + 128), F32),
    ]
    mid_specs, mid_shapes = [], []
    if last:
        width += 128
        in_specs.append(pl.BlockSpec((length, 128), lambda s: (s, 0)))
        args.append(other)
    else:
        mid_specs = [pl.BlockSpec((length, 128), lambda s: (s, 0))]
        mid_shapes = [jax.ShapeDtypeStruct((tokens, 128), BF16)]
    return pl.pallas_call(
        functools.partial(backward_kernel, head, last),
        grid=(count,),
        in_specs=in_specs,
        out_specs=[pl.BlockSpec((length, width), lambda s: (s, 0))] + mid_specs + tail_specs,
        out_shape=[jax.ShapeDtypeStruct((tokens, width), BF16)] + mid_shapes + tail_shapes,
        compiler_params=pltpu.CompilerParams(vmem_limit_bytes=60 << 20),
        cost_estimate=mixer_cost(count, 2),
        name="mixer_backward",
    )(*args)


MESH_ID = pl.DeviceIdType.MESH
HBM_SPEC = pl.BlockSpec(memory_space=pltpu.HBM)
VMEM_SPEC = pl.BlockSpec(memory_space=pltpu.VMEM)
STRIP = 16
GAIN_ROW, ATTN_ROW, FFN_ROW, REST_ROW, SMALL_ROWS = 32, 34, 50, 66, 72


def meet(targets):
    barrier = pltpu.get_barrier_semaphore()
    for target in targets:
        pl.semaphore_signal(barrier, inc=1, device_id=target, device_id_type=MESH_ID)
    pl.semaphore_wait(barrier, len(targets))


def remote(source, dest, send, recv, index, target):
    return pltpu.make_async_remote_copy(
        src_ref=source,
        dst_ref=dest,
        send_sem=send.at[index],
        recv_sem=recv.at[index],
        device_id=target,
        device_id_type=MESH_ID,
    )


class Team:
    def __init__(self, name):
        self.name, self.part, self.col = name, lax.axis_index(name), lax.axis_index("col")
        self.across, self.twin = lax.rem(self.part + 2, 4), self.part + 1 - 2 * lax.rem(self.part, 2)
        self.far, self.other = lax.rem(self.twin + 2, 4), 1 - self.col
        self.x, self.y, self.core = {name: self.across}, {"col": self.other}, {name: self.twin}

    def partners(self):
        return [self.x, self.y, self.core]


class Gather:
    def __init__(self, team, src, out, keep, send, recv):
        self.out, self.send, self.recv = out, send, recv
        half = src.shape[0] // 2
        first, second = pl.ds(0, half), pl.ds(half, half)
        own, across = team.part * 2 + team.col, team.across * 2 + team.col
        other, diag = team.part * 2 + team.other, team.across * 2 + team.other
        self.local = pltpu.make_async_copy(src, out.at[own], keep)
        self.x_first = self.copy(src.at[first], out.at[own, first], 0, team.x)
        self.x_second = self.copy(src.at[second], out.at[own, second], 1, team.x)
        self.y_second = self.copy(src.at[second], out.at[own, second], 2, team.y)
        self.y_first = self.copy(src.at[first], out.at[own, first], 3, team.y)
        self.core_own = self.copy(src, out.at[own], 4, team.core)
        self.y_pass = self.copy(out.at[across, first], out.at[across, first], 5, team.y)
        self.x_pass = self.copy(out.at[other, second], out.at[other, second], 6, team.x)
        self.core_x = self.copy(out.at[across], out.at[across], 7, team.core)
        self.core_y = self.copy(out.at[other], out.at[other], 8, team.core)
        self.core_first = self.copy(out.at[diag, first], out.at[diag, first], 9, team.core)
        self.core_second = self.copy(out.at[diag, second], out.at[diag, second], 10, team.core)

    def copy(self, source, dest, index, target):
        return remote(source, dest, self.send, self.recv, index, target)

    def start_first(self):
        self.x_first.start()
        self.y_first.start()

    def start_second(self):
        for copy in (self.y_second, self.x_second, self.core_own, self.local):
            copy.start()

    def finish(self):
        self.x_first.wait_recv()
        self.y_pass.start()
        self.y_first.wait_recv()
        self.y_second.wait_recv()
        self.x_pass.start()
        self.core_y.start()
        self.x_second.wait_recv()
        self.core_x.start()
        self.y_pass.wait_recv()
        self.core_first.start()
        self.x_pass.wait_recv()
        self.core_second.start()
        cores = (self.core_own, self.core_x, self.core_y, self.core_first, self.core_second)
        for copy in cores:
            copy.wait_recv()
        for copy in (self.x_first, self.x_second, self.y_second, self.y_first, self.y_pass, self.x_pass) + cores:
            copy.wait_send()
        self.local.wait()


def gather_phase(team, src, out, *sems):
    gather = Gather(team, src, out, *sems)
    gather.start_first()
    gather.start_second()
    gather.finish()


GATHER_SEMS = [pltpu.SemaphoreType.DMA, pltpu.SemaphoreType.DMA((11,)), pltpu.SemaphoreType.DMA((11,))]


class Spread:
    def __init__(self, src, out, middle, keep, send, recv):
        self.src, self.out, self.middle, self.keep, self.send, self.recv = src, out, middle, keep, send, recv
        self.row, self.col = lax.axis_index("row"), lax.axis_index("col")
        self.hops = [
            remote(src.at[2 * item + 1 - self.col], middle.at[item], send, recv, item, {"col": 1 - self.col})
            for item in range(2)
        ]

    def pieces(self, side):
        home = self.col if side == 0 else 1 - self.col
        for item in range(2):
            source = self.src.at[2 * item + self.col] if side == 0 else self.middle.at[item]
            to_row = 2 * home + item
            copy = pltpu.make_async_remote_copy(
                src_ref=source,
                dst_ref=self.out.at[self.row],
                send_sem=self.send.at[2 + 2 * side + item],
                recv_sem=self.recv.at[2 + self.row],
                device_id={"row": to_row},
                device_id_type=MESH_ID,
            )
            yield to_row == self.row, copy, pltpu.make_async_copy(source, self.out.at[self.row], self.keep)

    def start(self):
        for hop in self.hops:
            hop.start()
        self.send_side(0)

    def send_side(self, side):
        for here, far, near in self.pieces(side):
            pl.when(here)(near.start)
            pl.when(jnp.logical_not(here))(far.start)

    def turn(self):
        for hop in self.hops:
            hop.wait_recv()
        self.send_side(1)

    def finish(self):
        for hop in range(1, 4):
            index = lax.rem(self.row + hop, 4)
            pltpu.make_async_remote_copy(
                src_ref=self.src.at[0],
                dst_ref=self.out.at[index],
                send_sem=self.send.at[0],
                recv_sem=self.recv.at[2 + index],
                device_id={"row": index},
                device_id_type=MESH_ID,
            ).wait_recv()
        for side in range(2):
            for here, far, near in self.pieces(side):
                pl.when(here)(near.wait)
                pl.when(jnp.logical_not(here))(far.wait_send)
        for hop in self.hops:
            hop.wait_send()


class Line:
    def __init__(self, src, out, keep, send, recv):
        self.src, self.out, self.send, self.recv = src, out, send, recv
        self.row = lax.axis_index("row")
        self.near = pltpu.make_async_copy(src, out.at[self.row], keep)

    def copy(self, hops, up):
        step = 1 if up else -1
        mark = self.row - hops * step
        return pltpu.make_async_remote_copy(
            src_ref=self.src if hops == 0 else self.out.at[mark],
            dst_ref=self.out.at[mark],
            send_sem=self.send.at[hops if up else 3 + hops],
            recv_sem=self.recv.at[mark],
            device_id={"row": self.row + step},
            device_id_type=MESH_ID,
        )

    def sends(self, hops, up):
        return (self.row >= hops) & (self.row < 3) if up else (self.row + hops <= 3) & (self.row > 0)

    def start(self):
        self.near.start()
        for up in (True, False):
            pl.when(self.sends(0, up))(lambda: self.copy(0, up).start())

    def arrive(self, hops):
        for up in (True, False):
            mark = self.row - hops if up else self.row + hops

            @pl.when((self.row >= hops) if up else (self.row + hops <= 3))
            def _():
                pltpu.make_async_remote_copy(
                    src_ref=self.src,
                    dst_ref=self.out.at[mark],
                    send_sem=self.send.at[0],
                    recv_sem=self.recv.at[mark],
                    device_id={"row": self.row - 1 if up else self.row + 1},
                    device_id_type=MESH_ID,
                ).wait_recv()

    def pass_on(self, hops):
        self.arrive(hops)
        for up in (True, False):
            pl.when(self.sends(hops, up))(lambda: self.copy(hops, up).start())

    def finish(self):
        self.arrive(3)
        for hops in range(3):
            for up in (True, False):
                pl.when(self.sends(hops, up))(lambda: self.copy(hops, up).wait_send())
        self.near.wait()


def share(source, dest, mark, others, keep, send, recv):
    near = pltpu.make_async_copy(source, dest.at[mark], keep)
    near.start()
    copies = []
    for item, (target, _) in enumerate(others):
        copies.append(
            pltpu.make_async_remote_copy(
                src_ref=source,
                dst_ref=dest.at[mark],
                send_sem=send.at[item],
                recv_sem=recv.at[mark],
                device_id=target,
                device_id_type=MESH_ID,
            )
        )
        copies[item].start()

    def finish():
        near.wait()
        for target, index in others:
            pltpu.make_async_remote_copy(
                src_ref=source,
                dst_ref=dest.at[index],
                send_sem=send.at[0],
                recv_sem=recv.at[index],
                device_id=target,
                device_id_type=MESH_ID,
            ).wait_recv()
        for copy in copies:
            copy.wait_send()

    return finish


def enter_kernel(part_name, *refs):
    sources, outs, scratch = refs[:5], refs[5:12], refs[12:]
    first, second, gains, segs, weight = sources
    first_tok, first_all, second_tok, second_all, gains_all, segs_all, weight_all = outs
    (stage_one, middle_one, stage_two, middle_two, ready_one, ready_two, line_keep, line_send, line_recv, small_keep,
     gain_send, gain_recv, seg_send, seg_recv) = scratch[:14]
    spread_one, spread_two, gather_one, gather_two = (scratch[14 + 3 * index : 17 + 3 * index] for index in range(4))
    team = Team(part_name)
    row = lax.axis_index("row")
    rows = [({"row": lax.rem(row + hop, 4)}, lax.rem(row + hop, 4)) for hop in range(1, 4)]
    meet(team.partners() + [target for target, _ in rows] + [{part_name: team.far}])
    one = Spread(first, stage_one, middle_one, *spread_one)
    two = Spread(second, stage_two, middle_two, *spread_two)
    line = Line(weight, weight_all, line_keep, line_send, line_recv)
    one.start()
    done_gains = share(gains, gains_all, row, rows, small_keep.at[0], gain_send, gain_recv)
    parts = [({part_name: index}, index) for index in (team.across, team.twin, team.far)]
    done_segs = share(segs, segs_all, team.part, parts, small_keep.at[1], seg_send, seg_recv)
    line.start()
    one.turn()
    two.start()
    one.finish()
    done_gains()
    done_segs()
    tokens, width = first.shape[1], first.shape[2]

    def norm(rows, _):
        wides = [stage_one[index, rows, :].astype(F32) for index in range(4)]
        square = sum(jnp.sum(wide * wide, axis=1, keepdims=True) for wide in wides)
        scale = lax.rsqrt(square * (1.0 / (4 * width)) + 1e-05)
        for index in range(4):
            cols = slice(index * width, (index + 1) * width)
            first_tok[rows, cols] = stage_one[index, rows, :]
            ready_one[rows, cols] = (wides[index] * scale * gains_all[index, 0:1, :]).astype(BF16)

    strips(0, tokens, norm)
    two.turn()
    line.pass_on(1)
    gather_phase(team, ready_one, first_all, *gather_one)
    two.finish()

    def join_blocks(rows, _):
        for index in range(4):
            cols = slice(index * width, (index + 1) * width)
            second_tok[rows, cols] = stage_two[index, rows, :]
            ready_two[rows, cols] = stage_two[index, rows, :]

    strips(0, tokens, join_blocks)
    line.pass_on(2)
    gather_phase(team, ready_two, second_all, *gather_two)
    line.finish()


def enter_call(lay, first, second, gains, segs, weight):
    tokens, width = first.shape[0] // 4, first.shape[1]
    wide = 4 * width
    tok, everyone = jax.ShapeDtypeStruct((tokens, wide), BF16), jax.ShapeDtypeStruct((8, tokens, wide), BF16)
    stage = [pltpu.VMEM((4, tokens, width), BF16), pltpu.VMEM((2, tokens, width), BF16)]
    line_sems = [pltpu.SemaphoreType.DMA, pltpu.SemaphoreType.DMA((6,)), pltpu.SemaphoreType.DMA((4,))]
    small_sems = [pltpu.SemaphoreType.DMA((count,)) for count in (2, 3, 4, 3, 4)]
    spread_sems = [pltpu.SemaphoreType.DMA, pltpu.SemaphoreType.DMA((6,)), pltpu.SemaphoreType.DMA((6,))]
    results = pl.pallas_call(
        functools.partial(enter_kernel, lay.part),
        in_specs=[VMEM_SPEC] * 5,
        out_specs=[VMEM_SPEC, HBM_SPEC, VMEM_SPEC, HBM_SPEC, VMEM_SPEC, VMEM_SPEC, HBM_SPEC],
        out_shape=[
            tok,
            everyone,
            tok,
            everyone,
            jax.ShapeDtypeStruct((4,) + gains.shape, gains.dtype),
            jax.ShapeDtypeStruct((4,) + segs.shape, segs.dtype),
            jax.ShapeDtypeStruct((4,) + weight.shape, weight.dtype),
        ],
        scratch_shapes=stage
        + stage
        + [pltpu.VMEM((tokens, wide), BF16)] * 2
        + line_sems
        + small_sems
        + spread_sems
        + spread_sems
        + GATHER_SEMS
        + GATHER_SEMS,
        compiler_params=pltpu.CompilerParams(
            collective_id=lay.fresh_id(), has_side_effects=True, vmem_limit_bytes=60 << 20
        ),
        cost_estimate=pl.CostEstimate(flops=1 << 30, bytes_accessed=400 << 20, transcendentals=0),
        name="enter",
    )(first.reshape(4, tokens, width), second.reshape(4, tokens, width), gains, segs, weight)
    first_tok, first_all, second_tok, second_all, gains, segs, weight = results
    return (
        first_tok, first_all.reshape(-1, wide), second_tok, second_all.reshape(-1, wide), gains, segs, weight,
    )


def strips(start, count, body):
    @pl.loop(0, count // STRIP)
    def _(step):
        body(pl.ds(pl.multiple_of(start + step * STRIP, STRIP), STRIP), pl.ds(pl.multiple_of(step * STRIP, STRIP), STRIP))


class Scatter:
    def __init__(self, team, dots, finish, refs):
        self.team, self.dots, self.finish = team, dots, finish
        self.work, self.twin, self.sent, self.relay, self.final, self.send, self.recv = refs
        self.rows, self.chunk = self.twin.shape[1], self.twin.shape[2] // 4
        self.half = self.rows // 2
        first, second = pl.ds(0, self.half), pl.ds(self.half, self.half)
        sent, relay, final = self.sent, self.relay, self.final
        self.relay_x = self.copy(sent.at[0, first], relay.at[0], 4, team.x)
        self.relay_y = self.copy(sent.at[0, second], relay.at[1], 5, team.y)
        self.x_first = self.copy(sent.at[1, first], final.at[0, first], 6, team.x)
        self.x_second = self.copy(sent.at[1, second], final.at[0, second], 7, team.x)
        self.y_second = self.copy(sent.at[2, second], final.at[1, second], 8, team.y)
        self.y_first = self.copy(sent.at[2, first], final.at[1, first], 9, team.y)

    def copy(self, source, dest, index, target):
        return remote(source, dest, self.send, self.recv, index, target)

    def swap(self, item):
        return self.copy(self.work.at[item, 0], self.twin.at[item], item, self.team.core)

    def total(self, item, start, passed=None):
        def add(rows, local):
            value = self.work[item, 1, rows, :].astype(F32) + self.twin[item, rows, :].astype(F32)
            if passed is not None:
                value = value + self.relay[passed, local, :].astype(F32)
            self.sent[item, rows, :] = value.astype(BF16)

        strips(start, self.half, add)

    def begin(self):
        team = self.team

        @pl.loop(0, 4)
        def _(item):
            @pl.loop(0, 8)
            def _(step):
                which, chunk = step // 4, lax.rem(step, 4)
                base = team.part * which + team.twin * (1 - which)
                slot = lax.rem(base + 2 * (1 - item // 2), 4) * 2 + lax.rem(team.col + 1 + item, 2)
                columns = pl.ds(pl.multiple_of(chunk * self.chunk, self.chunk), self.chunk)
                rows = pl.ds(pl.multiple_of(slot * self.rows, STRIP), self.rows)
                self.work[item, which, :, columns] = self.dots(rows, chunk).astype(BF16)

            self.swap(item).start()

            @pl.when(item == 1)
            def _():
                self.swap(0).wait_recv()
                self.total(0, 0)
                self.relay_x.start()
                self.total(0, self.half)
                self.relay_y.start()

            @pl.when(item == 2)
            def _():
                self.swap(1).wait_recv()
                self.total(1, 0)
                self.x_first.start()

            @pl.when(item == 3)
            def _():
                self.swap(2).wait_recv()
                self.total(2, self.half)
                self.y_second.start()

    def pass_on(self):
        self.relay_y.wait_recv()
        self.total(1, self.half, 1)
        self.x_second.start()
        self.relay_x.wait_recv()
        self.total(2, 0, 0)
        self.y_first.start()

    def last(self, rows, _):
        value = self.work[3, 1, rows, :].astype(F32) + self.twin[3, rows, :].astype(F32)
        self.finish(rows, value + self.final[0, rows, :].astype(F32) + self.final[1, rows, :].astype(F32))

    def conclude(self, between=None):
        self.swap(3).wait_recv()
        self.x_first.wait_recv()
        self.y_first.wait_recv()
        strips(0, self.half, self.last)
        if between:
            between()
        self.x_second.wait_recv()
        self.y_second.wait_recv()
        strips(self.half, self.half, self.last)
        for copy in [self.swap(item) for item in range(4)]:
            copy.wait_send()
        for copy in (self.relay_x, self.relay_y, self.x_first, self.x_second, self.y_second, self.y_first):
            copy.wait_send()


def scatter_scratch(tokens, wide):
    return [
        pltpu.VMEM((4, 2, tokens, wide), BF16),
        pltpu.VMEM((4, tokens, wide), BF16),
        pltpu.VMEM((3, tokens, wide), BF16),
        pltpu.VMEM((2, tokens // 2, wide), BF16),
        pltpu.VMEM((2, tokens, wide), BF16),
        pltpu.SemaphoreType.DMA((10,)),
        pltpu.SemaphoreType.DMA((10,)),
    ]


def whole_rights(rights):
    return [(index, 0, right.shape[1]) for index, right in enumerate(rights)]


def make_dots(lefts, rights, starts):
    def dots(rows, chunk):
        value = 0.0
        for left, (index, start, size) in zip(lefts, starts):
            part = rights[index][chunk, start : start + size, :]
            value = value + lax.dot_general(left[rows, :size], part, NN, preferred_element_type=F32)
        return value

    return dots


def norm_back(value, total, gain, gain_sum):
    scale = lax.rsqrt(jnp.sum(value * value, axis=1, keepdims=True) * (1.0 / value.shape[1]) + 1e-05)
    normed = value * scale
    gain_sum[...] += total * normed
    scaled = total * gain
    inner = jnp.sum(scaled * normed, axis=1, keepdims=True) * (1.0 / value.shape[1])
    return scale * (scaled - normed * inner)


def deal_out(out, rows, value):
    width = value.shape[1] // 4
    for index in range(4):
        out[index, rows, :] = value[:, index * width : (index + 1) * width].astype(BF16)


def fetch(sources, places, sems):
    copies = []
    for index, (source, place) in enumerate(zip(sources, places)):
        if isinstance(source, tuple):
            ref, start = source
            source = ref.at[:, pl.ds(start, place.shape[1]), :]
        copies.append(pltpu.make_async_copy(source, place, sems.at[index]))
        copies[index].start()
    return copies


def fetched(shapes):
    return [pltpu.VMEM(shape, dtype) for shape, dtype in shapes] + [pltpu.SemaphoreType.DMA((len(shapes),))]


def whole(values):
    return values.shape, values.dtype


def mid_kernel(part_name, starts, *refs):
    count = len(starts)
    sources, (out, everyone), scratch = refs[: count + 3], refs[count + 3 : count + 5], refs[count + 5 :]
    places, sems, scratch = scratch[: count + 3], scratch[count + 3], scratch[count + 4 :]
    loads = fetch(sources, places, sems)
    lefts, (right, stored, gain) = places[:count], places[count:]
    ready = scratch[7]
    team = Team(part_name)
    meet(team.partners())
    for load in loads:
        load.wait()

    def finish(rows, total):
        value = stored[rows, :].astype(F32) + total
        out[rows, :] = value
        scale = lax.rsqrt(jnp.sum(value * value, axis=1, keepdims=True) * (1.0 / value.shape[1]) + 1e-05)
        ready[rows, :] = (value * scale * gain[...]).astype(BF16)

    scatter = Scatter(team, make_dots(lefts, [right], [(0, *place) for place in starts]), finish, scratch[:7])
    scatter.begin()
    scatter.pass_on()
    gather = Gather(team, ready, everyone, *scratch[8:])
    scatter.conclude(gather.start_first)
    gather.start_second()
    gather.finish()


def mid_call(lay, lefts, right, starts, stored, gain):
    tokens, wide = stored.shape
    residual, everyone = pl.pallas_call(
        functools.partial(mid_kernel, lay.part, starts),
        in_specs=[HBM_SPEC] * (len(lefts) + 3),
        out_specs=[VMEM_SPEC, HBM_SPEC],
        out_shape=[jax.ShapeDtypeStruct((tokens, wide), F32), jax.ShapeDtypeStruct((8, tokens, wide), BF16)],
        scratch_shapes=fetched([whole(values) for values in (*lefts, right, stored, gain)])
        + scatter_scratch(tokens, wide) + [pltpu.VMEM((tokens, wide), BF16)] + GATHER_SEMS,
        compiler_params=pltpu.CompilerParams(
            collective_id=lay.fresh_id(), has_side_effects=True, vmem_limit_bytes=60 << 20
        ),
        cost_estimate=pl.CostEstimate(flops=1 << 35, bytes_accessed=200 << 20, transcendentals=0),
        name="team_mid",
    )(*lefts, right, stored, gain)
    return residual, everyone.reshape(8 * tokens, wide)


def branch_kernel(part_name, count, *refs):
    total = 2 * count + 3
    sources, (out, everyone, gain_out), scratch = refs[:total], refs[total : total + 3], refs[total + 3 :]
    places, sems, scratch = scratch[:total], scratch[total], scratch[total + 1 :]
    sources = [(ref, 0) if count <= index < 2 * count else ref for index, ref in enumerate(sources)]
    loads = fetch(sources, places, sems)
    lefts, rights, (residual, through, gain) = places[:count], places[count : 2 * count], places[2 * count :]
    gain_sum, ready = scratch[7:9]
    team = Team(part_name)
    meet(team.partners())
    for load in loads:
        load.wait()
    gain_sum[...] = jnp.zeros_like(gain_sum)

    def finish(rows, total):
        value = through[rows, :].astype(F32) + norm_back(residual[rows, :], total, gain[...], gain_sum)
        out[rows, :] = value
        ready[rows, :] = value.astype(BF16)

    scatter = Scatter(team, make_dots(lefts, rights, whole_rights(rights)), finish, scratch[:7])
    scatter.begin()
    scatter.pass_on()
    gather = Gather(team, ready, everyone, *scratch[9:])
    scatter.conclude(gather.start_first)
    gather.start_second()
    gain_out[...] = jnp.sum(gain_sum[...], axis=0, keepdims=True)
    gather.finish()


def branch_call(lay, lefts, rights, residual, through, gain):
    tokens, wide = residual.shape
    width = rights[0].shape[2]
    out, everyone, gain_part = pl.pallas_call(
        functools.partial(branch_kernel, lay.part, len(lefts)),
        in_specs=[HBM_SPEC] * (2 * len(lefts) + 3),
        out_specs=[VMEM_SPEC, HBM_SPEC, VMEM_SPEC],
        out_shape=[
            jax.ShapeDtypeStruct((tokens, wide), F32),
            jax.ShapeDtypeStruct((8, tokens, wide), BF16),
            jax.ShapeDtypeStruct((1, wide), F32),
        ],
        scratch_shapes=fetched(
            [whole(left) for left in lefts]
            + [((4, left.shape[1], width), BF16) for left in lefts]
            + [whole(values) for values in (residual, through, gain)]
        )
        + scatter_scratch(tokens, wide)
        + [pltpu.VMEM((STRIP, wide), F32), pltpu.VMEM((tokens, wide), BF16)]
        + GATHER_SEMS,
        compiler_params=pltpu.CompilerParams(
            collective_id=lay.fresh_id(), has_side_effects=True, vmem_limit_bytes=60 << 20
        ),
        cost_estimate=pl.CostEstimate(flops=1 << 35, bytes_accessed=250 << 20, transcendentals=0),
        name="team_branch",
    )(*lefts, *rights, residual, through, gain)
    return out, everyone.reshape(8 * tokens, wide), gain_part


def finish_kernel(part_name, count, starts, *refs):
    total = 2 * count + len(starts) + 5
    sources, (block_out, input_out, gain_out), scratch = refs[:total], refs[total : total + 3], refs[total + 3 :]
    places, sems, scratch = scratch[:total], scratch[total], scratch[total + 1 :]
    hidden, downs, grads = places[:count], places[count : 2 * count], places[2 * count : -5]
    mix, residual, stored, through, gain = places[-5:]
    downs_from = [(ref, 2 * values.shape[1]) for ref, values in zip(sources[count : 2 * count], hidden)]
    loads = fetch([*sources[:count], *downs_from, *sources[2 * count :]], places, sems)
    gain_sum = scratch[14]
    team = Team(part_name)
    meet(team.partners())
    for load in loads[: 2 * count]:
        load.wait()
    gain_sum[...] = jnp.zeros_like(gain_sum)

    def finish_block(rows, total):
        deal_out(block_out, rows, residual[rows, :] + total)

    def finish_input(rows, total):
        value = norm_back(stored[rows, :].astype(F32), total, gain[...], gain_sum)
        deal_out(input_out, rows, through[rows, :] + value)

    block = Scatter(
        team, make_dots(hidden, downs, whole_rights(downs)), finish_block, scratch[:7]
    )
    inputs = Scatter(team, make_dots(grads, [mix], [(0, *place) for place in starts]), finish_input, scratch[7:14])
    block.begin()
    for load in loads[2 * count :]:
        load.wait()
    inputs.begin()
    block.pass_on()
    inputs.pass_on()
    block.conclude()
    inputs.conclude()
    gain_out[...] = jnp.sum(gain_sum[...], axis=0, keepdims=True)


def finish_call(lay, hidden, stacks, grads, mix, starts, residual, stored, through, gain):
    tokens, wide = residual.shape
    width = stacks[0].shape[2]
    pieces = jax.ShapeDtypeStruct((4, tokens, width), BF16)
    return pl.pallas_call(
        functools.partial(finish_kernel, lay.part, len(hidden), starts),
        in_specs=[HBM_SPEC] * (2 * len(hidden) + len(grads) + 5),
        out_specs=[VMEM_SPEC] * 3,
        out_shape=[pieces, pieces, jax.ShapeDtypeStruct((1, wide), F32)],
        scratch_shapes=fetched(
            [whole(values) for values in hidden]
            + [((4, values.shape[1], width), BF16) for values in hidden]
            + [whole(values) for values in (*grads, mix, residual, stored, through, gain)]
        )
        + scatter_scratch(tokens, wide)
        + scatter_scratch(tokens, wide)
        + [pltpu.VMEM((STRIP, wide), F32)],
        compiler_params=pltpu.CompilerParams(
            collective_id=lay.fresh_id(), has_side_effects=True, vmem_limit_bytes=60 << 20
        ),
        cost_estimate=pl.CostEstimate(flops=1 << 35, bytes_accessed=250 << 20, transcendentals=0),
        name="team_finish",
    )(*hidden, *stacks, *grads, mix, residual, stored, through, gain)


class Deal:
    def __init__(self, src, out, keep, send, recv):
        self.src, self.out, self.keep, self.send, self.recv = src, out, keep, send, recv
        self.row, self.col = lax.axis_index("row"), lax.axis_index("col")
        spot = self.row * 2 + self.col
        self.mark, self.home = lax.rem(spot, 4), spot // 4

    def owner(self, index):
        place = self.col * 4 + index
        return {"row": place // 2, "col": lax.rem(place, 2)}

    def apart(self, index):
        owner = self.owner(index)
        return (owner["row"] != self.row) | (owner["col"] != self.col)

    def greet(self, barrier):
        for index in range(4):

            @pl.when(self.apart(index))
            def _():
                pl.semaphore_signal(barrier, inc=1, device_id=self.owner(index), device_id_type=MESH_ID)

        return 4 - (self.home == self.col).astype(jnp.int32)

    def each(self, act_near, act_far):
        for index in range(4):
            here = (self.row == index) & (self.home == self.col)

            @pl.when(here)
            def _():
                act_near(pltpu.make_async_copy(self.src.at[index], self.out.at[self.mark], self.keep))

            @pl.when(jnp.logical_not(here))
            def _():
                act_far(
                    pltpu.make_async_remote_copy(
                        src_ref=self.src.at[index],
                        dst_ref=self.out.at[self.mark],
                        send_sem=self.send.at[index],
                        recv_sem=self.recv.at[self.mark],
                        device_id={"row": index, "col": self.home},
                        device_id_type=MESH_ID,
                    )
                )

    def start(self):
        self.each(lambda copy: copy.start(), lambda copy: copy.start())

    def finish(self):
        for index in range(4):

            @pl.when(self.apart(index))
            def _():
                pltpu.make_async_remote_copy(
                    src_ref=self.src.at[0],
                    dst_ref=self.out.at[index],
                    send_sem=self.send.at[0],
                    recv_sem=self.recv.at[index],
                    device_id=self.owner(index),
                    device_id_type=MESH_ID,
                ).wait_recv()

        self.each(lambda copy: copy.wait(), lambda copy: copy.wait_send())


DEAL_SEMS = [pltpu.SemaphoreType.DMA, pltpu.SemaphoreType.DMA((4,)), pltpu.SemaphoreType.DMA((4,))]


def leave_kernel(part_name, *refs):
    first, second, block, src, first_out, second_out, blocks, out = refs[:8]
    deals = [Deal(first, first_out, *refs[8:11]), Deal(second, second_out, *refs[11:14])]
    rows_in, summed, near, row_send, row_recv, team_send, team_recv, join_send, join_recv = refs[14:]
    team = Team(part_name)
    row = lax.axis_index("row")
    rows = [({"row": lax.rem(row + hop, 4)}, lax.rem(row + hop, 4)) for hop in range(1, 4)]
    mates = []
    for part in (team.part, team.across, team.twin, team.far):
        for side in (team.col, team.other):
            mates.append(({part_name: part, "col": side}, part * 2 + side))
    mates = mates[1:]
    barrier = pltpu.get_barrier_semaphore()
    for target, _ in rows + mates:
        pl.semaphore_signal(barrier, inc=1, device_id=target, device_id_type=MESH_ID)
    pl.semaphore_wait(barrier, len(rows + mates) + deals[0].greet(barrier))
    own, across = blocks.at[team.part], blocks.at[team.across]
    join_x = remote(block, own, join_send, join_recv, 0, team.x)
    join_core = remote(block, own, join_send, join_recv, 1, team.core)
    join_pass = remote(across, across, join_send, join_recv, 2, team.core)
    join_near = pltpu.make_async_copy(block, own, near.at[2])
    finish_rows = share(src, rows_in, row, rows, near.at[0], row_send, row_recv)
    for copy in (join_x, join_core, join_near):
        copy.start()
    for deal in deals:
        deal.start()
    finish_rows()
    summed[...] = (rows_in[0] + rows_in[1]) + (rows_in[2] + rows_in[3])
    finish_team = share(summed, out, team.part * 2 + team.col, mates, near.at[1], team_send, team_recv)
    join_x.wait_recv()
    join_pass.start()
    for deal in deals:
        deal.finish()
    finish_team()
    join_core.wait_recv()
    join_pass.wait_recv()
    for copy in (join_x, join_core, join_pass):
        copy.wait_send()
    join_near.wait()


def leave_call(lay, first, second, block, small):
    whole_array = jax.ShapeDtypeStruct(first.shape, first.dtype)
    return pl.pallas_call(
        functools.partial(leave_kernel, lay.part),
        in_specs=[VMEM_SPEC] * 4,
        out_specs=[HBM_SPEC, HBM_SPEC, HBM_SPEC, VMEM_SPEC],
        out_shape=[
            whole_array,
            whole_array,
            jax.ShapeDtypeStruct((4,) + block.shape, block.dtype),
            jax.ShapeDtypeStruct((8,) + small.shape, F32),
        ],
        scratch_shapes=DEAL_SEMS
        + DEAL_SEMS
        + [pltpu.VMEM((4,) + small.shape, F32), pltpu.VMEM(small.shape, F32)]
        + [pltpu.SemaphoreType.DMA((count,)) for count in (3, 3, 4, 7, 8, 3, 3)],
        compiler_params=pltpu.CompilerParams(
            collective_id=lay.fresh_id(), has_side_effects=True, vmem_limit_bytes=60 << 20
        ),
        cost_estimate=pl.CostEstimate(flops=1 << 30, bytes_accessed=120 << 20, transcendentals=0),
        name="leave",
    )(first, second, block, small)


def cross(lay, value):
    return lax.ppermute(value, lay.part, [(0, 2), (2, 0), (1, 3), (3, 1)])


def link(lay, value):
    return lax.ppermute(value, lay.part, [(0, 1), (1, 0), (2, 3), (3, 2)])


def part_order(lay):
    part = lax.axis_index(lay.part)
    twin = part + 1 - 2 * (part % 2)
    return jnp.stack([part, (part + 2) % 4, twin, (twin + 2) % 4]).astype(jnp.int32)


def rows_kernel(order, *refs):
    for index, ref in enumerate(refs[:4]):

        @pl.when(pl.program_id(1) == index)
        def _():
            refs[4][...] = ref[...].astype(F32)


def place_rows(order, pieces, start, rows):
    width = pieces[0].shape[1]
    block = rows
    while start % block:
        block //= 2
    steps = rows // block
    return pl.pallas_call(
        rows_kernel,
        grid_spec=pltpu.PrefetchScalarGridSpec(
            num_scalar_prefetch=1,
            grid=(steps, 4),
            in_specs=[pl.BlockSpec((block, width), lambda j, i, order: (start // block + j, 0))] * 4,
            out_specs=pl.BlockSpec((block, width), lambda j, i, order: (order[i] * steps + j, 0)),
        ),
        out_shape=jax.ShapeDtypeStruct((4 * rows, width), F32),
        compiler_params=pltpu.CompilerParams(vmem_limit_bytes=60 << 20),
        name="place_rows",
    )(order, *pieces)


def late_head_kernel(order, *refs):
    for index, ref in enumerate(refs[:4]):

        @pl.when(pl.program_id(0) == index)
        def _():
            refs[4][...] = ref[...].T.astype(F32)


def place_late_head(order, heads, head, pieces):
    features = pieces[0].shape[1]
    return pl.pallas_call(
        late_head_kernel,
        grid_spec=pltpu.PrefetchScalarGridSpec(
            num_scalar_prefetch=1,
            grid=(4,),
            in_specs=[pl.BlockSpec((PER_HEAD, features), lambda i, order: (0, 0))] * 4,
            out_specs=pl.BlockSpec((features, PER_HEAD), lambda i, order: (0, order[i] * heads + head)),
        ),
        out_shape=jax.ShapeDtypeStruct((features, 4 * heads * PER_HEAD), F32),
        compiler_params=pltpu.CompilerParams(vmem_limit_bytes=60 << 20),
        name="place_late_head",
    )(order, *pieces)


def close_kernel(heads, src, tail, _, sums, first, second, out, decay, conv, gain, attn, ffn, rest, first_out,
                 second_out):
    step = pl.program_id(0)
    first_out[...] = first[...]
    second_out[...] = second[...]
    out[...] = src[0].T.astype(F32)
    for part in range(4):

        @pl.when(step == part)
        def _():
            decay[part * 2 * heads : (part + 1) * 2 * heads, :] = tail[0, : 2 * heads, :].astype(F32)

    @pl.when(step == 1)
    def _():
        row, col = lax.axis_index("row"), lax.axis_index("col")
        blocks = conv.shape[1] // 512
        for part in range(4):
            own = sums[2 * part + col]
            for tap in range(TAPS):
                for block in range(blocks):
                    start = (part * blocks + block) * 128
                    conv[tap : tap + 1, start : start + 128] = own[tap * blocks + block : tap * blocks + block + 1]
            rest[part : part + 1, :] = own[REST_ROW : REST_ROW + 1]
        total = sums[0]
        for slot in range(1, 8):
            total = total + sums[slot]
        gain[...] = total[GAIN_ROW:ATTN_ROW]
        for index in range(4):

            @pl.when(row == index)
            def _():
                attn[...] = total[ATTN_ROW + 4 * index : ATTN_ROW + 4 * index + 4]
                ffn[...] = total[FFN_ROW + 4 * index : FFN_ROW + 4 * index + 4]


def close_call(heads, stack, whole_grad, sums, first, second):
    features = stack.shape[2]
    channels = 4 * heads * INNER

    def fixed(*shape):
        return pl.BlockSpec(shape, lambda i: (0,) * len(shape))

    piece = pl.BlockSpec((1,) + first.shape[1:], lambda i: (i, 0, 0))
    return pl.pallas_call(
        functools.partial(close_kernel, heads),
        grid=(4,),
        in_specs=[
            pl.BlockSpec((1, PER_HEAD, features), lambda i: (i, 0, 0)),
            pl.BlockSpec((1, DECAY_ROWS, features), lambda i: (i, PER_HEAD // DECAY_ROWS, 0)),
            HBM_SPEC,
            fixed(*sums.shape),
            piece,
            piece,
        ],
        out_specs=[
            pl.BlockSpec((features, PER_HEAD), lambda i: (0, i * heads)),
            fixed(8 * heads, features),
            fixed(TAPS, channels),
            fixed(DV // 128, 128),
            fixed(4, 128),
            fixed(4, 128),
            fixed(4, 128),
            piece,
            piece,
        ],
        out_shape=[
            jax.ShapeDtypeStruct((features, 4 * heads * PER_HEAD), F32),
            jax.ShapeDtypeStruct((8 * heads, features), F32),
            jax.ShapeDtypeStruct((TAPS, channels), F32),
            jax.ShapeDtypeStruct((DV // 128, 128), F32),
            jax.ShapeDtypeStruct((4, 128), F32),
            jax.ShapeDtypeStruct((4, 128), F32),
            jax.ShapeDtypeStruct((4, 128), F32),
            jax.ShapeDtypeStruct(first.shape, first.dtype),
            jax.ShapeDtypeStruct(second.shape, second.dtype),
        ],
        input_output_aliases={2: 0},
        compiler_params=pltpu.CompilerParams(vmem_limit_bytes=60 << 20),
        name="close",
    )(stack, stack, whole_grad, sums, first, second)


def place_ffn_kernel(counts, order, *refs):
    units = sum(counts)
    blocks = len(counts)
    pairs, downs = refs[: 4 * blocks], refs[4 * blocks : 8 * blocks]
    gate, up, down = refs[8 * blocks : 8 * blocks + 3]
    turned = refs[8 * blocks + 3 :]
    base = 0
    for block, count in enumerate(counts):
        for index in range(4):
            turned[block][order[index]] = pairs[4 * block + index][...].T.astype(F32)
            start = pl.multiple_of(order[index] * units + base, 64)
            down[pl.ds(start, count), :] = downs[4 * block + index][...].astype(F32)
        for part in range(4):
            place = slice(part * units + base, part * units + base + count)
            gate[:, place] = turned[block][part, :, :count]
            up[:, place] = turned[block][part, :, count:]
        base += count


def place_ffn(order, pieces):
    counts = [group[0].shape[0] // 3 for group in pieces]
    flat = [piece for group in pieces for piece in group]
    features, units = flat[0].shape[1], sum(counts)
    wide = jax.ShapeDtypeStruct((features, 4 * units), F32)
    return pl.pallas_call(
        functools.partial(place_ffn_kernel, counts),
        grid_spec=pltpu.PrefetchScalarGridSpec(
            num_scalar_prefetch=1,
            grid=(features // 128,),
            in_specs=[pl.BlockSpec((2 * (p.shape[0] // 3), 128), lambda i, order: (0, i)) for p in flat]
            + [pl.BlockSpec((p.shape[0] // 3, 128), lambda i, order: (2, i)) for p in flat],
            out_specs=[
                pl.BlockSpec((128, 4 * units), lambda i, order: (i, 0)),
                pl.BlockSpec((128, 4 * units), lambda i, order: (i, 0)),
                pl.BlockSpec((4 * units, 128), lambda i, order: (0, i)),
            ],
            scratch_shapes=[pltpu.VMEM((4, 128, 2 * count), F32) for count in counts],
        ),
        out_shape=[wide, wide, jax.ShapeDtypeStruct((4 * units, features), F32)],
        compiler_params=pltpu.CompilerParams(vmem_limit_bytes=60 << 20),
        cost_estimate=pl.CostEstimate(flops=1 << 30, bytes_accessed=30 << 20, transcendentals=0),
        name="place_ffn",
    )(order, *flat, *flat)


def stack_kernel(counts, *refs):
    grads, values, out = refs[: len(counts)], refs[len(counts) : -1], refs[-1]
    base = 0
    for grad, value, count in zip(grads, values, counts):
        for start in range(0, count, 256):
            size = min(256, grad.shape[1] - start)
            part = lax.dot_general(grad[:, start : start + size], value[...], TN, preferred_element_type=F32)
            size = min(size, count - start)
            out[0, base + start : base + start + size, :] = part[:size].astype(BF16)
        base += count


def stack_call(rows_n, pairs, counts):
    tokens, wide = pairs[0][1].shape
    width = wide // rows_n
    total = sum(counts)
    flops = 2 * tokens * wide * sum(grad.shape[1] for grad, _ in pairs)
    return pl.pallas_call(
        functools.partial(stack_kernel, counts),
        grid=(rows_n,),
        in_specs=[
            pl.BlockSpec(grad.shape, lambda i: (0, 0), pipeline_mode=pl.Buffered(1)) for grad, _ in pairs
        ]
        + [pl.BlockSpec((tokens, width), lambda i: (0, i)) for _ in pairs],
        out_specs=pl.BlockSpec((1, total, width), lambda i: (i, 0, 0)),
        out_shape=jax.ShapeDtypeStruct((rows_n, total, width), BF16),
        compiler_params=pltpu.CompilerParams(vmem_limit_bytes=60 << 20),
        cost_estimate=pl.CostEstimate(flops=flops, bytes_accessed=40 << 20, transcendentals=0),
        name="weight_grads",
    )(*[grad for grad, _ in pairs], *[value for _, value in pairs])


def units_kernel(part_name, cuts, gate, up, down, *outs):
    part, units = lax.axis_index(part_name), cuts[-1]
    for index in range(gate.shape[1] // units):

        @pl.when(part == index)
        def _():
            base = index * units
            for which, ref in enumerate((gate, up)):
                turned = ref[:, base : base + units].T
                for out, start, end in zip(outs, cuts[:-1], cuts[1:]):
                    out[which * (end - start) : (which + 1) * (end - start), :] = turned[start:end]
            for out, start, end in zip(outs, cuts[:-1], cuts[1:]):
                out[2 * (end - start) :, :] = down[base + start : base + end, :]


def own_mix_kernel(heads, ways, part, mix, decay, out):
    turned = mix[...].T
    out[:PER_HEAD, :] = turned[:PER_HEAD]
    if heads > 1:
        out[PER_HEAD + DECAY_ROWS :, :] = turned[PER_HEAD:]
    small = decay[...].astype(F32).T
    empty = jnp.zeros((DECAY_ROWS - 2 * heads, small.shape[1]), F32)
    for index in range(ways):

        @pl.when(part[0] == index)
        def _():
            rows = small[index * 2 * heads : (index + 1) * 2 * heads]
            out[PER_HEAD : PER_HEAD + DECAY_ROWS, :] = jnp.concatenate([rows, empty]).astype(BF16)


def own_kernel(part_name, cuts, heads, ways, part, mix, decay, gate, up, down, mix_out, *outs):
    own_mix_kernel(heads, ways, part, mix, decay, mix_out)
    units_kernel(part_name, cuts, gate, up, down, *outs)


def own_call(lay, cuts, heads, mix, decay, gate, up, down):
    features, wide = gate.shape
    rows = [heads * PER_HEAD + DECAY_ROWS] + [3 * (end - start) for start, end in zip(cuts[:-1], cuts[1:])]
    part = lax.axis_index(lay.part).astype(jnp.int32).reshape(1)
    return pl.pallas_call(
        functools.partial(own_kernel, lay.part, cuts, heads, lay.ways),
        grid_spec=pltpu.PrefetchScalarGridSpec(
            num_scalar_prefetch=1,
            grid=(features // 128,),
            in_specs=[
                pl.BlockSpec((128, heads * PER_HEAD), lambda i, part: (i, part[0])),
                pl.BlockSpec((128, decay.shape[1]), lambda i, part: (i, 0)),
                pl.BlockSpec((128, wide), lambda i, part: (i, 0)),
                pl.BlockSpec((128, wide), lambda i, part: (i, 0)),
                pl.BlockSpec((wide, 128), lambda i, part: (0, i)),
            ],
            out_specs=[pl.BlockSpec((count, 128), lambda i, part: (0, i)) for count in rows],
        ),
        out_shape=[jax.ShapeDtypeStruct((count, features), BF16) for count in rows],
        compiler_params=pltpu.CompilerParams(vmem_limit_bytes=60 << 20),
        name="own_weights",
    )(part, mix, decay, gate, up, down)


def ffn_kernel(values, grads, stack, hidden, both_grad):
    units, width = hidden.shape[1], stack.shape[2]
    both, grad = 0.0, 0.0
    for index in range(stack.shape[0]):
        cols = slice(index * width, (index + 1) * width)
        both = both + lax.dot_general(
            values[:, cols], stack[index, : 2 * units, :], NT, preferred_element_type=F32
        )
        grad = grad + lax.dot_general(grads[:, cols], stack[index, 2 * units :, :], NT, preferred_element_type=F32)
    gate, up = both[:, :units], both[:, units:]
    sig = sigmoid(gate)
    act = gate * sig
    hidden[...] = (act * up).astype(BF16)
    both_grad[:, :units] = (grad * up * (sig + act * (1.0 - sig))).astype(BF16)
    both_grad[:, units:] = (grad * act).astype(BF16)


def ffn_call(values, grads, stack):
    tokens, width = values.shape
    units = stack.shape[1] // 3
    block = 256
    while tokens % block:
        block //= 2
    row = pl.BlockSpec((block, width), lambda i: (i, 0))
    return pl.pallas_call(
        ffn_kernel,
        grid=(tokens // block,),
        in_specs=[row, row, pl.BlockSpec(stack.shape, lambda i: (0, 0, 0))],
        out_specs=[
            pl.BlockSpec((block, units), lambda i: (i, 0)),
            pl.BlockSpec((block, 2 * units), lambda i: (i, 0)),
        ],
        out_shape=[
            jax.ShapeDtypeStruct((tokens, units), BF16),
            jax.ShapeDtypeStruct((tokens, 2 * units), BF16),
        ],
        compiler_params=pltpu.CompilerParams(vmem_limit_bytes=60 << 20),
        cost_estimate=pl.CostEstimate(
            flops=6 * tokens * width * units, bytes_accessed=30 << 20, transcendentals=tokens * units
        ),
        name="ffn",
    )(values, grads, stack)


SEQ = 448


def project(left, right):
    return jnp.dot(left, right, preferred_element_type=F32)


def project_back(left, right):
    return lax.dot_general(left, right, NT, preferred_element_type=F32)


def weight_grads(lay, *pairs):
    if lay.native:
        return stack_call(lay.rows, [pair[:2] for pair in pairs], [count for _, _, count in pairs])
    stacks = []
    for grad, value, count in pairs:
        whole = lax.dot_general(grad, value, TN, preferred_element_type=F32)[:count].astype(BF16)
        stacks.append(jnp.moveaxis(whole.reshape(count, lay.rows, -1), 1, 0))
    return jnp.concatenate(stacks, axis=1)


def after(value, *others):
    return lax.optimization_barrier((value,) + others)[0]


class Plan:
    def __init__(self, mesh, heads):
        dp, self.rows, self.cols = (mesh.shape[name] for name in ("dp", "row", "col"))
        ways = dp
        while dp % ways or (heads // self.cols) % ways:
            ways -= 1
        self.ways = ways
        if ways == dp:
            self.mesh, self.shared, self.part = mesh, (), "dp"
        else:
            devices = mesh.devices.reshape(dp // ways, ways, self.rows, self.cols)
            self.mesh = Mesh(devices, ("group", "part", "row", "col"))
            self.shared, self.part = ("group",), "part"
        self.data = self.shared + (self.part,)
        self.team = (self.part, "col")
        self.native = (ways, self.rows, self.cols) == (4, 4, 2) and heads == 2 * ways * self.cols
        self.next_id = 0

    def fresh_id(self):
        self.next_id += 1
        return self.next_id


def spread(lay, values):
    local = values.shape[0]
    whole = lax.all_gather(values, "col", axis=0, tiled=True)
    whole = lax.all_to_all(whole, "row", split_axis=0, concat_axis=1, tiled=True)
    mine = local // lay.rows
    return lax.dynamic_slice_in_dim(whole, lax.axis_index("col") * mine, mine, 0)


def unspread(lay, value):
    local = value.shape[0] * lay.rows
    whole = lax.all_gather(value, "col", axis=0, tiled=True)
    whole = lax.all_to_all(whole, "row", split_axis=1, concat_axis=0, tiled=True)
    return lax.dynamic_slice_in_dim(whole, lax.axis_index("col") * local, local, 0)


def team_gather(lay, values):
    return lax.all_gather(values, lay.team, axis=0, tiled=True)


def team_scatter(lay, values):
    return lax.psum_scatter(values.astype(BF16), lay.team, scatter_dimension=0, tiled=True).astype(F32)


def norm_forward(values):
    scale = lax.rsqrt(jnp.mean(values * values, axis=1, keepdims=True) + 1e-05)
    return values * scale, scale


def norm_backward(grad, values, gain):
    normed, scale = norm_forward(values)
    scaled = grad * gain
    inner = jnp.mean(scaled * normed, axis=1, keepdims=True)
    return scale * (scaled - normed * inner), jnp.sum(grad * normed, axis=0, keepdims=True)


def enter(lay, values, grads, gains, segments, weight):
    if lay.native:
        return enter_call(lay, values, grads, gains, segments, weight)
    mine, grads = spread(lay, values), spread(lay, grads)
    gains, weight = (lax.all_gather(value, "row", axis=0, tiled=False) for value in (gains, weight))
    segments = lax.all_gather(segments, lay.part, axis=0, tiled=False)
    normed, _ = norm_forward(mine.astype(F32))
    everyone = team_gather(lay, (normed * gains[:, 0].reshape(1, -1)).astype(BF16))
    return mine, everyone, grads, team_gather(lay, grads), gains, segments, weight


def beside(stack, start, size):
    return jnp.moveaxis(stack[:, start : start + size], 0, 1).reshape(size, -1)


def own_mix(lay, heads, mix, decay):
    part = lax.axis_index(lay.part)
    mix = lax.dynamic_slice_in_dim(mix, part * heads * PER_HEAD, heads * PER_HEAD, 1).T
    decay = lax.dynamic_slice_in_dim(decay, part * 2 * heads, 2 * heads, 1).T
    decay = jnp.pad(decay, ((0, DECAY_ROWS - 2 * heads), (0, 0)))
    return jnp.concatenate([mix[:PER_HEAD], decay, mix[PER_HEAD:]], axis=0)


def own_units(lay, cuts, gate, up, down):
    start, size = lax.axis_index(lay.part) * cuts[-1], cuts[-1]
    gate, up = (lax.dynamic_slice_in_dim(values, start, size, 1).T for values in (gate, up))
    down = lax.dynamic_slice_in_dim(down, start, size, 0)
    return [
        jnp.concatenate([values[first:last] for values in (gate, up, down)], axis=0)
        for first, last in zip(cuts[:-1], cuts[1:])
    ]


def mid_step(lay, mixed, out_all, stored, gain):
    starts = [head * DV for head in range(len(mixed))]
    if lay.native:
        return mid_call(lay, mixed, out_all, [(start, DV) for start in starts], stored, gain)
    total = sum(project(left, beside(out_all, start, DV)) for left, start in zip(mixed, starts))
    residual = stored.astype(F32) + team_scatter(lay, total)
    normed, _ = norm_forward(residual)
    return residual, team_gather(lay, (normed * gain).astype(BF16))


def feed_forward(lay, values, grads, stack):
    if lay.native:
        return ffn_call(values, grads, stack)
    units = stack.shape[1] // 3
    gate, up = (project_back(values, beside(stack, start, units)) for start in (0, units))
    sig = jax.nn.sigmoid(gate)
    grad = project_back(grads, beside(stack, 2 * units, units))
    grad_gate = grad * up * sig * (1.0 + gate * (1.0 - sig))
    both = jnp.concatenate([grad_gate.astype(BF16), (grad * gate * sig).astype(BF16)], axis=1)
    return (gate * sig * up).astype(BF16), both


def branch_step(lay, lefts, stacks, residual, out_grads, gain):
    if lay.native:
        return branch_call(lay, lefts, stacks, residual, out_grads, gain)
    total = sum(project(left, beside(stack, 0, left.shape[1])) for left, stack in zip(lefts, stacks))
    grad, gain_part = norm_backward(team_scatter(lay, total), residual, gain)
    grad = out_grads.astype(F32) + grad
    return grad, team_gather(lay, grad.astype(BF16)), gain_part


def finish_step(lay, hidden, stacks, grads, mix, places, residual, stored, grad_residual, gain):
    if lay.native:
        return finish_call(lay, hidden, stacks, grads, mix, places, residual, stored, grad_residual, gain)
    total = sum(
        project(left, beside(stack, 2 * left.shape[1], left.shape[1])) for left, stack in zip(hidden, stacks)
    )
    block_output = (residual + team_scatter(lay, total)).astype(BF16)
    total = sum(project(left[:, :size], beside(mix, start, size)) for left, (start, size) in zip(grads, places))
    grad, gain_part = norm_backward(team_scatter(lay, total), stored.astype(F32), gain)
    return block_output, (grad_residual + grad).astype(BF16), gain_part


def columns(stack):
    return jnp.moveaxis(stack, 2, 0).reshape(stack.shape[2], -1).astype(F32)


def on_device(
    lay,
    block_input,
    segment_ids,
    attn_gain,
    mix_weight,
    decay_weight,
    conv_weight,
    decay_log,
    decay_bias,
    out_gain,
    out_weight,
    ffn_gain,
    gate_weight,
    up_weight,
    down_weight,
    cotangent,
):
    part = lax.axis_index(lay.part)
    heads = decay_log.shape[0] // lay.ways
    units = gate_weight.shape[1] // lay.ways
    width = mix_weight.shape[0]

    def mine(values, dim, size):
        return lax.dynamic_slice_in_dim(values, part * size, size, dim)

    def gather_rows(values):
        return lax.all_gather(values, "row", axis=0, tiled=False)

    places = [(0, PER_HEAD + DECAY_ROWS)]
    for head in range(1, heads):
        places.append((sum(places[-1]), PER_HEAD))
    out_all = gather_rows(mine(out_weight, 0, heads * DV))
    cuts = [0, min(units, 320), units]
    if lay.native:
        mix_mine, *unit_blocks = own_call(
            lay, cuts, heads, mix_weight, decay_weight, gate_weight, up_weight, down_weight
        )
    else:
        mix_mine = own_mix(lay, heads, mix_weight, decay_weight)
        unit_blocks = own_units(lay, cuts, gate_weight, up_weight, down_weight)
    conv_mine = mine(conv_weight, 1, heads * INNER)
    log_mine, bias_mine = mine(decay_log, 0, heads), mine(decay_bias, 0, heads)

    gains = jnp.stack([attn_gain, ffn_gain])
    stored, attn_all, out_grads, out_grads_all, gains, segments, mix_all = enter(
        lay, block_input, cotangent, gains, segment_ids.reshape(1, -1), after(mix_mine, *unit_blocks)
    )
    gain_one, gain_two = gains[:, 0].reshape(1, -1), gains[:, 1].reshape(1, -1)
    seg_row = segments.reshape(-1, 1, SEQ)
    waiting = lax.optimization_barrier((*unit_blocks, attn_all))[:-1]
    stacks = [gather_rows(values) for values in waiting]
    tokens = attn_all.shape[0]
    shared = (seg_row, conv_mine, log_mine, bias_mine, out_gain.reshape(1, -1))
    mixed, solves, projs, extra = [], [], [], None
    for head in range(heads):
        values, solve, proj, *made = mixer_forward(
            head, places[head][0], after(attn_all, *mixed), mix_all, extra, *shared
        )
        extra = made[0] if made else extra
        mixed.append(values)
        solves.append(solve)
        projs.append(proj)
    residual, ffn_all = mid_step(lay, mixed, out_all, stored, gain_two)

    def sum_rows(grads):
        grads = lax.psum_scatter(grads, "row", scatter_dimension=0, tiled=False)
        return lax.psum(grads, lay.shared) if lay.shared else grads

    hidden, grad_both, ffn_grads = [], [], []
    for stack in stacks:
        values, grads = feed_forward(lay, ffn_all, out_grads_all, stack)
        count = values.shape[1]
        ffn_part = weight_grads(lay, (grads, ffn_all, 2 * count), (values, out_grads_all, count))
        ffn_all, values, grads = lax.optimization_barrier((ffn_all, values, grads, ffn_part))[:3]
        hidden.append(values)
        grad_both.append(grads)
        ffn_grads.append(sum_rows(ffn_part))
    grad_residual, branch_all, ffn_gain_part = branch_step(lay, grad_both, stacks, residual, out_grads, gain_two)

    branch = branch_all
    if lay.native:
        branch = after(branch, ffn_grads[0])
        crossed = [cross(lay, grads) for grads in ffn_grads]
    other = jnp.zeros((tokens, 128), BF16)
    proj_grads, mix_grads, conv_parts, small_parts = [], [], [], []
    for head in reversed(range(heads)):
        common = (head, projs[head], extra, *shared, solves[head], branch, out_all)
        if head:
            grad, passed, conv_part, small_part = mixer_backward(*common, None)
            if lay.native:
                grad = after(grad, crossed[0])
            other = other + passed
        else:
            grad, conv_part, small_part = mixer_backward(*common, other)
            if lay.native:
                grad = after(grad, *crossed)
        triples = [(grad, attn_all, PER_HEAD if head else PER_HEAD + DECAY_ROWS)]
        if head == heads - 1:
            triples += [(values, branch_all, DV) for values in mixed]
        mix_part = weight_grads(lay, *triples)
        branch, grad = lax.optimization_barrier((branch, grad, mix_part))[:2]
        if lay.native:
            branch = after(branch, *ffn_grads[1:])
        proj_grads.insert(0, grad)
        conv_parts.insert(0, conv_part.sum(0))
        small_parts.insert(0, small_part.sum(0)[0])
        mix_grads.insert(0, sum_rows(mix_part))
    if lay.native:
        ffn_pieces = [[ffn_grads[0], crossed[0], link(lay, ffn_grads[0]), link(lay, crossed[0])]]
        hidden[0] = after(hidden[0], *ffn_pieces[0])
    block_output, input_grad, attn_gain_part = finish_step(
        lay, hidden, stacks, proj_grads, mix_all, places, residual, stored, grad_residual, gain_one
    )

    conv_part = jnp.concatenate(conv_parts, axis=1)
    rest_part = jnp.concatenate([part_of[DV + item : DV + item + 1] for item in range(2) for part_of in small_parts])
    gain_part = sum(part_of[:DV] for part_of in small_parts)
    row, col = lax.axis_index("row"), lax.axis_index("col")
    if lay.native:
        lines = [conv_part, gain_part, attn_gain_part, ffn_gain_part, jnp.pad(rest_part, (0, 128 - rest_part.size))]
        flat = jnp.concatenate([values.reshape(-1, 128) for values in lines])
        flat = jnp.pad(flat, ((0, SMALL_ROWS - flat.shape[0]), (0, 0)))
        order = part_order(lay)
        for grads, passed in zip(ffn_grads[1:], crossed[1:]):
            ffn_pieces.append([grads, passed, link(lay, grads), link(lay, passed)])
        late = after(mix_grads[1], block_output)
        late_passed = cross(lay, late)
        ffn_pieces[0][0] = after(ffn_pieces[0][0], block_output)
        gate_grad, up_grad, down_weight_grad = place_ffn(order, ffn_pieces)
        passed = after(late_passed, gate_grad)
        late_pieces = [late, passed, link(lay, late), link(lay, passed)]
        out_weight_grad = place_rows(order, late_pieces, PER_HEAD, heads * DV)
        mix_grad = place_late_head(order, heads, 1, late_pieces)
        first = after(mix_grads[0], mix_grad)
        flat = after(flat, mix_grad, out_weight_grad)
        block_output, input_grad, first_stack, sums = leave_call(lay, block_output, input_grad, first, flat)
        mix_grad, decay_grad, conv_grad, gain_sum, attn_sum, ffn_sum, rest, block_output, input_grad = close_call(
            heads, first_stack, mix_grad, sums, block_output, input_grad
        )
        block_output, input_grad = (value.reshape(-1, value.shape[2]) for value in (block_output, input_grad))
        decay_grad, gain_sum = decay_grad.T, gain_sum.reshape(-1)
        attn_gain_grad, ffn_gain_grad = attn_sum.reshape(-1), ffn_sum.reshape(-1)
        log_grad, bias_grad = rest[:, :heads].reshape(-1), rest[:, heads : 2 * heads].reshape(-1)
    else:
        block_output, input_grad = unspread(lay, block_output), unspread(lay, input_grad)
        own = jnp.concatenate([conv_part.reshape(-1), rest_part])
        pick = (jnp.arange(lay.ways * lay.cols) == part * lay.cols + col).astype(F32)[:, None]
        sums, gain_sum, ffn_sum, attn_sum = lax.psum(
            (pick * own[None, :], gain_part, ffn_gain_part[0], attn_gain_part[0]), lay.data + ("row", "col")
        )
        sums = lax.dynamic_index_in_dim(sums.reshape(lay.ways, lay.cols, -1), col, 1, keepdims=False)
        split = conv_part.size
        conv_grad = jnp.moveaxis(sums[:, :split].reshape(lay.ways, TAPS, -1), 0, 1).reshape(TAPS, -1)
        log_grad = sums[:, split : split + heads].reshape(-1)
        bias_grad = sums[:, split + heads :].reshape(-1)
        attn_gain_grad = lax.dynamic_slice_in_dim(attn_sum, row * width, width, 0)
        ffn_gain_grad = lax.dynamic_slice_in_dim(ffn_sum, row * width, width, 0)

    out_start = PER_HEAD if heads > 1 else PER_HEAD + DECAY_ROWS
    if not lay.native:
        mix_stacks = [lax.all_gather(value, lay.part, axis=0, tiled=False) for value in mix_grads]
        ffn_stacks = [lax.all_gather(value, lay.part, axis=0, tiled=False) for value in ffn_grads]
        decay_grad = columns(mix_stacks[0][:, PER_HEAD : PER_HEAD + 2 * heads])
        mix_grad = columns(jnp.concatenate([stack[:, :PER_HEAD] for stack in mix_stacks], axis=1))
        gate_grad, up_grad, down_weight_grad = (
            jnp.concatenate([jnp.split(stack, 3, axis=1)[item] for stack in ffn_stacks], axis=1) for item in range(3)
        )
        gate_grad, up_grad = columns(gate_grad), columns(up_grad)
        down_weight_grad = down_weight_grad.reshape(-1, width).astype(F32)
        out_weight_grad = mix_stacks[-1][:, out_start : out_start + heads * DV].reshape(-1, width).astype(F32)
    return (
        block_output,
        input_grad,
        attn_gain_grad,
        mix_grad,
        decay_grad,
        conv_grad,
        log_grad,
        bias_grad,
        gain_sum,
        out_weight_grad,
        ffn_gain_grad,
        gate_grad,
        up_grad,
        down_weight_grad,
    )


def solution(mesh):
    def run(*args):
        lay = Plan(mesh, args[6].shape[0])
        tokens, grid = P(lay.data + ("col",), "row"), P("row", "col")
        turned, features, inner = P("col", "row"), P("row"), P("col")
        conv = P(None, "col")
        return jax.shard_map(
            functools.partial(on_device, lay),
            mesh=lay.mesh,
            in_specs=(
                tokens, P(lay.data + ("row",)), features, grid, grid, conv, inner, inner, P(),
                turned, features, grid, grid, turned, tokens,
            ),
            out_specs=(
                tokens, tokens, features, grid, grid, conv, inner, inner, P(),
                turned, features, grid, grid, turned,
            ),
            check_vma=False,
        )(*args)

    return run
```
